32 devices in a mesh: batch: 4 (over z), dp: 4 (over y, x), narrow: 2 (over core).
Axes of the slice: x: 2, y: 2, z: 4, core: 2. Of those that a mesh axis runs over, the one named last changes fastest.
Arguments:
- tokens: bfloat16 [36864, 1024], P(('batch', 'dp', 'narrow')), may hold values from -6 to 6
- row_kind: int32 [32], P(('batch', 'dp', 'narrow')), may hold values 0 or 1
- text_length: int32 [32, 3], P(('batch', 'dp', 'narrow')), may hold values from 1 to 128, as said below
- gain_attn: bfloat16 [1024], P(('dp', 'narrow')), may hold values from 0.099609375 to 1.8984375
- position_bias_table: bfloat16 [512], P(('dp', 'narrow')), may hold values from -4 to 4
- weight_query: bfloat16 [1024, 1024], P(('dp', 'narrow')), may hold values from -0.09375 to 0.09375
- weight_key: bfloat16 [1024, 1024], P(('dp', 'narrow')), may hold values from -0.09375 to 0.09375
- weight_value: bfloat16 [1024, 1024], P(('dp', 'narrow')), may hold values from -0.1875 to 0.1875
- weight_out: bfloat16 [1024, 1024], P(('dp', 'narrow')), may hold values from -0.5 to 0.5
- gain_ffn: bfloat16 [1024], P(('dp', 'narrow')), may hold values from 0.099609375 to 1.8984375
- weight_gate: bfloat16 [1024, 2816], P(('dp', 'narrow')), may hold values from -0.1875 to 0.1875
- weight_up: bfloat16 [1024, 2816], P(('dp', 'narrow')), may hold values from -0.1875 to 0.1875
- weight_down: bfloat16 [2816, 1024], P(('dp', 'narrow')), may hold values from -0.109375 to 0.109375
- cotangent: bfloat16 [36864, 1024], P(('batch', 'dp', 'narrow')), may hold values from -6 to 6
Outputs:
- output: bfloat16 [36864, 1024], P(('batch', 'dp', 'narrow'))
- grad_tokens: float32 [36864, 1024], P(('batch', 'dp', 'narrow'))
- grad_gain_attn: float32 [1024], P(('dp', 'narrow'))
- grad_bias_table: float32 [512], P(('dp', 'narrow'))
- grad_weight_query: float32 [1024, 1024], P(('dp', 'narrow'))
- grad_weight_key: float32 [1024, 1024], P(('dp', 'narrow'))
- grad_weight_value: float32 [1024, 1024], P(('dp', 'narrow'))
- output_weight_gradient: float32 [1024, 1024], P(('dp', 'narrow'))
- grad_gain_ffn: float32 [1024], P(('dp', 'narrow'))
- grad_weight_gate: float32 [1024, 2816], P(('dp', 'narrow'))
- grad_weight_up: float32 [1024, 2816], P(('dp', 'narrow'))
- grad_weight_down: float32 [2816, 1024], P(('dp', 'narrow'))
The draws below stay inside these ranges and needn't reach their ends.
Inputs may be any that keep to these rules, and one draw needn't show every extreme that they name: `row_kind`: 0: the row holds one image of 1024 patches and its text; 1: three images of 256 patches, each followed by its text. `text_length`: live text tokens after each image of a row, in order; a row of kind 0 uses only the first entry.
All inputs are finite; a program needn't handle non-finite values. No bound on the sum of `row_kind` on one device may be relied on, other than what follows from the above.
Results may differ from the reference program's by a relative error of at most 0.018.
Values may be sent and summed in bfloat16 or wider, within the bound.
A program may use at most 256 MiB of HBM per device.

```python
import jax
import jax.numpy as jnp
from jax import lax

D = 1024
HEADS = 16
HEAD_DIM = 64
FF = 2816
BUCKETS = 32
PATCH_SHORT = 256
TEXT = 128
PATCH_LONG = 1024
ROW_LEN = 1152
ROWS = 32
TOKENS = 36864


def draw_text_length(key, part):
    drawn = jax.random.randint(key, (ROWS, 3), 1, TEXT + 1, dtype=jnp.int32)
    drawn = drawn.at[0, 0].set(TEXT)
    drawn = drawn.at[0, 1].set(1)
    return drawn


def with_ends(values, rng, low, high):
    longest = values.shape.index(max(values.shape))
    spots = []
    for shift in (0, 1):
        where = [jax.random.randint(jax.random.fold_in(rng, axis), (), 0, length) for axis, length in enumerate(values.shape)]
        where[longest] = (where[longest] + shift) % values.shape[longest]
        spots.append(tuple(where))
    return values.at[spots[0]].set(low).at[spots[1]].set(high)


def levels(stream_key, extent, pieces, low, largest):
    level, own = 1.0, jax.random.fold_in(stream_key, 6)
    for position, shards_of in pieces:
        steps = jnp.exp(jax.random.uniform(jax.random.fold_in(own, position), (shards_of,), jnp.float32, low / len(pieces), largest / len(pieces)))
        level = level * jnp.repeat(steps, extent[position] // shards_of).reshape([-1 if axis == position else 1 for axis in range(len(extent))])
    return level


def normal_values(stream_key, extent, width, most, cuts=(), kind=jnp.bfloat16):
    values = jax.random.normal(stream_key, extent, jnp.float32) * width
    if len(cuts) > 0:
        values = levels(stream_key, extent, cuts, -0.22, 0.18) * values
    return jnp.clip(values, min=-most, max=most).astype(kind)


def setup_inputs(seed: int = 0) -> dict:
    arg_keys = jax.random.split(jax.random.key(seed), 15)
    tokens = normal_values(arg_keys[0], (TOKENS, D), 1.0, 6.0, ((0, 32),))
    row_kind = with_ends((jax.random.randint(arg_keys[1], (ROWS,), 0, 2) < 1).astype(jnp.int32), jax.random.fold_in(arg_keys[1], 1), 0, 1)
    text_length = draw_text_length(jax.random.fold_in(arg_keys[14], 71), 0)
    gain_attn = jnp.clip(1.0 + 0.18 * jax.random.normal(arg_keys[3], (D,), jnp.float32), 0.099609375, 1.8984375).astype(jnp.bfloat16)
    position_bias_table = normal_values(arg_keys[4], (HEADS * BUCKETS,), 1.0, 4.0, ((0, 8),))
    weight_query = normal_values(arg_keys[5], (D, D), (4 * D) ** -0.5, 0.09375, ((0, 8),))
    weight_key = normal_values(arg_keys[6], (D, D), (4 * D) ** -0.5, 0.09375, ((0, 8),))
    weight_value = normal_values(arg_keys[7], (D, D), D ** -0.5, 0.1875, ((0, 8),))
    weight_out = normal_values(arg_keys[8], (D, D), (D // 8) ** -0.5, 0.5, ((0, 8),))
    gain_ffn = jnp.clip(1.0 + 0.18 * jax.random.normal(arg_keys[9], (D,), jnp.float32), 0.099609375, 1.8984375).astype(jnp.bfloat16)
    weight_gate = normal_values(arg_keys[10], (D, FF), D ** -0.5, 0.1875, ((0, 8),))
    weight_up = normal_values(arg_keys[11], (D, FF), D ** -0.5, 0.1875, ((0, 8),))
    weight_down = normal_values(arg_keys[12], (FF, D), FF ** -0.5, 0.109375, ((0, 8),))
    cotangent = normal_values(arg_keys[13], (TOKENS, D), 1.0, 6.0, ((0, 32),))
    return {"tokens": tokens, "row_kind": row_kind, "text_length": text_length, "gain_attn": gain_attn, "position_bias_table": position_bias_table, "weight_query": weight_query, "weight_key": weight_key, "weight_value": weight_value, "weight_out": weight_out, "gain_ffn": gain_ffn, "weight_gate": weight_gate, "weight_up": weight_up, "weight_down": weight_down, "cotangent": cotangent}


EPS = 1e-06
THRESHOLDS = (12, 16, 23, 32, 46, 64, 91)

@jax.custom_vjp
def low(v):
    return lax.optimization_barrier(v.astype(jnp.bfloat16)).astype(jnp.float32)

@jax.custom_vjp
def low_back(v):
    return v

def low_keep(v):
    return (low(v), None)

def low_pass(kept, grad):
    return (grad,)

def back_keep(v):
    return (v, None)

def backward_reduced(kept, grad):
    return (low(grad),)
low.defvjp(low_keep, low_pass)
low_back.defvjp(back_keep, backward_reduced)

def bucket_ids(length):
    offsets = jnp.arange(2 * length - 1, dtype=jnp.int32) - (length - 1)
    distance = jnp.abs(offsets)
    coarse = jnp.full_like(distance, BUCKETS // 4)
    for bound_value in THRESHOLDS:
        coarse = coarse + (distance >= bound_value).astype(jnp.int32)
    near_mask = distance < BUCKETS // 4
    return jnp.where(near_mask, distance, coarse) + BUCKETS // 2 * (offsets > 0).astype(jnp.int32)

def bucket_onehot(length):
    ids_all = bucket_ids(length)
    return (jnp.arange(BUCKETS, dtype=jnp.int32)[:, None] == ids_all[None, :]).astype(jnp.float32)

def row_layout(row_kind, text_length, length):
    positions = jnp.arange(length, dtype=jnp.int32)
    span_size = PATCH_SHORT + TEXT
    segment = row_kind[:, None] * (positions[None, :] // span_size)
    offsets = positions[None, :] - segment * span_size
    image_len = PATCH_LONG - (PATCH_LONG - PATCH_SHORT) * row_kind
    live_text = jnp.zeros_like(segment)
    for slot_index in range(3):
        live_text = live_text + jnp.where(segment == slot_index, text_length[:, slot_index:slot_index + 1], 0)
    valid_mask = offsets < image_len[:, None] + live_text
    return (segment, valid_mask)

def rms_norm(inputs, gain):
    return inputs * lax.rsqrt(lax.optimization_barrier(jnp.mean(inputs * inputs, axis=-1, keepdims=True)) + EPS) * gain

def matmul(left, right):
    return jnp.dot(left, right, precision=lax.Precision.HIGHEST)

def reference(tokens, row_kind, text_length, gain_attn, position_bias_table, weight_query, weight_key, weight_value, weight_out, gain_ffn, weight_gate, weight_up, weight_down, cotangent):
    length = ROW_LEN
    row_total = row_kind.shape[0]
    segment, valid_mask = row_layout(row_kind, text_length, length)
    positions = jnp.arange(length, dtype=jnp.int32)
    diff_index = positions[None, :] - positions[:, None] + (length - 1)
    onehot = bucket_onehot(length)
    floats = tuple((weight.astype(jnp.float32) for weight in (gain_attn, position_bias_table, weight_query, weight_key, weight_value, weight_out, gain_ffn, weight_gate, weight_up, weight_down)))

    def forward(inputs, params):
        gain_one, table_rel, query_w, key_w, value_w, out_w, gain_two, gate_w, upper_w, down_w = params
        normalized_rows = low(rms_norm(inputs, gain_one))
        queries = low(low_back(matmul(normalized_rows, query_w)))
        key_all = low(low_back(matmul(normalized_rows, key_w)))
        values = low(low_back(matmul(normalized_rows, value_w)))
        bias_diff = matmul(table_rel.reshape(HEADS, BUCKETS), onehot)
        bias_full = bias_diff[:, diff_index]

        def row_step(bias_carry, row_items):
            row_query, row_key, row_value, row_segment, row_valid = row_items
            scores = jnp.einsum('qhd,khd->hqk', row_query, row_key, precision=lax.Precision.HIGHEST) + bias_carry
            scores = low_back(scores)
            allowed = (row_segment[:, None] == row_segment[None, :]) & row_valid[None, :]
            scores = jnp.where(allowed[None], scores, -1e+30)
            soft_weights = jnp.exp(scores - jax.nn.logsumexp(scores, axis=-1, keepdims=True))
            soft_weights = low(soft_weights)
            attended = jnp.einsum('hqk,khd->qhd', soft_weights, row_value, precision=lax.Precision.HIGHEST)
            return (bias_carry, attended.reshape(length, HEADS * HEAD_DIM))

        def shaped(values_in):
            return values_in.reshape(row_total, length, HEADS, HEAD_DIM)
        _, attended_all = lax.scan(jax.checkpoint(row_step), bias_full, (shaped(queries), shaped(key_all), shaped(values), segment, valid_mask))
        context = low(low_back(attended_all.reshape(row_total * length, HEADS * HEAD_DIM)))
        residual_stream = inputs + low_back(matmul(context, out_w))
        normed_ffn = low(rms_norm(residual_stream, gain_two))
        gate_pre = low_back(matmul(normed_ffn, gate_w))
        up_pre = low_back(matmul(normed_ffn, upper_w))
        hidden = low(jax.nn.gelu(gate_pre, approximate=True) * up_pre)
        return residual_stream + low_back(matmul(hidden, down_w))
    output, pullback = jax.vjp(forward, tokens.astype(jnp.float32), floats)
    grad_input, grad_params = pullback(cotangent.astype(jnp.float32))
    return (output.astype(jnp.bfloat16), grad_input, grad_params[0], grad_params[1], grad_params[2], grad_params[3], grad_params[4], grad_params[5], grad_params[6], grad_params[7], grad_params[8], grad_params[9])
```

```python
import jax
import jax.numpy as jnp
import numpy as np
from jax import lax
from jax.experimental import pallas as pl
from jax.experimental.pallas import tpu as pltpu
from jax.sharding import PartitionSpec as P

bf=jnp.bfloat16; f32=jnp.float32
T=128; L=1152; NT=L//T
NEG=-1e30
def dot(a,b): return jnp.dot(a,b,preferred_element_type=f32)
def dot_tl(a,b): return lax.dot_general(a,b,(((0,),(0,)),((),())),preferred_element_type=f32)

def fwd_kernel(q_ref,k_ref,v_ref,mask_ref,far_ref,w_ref,o_ref,e_ref,r_ref,rhs,kaug,vaug,bn,s_ref):
    @pl.when((pl.program_id(0)==0)&(pl.program_id(1)==0))
    def _():
        rhs[...]=jnp.zeros_like(rhs)
        row=lax.broadcasted_iota(jnp.int32,(128,NT*256),0)
        col=lax.broadcasted_iota(jnp.int32,(128,NT*256),1)
        rhs[128:256,:]=(row==col//128).astype(f32).astype(bf)
        vaug[:,128:256]=jnp.ones((L,128),bf)
    qT=q_ref[...].T
    for i in range(NT):
        rhs[0:64,256*i:256*i+128]=qT[0:64,128*i:128*i+128]
        rhs[64:128,256*i+128:256*i+256]=qT[64:128,128*i:128*i+128]
    kaug[:,0:128]=k_ref[...]
    row=lax.broadcasted_iota(jnp.int32,(L,128),0)//128
    col=lax.broadcasted_iota(jnp.int32,(L,128),1)//2
    far=jnp.where(row<col-1,far_ref[0:1,:],jnp.where(row>col+1,far_ref[1:2,:],0.0))
    kaug[:,128:256]=(mask_ref[...]+far).astype(bf)
    vaug[:,0:128]=v_ref[...]
    for a in range(2):
        wb=jnp.broadcast_to(w_ref[a:a+1,:],(384,512))
        bn[:,128*a:128*a+128]=pltpu.roll(wb,0,1,stride=1,stride_axis=0)[:,0:128]
    def scores(i,slot):
        ri=rhs[:,256*i:256*i+256]
        lo,hi=max(0,i-1)*128,min(NT,i+2)*128
        off=(lo//128-(i-1))*128
        x=dot(kaug[...],ri)
        xn=x[lo:hi]+bn[off:off+hi-lo,:]
        ms=[jnp.max(xn,axis=0,keepdims=True)]
        s_ref[slot,lo:hi,:]=xn
        if lo>0:
            s_ref[slot,0:lo,:]=x[0:lo]; ms.append(jnp.max(x[0:lo],axis=0,keepdims=True))
        if hi<L:
            s_ref[slot,hi:L,:]=x[hi:L]; ms.append(jnp.max(x[hi:L],axis=0,keepdims=True))
        m=ms[0]
        for y in ms[1:]: m=jnp.maximum(m,y)
        return m
    lane=lax.broadcasted_iota(jnp.int32,(128,128),1)<64
    def finish(i,slot,m):
        e=jnp.exp(s_ref[slot]-m).astype(bf)
        e_ref[:,pl.ds(i*256,256)]=e
        o=dot_tl(e,vaug[...])
        num=jnp.where(lane,o[0:128,0:128],o[128:256,0:128])
        den=jnp.where(lane,o[0:128,128:256],o[128:256,128:256])
        r=1.0/den
        rows=pl.ds(i*128,128)
        o_ref[rows,:]=(num*r).astype(bf)
        r_ref[rows,:]=r
    m=scores(0,0)
    for i in range(NT):
        mn=scores(i+1,(i+1)%2) if i+1<NT else None
        finish(i,i%2,m)
        m=mn

def attn_fwd(q,k,v,mask,far,w):
    rows=q.shape[0]//L
    spec=pl.BlockSpec((L,128),lambda r,p:(r,p))
    return pl.pallas_call(fwd_kernel,
        grid=(rows,8),
        in_specs=[spec,spec,spec,
            pl.BlockSpec((None,L,128),lambda r,p:(r,0,0)),
            pl.BlockSpec((None,8,128),lambda r,p:(p,0,0)),
            pl.BlockSpec((None,8,512),lambda r,p:(p,0,0))],
        out_specs=[spec,pl.BlockSpec((None,None,L,NT*256),lambda r,p:(r,p,0,0)),spec],
        out_shape=[jax.ShapeDtypeStruct(q.shape,bf),jax.ShapeDtypeStruct((rows,8,L,NT*256),bf),jax.ShapeDtypeStruct(q.shape,f32)],
        scratch_shapes=[pltpu.VMEM((256,NT*256),bf),pltpu.VMEM((L,256),bf),pltpu.VMEM((L,256),bf),pltpu.VMEM((384,256),f32),pltpu.VMEM((2,L,256),f32)],
        compiler_params=pltpu.CompilerParams(vmem_limit_bytes=56*2**20),
        name="attn_fwd",
    )(q,k,v,mask,far,w)

THR=(12,16,23,32,46,64,91)
def bucket_np(d):
    n=np.abs(d); c=np.full_like(n,8)
    for t in THR: c=c+(n>=t)
    return np.where(n<8,n,c)+16*(d>0)
def tables(table):
    t=table.reshape(16,32).astype(f32)
    y=np.arange(512); y=np.where(y>=128,y-512,y)
    d=-128-y
    oh=(np.arange(32)[:,None]==bucket_np(d)[None,:]).astype(np.float32)
    w=jnp.dot(t,jnp.asarray(oh),precision=lax.Precision.HIGHEST)
    w=jnp.pad(w.reshape(8,2,512),((0,0),(0,6),(0,0)))
    lo=jnp.tile(t[:,15].reshape(8,1,2),(1,1,64)); hi=jnp.tile(t[:,31].reshape(8,1,2),(1,1,64))
    far=jnp.pad(jnp.concatenate([lo,hi],1),((0,0),(0,6),(0,0)))
    return far,w
def mask_cols(row_kind,text_length):
    pos=np.arange(L)
    kind=row_kind[:,None]
    seg=kind*(pos//384)[None]
    off=pos[None]-seg*384
    img=jnp.where(kind==1,256,1024)
    tl=jnp.where(seg==0,text_length[:,0:1],jnp.where(seg==1,text_length[:,1:2],text_length[:,2:3]))
    live=off<img+tl
    qseg=kind*np.minimum(np.arange(128)//2//3,2)[None]
    ok=live[:,:,None]&(seg[:,:,None]==qseg[:,None,:])
    return jnp.where(ok,0.0,NEG).astype(f32)

def bwd_kernel(q_ref,k_ref,v_ref,do_ref,o_ref,r_ref,e_ref,dq_ref,dk_ref,dv_ref,near_ref,far_ref,rhs,vaug,dobd,qaug,ds_ref,nacc):
    @pl.when((pl.program_id(0)==0)&(pl.program_id(1)==0))
    def _():
        rhs[...]=jnp.zeros_like(rhs)
        c=lax.broadcasted_iota(jnp.int32,(L,128),1)
        vaug[:,128:256]=(c<3).astype(f32).astype(bf)
        row=lax.broadcasted_iota(jnp.int32,(NT*256,128),0)
        col=lax.broadcasted_iota(jnp.int32,(NT*256,128),1)
        qaug[:,128:256]=(row//128==col).astype(f32).astype(bf)
    q=q_ref[...]; k=k_ref[...]
    vaug[:,0:128]=v_ref[...]
    dof=do_ref[...].astype(f32)*r_ref[...]
    dos=dof.astype(bf)
    dT=dos.T
    pT=(dos.astype(f32)*o_ref[...].astype(f32)).T
    D=jnp.concatenate([jnp.sum(pT[0:64],axis=0,keepdims=True),jnp.sum(pT[64:128],axis=0,keepdims=True)],0)
    D=-D
    D1=D.astype(bf); D2=(D-D1.astype(f32)); D3=(D2-D2.astype(bf).astype(f32)).astype(bf); D2=D2.astype(bf)
    lane=lax.broadcasted_iota(jnp.int32,(128,128),1)<64
    zero=jnp.zeros((128,128),bf)
    z13=jnp.zeros((13,128),bf)
    for i in range(NT):
        t=slice(128*i,128*i+128)
        for a in range(2):
            h=slice(64*a,64*a+64)
            c=slice(256*i+128*a,256*i+128*a+128)
            rhs[h,c]=dT[h,t]
            rhs[128:144,c]=jnp.concatenate([D1[a:a+1,t],D2[a:a+1,t],D3[a:a+1,t],z13],0)
            dobd[c,:]=jnp.where(lane==(a==0),dos[t],zero)
            qaug[c,0:128]=jnp.where(lane==(a==0),q[t],zero)
    nacc[...]=jnp.zeros_like(nacc)
    for i in range(NT):
        c=slice(256*i,256*i+256)
        lo,hi=max(0,i-1)*128,min(NT,i+2)*128
        off=(lo//128-(i-1))*128
        dp=dot(vaug[...],rhs[:,c])
        ds=e_ref[:,c].astype(f32)*dp
        nacc[off:off+hi-lo,:]+=ds[lo:hi]
        dsb=ds.astype(bf)
        ds_ref[:,c]=dsb
        g=dot_tl(dsb,k)
        dq_ref[128*i:128*i+128,:]=jnp.where(lane,g[0:128],g[128:256]).astype(bf)
    dv_ref[...]=dot(e_ref[...],dobd[...]).astype(bf)
    g=dot(ds_ref[...],qaug[...])
    dk_ref[...]=g[:,0:128].astype(bf)
    G=g[:,128:256]
    row=lax.broadcasted_iota(jnp.int32,(L,128),0)//128
    col=lax.broadcasted_iota(jnp.int32,(L,128),1)//2
    far_ref[0:1,:]=jnp.sum(jnp.where(row<col-1,G,0.0),axis=0,keepdims=True)
    far_ref[1:2,:]=jnp.sum(jnp.where(row>col+1,G,0.0),axis=0,keepdims=True)
    far_ref[2:8,:]=jnp.zeros((6,128),f32)
    near_ref[2:8,:]=jnp.zeros((6,512),f32)
    rev=(lax.broadcasted_iota(jnp.int32,(128,128),0)+lax.broadcasted_iota(jnp.int32,(128,128),1)==127).astype(f32)
    for a in range(2):
        x=jnp.dot(nacc[:,128*a:128*a+128],rev,precision=lax.Precision.HIGHEST,preferred_element_type=f32)
        x=jnp.concatenate([x,jnp.zeros((384,384),f32)],1)
        x=pltpu.roll(x,0,1,stride=1,stride_axis=0)
        near_ref[a:a+1,:]=jnp.sum(x,axis=0,keepdims=True)
def attn_bwd(q,k,v,do,o,r,e):
    rows=q.shape[0]//L
    spec=pl.BlockSpec((L,128),lambda r,p:(r,p))
    sds=jax.ShapeDtypeStruct
    return pl.pallas_call(bwd_kernel,
        grid=(rows,8),
        in_specs=[spec]*6+[pl.BlockSpec((None,None,L,NT*256),lambda r,p:(r,p,0,0))],
        out_specs=[spec]*3+[pl.BlockSpec((None,None,8,512),lambda r,p:(r,p,0,0)),pl.BlockSpec((None,None,8,128),lambda r,p:(r,p,0,0))],
        out_shape=[sds(q.shape,bf)]*3+[sds((rows,8,8,512),f32),sds((rows,8,8,128),f32)],
        scratch_shapes=[pltpu.VMEM((256,NT*256),bf),pltpu.VMEM((L,256),bf),pltpu.VMEM((NT*256,128),bf),pltpu.VMEM((NT*256,256),bf),pltpu.VMEM((L,NT*256),bf),pltpu.VMEM((384,256),f32)],
        compiler_params=pltpu.CompilerParams(vmem_limit_bytes=58*2**20),
        name="attn_bwd",
    )(q,k,v,do,o,r,e)
def table_grad(near,far):
    y=np.arange(512)
    oh=(bucket_np(y-255)[:,None]==np.arange(32)[None,:]).astype(np.float32)
    n=jnp.sum(near[:,:,0:2],0).reshape(16,512)
    g=jnp.dot(n,jnp.asarray(oh),precision=lax.Precision.HIGHEST)
    f=jnp.sum(far[:,:,0:2],0).reshape(8,2,64,2).sum(2)
    lo=f[:,0].reshape(16,1); hi=f[:,1].reshape(16,1)
    g=g+lo*np.eye(32,dtype=np.float32)[15][None]+hi*np.eye(32,dtype=np.float32)[31][None]
    return g.reshape(512)

EPS = 1e-06
SHARD = ("dp", "narrow")

def rms_norm(inputs, gain):
    return inputs * lax.rsqrt(jnp.mean(inputs * inputs, axis=-1, keepdims=True) + EPS) * gain

def gated(gate_in, up_in):
    return jax.nn.gelu(gate_in, approximate=True) * up_in

def contract_rows(left, right):
    return lax.dot_general(left, right, (((0,), (0,)), ((), ())), preferred_element_type=f32)

def contract_cols(left, right):
    return lax.dot_general(left, right, (((1,), (1,)), ((), ())), preferred_element_type=f32)

def gather(x):
    return lax.all_gather(x, SHARD, axis=0, tiled=True)

def scatter(x):
    return lax.psum_scatter(x, SHARD, scatter_dimension=0, tiled=True)

def per_device(tokens, row_kind, text_length, gain_attn, position_bias_table, weight_query, weight_key, weight_value, weight_out, gain_ffn, weight_gate, weight_up, weight_down, cotangent):
    small = lax.all_gather(jnp.concatenate([gain_attn, gain_ffn, position_bias_table]), SHARD, axis=0, tiled=False)
    qkv_w = gather(jnp.concatenate([weight_query, weight_key, weight_value], 1))
    gu_w = gather(jnp.concatenate([weight_out, weight_gate, weight_up], 1))
    down_w = gather(weight_down)
    d = qkv_w.shape[0]
    ff = weight_gate.shape[1]
    n1 = gain_attn.shape[0]
    gain_one = small[:, :n1].reshape(d).astype(f32)
    gain_two = small[:, n1:2 * n1].reshape(d).astype(f32)
    table = small[:, 2 * n1:].reshape(-1)
    far, w = tables(table)
    mask = mask_cols(row_kind, text_length)
    inputs = tokens.astype(f32)
    normed = rms_norm(inputs, gain_one).astype(bf)
    q = dot(normed, qkv_w[:, :d]).astype(bf)
    k = dot(normed, qkv_w[:, d:2 * d]).astype(bf)
    v = dot(normed, qkv_w[:, 2 * d:]).astype(bf)
    context, e, r = attn_fwd(q, k, v, mask, far, w)
    out_w, gate_w, up_w = gu_w[:, :d], gu_w[:, d:d + ff], gu_w[:, d + ff:]
    residual = inputs + dot(context, out_w)
    normed_ffn = rms_norm(residual, gain_two).astype(bf)
    gate_pre = dot(normed_ffn, gate_w)
    up_pre = dot(normed_ffn, up_w)
    hidden = gated(gate_pre, up_pre).astype(bf)
    output = (residual + dot(hidden, down_w)).astype(bf)
    grad_output = cotangent.astype(f32)
    grad_down = contract_rows(hidden, cotangent).astype(bf)
    s_down = scatter(grad_down)
    grad_hidden = contract_cols(cotangent, down_w)
    _, gate_pull = jax.vjp(gated, gate_pre, up_pre)
    gg, gu = gate_pull(grad_hidden)
    gg = gg.astype(bf)
    gu = gu.astype(bf)
    grad_normed_ffn = contract_cols(gg, gate_w) + contract_cols(gu, up_w)
    gw_gate = contract_rows(normed_ffn, gg).astype(bf)
    gw_up = contract_rows(normed_ffn, gu).astype(bf)
    _, norm_pull = jax.vjp(rms_norm, residual, gain_two)
    part, g_gain_two = norm_pull(grad_normed_ffn)
    grad_residual = grad_output + part
    gr_low = grad_residual.astype(bf)
    grad_out_w = contract_rows(context, gr_low).astype(bf)
    s_gu = scatter(jnp.concatenate([grad_out_w, gw_gate, gw_up], 1))
    grad_context = contract_cols(gr_low, out_w).astype(bf)
    gq, gk, gv, near, farsum = attn_bwd(q, k, v, grad_context, context, r, e)
    g_table = table_grad(near, farsum)
    gqkv = jnp.concatenate([contract_rows(normed, x).astype(bf) for x in (gq, gk, gv)], 1)
    s_qkv = scatter(gqkv)
    grad_normed = contract_cols(gq, qkv_w[:, :d]) + contract_cols(gk, qkv_w[:, d:2 * d]) + contract_cols(gv, qkv_w[:, 2 * d:])
    _, first_pull = jax.vjp(rms_norm, inputs, gain_one)
    share, g_gain_one = first_pull(grad_normed)
    grad_tokens = grad_residual + share
    small_g = jnp.concatenate([g_gain_one, g_gain_two, g_table])
    small_g = lax.psum(small_g, ("batch", "dp", "narrow"))
    at = lax.axis_index("dp") * lax.axis_size("narrow") + lax.axis_index("narrow")
    n2 = position_bias_table.shape[0]
    r_gain_one = lax.dynamic_slice_in_dim(small_g, at * n1, n1)
    r_gain_two = lax.dynamic_slice_in_dim(small_g, d + at * n1, n1)
    r_table = lax.dynamic_slice_in_dim(small_g, 2 * d + at * n2, n2)
    ar = lambda x: lax.psum(x, "batch").astype(f32)
    s_gu, s_down, s_qkv = ar(s_gu), ar(s_down), ar(s_qkv)
    return (output, grad_tokens, r_gain_one, r_table, s_qkv[:, :d], s_qkv[:, d:2 * d], s_qkv[:, 2 * d:], s_gu[:, :d], r_gain_two, s_gu[:, d:d + ff], s_gu[:, d + ff:], s_down)

def solution(mesh):
    placed = (
        P(("batch", "dp", "narrow"), None),
        P(("batch", "dp", "narrow")),
        P(("batch", "dp", "narrow"), None),
        P(("dp", "narrow")),
        P(("dp", "narrow")),
        P(("dp", "narrow"), None),
        P(("dp", "narrow"), None),
        P(("dp", "narrow"), None),
        P(("dp", "narrow"), None),
        P(("dp", "narrow")),
        P(("dp", "narrow"), None),
        P(("dp", "narrow"), None),
        P(("dp", "narrow"), None),
        P(("batch", "dp", "narrow"), None),
    )
    return jax.shard_map(
        per_device,
        mesh=mesh,
        in_specs=placed,
        out_specs=(
            P(("batch", "dp", "narrow"), None),
            P(("batch", "dp", "narrow"), None),
            P(("dp", "narrow")),
            P(("dp", "narrow")),
            P(("dp", "narrow"), None),
            P(("dp", "narrow"), None),
            P(("dp", "narrow"), None),
            P(("dp", "narrow"), None),
            P(("dp", "narrow")),
            P(("dp", "narrow"), None),
            P(("dp", "narrow"), None),
            P(("dp", "narrow"), None),
        ),
        check_vma=False,
    )
```

```python
import functools

import jax
import jax.numpy as jnp
import numpy as np
from jax import lax
from jax.experimental import pallas as pl
from jax.experimental.pallas import tpu as pltpu
from jax.sharding import PartitionSpec as P

EPS = 1e-06
SHARD = ("dp", "narrow")
bf=jnp.bfloat16; f32=jnp.float32
T=128; L=1152; NT=L//T
NEG=-1e30
def dot(a,b): return jnp.dot(a,b,preferred_element_type=f32)
def dot_tl(a,b): return lax.dot_general(a,b,(((0,),(0,)),((),())),preferred_element_type=f32)

def fwd_kernel(q_ref,k_ref,v_ref,mask_ref,far_ref,w_ref,o_ref,e_ref,r_ref,rhs,kaug,vaug,bn,s_ref):
    @pl.when((pl.program_id(0)==0)&(pl.program_id(1)==0))
    def _():
        rhs[...]=jnp.zeros_like(rhs)
        row=lax.broadcasted_iota(jnp.int32,(128,NT*256),0)
        col=lax.broadcasted_iota(jnp.int32,(128,NT*256),1)
        rhs[128:256,:]=(row==col//128).astype(f32).astype(bf)
        vaug[:,128:256]=jnp.ones((L,128),bf)
    qT=q_ref[...].T
    for i in range(NT):
        rhs[0:64,256*i:256*i+128]=qT[0:64,128*i:128*i+128]
        rhs[64:128,256*i+128:256*i+256]=qT[64:128,128*i:128*i+128]
    kaug[:,0:128]=k_ref[...]
    row=lax.broadcasted_iota(jnp.int32,(L,128),0)//128
    col=lax.broadcasted_iota(jnp.int32,(L,128),1)//2
    far=jnp.where(row<col-1,far_ref[0:1,:],jnp.where(row>col+1,far_ref[1:2,:],0.0))
    kaug[:,128:256]=(mask_ref[...]+far).astype(bf)
    vaug[:,0:128]=v_ref[...]
    for a in range(2):
        wb=jnp.broadcast_to(w_ref[a:a+1,:],(384,512))
        bn[:,128*a:128*a+128]=pltpu.roll(wb,0,1,stride=1,stride_axis=0)[:,0:128]
    def scores(i,slot):
        ri=rhs[:,256*i:256*i+256]
        lo,hi=max(0,i-1)*128,min(NT,i+2)*128
        off=(lo//128-(i-1))*128
        x=dot(kaug[...],ri)
        xn=x[lo:hi]+bn[off:off+hi-lo,:]
        ms=[jnp.max(xn,axis=0,keepdims=True)]
        s_ref[slot,lo:hi,:]=xn
        if lo>0:
            s_ref[slot,0:lo,:]=x[0:lo]; ms.append(jnp.max(x[0:lo],axis=0,keepdims=True))
        if hi<L:
            s_ref[slot,hi:L,:]=x[hi:L]; ms.append(jnp.max(x[hi:L],axis=0,keepdims=True))
        m=ms[0]
        for y in ms[1:]: m=jnp.maximum(m,y)
        return m
    lane=lax.broadcasted_iota(jnp.int32,(128,128),1)<64
    def finish(i,slot,m):
        e=jnp.exp(s_ref[slot]-m).astype(bf)
        e_ref[:,pl.ds(i*256,256)]=e
        o=dot_tl(e,vaug[...])
        num=jnp.where(lane,o[0:128,0:128],o[128:256,0:128])
        den=jnp.where(lane,o[0:128,128:256],o[128:256,128:256])
        r=1.0/den
        rows=pl.ds(i*128,128)
        o_ref[rows,:]=(num*r).astype(bf)
        r_ref[rows,:]=r
    m=scores(0,0)
    for i in range(NT):
        mn=scores(i+1,(i+1)%2) if i+1<NT else None
        finish(i,i%2,m)
        m=mn

def attn_fwd(q,k,v,mask,far,w):
    rows=q.shape[0]//L
    spec=pl.BlockSpec((L,128),lambda r,p:(r,p))
    return pl.pallas_call(fwd_kernel,
        grid=(rows,8),
        in_specs=[spec,spec,spec,
            pl.BlockSpec((None,L,128),lambda r,p:(r,0,0)),
            pl.BlockSpec((None,8,128),lambda r,p:(p,0,0)),
            pl.BlockSpec((None,8,512),lambda r,p:(p,0,0))],
        out_specs=[spec,pl.BlockSpec((None,None,L,NT*256),lambda r,p:(r,p,0,0)),spec],
        out_shape=[jax.ShapeDtypeStruct(q.shape,bf),jax.ShapeDtypeStruct((rows,8,L,NT*256),bf),jax.ShapeDtypeStruct(q.shape,f32)],
        scratch_shapes=[pltpu.VMEM((256,NT*256),bf),pltpu.VMEM((L,256),bf),pltpu.VMEM((L,256),bf),pltpu.VMEM((384,256),f32),pltpu.VMEM((2,L,256),f32)],
        compiler_params=pltpu.CompilerParams(vmem_limit_bytes=56*2**20),
        name="attn_fwd",
    )(q,k,v,mask,far,w)

THR=(12,16,23,32,46,64,91)
def bucket_np(d):
    n=np.abs(d); c=np.full_like(n,8)
    for t in THR: c=c+(n>=t)
    return np.where(n<8,n,c)+16*(d>0)
def tables(table):
    t=table.reshape(16,32).astype(f32)
    y=np.arange(512); y=np.where(y>=128,y-512,y)
    d=-128-y
    oh=(np.arange(32)[:,None]==bucket_np(d)[None,:]).astype(np.float32)
    w=jnp.dot(t,jnp.asarray(oh),precision=lax.Precision.HIGHEST)
    w=jnp.pad(w.reshape(8,2,512),((0,0),(0,6),(0,0)))
    lo=jnp.tile(t[:,15].reshape(8,1,2),(1,1,64)); hi=jnp.tile(t[:,31].reshape(8,1,2),(1,1,64))
    far=jnp.pad(jnp.concatenate([lo,hi],1),((0,0),(0,6),(0,0)))
    return far,w
def mask_cols(row_kind,text_length):
    pos=np.arange(L)
    kind=row_kind[:,None]
    seg=kind*(pos//384)[None]
    off=pos[None]-seg*384
    img=jnp.where(kind==1,256,1024)
    tl=jnp.where(seg==0,text_length[:,0:1],jnp.where(seg==1,text_length[:,1:2],text_length[:,2:3]))
    live=off<img+tl
    qseg=kind*np.minimum(np.arange(128)//2//3,2)[None]
    ok=live[:,:,None]&(seg[:,:,None]==qseg[:,None,:])
    return jnp.where(ok,0.0,NEG).astype(f32)

def bwd_kernel(q_ref,k_ref,v_ref,do_ref,o_ref,r_ref,e_ref,dq_ref,dk_ref,dv_ref,near_ref,far_ref,rhs,vaug,dobd,qaug,ds_ref,nacc):
    @pl.when((pl.program_id(0)==0)&(pl.program_id(1)==0))
    def _():
        rhs[...]=jnp.zeros_like(rhs)
        c=lax.broadcasted_iota(jnp.int32,(L,128),1)
        vaug[:,128:256]=(c<3).astype(f32).astype(bf)
        row=lax.broadcasted_iota(jnp.int32,(NT*256,128),0)
        col=lax.broadcasted_iota(jnp.int32,(NT*256,128),1)
        qaug[:,128:256]=(row//128==col).astype(f32).astype(bf)
    q=q_ref[...]; k=k_ref[...]
    vaug[:,0:128]=v_ref[...]
    dof=do_ref[...].astype(f32)*r_ref[...]
    dos=dof.astype(bf)
    dT=dos.T
    pT=(dos.astype(f32)*o_ref[...].astype(f32)).T
    D=jnp.concatenate([jnp.sum(pT[0:64],axis=0,keepdims=True),jnp.sum(pT[64:128],axis=0,keepdims=True)],0)
    D=-D
    D1=D.astype(bf); D2=(D-D1.astype(f32)); D3=(D2-D2.astype(bf).astype(f32)).astype(bf); D2=D2.astype(bf)
    lane=lax.broadcasted_iota(jnp.int32,(128,128),1)<64
    zero=jnp.zeros((128,128),bf)
    z13=jnp.zeros((13,128),bf)
    for i in range(NT):
        t=slice(128*i,128*i+128)
        for a in range(2):
            h=slice(64*a,64*a+64)
            c=slice(256*i+128*a,256*i+128*a+128)
            rhs[h,c]=dT[h,t]
            rhs[128:144,c]=jnp.concatenate([D1[a:a+1,t],D2[a:a+1,t],D3[a:a+1,t],z13],0)
            dobd[c,:]=jnp.where(lane==(a==0),dos[t],zero)
            qaug[c,0:128]=jnp.where(lane==(a==0),q[t],zero)
    nacc[...]=jnp.zeros_like(nacc)
    for i in range(NT):
        c=slice(256*i,256*i+256)
        lo,hi=max(0,i-1)*128,min(NT,i+2)*128
        off=(lo//128-(i-1))*128
        dp=dot(vaug[...],rhs[:,c])
        ds=e_ref[:,c].astype(f32)*dp
        nacc[off:off+hi-lo,:]+=ds[lo:hi]
        dsb=ds.astype(bf)
        ds_ref[:,c]=dsb
        g=dot_tl(dsb,k)
        dq_ref[128*i:128*i+128,:]=jnp.where(lane,g[0:128],g[128:256]).astype(bf)
    dv_ref[...]=dot(e_ref[...],dobd[...]).astype(bf)
    g=dot(ds_ref[...],qaug[...])
    dk_ref[...]=g[:,0:128].astype(bf)
    G=g[:,128:256]
    row=lax.broadcasted_iota(jnp.int32,(L,128),0)//128
    col=lax.broadcasted_iota(jnp.int32,(L,128),1)//2
    far_ref[0:1,:]=jnp.sum(jnp.where(row<col-1,G,0.0),axis=0,keepdims=True)
    far_ref[1:2,:]=jnp.sum(jnp.where(row>col+1,G,0.0),axis=0,keepdims=True)
    far_ref[2:8,:]=jnp.zeros((6,128),f32)
    near_ref[2:8,:]=jnp.zeros((6,512),f32)
    rev=(lax.broadcasted_iota(jnp.int32,(128,128),0)+lax.broadcasted_iota(jnp.int32,(128,128),1)==127).astype(f32)
    for a in range(2):
        x=jnp.dot(nacc[:,128*a:128*a+128],rev,precision=lax.Precision.HIGHEST,preferred_element_type=f32)
        x=jnp.concatenate([x,jnp.zeros((384,384),f32)],1)
        x=pltpu.roll(x,0,1,stride=1,stride_axis=0)
        near_ref[a:a+1,:]=jnp.sum(x,axis=0,keepdims=True)
def attn_bwd(q,k,v,do,o,r,e):
    rows=q.shape[0]//L
    spec=pl.BlockSpec((L,128),lambda r,p:(r,p))
    sds=jax.ShapeDtypeStruct
    return pl.pallas_call(bwd_kernel,
        grid=(rows,8),
        in_specs=[spec]*6+[pl.BlockSpec((None,None,L,NT*256),lambda r,p:(r,p,0,0))],
        out_specs=[spec]*3+[pl.BlockSpec((None,None,8,512),lambda r,p:(r,p,0,0)),pl.BlockSpec((None,None,8,128),lambda r,p:(r,p,0,0))],
        out_shape=[sds(q.shape,bf)]*3+[sds((rows,8,8,512),f32),sds((rows,8,8,128),f32)],
        scratch_shapes=[pltpu.VMEM((256,NT*256),bf),pltpu.VMEM((L,256),bf),pltpu.VMEM((NT*256,128),bf),pltpu.VMEM((NT*256,256),bf),pltpu.VMEM((L,NT*256),bf),pltpu.VMEM((384,256),f32)],
        compiler_params=pltpu.CompilerParams(vmem_limit_bytes=58*2**20),
        name="attn_bwd",
    )(q,k,v,do,o,r,e)
def table_grad(near,far):
    y=np.arange(512)
    oh=(bucket_np(y-255)[:,None]==np.arange(32)[None,:]).astype(np.float32)
    n=jnp.sum(near[:,:,0:2],0).reshape(16,512)
    g=jnp.dot(n,jnp.asarray(oh),precision=lax.Precision.HIGHEST)
    f=jnp.sum(far[:,:,0:2],0).reshape(8,2,64,2).sum(2)
    lo=f[:,0].reshape(16,1); hi=f[:,1].reshape(16,1)
    g=g+lo*np.eye(32,dtype=np.float32)[15][None]+hi*np.eye(32,dtype=np.float32)[31][None]
    return g.reshape(512)

MESH = pl.DeviceIdType.MESH

def places():
    b, m, c = lax.axis_index("batch"), lax.axis_index("dp"), lax.axis_index("narrow")
    x, y = lax.rem(m, 2), m // 2
    mx = y * 2 + (1 - x)
    my = (1 - y) * 2 + x
    md = (1 - y) * 2 + (1 - x)
    return b, m, c, mx, my, md

def greet(devices):
    barrier = pltpu.get_barrier_semaphore()
    for d in devices:
        pl.semaphore_signal(barrier, inc=1, device_id=d, device_id_type=MESH)
    pl.semaphore_wait(barrier, len(devices))

def qkv_kernel(x_ref, small_ref, wq_ref, wk_ref, wv_ref, q_ref, k_ref, v_ref, n_ref, w_out, W, acc, xh, send, recv, local):
    b, m, c, mx, my, md = places()
    o = 1 - c
    nx, ny, nc = (b, mx, c), (b, my, c), (b, m, o)
    d = wq_ref.shape[1]
    rows = wq_ref.shape[0]
    half = rows // 2
    me = m * 2 + c
    W[me, :, 0:d] = wq_ref[...]
    W[me, :, d:2 * d] = wk_ref[...]
    W[me, :, 2 * d:3 * d] = wv_ref[...]
    W[me, :, 3 * d:3 * d + 128] = small_ref[...]
    greet([nx, ny, nc])
    def push(src, n, to):
        return pltpu.make_async_remote_copy(src_ref=src, dst_ref=src, send_sem=send.at[n], recv_sem=recv.at[n], device_id=to, device_id_type=MESH)
    top, low = pl.ds(0, half), pl.ds(half, half)
    s0, s1, s2 = push(W.at[me], 0, nx), push(W.at[me], 1, ny), push(W.at[me], 2, nc)
    s0.start(); s1.start(); s2.start()
    x = x_ref[...].astype(f32)
    xh[...] = x * lax.rsqrt(jnp.mean(x * x, axis=-1, keepdims=True) + EPS)
    def chunk(j, first):
        cols = pl.ds(pl.multiple_of(j * 2 * rows, 2 * rows), 2 * rows)
        gain = jnp.concatenate([W[2 * j, 0:1, 3 * d:3 * d + rows], W[2 * j + 1, 0:1, 3 * d:3 * d + rows]], 1).astype(f32)
        n = (xh[:, cols] * gain).astype(bf)
        n_ref[:, cols] = n
        for t in range(3):
            w = W[pl.ds(2 * j, 2), :, t * d:t * d + d].reshape(2 * rows, d)
            p = dot(n, w)
            if first:
                acc[:, t * d:t * d + d] = p
            else:
                acc[:, t * d:t * d + d] = acc[:, t * d:t * d + d] + p
    ix, iy, idg = mx * 2 + c, my * 2 + c, md * 2 + c
    jx, jy, jdg = mx * 2 + o, my * 2 + o, md * 2 + o
    def here(ref, n):
        return pltpu.make_async_remote_copy(src_ref=ref, dst_ref=ref, send_sem=send.at[n], recv_sem=recv.at[n], device_id=nc, device_id_type=MESH)
    here(W.at[m * 2 + o], 2).wait_recv()
    chunk(m, True)
    here(W.at[ix], 0).wait_recv()
    s3, s5 = push(W.at[ix, top], 3, ny), push(W.at[ix], 5, nc)
    s3.start(); s5.start()
    here(W.at[iy], 1).wait_recv()
    s4, s6 = push(W.at[iy, low], 4, nx), push(W.at[iy], 6, nc)
    s4.start(); s6.start()
    here(W.at[jx], 5).wait_recv()
    chunk(mx, False)
    here(W.at[jy], 6).wait_recv()
    chunk(my, False)
    here(W.at[idg, top], 3).wait_recv()
    here(W.at[idg, low], 4).wait_recv()
    s7 = push(W.at[idg], 7, nc)
    s7.start()
    here(W.at[jdg], 7).wait_recv()
    keep = pltpu.make_async_copy(W, w_out, local)
    keep.start()
    chunk(md, False)
    q_ref[...] = acc[:, 0:d].astype(bf)
    k_ref[...] = acc[:, d:2 * d].astype(bf)
    v_ref[...] = acc[:, 2 * d:3 * d].astype(bf)
    for s in (s0, s1, s2, s3, s4, s5, s6, s7):
        s.wait_send()
    keep.wait()

def gather_qkv(tokens, small, wq, wk, wv):
    L_, d = tokens.shape
    rows = wq.shape[0]
    sds = jax.ShapeDtypeStruct
    vm = pl.BlockSpec(memory_space=pltpu.VMEM)
    return pl.pallas_call(qkv_kernel,
        in_specs=[vm] * 5,
        out_specs=[vm] * 4 + [pl.BlockSpec(memory_space=pl.ANY)],
        out_shape=[sds((L_, d), bf)] * 4 + [sds((8, rows, 3 * d + 128), bf)],
        scratch_shapes=[pltpu.VMEM((8, rows, 3 * d + 128), bf), pltpu.VMEM((L_, 3 * d), f32), pltpu.VMEM((L_, d), f32),
                        pltpu.SemaphoreType.DMA((8,)), pltpu.SemaphoreType.DMA((8,)), pltpu.SemaphoreType.DMA],
        compiler_params=pltpu.CompilerParams(collective_id=1, has_side_effects=True, vmem_limit_bytes=60 * 2**20),
        name="gather_qkv")(tokens, small, wq, wk, wv)

def gather_steps(gu_in, dn_in, wo_in, gu, dn, wo, send, recv, local):
    b, m, c, mx, my, md = places()
    o = 1 - c
    z = lax.rem(b, 2)
    oz = 1 - z
    nx, ny, nc, nz = (b, mx, c), (b, my, c), (b, m, o), (b + 1 - 2 * z, m, c)
    me, it = m * 2 + c, m * 2 + o
    ix, iy, idg = mx * 2 + c, my * 2 + c, md * 2 + c
    jx, jy, jdg = mx * 2 + o, my * 2 + o, md * 2 + o
    def copy(src, dst, n, to):
        return pltpu.make_async_remote_copy(src_ref=src, dst_ref=dst, send_sem=send.at[n], recv_sem=recv.at[n], device_id=to, device_id_type=MESH)
    def push(ref, n, to):
        return copy(ref, ref, n, to)
    def got(ref, n):
        copy(ref, ref, n, nc).wait_recv()
    def first(src, dst, n):
        for t, to in enumerate((nx, ny, nc)):
            copy(src, dst, n + t, to).start()
    def halves(ref, i):
        h = ref.shape[1] // 2
        return ref.at[i, pl.ds(0, h)], ref.at[i, pl.ds(h, h)]
    def second(ref, n, onward=None):
        got(ref.at[ix], n)
        push(halves(ref, ix)[0], n + 3, ny).start()
        push(ref.at[ix], n + 5, nc).start()
        if onward is not None:
            push(ref.at[ix], onward, nz).start()
        got(ref.at[iy], n + 1)
        push(halves(ref, iy)[1], n + 4, nx).start()
        push(ref.at[iy], n + 6, nc).start()
        if onward is not None:
            push(ref.at[iy], onward + 1, nz).start()
    def third(ref, n, onward=None):
        got(halves(ref, idg)[0], n + 3)
        got(halves(ref, idg)[1], n + 4)
        push(ref.at[idg], n + 7, nc).start()
        if onward is not None:
            push(ref.at[idg], onward + 2, nz).start()
    def last(src, ref, n, onward=None):
        for t, i in ((2, it), (5, jx), (6, jy), (7, jdg)):
            got(ref.at[i], n + t)
        for t in (0, 1, 2):
            copy(src, ref.at[me], n + t, nc).wait_send()
        push(halves(ref, ix)[0], n + 3, ny).wait_send()
        push(halves(ref, iy)[1], n + 4, nx).wait_send()
        for t, i in ((5, ix), (6, iy), (7, idg)):
            push(ref.at[i], n + t, nc).wait_send()
        if onward is not None:
            for t, i in enumerate((ix, iy, idg)):
                push(ref.at[i], onward + t, nz).wait_send()
    mine, other = gu.at[z], gu.at[oz]
    keeps = [pltpu.make_async_copy(gu_in, gu.at[:, me], local.at[0]), pltpu.make_async_copy(dn_in, dn.at[me], local.at[1]), pltpu.make_async_copy(wo_in, wo.at[me], local.at[2])]
    def begin():
        greet([nx, ny, nc, nz])
        first(gu_in.at[z], mine.at[me], 0)
        first(dn_in, dn.at[me], 8)
        first(wo_in, wo.at[me], 16)
        copy(gu_in.at[oz], other.at[me], 24, nc).start()
        for k in keeps:
            k.start()
    def z_second(ts):
        for t, i in ts:
            got(other.at[i], 25 + t)
            push(other.at[i], 28 + t, nc).start()
    def end():
        third(wo, 16)
        z_second([(2, idg)])
        last(gu_in.at[z], mine, 0, 25)
        last(dn_in, dn, 8)
        last(wo_in, wo, 16)
        got(other.at[it], 24)
        copy(gu_in.at[oz], other.at[me], 24, nc).wait_send()
        for t, i, j in ((0, ix, jx), (1, iy, jy), (2, idg, jdg)):
            got(other.at[j], 28 + t)
            push(other.at[i], 28 + t, nc).wait_send()
        for k in keeps:
            k.wait()
    def at5():
        third(mine, 0, 25)
        second(dn, 8)
    def at7():
        z_second([(0, ix), (1, iy)])
        third(dn, 8)
        second(wo, 16)
    return {0: begin, 3: lambda: second(mine, 0, 25), 5: at5, 7: at7}, end

def fwd_gather_kernel(*refs):
    (q_ref, k_ref, v_ref, mask_ref, far_ref, w_ref, gu_in, dn_in, wo_in, o_ref, e_ref, r_ref, gu, dn, wo,
     rhs, kaug, vaug, bn, s_ref, send, recv, local) = refs
    before, end = gather_steps(gu_in, dn_in, wo_in, gu, dn, wo, send, recv, local)
    p = pl.program_id(1)
    for at, act in before.items():
        pl.when(p == at)(act)
    fwd_kernel(q_ref, k_ref, v_ref, mask_ref, far_ref, w_ref, o_ref, e_ref, r_ref, rhs, kaug, vaug, bn, s_ref)
    pl.when(p == 7)(end)

def attn_fwd_gather(q, k, v, mask, far, w, gu, dn, wo):
    rows = q.shape[0] // L
    spec = pl.BlockSpec((L, 128), lambda r, p: (r, p))
    hbm = pl.BlockSpec(memory_space=pl.ANY)
    sds = jax.ShapeDtypeStruct
    return pl.pallas_call(fwd_gather_kernel,
        grid=(rows, 8),
        in_specs=[spec, spec, spec,
            pl.BlockSpec((None, L, 128), lambda r, p: (r, 0, 0)),
            pl.BlockSpec((None, 8, 128), lambda r, p: (p, 0, 0)),
            pl.BlockSpec((None, 8, 512), lambda r, p: (p, 0, 0)), hbm, hbm, hbm],
        out_specs=[spec, pl.BlockSpec((None, None, L, NT * 256), lambda r, p: (r, p, 0, 0)), spec, hbm, hbm, hbm],
        out_shape=[sds(q.shape, bf), sds((rows, 8, L, NT * 256), bf), sds(q.shape, f32),
                   sds((2, 8) + gu.shape[1:], bf), sds((8,) + dn.shape, bf), sds((8,) + wo.shape, bf)],
        scratch_shapes=[pltpu.VMEM((256, NT * 256), bf), pltpu.VMEM((L, 256), bf), pltpu.VMEM((L, 256), bf), pltpu.VMEM((384, 256), f32), pltpu.VMEM((2, L, 256), f32),
                        pltpu.SemaphoreType.DMA((31,)), pltpu.SemaphoreType.DMA((31,)), pltpu.SemaphoreType.DMA((3,))],
        compiler_params=pltpu.CompilerParams(collective_id=2, has_side_effects=True, vmem_limit_bytes=56 * 2**20),
        name="attn_fwd_gather")(q, k, v, mask, far, w, gu, dn, wo)

GELU_C = float(np.sqrt(2.0 / np.pi))
def dot_nt(a, b):
    return lax.dot_general(a, b, (((1,), (1,)), ((), ())), preferred_element_type=f32)

def ffn_kernel(x_ref, ctx_ref, g_ref, gain_ref, wo_ref, gu_ref, dn_ref,
               out_ref, gres_ref, gctx_ref, dwo_ref, ggain_ref, dgu_ref, ddn_ref, res, n, acc):
    j = pl.program_id(0)
    steps = pl.num_programs(0)
    R = x_ref.shape[0]
    d = x_ref.shape[1]
    CH = 384
    @pl.when(j == 0)
    def _():
        for t in range(0, R, CH):
            s = slice(t, t + CH)
            y = x_ref[s, :].astype(f32) + dot(ctx_ref[s, :], wo_ref[...])
            res[s, :] = y
            acc[s, :] = y
            n[s, :] = (y * lax.rsqrt(jnp.mean(y * y, axis=-1, keepdims=True) + EPS) * gain_ref[0:1, :]).astype(bf)
        gres_ref[...] = jnp.zeros_like(gres_ref)
    wg = gu_ref[0].reshape(d, gu_ref.shape[-1])
    wu = gu_ref[1].reshape(d, gu_ref.shape[-1])
    wd = dn_ref[...]
    nn = n[...]
    g = g_ref[...]
    v = dot(nn, wg)
    u = dot(nn, wu)
    gh = dot_nt(g, wd)
    v2 = v * v
    th = jnp.tanh(GELU_C * v * (1.0 + 0.044715 * v2))
    half = 0.5 * (1.0 + th)
    gel = v * half
    h = (gel * u).astype(bf)
    dgel = half + 0.5 * v * (1.0 - th * th) * (GELU_C * (1.0 + 3 * 0.044715 * v2))
    gg = (gh * u * dgel).astype(bf)
    gu = (gh * gel).astype(bf)
    acc[...] = acc[...] + dot(h, wd)
    gres_ref[...] = gres_ref[...] + dot_nt(jnp.concatenate([gg, gu], 1), jnp.concatenate([wg, wu], 1))
    dgu_ref[0] = dot_tl(nn, gg).astype(bf).reshape(dgu_ref.shape[1:])
    dgu_ref[1] = dot_tl(nn, gu).astype(bf).reshape(dgu_ref.shape[1:])
    ddn_ref[...] = dot_tl(h, g).astype(bf)
    @pl.when(j == steps - 1)
    def _():
        total = jnp.zeros((1, d), f32)
        for t in range(0, R, CH):
            s = slice(t, t + CH)
            out_ref[s, :] = acc[s, :].astype(bf)
            y = res[s, :]
            r = lax.rsqrt(jnp.mean(y * y, axis=-1, keepdims=True) + EPS)
            m = y * r
            gn = gres_ref[s, :]
            total = total + jnp.sum(gn * m, axis=0, keepdims=True)
            w = gn * gain_ref[0:1, :]
            gr = g_ref[s, :].astype(f32) + r * (w - m * jnp.mean(w * m, axis=-1, keepdims=True))
            gres_ref[s, :] = gr
            low = gr.astype(bf)
            n[s, :] = low
            gctx_ref[s, :] = dot_nt(low, wo_ref[...]).astype(bf)
        ggain_ref[...] = jnp.broadcast_to(total, ggain_ref.shape)
        dwo_ref[...] = dot_tl(ctx_ref[...], n[...]).astype(bf)

def ffn(x, ctx, g, gain, wo, gu, dn, block=256):
    R, d = x.shape
    F = dn.shape[0]
    k = gu.shape[1]
    sds = jax.ShapeDtypeStruct
    one = lambda *s: pl.BlockSpec(s, lambda j: (0,) * len(s), pipeline_mode=pl.Buffered(1))
    gub = pl.BlockSpec((2, k, d // k, block), lambda j: (0, 0, 0, j))
    dnb = pl.BlockSpec((block, d), lambda j: (j, 0))
    return pl.pallas_call(ffn_kernel, grid=(F // block,),
        in_specs=[one(R, d), one(R, d), one(R, d), one(1, d), one(d, d), gub, dnb],
        out_specs=[one(R, d), one(R, d), one(R, d), one(d, d), one(8, d), gub, dnb],
        out_shape=[sds((R, d), bf), sds((R, d), f32), sds((R, d), bf), sds((d, d), bf), sds((8, d), f32), sds(gu.shape, bf), sds(dn.shape, bf)],
        scratch_shapes=[pltpu.VMEM((R, d), f32), pltpu.VMEM((R, d), bf), pltpu.VMEM((R, d), f32)],
        compiler_params=pltpu.CompilerParams(vmem_limit_bytes=61 * 2**20), name="ffn")(x, ctx, g, gain, wo, gu, dn)

def contract_rows(left, right):
    return lax.dot_general(left, right, (((0,), (0,)), ((), ())), preferred_element_type=f32)

def contract_cols(left, right):
    return lax.dot_general(left, right, (((1,), (1,)), ((), ())), preferred_element_type=f32)

def rms_norm(inputs, gain):
    return inputs * lax.rsqrt(jnp.mean(inputs * inputs, axis=-1, keepdims=True) + EPS) * gain

def gather(x):
    return lax.all_gather(x, SHARD, axis=0, tiled=False)

def scatter(x):
    return lax.psum_scatter(x, SHARD, scatter_dimension=0, tiled=True)

def per_device(near, tokens, row_kind, text_length, gain_attn, position_bias_table, weight_query, weight_key, weight_value, weight_out, gain_ffn, weight_gate, weight_up, weight_down, cotangent):
    n1, d = weight_query.shape
    n2 = position_bias_table.shape[0]
    gu_shard = jnp.stack([weight_gate, weight_up])
    mask = mask_cols(row_kind, text_length)
    inputs = tokens.astype(f32)
    if near:
        small = jnp.pad(jnp.stack([gain_attn, gain_ffn, jnp.pad(position_bias_table, (0, n1 - n2))]), ((0, n1 - 3), (0, 0)))
        q, k, v, normed, qkv_w = gather_qkv(tokens, small, weight_query, weight_key, weight_value)
        small = qkv_w[:, 0:3, 3 * d:]
        gain_one = small[:, 0].reshape(d).astype(f32)
    else:
        small = gather(jnp.stack([gain_attn, gain_ffn, jnp.pad(position_bias_table, (0, n1 - n2))]))
        qkv_w = gather(jnp.concatenate([weight_query, weight_key, weight_value], 1))
        gain_one = small[:, 0].reshape(d).astype(f32)
        normed = rms_norm(inputs, gain_one).astype(bf)
        q, k, v = (dot(normed, qkv_w[:, :, t * d:t * d + d].reshape(d, d)).astype(bf) for t in range(3))
    gain_two = small[:, 1].reshape(d).astype(f32)
    far, w = tables(small[:, 2, :n2].reshape(-1))
    if near:
        context, e, r, gu_w, down_w, out_w = attn_fwd_gather(q, k, v, mask, far, w, gu_shard, weight_down, weight_out)
    else:
        context, e, r = attn_fwd(q, k, v, mask, far, w)
        gu_w, down_w, out_w = jnp.moveaxis(gather(gu_shard), 0, 1), gather(weight_down), gather(weight_out)
    ff = gu_w.shape[-1]
    output, grad_residual, grad_context, grad_out_w, g_gain_two, dgu, ddn = ffn(
        tokens, context, cotangent, gain_two.reshape(1, d), out_w.reshape(d, d), gu_w, down_w.reshape(ff, d))
    g_gain_two = g_gain_two[0]
    s_gu = jnp.stack([scatter(dgu[0].reshape(d, ff)), scatter(dgu[1].reshape(d, ff))])
    s_down = scatter(ddn)
    s_out = scatter(grad_out_w)
    gq, gk, gv, near_sums, far_sums = attn_bwd(q, k, v, grad_context, context, r, e)
    g_table = table_grad(near_sums, far_sums)
    grads = (gq, gk, gv)
    s_qkv = scatter(jnp.concatenate([contract_rows(normed, x).astype(bf) for x in grads], 1))
    grad_normed = sum(contract_cols(x, qkv_w[:, :, t * d:t * d + d].reshape(d, d)) for t, x in enumerate(grads))
    _, first_pull = jax.vjp(rms_norm, inputs, gain_one)
    share, g_gain_one = first_pull(grad_normed)
    grad_tokens = grad_residual + share
    small_g = lax.psum(jnp.concatenate([g_gain_one, g_gain_two, g_table]), ("batch", "dp", "narrow"))
    at = lax.axis_index("dp") * lax.axis_size("narrow") + lax.axis_index("narrow")
    r_gain_one = lax.dynamic_slice_in_dim(small_g, at * n1, n1)
    r_gain_two = lax.dynamic_slice_in_dim(small_g, d + at * n1, n1)
    r_table = lax.dynamic_slice_in_dim(small_g, 2 * d + at * n2, n2)
    s_gu, s_down, s_out, s_qkv = (lax.psum(x, "batch").astype(f32) for x in (s_gu, s_down, s_out, s_qkv))
    return (output, grad_tokens, r_gain_one, r_table, s_qkv[:, :d], s_qkv[:, d:2 * d], s_qkv[:, 2 * d:], s_out, r_gain_two, s_gu[0], s_gu[1], s_down)

def solution(mesh):
    near = (mesh.shape["batch"], mesh.shape["dp"], mesh.shape["narrow"]) == (4, 4, 2)
    placed = (
        P(("batch", "dp", "narrow"), None),
        P(("batch", "dp", "narrow")),
        P(("batch", "dp", "narrow"), None),
        P(("dp", "narrow")),
        P(("dp", "narrow")),
        P(("dp", "narrow"), None),
        P(("dp", "narrow"), None),
        P(("dp", "narrow"), None),
        P(("dp", "narrow"), None),
        P(("dp", "narrow")),
        P(("dp", "narrow"), None),
        P(("dp", "narrow"), None),
        P(("dp", "narrow"), None),
        P(("batch", "dp", "narrow"), None),
    )
    return jax.shard_map(
        functools.partial(per_device, near),
        mesh=mesh,
        in_specs=placed,
        out_specs=(
            P(("batch", "dp", "narrow"), None),
            P(("batch", "dp", "narrow"), None),
            P(("dp", "narrow")),
            P(("dp", "narrow")),
            P(("dp", "narrow"), None),
            P(("dp", "narrow"), None),
            P(("dp", "narrow"), None),
            P(("dp", "narrow"), None),
            P(("dp", "narrow")),
            P(("dp", "narrow"), None),
            P(("dp", "narrow"), None),
            P(("dp", "narrow"), None),
        ),
        check_vma=False,
    )
```

```python
import functools

import jax
import jax.numpy as jnp
import numpy as np
from jax import lax
from jax.experimental import pallas as pl
from jax.experimental.pallas import tpu as pltpu
from jax.sharding import PartitionSpec as P

EPS = 1e-06
SHARD = ("dp", "narrow")
bf=jnp.bfloat16; f32=jnp.float32
T=128; L=1152; NT=L//T
NEG=-1e30
def dot(a,b): return jnp.dot(a,b,preferred_element_type=f32)
def dot_tl(a,b): return lax.dot_general(a,b,(((0,),(0,)),((),())),preferred_element_type=f32)

def fwd_kernel(q_ref,k_ref,v_ref,mask_ref,far_ref,w_ref,o_ref,e_ref,r_ref,rhs,kaug,vaug,bn,s_ref):
    @pl.when((pl.program_id(0)==0)&(pl.program_id(1)==0))
    def _():
        rhs[...]=jnp.zeros_like(rhs)
        row=lax.broadcasted_iota(jnp.int32,(128,NT*256),0)
        col=lax.broadcasted_iota(jnp.int32,(128,NT*256),1)
        rhs[128:256,:]=(row==col//128).astype(f32).astype(bf)
        vaug[:,128:256]=jnp.ones((L,128),bf)
    qT=q_ref[...].T
    for i in range(NT):
        rhs[0:64,256*i:256*i+128]=qT[0:64,128*i:128*i+128]
        rhs[64:128,256*i+128:256*i+256]=qT[64:128,128*i:128*i+128]
    kaug[:,0:128]=k_ref[...]
    row=lax.broadcasted_iota(jnp.int32,(L,128),0)//128
    col=lax.broadcasted_iota(jnp.int32,(L,128),1)//2
    far=jnp.where(row<col-1,far_ref[0:1,:],jnp.where(row>col+1,far_ref[1:2,:],0.0))
    kaug[:,128:256]=(mask_ref[...]+far).astype(bf)
    vaug[:,0:128]=v_ref[...]
    for a in range(2):
        wb=jnp.broadcast_to(w_ref[a:a+1,:],(384,512))
        bn[:,128*a:128*a+128]=pltpu.roll(wb,0,1,stride=1,stride_axis=0)[:,0:128]
    def scores(i,slot):
        ri=rhs[:,256*i:256*i+256]
        lo,hi=max(0,i-1)*128,min(NT,i+2)*128
        off=(lo//128-(i-1))*128
        x=dot(kaug[...],ri)
        xn=x[lo:hi]+bn[off:off+hi-lo,:]
        ms=[jnp.max(xn,axis=0,keepdims=True)]
        s_ref[slot,lo:hi,:]=xn
        if lo>0:
            s_ref[slot,0:lo,:]=x[0:lo]; ms.append(jnp.max(x[0:lo],axis=0,keepdims=True))
        if hi<L:
            s_ref[slot,hi:L,:]=x[hi:L]; ms.append(jnp.max(x[hi:L],axis=0,keepdims=True))
        m=ms[0]
        for y in ms[1:]: m=jnp.maximum(m,y)
        return m
    lane=lax.broadcasted_iota(jnp.int32,(128,128),1)<64
    def finish(i,slot,m):
        e=jnp.exp(s_ref[slot]-m).astype(bf)
        e_ref[:,pl.ds(i*256,256)]=e
        o=dot_tl(e,vaug[...])
        num=jnp.where(lane,o[0:128,0:128],o[128:256,0:128])
        den=jnp.where(lane,o[0:128,128:256],o[128:256,128:256])
        r=1.0/den
        rows=pl.ds(i*128,128)
        o_ref[rows,:]=(num*r).astype(bf)
        r_ref[rows,:]=r
    m=scores(0,0)
    for i in range(NT):
        mn=scores(i+1,(i+1)%2) if i+1<NT else None
        finish(i,i%2,m)
        m=mn

def attn_fwd(q,k,v,mask,far,w):
    rows=q.shape[0]//L
    spec=pl.BlockSpec((L,128),lambda r,p:(r,p))
    return pl.pallas_call(fwd_kernel,
        grid=(rows,8),
        in_specs=[spec,spec,spec,
            pl.BlockSpec((None,L,128),lambda r,p:(r,0,0)),
            pl.BlockSpec((None,8,128),lambda r,p:(p,0,0)),
            pl.BlockSpec((None,8,512),lambda r,p:(p,0,0))],
        out_specs=[spec,pl.BlockSpec((None,None,L,NT*256),lambda r,p:(r,p,0,0)),spec],
        out_shape=[jax.ShapeDtypeStruct(q.shape,bf),jax.ShapeDtypeStruct((rows,8,L,NT*256),bf),jax.ShapeDtypeStruct(q.shape,f32)],
        scratch_shapes=[pltpu.VMEM((256,NT*256),bf),pltpu.VMEM((L,256),bf),pltpu.VMEM((L,256),bf),pltpu.VMEM((384,256),f32),pltpu.VMEM((2,L,256),f32)],
        compiler_params=pltpu.CompilerParams(vmem_limit_bytes=56*2**20),
        name="attn_fwd",
    )(q,k,v,mask,far,w)

THR=(12,16,23,32,46,64,91)
def bucket_np(d):
    n=np.abs(d); c=np.full_like(n,8)
    for t in THR: c=c+(n>=t)
    return np.where(n<8,n,c)+16*(d>0)
def tables(table):
    t=table.reshape(16,32).astype(f32)
    y=np.arange(512); y=np.where(y>=128,y-512,y)
    d=-128-y
    oh=(np.arange(32)[:,None]==bucket_np(d)[None,:]).astype(np.float32)
    w=jnp.dot(t,jnp.asarray(oh),precision=lax.Precision.HIGHEST)
    w=jnp.pad(w.reshape(8,2,512),((0,0),(0,6),(0,0)))
    lo=jnp.tile(t[:,15].reshape(8,1,2),(1,1,64)); hi=jnp.tile(t[:,31].reshape(8,1,2),(1,1,64))
    far=jnp.pad(jnp.concatenate([lo,hi],1),((0,0),(0,6),(0,0)))
    return far,w
def mask_cols(row_kind,text_length):
    pos=np.arange(L)
    kind=row_kind[:,None]
    seg=kind*(pos//384)[None]
    off=pos[None]-seg*384
    img=jnp.where(kind==1,256,1024)
    tl=jnp.where(seg==0,text_length[:,0:1],jnp.where(seg==1,text_length[:,1:2],text_length[:,2:3]))
    live=off<img+tl
    qseg=kind*np.minimum(np.arange(128)//2//3,2)[None]
    ok=live[:,:,None]&(seg[:,:,None]==qseg[:,None,:])
    return jnp.where(ok,0.0,NEG).astype(f32)

def bwd_open(rhs,vaug,qaug):
    rhs[...]=jnp.zeros_like(rhs)
    c=lax.broadcasted_iota(jnp.int32,(L,128),1)
    vaug[:,128:256]=(c<3).astype(f32).astype(bf)
    row=lax.broadcasted_iota(jnp.int32,(NT*256,128),0)
    col=lax.broadcasted_iota(jnp.int32,(NT*256,128),1)
    qaug[:,128:256]=(row//128==col).astype(f32).astype(bf)

def bwd_pair(q_ref,k_ref,v_ref,do_ref,o_ref,r_ref,e_ref,near_ref,far_ref,rhs,vaug,dobd,qaug,ds_ref,nacc):
    q=q_ref[...]; k=k_ref[...]
    vaug[:,0:128]=v_ref[...]
    dof=do_ref[...].astype(f32)*r_ref[...]
    dos=dof.astype(bf)
    dT=dos.T
    pT=(dos.astype(f32)*o_ref[...].astype(f32)).T
    D=jnp.concatenate([jnp.sum(pT[0:64],axis=0,keepdims=True),jnp.sum(pT[64:128],axis=0,keepdims=True)],0)
    D=-D
    D1=D.astype(bf); D2=(D-D1.astype(f32)); D3=(D2-D2.astype(bf).astype(f32)).astype(bf); D2=D2.astype(bf)
    lane=lax.broadcasted_iota(jnp.int32,(128,128),1)<64
    zero=jnp.zeros((128,128),bf)
    z13=jnp.zeros((13,128),bf)
    for i in range(NT):
        t=slice(128*i,128*i+128)
        for a in range(2):
            h=slice(64*a,64*a+64)
            c=slice(256*i+128*a,256*i+128*a+128)
            rhs[h,c]=dT[h,t]
            rhs[128:144,c]=jnp.concatenate([D1[a:a+1,t],D2[a:a+1,t],D3[a:a+1,t],z13],0)
            dobd[c,:]=jnp.where(lane==(a==0),dos[t],zero)
            qaug[c,0:128]=jnp.where(lane==(a==0),q[t],zero)
    nacc[...]=jnp.zeros_like(nacc)
    dqs=[]
    for i in range(NT):
        c=slice(256*i,256*i+256)
        lo,hi=max(0,i-1)*128,min(NT,i+2)*128
        off=(lo//128-(i-1))*128
        dp=dot(vaug[...],rhs[:,c])
        ds=e_ref[:,c].astype(f32)*dp
        nacc[off:off+hi-lo,:]+=ds[lo:hi]
        dsb=ds.astype(bf)
        ds_ref[:,c]=dsb
        g=dot_tl(dsb,k)
        dqs.append(jnp.where(lane,g[0:128],g[128:256]).astype(bf))
    dv=dot(e_ref[...],dobd[...]).astype(bf)
    g=dot(ds_ref[...],qaug[...])
    dk=g[:,0:128].astype(bf)
    G=g[:,128:256]
    row=lax.broadcasted_iota(jnp.int32,(L,128),0)//128
    col=lax.broadcasted_iota(jnp.int32,(L,128),1)//2
    far_ref[0:1,:]=jnp.sum(jnp.where(row<col-1,G,0.0),axis=0,keepdims=True)
    far_ref[1:2,:]=jnp.sum(jnp.where(row>col+1,G,0.0),axis=0,keepdims=True)
    far_ref[2:8,:]=jnp.zeros((6,128),f32)
    near_ref[2:8,:]=jnp.zeros((6,512),f32)
    rev=(lax.broadcasted_iota(jnp.int32,(128,128),0)+lax.broadcasted_iota(jnp.int32,(128,128),1)==127).astype(f32)
    for a in range(2):
        x=jnp.dot(nacc[:,128*a:128*a+128],rev,precision=lax.Precision.HIGHEST,preferred_element_type=f32)
        x=jnp.concatenate([x,jnp.zeros((384,384),f32)],1)
        x=pltpu.roll(x,0,1,stride=1,stride_axis=0)
        near_ref[a:a+1,:]=jnp.sum(x,axis=0,keepdims=True)
    return jnp.concatenate(dqs,0),dk,dv

def bwd_kernel(q_ref,k_ref,v_ref,do_ref,o_ref,r_ref,e_ref,dq_ref,dk_ref,dv_ref,near_ref,far_ref,rhs,vaug,dobd,qaug,ds_ref,nacc):
    @pl.when((pl.program_id(0)==0)&(pl.program_id(1)==0))
    def _():
        bwd_open(rhs,vaug,qaug)
    dq_ref[...],dk_ref[...],dv_ref[...]=bwd_pair(q_ref,k_ref,v_ref,do_ref,o_ref,r_ref,e_ref,near_ref,far_ref,rhs,vaug,dobd,qaug,ds_ref,nacc)

def attn_bwd(q,k,v,do,o,r,e):
    rows=q.shape[0]//L
    spec=pl.BlockSpec((L,128),lambda r,p:(r,p))
    sds=jax.ShapeDtypeStruct
    return pl.pallas_call(bwd_kernel,
        grid=(rows,8),
        in_specs=[spec]*6+[pl.BlockSpec((None,None,L,NT*256),lambda r,p:(r,p,0,0))],
        out_specs=[spec]*3+[pl.BlockSpec((None,None,8,512),lambda r,p:(r,p,0,0)),pl.BlockSpec((None,None,8,128),lambda r,p:(r,p,0,0))],
        out_shape=[sds(q.shape,bf)]*3+[sds((rows,8,8,512),f32),sds((rows,8,8,128),f32)],
        scratch_shapes=[pltpu.VMEM((256,NT*256),bf),pltpu.VMEM((L,256),bf),pltpu.VMEM((NT*256,128),bf),pltpu.VMEM((NT*256,256),bf),pltpu.VMEM((L,NT*256),bf),pltpu.VMEM((384,256),f32)],
        compiler_params=pltpu.CompilerParams(vmem_limit_bytes=58*2**20),
        name="attn_bwd",
    )(q,k,v,do,o,r,e)
def table_grad(near,far):
    y=np.arange(512)
    oh=(bucket_np(y-255)[:,None]==np.arange(32)[None,:]).astype(np.float32)
    n=jnp.sum(near[:,:,0:2],0).reshape(16,512)
    g=jnp.dot(n,jnp.asarray(oh),precision=lax.Precision.HIGHEST)
    f=jnp.sum(far[:,:,0:2],0).reshape(8,2,64,2).sum(2)
    lo=f[:,0].reshape(16,1); hi=f[:,1].reshape(16,1)
    g=g+lo*np.eye(32,dtype=np.float32)[15][None]+hi*np.eye(32,dtype=np.float32)[31][None]
    return g.reshape(512)

MESH = pl.DeviceIdType.MESH

def places():
    b, m, c = lax.axis_index("batch"), lax.axis_index("dp"), lax.axis_index("narrow")
    x, y = lax.rem(m, 2), m // 2
    mx = y * 2 + (1 - x)
    my = (1 - y) * 2 + x
    md = (1 - y) * 2 + (1 - x)
    return b, m, c, mx, my, md

def greet(devices):
    barrier = pltpu.get_barrier_semaphore()
    for d in devices:
        pl.semaphore_signal(barrier, inc=1, device_id=d, device_id_type=MESH)
    pl.semaphore_wait(barrier, len(devices))

def qkv_kernel(x_ref, small_ref, wq_ref, wk_ref, wv_ref, q_ref, k_ref, v_ref, n_ref, w_out, W, acc, xh, send, recv, local):
    b, m, c, mx, my, md = places()
    o = 1 - c
    nx, ny, nc = (b, mx, c), (b, my, c), (b, m, o)
    d = wq_ref.shape[1]
    rows = wq_ref.shape[0]
    half = rows // 2
    me = m * 2 + c
    W[me, :, 0:d] = wq_ref[...]
    W[me, :, d:2 * d] = wk_ref[...]
    W[me, :, 2 * d:3 * d] = wv_ref[...]
    W[me, :, 3 * d:3 * d + 128] = small_ref[...]
    greet([nx, ny, nc])
    def push(src, n, to):
        return pltpu.make_async_remote_copy(src_ref=src, dst_ref=src, send_sem=send.at[n], recv_sem=recv.at[n], device_id=to, device_id_type=MESH)
    top, low = pl.ds(0, half), pl.ds(half, half)
    s0, s1, s2 = push(W.at[me], 0, nx), push(W.at[me], 1, ny), push(W.at[me], 2, nc)
    s0.start(); s1.start(); s2.start()
    x = x_ref[...].astype(f32)
    xh[...] = x * lax.rsqrt(jnp.mean(x * x, axis=-1, keepdims=True) + EPS)
    def chunk(j, first):
        cols = pl.ds(pl.multiple_of(j * 2 * rows, 2 * rows), 2 * rows)
        gain = jnp.concatenate([W[2 * j, 0:1, 3 * d:3 * d + rows], W[2 * j + 1, 0:1, 3 * d:3 * d + rows]], 1).astype(f32)
        n = (xh[:, cols] * gain).astype(bf)
        n_ref[:, cols] = n
        for t in range(3):
            w = W[pl.ds(2 * j, 2), :, t * d:t * d + d].reshape(2 * rows, d)
            p = dot(n, w)
            if first:
                acc[:, t * d:t * d + d] = p
            else:
                acc[:, t * d:t * d + d] = acc[:, t * d:t * d + d] + p
    ix, iy, idg = mx * 2 + c, my * 2 + c, md * 2 + c
    jx, jy, jdg = mx * 2 + o, my * 2 + o, md * 2 + o
    def here(ref, n):
        return pltpu.make_async_remote_copy(src_ref=ref, dst_ref=ref, send_sem=send.at[n], recv_sem=recv.at[n], device_id=nc, device_id_type=MESH)
    here(W.at[m * 2 + o], 2).wait_recv()
    chunk(m, True)
    here(W.at[ix], 0).wait_recv()
    s3, s5 = push(W.at[ix, top], 3, ny), push(W.at[ix], 5, nc)
    s3.start(); s5.start()
    here(W.at[iy], 1).wait_recv()
    s4, s6 = push(W.at[iy, low], 4, nx), push(W.at[iy], 6, nc)
    s4.start(); s6.start()
    here(W.at[jx], 5).wait_recv()
    chunk(mx, False)
    here(W.at[jy], 6).wait_recv()
    chunk(my, False)
    here(W.at[idg, top], 3).wait_recv()
    here(W.at[idg, low], 4).wait_recv()
    s7 = push(W.at[idg], 7, nc)
    s7.start()
    here(W.at[jdg], 7).wait_recv()
    keep = pltpu.make_async_copy(W, w_out, local)
    keep.start()
    chunk(md, False)
    q_ref[...] = acc[:, 0:d].astype(bf)
    k_ref[...] = acc[:, d:2 * d].astype(bf)
    v_ref[...] = acc[:, 2 * d:3 * d].astype(bf)
    for s in (s0, s1, s2, s3, s4, s5, s6, s7):
        s.wait_send()
    keep.wait()

def gather_qkv(tokens, small, wq, wk, wv):
    L_, d = tokens.shape
    rows = wq.shape[0]
    sds = jax.ShapeDtypeStruct
    vm = pl.BlockSpec(memory_space=pltpu.VMEM)
    return pl.pallas_call(qkv_kernel,
        in_specs=[vm] * 5,
        out_specs=[vm] * 4 + [pl.BlockSpec(memory_space=pl.ANY)],
        out_shape=[sds((L_, d), bf)] * 4 + [sds((8, rows, 3 * d + 128), bf)],
        scratch_shapes=[pltpu.VMEM((8, rows, 3 * d + 128), bf), pltpu.VMEM((L_, 3 * d), f32), pltpu.VMEM((L_, d), f32),
                        pltpu.SemaphoreType.DMA((8,)), pltpu.SemaphoreType.DMA((8,)), pltpu.SemaphoreType.DMA],
        compiler_params=pltpu.CompilerParams(collective_id=1, has_side_effects=True, vmem_limit_bytes=60 * 2**20),
        name="gather_qkv")(tokens, small, wq, wk, wv)

def gather_steps(gu_in, dn_in, wo_in, gu, dn, wo, send, recv, local):
    b, m, c, mx, my, md = places()
    o = 1 - c
    z = lax.rem(b, 2)
    oz = 1 - z
    nx, ny, nc, nz = (b, mx, c), (b, my, c), (b, m, o), (b + 1 - 2 * z, m, c)
    me, it = m * 2 + c, m * 2 + o
    ix, iy, idg = mx * 2 + c, my * 2 + c, md * 2 + c
    jx, jy, jdg = mx * 2 + o, my * 2 + o, md * 2 + o
    def copy(src, dst, n, to):
        return pltpu.make_async_remote_copy(src_ref=src, dst_ref=dst, send_sem=send.at[n], recv_sem=recv.at[n], device_id=to, device_id_type=MESH)
    def push(ref, n, to):
        return copy(ref, ref, n, to)
    def got(ref, n):
        copy(ref, ref, n, nc).wait_recv()
    def first(src, dst, n):
        for t, to in enumerate((nx, ny, nc)):
            copy(src, dst, n + t, to).start()
    def halves(ref, i):
        h = ref.shape[1] // 2
        return ref.at[i, pl.ds(0, h)], ref.at[i, pl.ds(h, h)]
    def second(ref, n, onward=None):
        got(ref.at[ix], n)
        push(halves(ref, ix)[0], n + 3, ny).start()
        push(ref.at[ix], n + 5, nc).start()
        if onward is not None:
            push(ref.at[ix], onward, nz).start()
        got(ref.at[iy], n + 1)
        push(halves(ref, iy)[1], n + 4, nx).start()
        push(ref.at[iy], n + 6, nc).start()
        if onward is not None:
            push(ref.at[iy], onward + 1, nz).start()
    def third(ref, n, onward=None):
        got(halves(ref, idg)[0], n + 3)
        got(halves(ref, idg)[1], n + 4)
        push(ref.at[idg], n + 7, nc).start()
        if onward is not None:
            push(ref.at[idg], onward + 2, nz).start()
    def last(src, ref, n, onward=None):
        for t, i in ((2, it), (5, jx), (6, jy), (7, jdg)):
            got(ref.at[i], n + t)
        for t in (0, 1, 2):
            copy(src, ref.at[me], n + t, nc).wait_send()
        push(halves(ref, ix)[0], n + 3, ny).wait_send()
        push(halves(ref, iy)[1], n + 4, nx).wait_send()
        for t, i in ((5, ix), (6, iy), (7, idg)):
            push(ref.at[i], n + t, nc).wait_send()
        if onward is not None:
            for t, i in enumerate((ix, iy, idg)):
                push(ref.at[i], onward + t, nz).wait_send()
    mine, other = gu.at[z], gu.at[oz]
    keeps = [pltpu.make_async_copy(gu_in, gu.at[:, me], local.at[0]), pltpu.make_async_copy(dn_in, dn.at[me], local.at[1]), pltpu.make_async_copy(wo_in, wo.at[me], local.at[2])]
    def begin():
        greet([nx, ny, nc, nz])
        first(gu_in.at[z], mine.at[me], 0)
        first(dn_in, dn.at[me], 8)
        first(wo_in, wo.at[me], 16)
        copy(gu_in.at[oz], other.at[me], 24, nc).start()
        for k in keeps:
            k.start()
    def z_second(ts):
        for t, i in ts:
            got(other.at[i], 25 + t)
            push(other.at[i], 28 + t, nc).start()
    def end():
        third(wo, 16)
        z_second([(2, idg)])
        last(gu_in.at[z], mine, 0, 25)
        last(dn_in, dn, 8)
        last(wo_in, wo, 16)
        got(other.at[it], 24)
        copy(gu_in.at[oz], other.at[me], 24, nc).wait_send()
        for t, i, j in ((0, ix, jx), (1, iy, jy), (2, idg, jdg)):
            got(other.at[j], 28 + t)
            push(other.at[i], 28 + t, nc).wait_send()
        for k in keeps:
            k.wait()
    def at5():
        third(mine, 0, 25)
        second(dn, 8)
    def at7():
        z_second([(0, ix), (1, iy)])
        third(dn, 8)
        second(wo, 16)
    return {0: begin, 3: lambda: second(mine, 0, 25), 5: at5, 7: at7}, end

def fwd_gather_kernel(*refs):
    (q_ref, k_ref, v_ref, mask_ref, far_ref, w_ref, gu_in, dn_in, wo_in, o_ref, e_ref, r_ref, gu, dn, wo,
     rhs, kaug, vaug, bn, s_ref, send, recv, local) = refs
    before, end = gather_steps(gu_in, dn_in, wo_in, gu, dn, wo, send, recv, local)
    p = pl.program_id(1)
    for at, act in before.items():
        pl.when(p == at)(act)
    fwd_kernel(q_ref, k_ref, v_ref, mask_ref, far_ref, w_ref, o_ref, e_ref, r_ref, rhs, kaug, vaug, bn, s_ref)
    pl.when(p == 7)(end)

def attn_fwd_gather(q, k, v, mask, far, w, gu, dn, wo):
    rows = q.shape[0] // L
    spec = pl.BlockSpec((L, 128), lambda r, p: (r, p))
    hbm = pl.BlockSpec(memory_space=pl.ANY)
    sds = jax.ShapeDtypeStruct
    return pl.pallas_call(fwd_gather_kernel,
        grid=(rows, 8),
        in_specs=[spec, spec, spec,
            pl.BlockSpec((None, L, 128), lambda r, p: (r, 0, 0)),
            pl.BlockSpec((None, 8, 128), lambda r, p: (p, 0, 0)),
            pl.BlockSpec((None, 8, 512), lambda r, p: (p, 0, 0)), hbm, hbm, hbm],
        out_specs=[spec, pl.BlockSpec((None, None, L, NT * 256), lambda r, p: (r, p, 0, 0)), spec, hbm, hbm, hbm],
        out_shape=[sds(q.shape, bf), sds((rows, 8, L, NT * 256), bf), sds(q.shape, f32),
                   sds((2, 8) + gu.shape[1:], bf), sds((8,) + dn.shape, bf), sds((8,) + wo.shape, bf)],
        scratch_shapes=[pltpu.VMEM((256, NT * 256), bf), pltpu.VMEM((L, 256), bf), pltpu.VMEM((L, 256), bf), pltpu.VMEM((384, 256), f32), pltpu.VMEM((2, L, 256), f32),
                        pltpu.SemaphoreType.DMA((31,)), pltpu.SemaphoreType.DMA((31,)), pltpu.SemaphoreType.DMA((3,))],
        compiler_params=pltpu.CompilerParams(collective_id=2, has_side_effects=True, vmem_limit_bytes=56 * 2**20),
        name="attn_fwd_gather")(q, k, v, mask, far, w, gu, dn, wo)

DRAIN = 6

def rs_scratch(n, rows, cols):
    h = rows // 2
    pair = pltpu.VMEM((2, 2, h, cols), bf)
    single = pltpu.VMEM((2, h, cols), bf)
    ring = lambda k: pltpu.VMEM((k, rows, cols), bf)
    dma = pltpu.SemaphoreType.DMA
    return [pltpu.VMEM((2, 4, 2, rows, cols), bf), pltpu.VMEM((2, 4, rows, cols), bf)] + [pair] * 6 + [single] * 2 + [ring(4), ring(4), ring(2), ring(n)] + [dma((5, 2)), dma((5, 2)), dma((3, n)), dma((3, n))]

def plus(a, b):
    return a + b

def rs_greet():
    b, m, c, mx, my, md = places()
    greet([(b, mx, c), (b, my, c), (b, m, 1 - c), (b + 1 - 2 * lax.rem(b, 2), m, c), (3 - b, m, c)])

def rs_step(s, n, bufs):
    src, cbuf, sx, sy, kt, kb, xt, yb, t2, b2, part, inward, across, done, send, recv, zsend, zrecv = bufs
    b, m, c, mx, my, md = places()
    o = 1 - c
    nx, ny, nc = (b, mx, c), (b, my, c), (b, m, o)
    nz, na = (b + 1 - 2 * lax.rem(b, 2), m, c), (3 - b, m, c)
    outer = (b == 0) | (b == 3)
    inner = (b == 1) | (b == 2)
    h = kt.shape[2]
    def copy(kind, k, a, z, to):
        return pltpu.make_async_remote_copy(src_ref=a, dst_ref=z, send_sem=send.at[kind, k], recv_sem=recv.at[kind, k], device_id=to, device_id_type=MESH)
    def zcopy(kind, t, a, z, to):
        return pltpu.make_async_remote_copy(src_ref=a, dst_ref=z, send_sem=zsend.at[kind, t], recv_sem=zrecv.at[kind, t], device_id=to, device_id_type=MESH)
    core = lambda k: copy(0, k, src.at[k, :, o], cbuf.at[k], nc)
    x1 = lambda k: copy(1, k, sx.at[k], xt.at[k], nx)
    y1 = lambda k: copy(2, k, sy.at[k], yb.at[k], ny)
    y2 = lambda k: copy(3, k, kt.at[k, 1], t2.at[k], ny)
    x2 = lambda k: copy(4, k, kb.at[k, 1], b2.at[k], nx)
    up = lambda t: zcopy(0, t, part.at[lax.rem(t, 4)], inward.at[lax.rem(t, 4)], nz)
    over = lambda t: zcopy(1, t, part.at[lax.rem(t, 4)], across.at[lax.rem(t, 2)], na)
    down = lambda t: zcopy(2, t, done.at[t], done.at[t], nz)
    def stage(t, act, also=None):
        live = (t >= 0) & (t < n)
        pl.when(live if also is None else live & also)(lambda: act(t))
    def outer_done(t):
        up(t).wait_send()
        down(t).wait_recv()
    def inner_done(t):
        down(t).wait_send()
    def inner_sum(t):
        over(t).wait()
        done[t] = plus(part[lax.rem(t, 4)], across[lax.rem(t, 2)])
        down(t).start()
    def inner_part(t):
        up(t).wait_recv()
        part[lax.rem(t, 4)] = plus(part[lax.rem(t, 4)], inward[lax.rem(t, 4)])
        over(t).start()
    def finish_plane(t):
        k = lax.rem(t, 2)
        y2(k).wait()
        x2(k).wait()
        part[lax.rem(t, 4), 0:h] = plus(kt[k, 0], t2[k])
        part[lax.rem(t, 4), h:2 * h] = plus(kb[k, 0], b2[k])
    def second(t):
        k = lax.rem(t, 2)
        x1(k).wait()
        y1(k).wait()
        kt[k] = plus(kt[k], xt[k])
        kb[k] = plus(kb[k], yb[k])
        y2(k).start()
        x2(k).start()
    def first(t):
        k = lax.rem(t, 2)
        core(k).wait()
        top = lambda i: plus(src[k, i, c, 0:h], cbuf[k, i, 0:h])
        low = lambda i: plus(src[k, i, c, h:2 * h], cbuf[k, i, h:2 * h])
        sx[k, 0], sx[k, 1] = top(mx), top(md)
        sy[k, 0], sy[k, 1] = low(my), low(md)
        x1(k).start()
        y1(k).start()
        kt[k, 0], kt[k, 1] = top(m), top(my)
        kb[k, 0], kb[k, 1] = low(m), low(mx)
    stage(s - 6, outer_done, outer)
    stage(s - 6, inner_done, inner)
    stage(s - 5, inner_sum, inner)
    stage(s - 4, inner_part, inner)
    stage(s - 3, finish_plane)
    stage(s - 3, lambda t: up(t).start(), outer)
    stage(s - 2, second)
    stage(s - 1, first)
    stage(s, lambda t: core(lax.rem(t, 2)).start())

GELU_C = float(np.sqrt(2.0 / np.pi))
def dot_nt(a, b):
    return lax.dot_general(a, b, (((1,), (1,)), ((), ())), preferred_element_type=f32)

def ffn_open(x_ref, ctx_ref, gain_ref, wo_ref, gres_ref, res, n, acc):
    for t in range(0, x_ref.shape[0], 384):
        s = slice(t, t + 384)
        y = x_ref[s, :].astype(f32) + dot(ctx_ref[s, :], wo_ref[...])
        res[s, :] = y
        acc[s, :] = y
        n[s, :] = (y * lax.rsqrt(jnp.mean(y * y, axis=-1, keepdims=True) + EPS) * gain_ref[0:1, :]).astype(bf)
    gres_ref[...] = jnp.zeros_like(gres_ref)

def ffn_block(g_ref, gu_ref, dn_ref, gres_ref, ddn_ref, n, acc):
    d = n.shape[1]
    wg = gu_ref[0].reshape(d, gu_ref.shape[-1])
    wu = gu_ref[1].reshape(d, gu_ref.shape[-1])
    wd = dn_ref[...]
    nn = n[...]
    g = g_ref[...]
    v = dot(nn, wg)
    u = dot(nn, wu)
    gh = dot_nt(g, wd)
    v2 = v * v
    th = jnp.tanh(GELU_C * v * (1.0 + 0.044715 * v2))
    half = 0.5 * (1.0 + th)
    gel = v * half
    h = (gel * u).astype(bf)
    dgel = half + 0.5 * v * (1.0 - th * th) * (GELU_C * (1.0 + 3 * 0.044715 * v2))
    gg = (gh * u * dgel).astype(bf)
    gu = (gh * gel).astype(bf)
    acc[...] = acc[...] + dot(h, wd)
    gres_ref[...] = gres_ref[...] + dot_nt(jnp.concatenate([gg, gu], 1), jnp.concatenate([wg, wu], 1))
    ddn_ref[...] = dot_tl(h, g).astype(bf)
    return dot_tl(nn, gg).astype(bf), dot_tl(nn, gu).astype(bf)

def ffn_close(s, g_ref, gain_ref, wo_ref, out_ref, gres_ref, gctx_ref, res, n, acc):
    out_ref[s, :] = acc[s, :].astype(bf)
    y = res[s, :]
    r = lax.rsqrt(jnp.mean(y * y, axis=-1, keepdims=True) + EPS)
    m = y * r
    gn = gres_ref[s, :]
    w = gn * gain_ref[0:1, :]
    gr = g_ref[s, :].astype(f32) + r * (w - m * jnp.mean(w * m, axis=-1, keepdims=True))
    gres_ref[s, :] = gr
    low = gr.astype(bf)
    n[s, :] = low
    gctx_ref[s, :] = dot_nt(low, wo_ref[...]).astype(bf)
    return jnp.sum(gn * m, axis=0, keepdims=True)

def ffn_kernel(x_ref, ctx_ref, g_ref, gain_ref, wo_ref, gu_ref, dn_ref,
               out_ref, gres_ref, gctx_ref, dwo_ref, ggain_ref, ddn_ref, dgu_ref, res, n, acc):
    j = pl.program_id(0)
    @pl.when(j == 0)
    def _():
        ffn_open(x_ref, ctx_ref, gain_ref, wo_ref, gres_ref, res, n, acc)
    a, b = ffn_block(g_ref, gu_ref, dn_ref, gres_ref, ddn_ref, n, acc)
    dgu_ref[0] = a.reshape(dgu_ref.shape[1:])
    dgu_ref[1] = b.reshape(dgu_ref.shape[1:])
    @pl.when(j == pl.num_programs(0) - 1)
    def _():
        R = x_ref.shape[0]
        total = sum(ffn_close(slice(t, t + 384), g_ref, gain_ref, wo_ref, out_ref, gres_ref, gctx_ref, res, n, acc) for t in range(0, R, 384))
        ggain_ref[...] = jnp.broadcast_to(total, ggain_ref.shape)
        dwo_ref[...] = dot_tl(ctx_ref[...], n[...]).astype(bf)

def ffn_sum_kernel(x_ref, ctx_ref, g_ref, gain_ref, wo_ref, gu_ref, dn_ref,
                   out_ref, gres_ref, gctx_ref, dwo_ref, ggain_ref, ddn_ref, dgu_ref, res, n, acc, *bufs):
    j = pl.program_id(0)
    N = pl.num_programs(0) - DRAIN
    src, done = bufs[0], bufs[13]
    @pl.when(j == 0)
    def _():
        rs_greet()
        ffn_open(x_ref, ctx_ref, gain_ref, wo_ref, gres_ref, res, n, acc)
        ggain_ref[...] = jnp.zeros_like(ggain_ref)
    @pl.when(j < N)
    def _():
        a, b = ffn_block(g_ref, gu_ref, dn_ref, gres_ref, ddn_ref, n, acc)
        k = lax.rem(j, 2)
        rows = a.shape[0] // 8
        src[k, :, :, 0:rows] = a.reshape(4, 2, rows, a.shape[1])
        src[k, :, :, rows:2 * rows] = b.reshape(4, 2, rows, a.shape[1])
    @pl.when(j >= N)
    def _():
        part = x_ref.shape[0] // DRAIN
        s = pl.ds(pl.multiple_of((j - N) * part, part), part)
        total = ffn_close(s, g_ref, gain_ref, wo_ref, out_ref, gres_ref, gctx_ref, res, n, acc)
        ggain_ref[...] = ggain_ref[...] + jnp.broadcast_to(total, ggain_ref.shape)
    rs_step(j, N, bufs)
    @pl.when(j == N + DRAIN - 1)
    def _():
        dwo_ref[...] = dot_tl(ctx_ref[...], n[...]).astype(bf)
        dgu_ref[...] = done[...]

def ffn(x, ctx, g, gain, wo, gu, dn, near, block=256):
    R, d = x.shape
    F = dn.shape[0]
    k = gu.shape[1]
    N = F // block
    sds = jax.ShapeDtypeStruct
    one = lambda *s: pl.BlockSpec(s, lambda j: (0,) * len(s), pipeline_mode=pl.Buffered(1))
    at = lambda j: jnp.minimum(j, N - 1)
    gub = pl.BlockSpec((2, k, d // k, block), lambda j: (0, 0, 0, at(j)))
    dnb = pl.BlockSpec((block, d), lambda j: (at(j), 0))
    rows = 2 * (d // k)
    if near:
        body, extra, steps, last = ffn_sum_kernel, rs_scratch(N, rows, block), N + DRAIN, (one(N, rows, block), sds((N, rows, block), bf))
        params = pltpu.CompilerParams(vmem_limit_bytes=61 * 2**20, collective_id=3, has_side_effects=True)
    else:
        body, extra, steps, last = ffn_kernel, [], N, (gub, sds(gu.shape, bf))
        params = pltpu.CompilerParams(vmem_limit_bytes=61 * 2**20)
    return pl.pallas_call(body, grid=(steps,),
        in_specs=[one(R, d), one(R, d), one(R, d), one(1, d), one(d, d), gub, dnb],
        out_specs=[one(R, d), one(R, d), one(R, d), one(d, d), one(8, d), dnb, last[0]],
        out_shape=[sds((R, d), bf), sds((R, d), f32), sds((R, d), bf), sds((d, d), bf), sds((8, d), f32), sds(dn.shape, bf), last[1]],
        scratch_shapes=[pltpu.VMEM((R, d), f32), pltpu.VMEM((R, d), bf), pltpu.VMEM((R, d), f32)] + extra,
        compiler_params=params, name="ffn")(x, ctx, g, gain, wo, gu, dn)

def bwd_sum_kernel(q_ref, k_ref, v_ref, do_ref, o_ref, r_ref, e_ref, n_ref, x_ref, gres_ref, gain_ref, wq_ref, wk_ref, wv_ref, dn_ref, wo_ref,
                   gtok_ref, ggain_ref, near_ref, far_ref, out_ref, rhs, vaug, dobd, qaug, ds_ref, nacc, *bufs):
    p = pl.program_id(0)
    N = pl.num_programs(0) - DRAIN
    src, done = bufs[0], bufs[13]
    h = src.shape[3] // 2
    @pl.when(p == 0)
    def _():
        rs_greet()
        bwd_open(rhs, vaug, qaug)
        gtok_ref[...] = jnp.zeros_like(gtok_ref)
        ggain_ref[...] = jnp.zeros_like(ggain_ref)
    @pl.when(p < N)
    def _():
        k = lax.rem(p, 2)
        at = 0
        def put(a):
            nonlocal at
            r = a.shape[1] // 2
            a = a.reshape((4, 2) + a.shape[1:])
            src[k, :, :, at:at + r] = a[:, :, 0:r]
            src[k, :, :, h + at:h + at + r] = a[:, :, r:2 * r]
            at += r
        put(dn_ref[...])
        put(wo_ref[...])
        d = gtok_ref.shape[1]
        g = jnp.concatenate(bwd_pair(q_ref, k_ref, v_ref, do_ref, o_ref, r_ref, e_ref, near_ref, far_ref, rhs, vaug, dobd, qaug, ds_ref, nacc), 1)
        gw = dot_tl(n_ref[...], g).astype(bf)
        for t in range(3):
            put(gw[:, 128 * t:128 * t + 128].reshape(8, d // 8, 128))
        w = jnp.concatenate([w_ref[...].reshape(d, 128) for w_ref in (wq_ref, wk_ref, wv_ref)], 1)
        gtok_ref[...] = gtok_ref[...] + dot_nt(g, w)
    @pl.when(p >= N)
    def _():
        part = x_ref.shape[0]
        s = pl.ds(pl.multiple_of((p - N) * part, part), part)
        x = x_ref[...].astype(f32)
        r = lax.rsqrt(jnp.mean(x * x, axis=-1, keepdims=True) + EPS)
        m = x * r
        gn = gtok_ref[s, :]
        w = gn * gain_ref[0:1, :]
        gtok_ref[s, :] = gres_ref[...] + r * (w - m * jnp.mean(w * m, axis=-1, keepdims=True))
        ggain_ref[...] = ggain_ref[...] + jnp.broadcast_to(jnp.sum(gn * m, axis=0, keepdims=True), ggain_ref.shape)
    rs_step(p, N, bufs)
    @pl.when(p == N + DRAIN - 1)
    def _():
        out_ref[...] = done[...]

def attn_bwd_sum(q, k, v, do, o, r, e, n, x, gres, gain, qkv_w, dn, wo):
    R, d = q.shape
    N = d // 128
    rows = dn.shape[1] + wo.shape[1] + 3 * (d // 8)
    sds = jax.ShapeDtypeStruct
    at = lambda p: jnp.minimum(p, N - 1)
    after = lambda p: jnp.maximum(p - N, 0)
    spec = pl.BlockSpec((R, 128), lambda p: (0, at(p)))
    one = lambda *s: pl.BlockSpec(s, lambda p: (0,) * len(s), pipeline_mode=pl.Buffered(1))
    part = pl.BlockSpec((R // DRAIN, d), lambda p: (after(p), 0))
    cols = lambda a, t: pl.BlockSpec((8, a.shape[1], 128), lambda p: (0, 0, t * N + at(p)))
    sums = lambda w: pl.BlockSpec((None, None, 8, w), lambda p: (0, at(p), 0, 0))
    return pl.pallas_call(bwd_sum_kernel, grid=(N + DRAIN,),
        in_specs=[spec] * 6 + [pl.BlockSpec((None, None, R, NT * 256), lambda p: (0, at(p), 0, 0)), one(R, d), part, part, one(1, d),
                  cols(qkv_w, 0), cols(qkv_w, 1), cols(qkv_w, 2), cols(dn, 0), cols(wo, 0)],
        out_specs=[one(R, d), one(8, d), sums(512), sums(128), one(N, rows, 128)],
        out_shape=[sds((R, d), f32), sds((8, d), f32), sds((1, N, 8, 512), f32), sds((1, N, 8, 128), f32), sds((N, rows, 128), bf)],
        scratch_shapes=[pltpu.VMEM((256, NT * 256), bf), pltpu.VMEM((R, 256), bf), pltpu.VMEM((NT * 256, 128), bf), pltpu.VMEM((NT * 256, 256), bf), pltpu.VMEM((R, NT * 256), bf), pltpu.VMEM((384, 256), f32)] + rs_scratch(N, rows, 128),
        compiler_params=pltpu.CompilerParams(vmem_limit_bytes=62 * 2**20, collective_id=4, has_side_effects=True), name="attn_bwd_sum")(
            q, k, v, do, o, r, e, n, x, gres, gain, qkv_w, qkv_w, qkv_w, dn, wo)

def split_sums(out, sizes):
    h = out.shape[1] // 2
    parts, at = [], 0
    for r in sizes:
        r = r // 2
        a = jnp.concatenate([out[:, at:at + r], out[:, h + at:h + at + r]], 1)
        parts.append(jnp.moveaxis(a, 0, 1).reshape(2 * r, -1).astype(f32))
        at += r
    return parts

def contract_rows(left, right):
    return lax.dot_general(left, right, (((0,), (0,)), ((), ())), preferred_element_type=f32)

def contract_cols(left, right):
    return lax.dot_general(left, right, (((1,), (1,)), ((), ())), preferred_element_type=f32)

def rms_norm(inputs, gain):
    return inputs * lax.rsqrt(jnp.mean(inputs * inputs, axis=-1, keepdims=True) + EPS) * gain

def gather(x):
    return lax.all_gather(x, SHARD, axis=0, tiled=False)

def scatter(x):
    return lax.psum_scatter(x, SHARD, scatter_dimension=0, tiled=True)

def per_device(near, tokens, row_kind, text_length, gain_attn, position_bias_table, weight_query, weight_key, weight_value, weight_out, gain_ffn, weight_gate, weight_up, weight_down, cotangent):
    n1, d = weight_query.shape
    n2 = position_bias_table.shape[0]
    gu_shard = jnp.stack([weight_gate, weight_up])
    mask = mask_cols(row_kind, text_length)
    inputs = tokens.astype(f32)
    if near:
        small = jnp.pad(jnp.stack([gain_attn, gain_ffn, jnp.pad(position_bias_table, (0, n1 - n2))]), ((0, n1 - 3), (0, 0)))
        q, k, v, normed, qkv_w = gather_qkv(tokens, small, weight_query, weight_key, weight_value)
        small = qkv_w[:, 0:3, 3 * d:]
        gain_one = small[:, 0].reshape(d).astype(f32)
    else:
        small = gather(jnp.stack([gain_attn, gain_ffn, jnp.pad(position_bias_table, (0, n1 - n2))]))
        qkv_w = gather(jnp.concatenate([weight_query, weight_key, weight_value], 1))
        gain_one = small[:, 0].reshape(d).astype(f32)
        normed = rms_norm(inputs, gain_one).astype(bf)
        q, k, v = (dot(normed, qkv_w[:, :, t * d:t * d + d].reshape(d, d)).astype(bf) for t in range(3))
    gain_two = small[:, 1].reshape(d).astype(f32)
    far, w = tables(small[:, 2, :n2].reshape(-1))
    if near:
        context, e, r, gu_w, down_w, out_w = attn_fwd_gather(q, k, v, mask, far, w, gu_shard, weight_down, weight_out)
    else:
        context, e, r = attn_fwd(q, k, v, mask, far, w)
        gu_w, down_w, out_w = jnp.moveaxis(gather(gu_shard), 0, 1), gather(weight_down), gather(weight_out)
    ff = gu_w.shape[-1]
    output, grad_residual, grad_context, grad_out_w, g_gain_two, ddn, dgu = ffn(
        tokens, context, cotangent, gain_two.reshape(1, d), out_w.reshape(d, d), gu_w, down_w.reshape(ff, d), near)
    if near:
        shards = gu_w.shape[1]
        grad_tokens, g_gain_one, near_sums, far_sums, sums = attn_bwd_sum(
            q, k, v, grad_context, context, r, e, normed, tokens, grad_residual, gain_one.reshape(1, d), qkv_w,
            ddn.reshape(shards, ff // shards, d), grad_out_w.reshape(shards, n1, d))
        g_gain_one = g_gain_one[0]
        s_down, s_out, s_q, s_k, s_v = split_sums(sums, (ff // shards, n1, n1, n1, n1))
        dgu = dgu.reshape(dgu.shape[0], 2, n1, -1).transpose(1, 2, 0, 3).reshape(2, n1, ff).astype(f32)
        s_gate, s_up = dgu[0], dgu[1]
    else:
        total = lambda x: lax.psum(scatter(x), "batch").astype(f32)
        gq, gk, gv, near_sums, far_sums = attn_bwd(q, k, v, grad_context, context, r, e)
        grads = (gq, gk, gv)
        s_gate, s_up, s_down, s_out = (total(x) for x in (dgu[0].reshape(d, ff), dgu[1].reshape(d, ff), ddn, grad_out_w))
        s_q, s_k, s_v = (total(contract_rows(normed, x).astype(bf)) for x in grads)
        grad_normed = sum(contract_cols(x, qkv_w[:, :, t * d:t * d + d].reshape(d, d)) for t, x in enumerate(grads))
        _, first_pull = jax.vjp(rms_norm, inputs, gain_one)
        share, g_gain_one = first_pull(grad_normed)
        grad_tokens = grad_residual + share
    g_table = table_grad(near_sums, far_sums)
    small_g = lax.psum(jnp.concatenate([g_gain_one, g_gain_two[0], g_table]), ("batch", "dp", "narrow"))
    at = lax.axis_index("dp") * lax.axis_size("narrow") + lax.axis_index("narrow")
    r_gain_one = lax.dynamic_slice_in_dim(small_g, at * n1, n1)
    r_gain_two = lax.dynamic_slice_in_dim(small_g, d + at * n1, n1)
    r_table = lax.dynamic_slice_in_dim(small_g, 2 * d + at * n2, n2)
    return (output, grad_tokens, r_gain_one, r_table, s_q, s_k, s_v, s_out, r_gain_two, s_gate, s_up, s_down)

def solution(mesh):
    near = (mesh.shape["batch"], mesh.shape["dp"], mesh.shape["narrow"]) == (4, 4, 2)
    placed = (
        P(("batch", "dp", "narrow"), None),
        P(("batch", "dp", "narrow")),
        P(("batch", "dp", "narrow"), None),
        P(("dp", "narrow")),
        P(("dp", "narrow")),
        P(("dp", "narrow"), None),
        P(("dp", "narrow"), None),
        P(("dp", "narrow"), None),
        P(("dp", "narrow"), None),
        P(("dp", "narrow")),
        P(("dp", "narrow"), None),
        P(("dp", "narrow"), None),
        P(("dp", "narrow"), None),
        P(("batch", "dp", "narrow"), None),
    )
    return jax.shard_map(
        functools.partial(per_device, near),
        mesh=mesh,
        in_specs=placed,
        out_specs=(
            P(("batch", "dp", "narrow"), None),
            P(("batch", "dp", "narrow"), None),
            P(("dp", "narrow")),
            P(("dp", "narrow")),
            P(("dp", "narrow"), None),
            P(("dp", "narrow"), None),
            P(("dp", "narrow"), None),
            P(("dp", "narrow"), None),
            P(("dp", "narrow")),
            P(("dp", "narrow"), None),
            P(("dp", "narrow"), None),
            P(("dp", "narrow"), None),
        ),
        check_vma=False,
    )
```

```python
import functools

import jax
import jax.numpy as jnp
import numpy as np
from jax import lax
from jax.experimental import pallas as pl
from jax.experimental.pallas import tpu as pltpu
from jax.sharding import PartitionSpec as P

EPS = 1e-06
SHARD = ("dp", "narrow")
bf=jnp.bfloat16; f32=jnp.float32
T=128; L=1152; NT=L//T
NEG=-1e30
def dot(a,b): return jnp.dot(a,b,preferred_element_type=f32)
def dot_tl(a,b): return lax.dot_general(a,b,(((0,),(0,)),((),())),preferred_element_type=f32)

def fwd_kernel(q_ref,k_ref,v_ref,mask_ref,far_ref,w_ref,o_ref,e_ref,r_ref,rhs,kaug,vaug,bn,s_ref):
    @pl.when((pl.program_id(0)==0)&(pl.program_id(1)==0))
    def _():
        rhs[...]=jnp.zeros_like(rhs)
        row=lax.broadcasted_iota(jnp.int32,(128,NT*256),0)
        col=lax.broadcasted_iota(jnp.int32,(128,NT*256),1)
        rhs[128:256,:]=(row==col//128).astype(f32).astype(bf)
        vaug[:,128:256]=jnp.ones((L,128),bf)
    qT=q_ref[...].T
    for i in range(NT):
        rhs[0:64,256*i:256*i+128]=qT[0:64,128*i:128*i+128]
        rhs[64:128,256*i+128:256*i+256]=qT[64:128,128*i:128*i+128]
    kaug[:,0:128]=k_ref[...]
    row=lax.broadcasted_iota(jnp.int32,(L,128),0)//128
    col=lax.broadcasted_iota(jnp.int32,(L,128),1)//2
    far=jnp.where(row<col-1,far_ref[0:1,:],jnp.where(row>col+1,far_ref[1:2,:],0.0))
    kaug[:,128:256]=(mask_ref[...]+far).astype(bf)
    vaug[:,0:128]=v_ref[...]
    for a in range(2):
        wb=jnp.broadcast_to(w_ref[a:a+1,:],(384,512))
        bn[:,128*a:128*a+128]=pltpu.roll(wb,0,1,stride=1,stride_axis=0)[:,0:128]
    def scores(i,slot):
        ri=rhs[:,256*i:256*i+256]
        lo,hi=max(0,i-1)*128,min(NT,i+2)*128
        off=(lo//128-(i-1))*128
        x=dot(kaug[...],ri)
        xn=x[lo:hi]+bn[off:off+hi-lo,:]
        ms=[jnp.max(xn,axis=0,keepdims=True)]
        s_ref[slot,lo:hi,:]=xn
        if lo>0:
            s_ref[slot,0:lo,:]=x[0:lo]; ms.append(jnp.max(x[0:lo],axis=0,keepdims=True))
        if hi<L:
            s_ref[slot,hi:L,:]=x[hi:L]; ms.append(jnp.max(x[hi:L],axis=0,keepdims=True))
        m=ms[0]
        for y in ms[1:]: m=jnp.maximum(m,y)
        return m
    lane=lax.broadcasted_iota(jnp.int32,(128,128),1)<64
    def finish(i,slot,m):
        e=jnp.exp(s_ref[slot]-m).astype(bf)
        e_ref[:,pl.ds(i*256,256)]=e
        o=dot_tl(e,vaug[...])
        num=jnp.where(lane,o[0:128,0:128],o[128:256,0:128])
        den=jnp.where(lane,o[0:128,128:256],o[128:256,128:256])
        r=1.0/den
        rows=pl.ds(i*128,128)
        o_ref[rows,:]=(num*r).astype(bf)
        r_ref[rows,:]=r
    m=scores(0,0)
    for i in range(NT):
        mn=scores(i+1,(i+1)%2) if i+1<NT else None
        finish(i,i%2,m)
        m=mn

def attn_fwd(q,k,v,mask,far,w):
    rows=q.shape[0]//L
    spec=pl.BlockSpec((L,128),lambda r,p:(r,p))
    return pl.pallas_call(fwd_kernel,
        grid=(rows,8),
        in_specs=[spec,spec,spec,
            pl.BlockSpec((None,L,128),lambda r,p:(r,0,0)),
            pl.BlockSpec((None,8,128),lambda r,p:(p,0,0)),
            pl.BlockSpec((None,8,512),lambda r,p:(p,0,0))],
        out_specs=[spec,pl.BlockSpec((None,None,L,NT*256),lambda r,p:(r,p,0,0)),spec],
        out_shape=[jax.ShapeDtypeStruct(q.shape,bf),jax.ShapeDtypeStruct((rows,8,L,NT*256),bf),jax.ShapeDtypeStruct(q.shape,f32)],
        scratch_shapes=[pltpu.VMEM((256,NT*256),bf),pltpu.VMEM((L,256),bf),pltpu.VMEM((L,256),bf),pltpu.VMEM((384,256),f32),pltpu.VMEM((2,L,256),f32)],
        compiler_params=pltpu.CompilerParams(vmem_limit_bytes=56*2**20),
        name="attn_fwd",
    )(q,k,v,mask,far,w)

THR=(12,16,23,32,46,64,91)
def bucket_np(d):
    n=np.abs(d); c=np.full_like(n,8)
    for t in THR: c=c+(n>=t)
    return np.where(n<8,n,c)+16*(d>0)
def tables(table):
    t=table.reshape(16,32).astype(f32)
    y=np.arange(512); y=np.where(y>=128,y-512,y)
    d=-128-y
    oh=(np.arange(32)[:,None]==bucket_np(d)[None,:]).astype(np.float32)
    w=jnp.dot(t,jnp.asarray(oh),precision=lax.Precision.HIGHEST)
    w=jnp.pad(w.reshape(8,2,512),((0,0),(0,6),(0,0)))
    lo=jnp.tile(t[:,15].reshape(8,1,2),(1,1,64)); hi=jnp.tile(t[:,31].reshape(8,1,2),(1,1,64))
    far=jnp.pad(jnp.concatenate([lo,hi],1),((0,0),(0,6),(0,0)))
    return far,w
def mask_cols(row_kind,text_length):
    pos=np.arange(L)
    kind=row_kind[:,None]
    seg=kind*(pos//384)[None]
    off=pos[None]-seg*384
    img=jnp.where(kind==1,256,1024)
    tl=jnp.where(seg==0,text_length[:,0:1],jnp.where(seg==1,text_length[:,1:2],text_length[:,2:3]))
    live=off<img+tl
    qseg=kind*np.minimum(np.arange(128)//2//3,2)[None]
    ok=live[:,:,None]&(seg[:,:,None]==qseg[:,None,:])
    return jnp.where(ok,0.0,NEG).astype(f32)

def bwd_open(rhs,vaug,qaug):
    rhs[...]=jnp.zeros_like(rhs)
    c=lax.broadcasted_iota(jnp.int32,(L,128),1)
    vaug[:,128:256]=(c<3).astype(f32).astype(bf)
    row=lax.broadcasted_iota(jnp.int32,(NT*256,128),0)
    col=lax.broadcasted_iota(jnp.int32,(NT*256,128),1)
    qaug[:,128:256]=(row//128==col).astype(f32).astype(bf)

def bwd_pair(q_ref,k_ref,v_ref,do_ref,o_ref,r_ref,e_ref,near_ref,far_ref,rhs,vaug,dobd,qaug,ds_ref,nacc):
    q=q_ref[...]; k=k_ref[...]
    vaug[:,0:128]=v_ref[...]
    dof=do_ref[...].astype(f32)*r_ref[...]
    dos=dof.astype(bf)
    dT=dos.T
    pT=(dos.astype(f32)*o_ref[...].astype(f32)).T
    D=jnp.concatenate([jnp.sum(pT[0:64],axis=0,keepdims=True),jnp.sum(pT[64:128],axis=0,keepdims=True)],0)
    D=-D
    D1=D.astype(bf); D2=(D-D1.astype(f32)); D3=(D2-D2.astype(bf).astype(f32)).astype(bf); D2=D2.astype(bf)
    lane=lax.broadcasted_iota(jnp.int32,(128,128),1)<64
    zero=jnp.zeros((128,128),bf)
    z13=jnp.zeros((13,128),bf)
    for i in range(NT):
        t=slice(128*i,128*i+128)
        for a in range(2):
            h=slice(64*a,64*a+64)
            c=slice(256*i+128*a,256*i+128*a+128)
            rhs[h,c]=dT[h,t]
            rhs[128:144,c]=jnp.concatenate([D1[a:a+1,t],D2[a:a+1,t],D3[a:a+1,t],z13],0)
            dobd[c,:]=jnp.where(lane==(a==0),dos[t],zero)
            qaug[c,0:128]=jnp.where(lane==(a==0),q[t],zero)
    nacc[...]=jnp.zeros_like(nacc)
    dqs=[]
    for i in range(NT):
        c=slice(256*i,256*i+256)
        lo,hi=max(0,i-1)*128,min(NT,i+2)*128
        off=(lo//128-(i-1))*128
        dp=dot(vaug[...],rhs[:,c])
        ds=e_ref[:,c].astype(f32)*dp
        nacc[off:off+hi-lo,:]+=ds[lo:hi]
        dsb=ds.astype(bf)
        ds_ref[:,c]=dsb
        g=dot_tl(dsb,k)
        dqs.append(jnp.where(lane,g[0:128],g[128:256]).astype(bf))
    dv=dot(e_ref[...],dobd[...]).astype(bf)
    g=dot(ds_ref[...],qaug[...])
    dk=g[:,0:128].astype(bf)
    G=g[:,128:256]
    row=lax.broadcasted_iota(jnp.int32,(L,128),0)//128
    col=lax.broadcasted_iota(jnp.int32,(L,128),1)//2
    far_ref[0:1,:]=jnp.sum(jnp.where(row<col-1,G,0.0),axis=0,keepdims=True)
    far_ref[1:2,:]=jnp.sum(jnp.where(row>col+1,G,0.0),axis=0,keepdims=True)
    far_ref[2:8,:]=jnp.zeros((6,128),f32)
    near_ref[2:8,:]=jnp.zeros((6,512),f32)
    rev=(lax.broadcasted_iota(jnp.int32,(128,128),0)+lax.broadcasted_iota(jnp.int32,(128,128),1)==127).astype(f32)
    for a in range(2):
        x=jnp.dot(nacc[:,128*a:128*a+128],rev,precision=lax.Precision.HIGHEST,preferred_element_type=f32)
        x=jnp.concatenate([x,jnp.zeros((384,384),f32)],1)
        x=pltpu.roll(x,0,1,stride=1,stride_axis=0)
        near_ref[a:a+1,:]=jnp.sum(x,axis=0,keepdims=True)
    return jnp.concatenate(dqs,0),dk,dv

def bwd_kernel(q_ref,k_ref,v_ref,do_ref,o_ref,r_ref,e_ref,dq_ref,dk_ref,dv_ref,near_ref,far_ref,rhs,vaug,dobd,qaug,ds_ref,nacc):
    @pl.when((pl.program_id(0)==0)&(pl.program_id(1)==0))
    def _():
        bwd_open(rhs,vaug,qaug)
    dq_ref[...],dk_ref[...],dv_ref[...]=bwd_pair(q_ref,k_ref,v_ref,do_ref,o_ref,r_ref,e_ref,near_ref,far_ref,rhs,vaug,dobd,qaug,ds_ref,nacc)

def attn_bwd(q,k,v,do,o,r,e):
    rows=q.shape[0]//L
    spec=pl.BlockSpec((L,128),lambda r,p:(r,p))
    sds=jax.ShapeDtypeStruct
    return pl.pallas_call(bwd_kernel,
        grid=(rows,8),
        in_specs=[spec]*6+[pl.BlockSpec((None,None,L,NT*256),lambda r,p:(r,p,0,0))],
        out_specs=[spec]*3+[pl.BlockSpec((None,None,8,512),lambda r,p:(r,p,0,0)),pl.BlockSpec((None,None,8,128),lambda r,p:(r,p,0,0))],
        out_shape=[sds(q.shape,bf)]*3+[sds((rows,8,8,512),f32),sds((rows,8,8,128),f32)],
        scratch_shapes=[pltpu.VMEM((256,NT*256),bf),pltpu.VMEM((L,256),bf),pltpu.VMEM((NT*256,128),bf),pltpu.VMEM((NT*256,256),bf),pltpu.VMEM((L,NT*256),bf),pltpu.VMEM((384,256),f32)],
        compiler_params=pltpu.CompilerParams(vmem_limit_bytes=58*2**20),
        name="attn_bwd",
    )(q,k,v,do,o,r,e)
def table_grad(near,far):
    y=np.arange(512)
    oh=(bucket_np(y-255)[:,None]==np.arange(32)[None,:]).astype(np.float32)
    n=jnp.sum(near[:,:,0:2],0).reshape(16,512)
    g=jnp.dot(n,jnp.asarray(oh),precision=lax.Precision.HIGHEST)
    f=jnp.sum(far[:,:,0:2],0).reshape(8,2,64,2).sum(2)
    lo=f[:,0].reshape(16,1); hi=f[:,1].reshape(16,1)
    g=g+lo*np.eye(32,dtype=np.float32)[15][None]+hi*np.eye(32,dtype=np.float32)[31][None]
    return g.reshape(512)

MESH = pl.DeviceIdType.MESH

def places():
    b, m, c = lax.axis_index("batch"), lax.axis_index("dp"), lax.axis_index("narrow")
    x, y = lax.rem(m, 2), m // 2
    mx = y * 2 + (1 - x)
    my = (1 - y) * 2 + x
    md = (1 - y) * 2 + (1 - x)
    return b, m, c, mx, my, md

def greet(devices):
    barrier = pltpu.get_barrier_semaphore()
    for d in devices:
        pl.semaphore_signal(barrier, inc=1, device_id=d, device_id_type=MESH)
    pl.semaphore_wait(barrier, len(devices))

def qkv_kernel(x_ref, small_ref, wq_ref, wk_ref, wv_ref, q_ref, k_ref, v_ref, n_ref, w_out, W, acc, xh, send, recv, local):
    b, m, c, mx, my, md = places()
    o = 1 - c
    nx, ny, nc = (b, mx, c), (b, my, c), (b, m, o)
    d = wq_ref.shape[1]
    rows = wq_ref.shape[0]
    half = rows // 2
    me = m * 2 + c
    W[me, :, 0:d] = wq_ref[...]
    W[me, :, d:2 * d] = wk_ref[...]
    W[me, :, 2 * d:3 * d] = wv_ref[...]
    W[me, :, 3 * d:3 * d + 128] = small_ref[...]
    greet([nx, ny, nc])
    def push(src, n, to):
        return pltpu.make_async_remote_copy(src_ref=src, dst_ref=src, send_sem=send.at[n], recv_sem=recv.at[n], device_id=to, device_id_type=MESH)
    top, low = pl.ds(0, half), pl.ds(half, half)
    s0, s1, s2 = push(W.at[me], 0, nx), push(W.at[me], 1, ny), push(W.at[me], 2, nc)
    s0.start(); s1.start(); s2.start()
    x = x_ref[...].astype(f32)
    xh[...] = x * lax.rsqrt(jnp.mean(x * x, axis=-1, keepdims=True) + EPS)
    def chunk(j, first):
        cols = pl.ds(pl.multiple_of(j * 2 * rows, 2 * rows), 2 * rows)
        gain = jnp.concatenate([W[2 * j, 0:1, 3 * d:3 * d + rows], W[2 * j + 1, 0:1, 3 * d:3 * d + rows]], 1).astype(f32)
        n = (xh[:, cols] * gain).astype(bf)
        n_ref[:, cols] = n
        for t in range(3):
            w = W[pl.ds(2 * j, 2), :, t * d:t * d + d].reshape(2 * rows, d)
            p = dot(n, w)
            if first:
                acc[:, t * d:t * d + d] = p
            else:
                acc[:, t * d:t * d + d] = acc[:, t * d:t * d + d] + p
    ix, iy, idg = mx * 2 + c, my * 2 + c, md * 2 + c
    jx, jy, jdg = mx * 2 + o, my * 2 + o, md * 2 + o
    def here(ref, n):
        return pltpu.make_async_remote_copy(src_ref=ref, dst_ref=ref, send_sem=send.at[n], recv_sem=recv.at[n], device_id=nc, device_id_type=MESH)
    here(W.at[m * 2 + o], 2).wait_recv()
    chunk(m, True)
    here(W.at[ix], 0).wait_recv()
    s3, s5 = push(W.at[ix, top], 3, ny), push(W.at[ix], 5, nc)
    s3.start(); s5.start()
    here(W.at[iy], 1).wait_recv()
    s4, s6 = push(W.at[iy, low], 4, nx), push(W.at[iy], 6, nc)
    s4.start(); s6.start()
    here(W.at[jx], 5).wait_recv()
    chunk(mx, False)
    here(W.at[jy], 6).wait_recv()
    chunk(my, False)
    here(W.at[idg, top], 3).wait_recv()
    here(W.at[idg, low], 4).wait_recv()
    s7 = push(W.at[idg], 7, nc)
    s7.start()
    here(W.at[jdg], 7).wait_recv()
    keep = pltpu.make_async_copy(W, w_out, local)
    keep.start()
    chunk(md, False)
    q_ref[...] = acc[:, 0:d].astype(bf)
    k_ref[...] = acc[:, d:2 * d].astype(bf)
    v_ref[...] = acc[:, 2 * d:3 * d].astype(bf)
    for s in (s0, s1, s2, s3, s4, s5, s6, s7):
        s.wait_send()
    keep.wait()

def gather_qkv(tokens, small, wq, wk, wv):
    L_, d = tokens.shape
    rows = wq.shape[0]
    sds = jax.ShapeDtypeStruct
    vm = pl.BlockSpec(memory_space=pltpu.VMEM)
    return pl.pallas_call(qkv_kernel,
        in_specs=[vm] * 5,
        out_specs=[vm] * 4 + [pl.BlockSpec(memory_space=pl.ANY)],
        out_shape=[sds((L_, d), bf)] * 4 + [sds((8, rows, 3 * d + 128), bf)],
        scratch_shapes=[pltpu.VMEM((8, rows, 3 * d + 128), bf), pltpu.VMEM((L_, 3 * d), f32), pltpu.VMEM((L_, d), f32),
                        pltpu.SemaphoreType.DMA((8,)), pltpu.SemaphoreType.DMA((8,)), pltpu.SemaphoreType.DMA],
        compiler_params=pltpu.CompilerParams(collective_id=1, has_side_effects=True, vmem_limit_bytes=60 * 2**20),
        name="gather_qkv")(tokens, small, wq, wk, wv)

def gather_steps(gu_in, dn_in, wo_in, gu, dn, wo, send, recv, local):
    b, m, c, mx, my, md = places()
    o = 1 - c
    z = lax.rem(b, 2)
    oz = 1 - z
    nx, ny, nc, nz = (b, mx, c), (b, my, c), (b, m, o), (b + 1 - 2 * z, m, c)
    me, it = m * 2 + c, m * 2 + o
    ix, iy, idg = mx * 2 + c, my * 2 + c, md * 2 + c
    jx, jy, jdg = mx * 2 + o, my * 2 + o, md * 2 + o
    def copy(src, dst, n, to):
        return pltpu.make_async_remote_copy(src_ref=src, dst_ref=dst, send_sem=send.at[n], recv_sem=recv.at[n], device_id=to, device_id_type=MESH)
    def push(ref, n, to):
        return copy(ref, ref, n, to)
    def got(ref, n):
        copy(ref, ref, n, nc).wait_recv()
    def first(src, dst, n):
        for t, to in enumerate((nx, ny, nc)):
            copy(src, dst, n + t, to).start()
    def halves(ref, i):
        h = ref.shape[1] // 2
        return ref.at[i, pl.ds(0, h)], ref.at[i, pl.ds(h, h)]
    def second(ref, n, onward=None):
        got(ref.at[ix], n)
        push(halves(ref, ix)[0], n + 3, ny).start()
        push(ref.at[ix], n + 5, nc).start()
        if onward is not None:
            push(ref.at[ix], onward, nz).start()
        got(ref.at[iy], n + 1)
        push(halves(ref, iy)[1], n + 4, nx).start()
        push(ref.at[iy], n + 6, nc).start()
        if onward is not None:
            push(ref.at[iy], onward + 1, nz).start()
    def third(ref, n, onward=None):
        got(halves(ref, idg)[0], n + 3)
        got(halves(ref, idg)[1], n + 4)
        push(ref.at[idg], n + 7, nc).start()
        if onward is not None:
            push(ref.at[idg], onward + 2, nz).start()
    def last(src, ref, n, onward=None):
        for t, i in ((2, it), (5, jx), (6, jy), (7, jdg)):
            got(ref.at[i], n + t)
        for t in (0, 1, 2):
            copy(src, ref.at[me], n + t, nc).wait_send()
        push(halves(ref, ix)[0], n + 3, ny).wait_send()
        push(halves(ref, iy)[1], n + 4, nx).wait_send()
        for t, i in ((5, ix), (6, iy), (7, idg)):
            push(ref.at[i], n + t, nc).wait_send()
        if onward is not None:
            for t, i in enumerate((ix, iy, idg)):
                push(ref.at[i], onward + t, nz).wait_send()
    def part(ref, i):
        cut = ref.shape[-1] // 384 * 128
        return ref.at[..., pl.ds(0, cut)] if i == 0 else ref.at[..., pl.ds(cut, ref.shape[-1] - cut)]
    mine, other = gu.at[z], gu.at[oz]
    m0, m1, o0, o1 = part(mine, 0), part(mine, 1), part(other, 0), part(other, 1)
    in0, in1 = part(gu_in.at[z], 0), part(gu_in.at[z], 1)
    d0, d1, dn0, dn1 = part(dn, 0), part(dn, 1), part(dn_in, 0), part(dn_in, 1)
    keeps = [pltpu.make_async_copy(gu_in.at[0], gu.at[0, me], local.at[0]), pltpu.make_async_copy(gu_in.at[1], gu.at[1, me], local.at[1]),
             pltpu.make_async_copy(dn_in, dn.at[me], local.at[2]), pltpu.make_async_copy(wo_in, wo.at[me], local.at[3])]
    W, D0, D1, G0, G1, Z0, Z1, OWN = 0, 8, 16, 24, 32, 40, 46, 52
    def z_second(ref, n, ts):
        for t in ts:
            i = (ix, iy, idg)[t]
            got(ref.at[i], n + t)
            push(ref.at[i], n + 3 + t, nc).start()
    def at0():
        greet([nx, ny, nc, nz])
        first(in0, m0.at[me], G0)
        first(in1, m1.at[me], G1)
        copy(gu_in.at[oz], other.at[me], OWN, nc).start()
        for k in keeps:
            k.start()
    def at1():
        second(m0, G0, Z0)
        first(wo_in, wo.at[me], W)
    def at3():
        second(m1, G1, Z1)
        first(dn0, d0.at[me], D0)
    def at4():
        third(m0, G0, Z0)
    def at5():
        second(wo, W)
        z_second(o0, Z0, (0, 1))
        first(dn1, d1.at[me], D1)
    def at6():
        third(m1, G1, Z1)
    def at7():
        second(d0, D0)
        third(wo, W)
    def end():
        z_second(o1, Z1, (0, 1))
        z_second(o0, Z0, (2,))
        second(d1, D1)
        third(d0, D0)
        z_second(o1, Z1, (2,))
        third(d1, D1)
        last(wo_in, wo, W)
        last(in0, m0, G0, Z0)
        last(in1, m1, G1, Z1)
        got(other.at[it], OWN)
        copy(gu_in.at[oz], other.at[me], OWN, nc).wait_send()
        for ref, n in ((o0, Z0), (o1, Z1)):
            for t, i, j in ((0, ix, jx), (1, iy, jy), (2, idg, jdg)):
                got(ref.at[j], n + 3 + t)
                push(ref.at[i], n + 3 + t, nc).wait_send()
        last(dn0, d0, D0)
        last(dn1, d1, D1)
        for k in keeps:
            k.wait()
    return {0: at0, 1: at1, 3: at3, 4: at4, 5: at5, 6: at6, 7: at7}, end

def fwd_gather_kernel(*refs):
    (q_ref, k_ref, v_ref, mask_ref, far_ref, w_ref, gu_in, dn_in, wo_in, o_ref, e_ref, r_ref, gu, dn, wo,
     rhs, kaug, vaug, bn, s_ref, send, recv, local) = refs
    before, end = gather_steps(gu_in, dn_in, wo_in, gu, dn, wo, send, recv, local)
    p = pl.program_id(1)
    for at, act in before.items():
        pl.when(p == at)(act)
    fwd_kernel(q_ref, k_ref, v_ref, mask_ref, far_ref, w_ref, o_ref, e_ref, r_ref, rhs, kaug, vaug, bn, s_ref)
    pl.when(p == 7)(end)

def attn_fwd_gather(q, k, v, mask, far, w, gu, dn, wo):
    rows = q.shape[0] // L
    spec = pl.BlockSpec((L, 128), lambda r, p: (r, p))
    hbm = pl.BlockSpec(memory_space=pl.ANY)
    whole = lambda a: pl.BlockSpec(a.shape, lambda r, p: (0,) * a.ndim, pipeline_mode=pl.Buffered(1))
    sds = jax.ShapeDtypeStruct
    return pl.pallas_call(fwd_gather_kernel,
        grid=(rows, 8),
        in_specs=[spec, spec, spec,
            pl.BlockSpec((None, L, 128), lambda r, p: (r, 0, 0)),
            pl.BlockSpec((None, 8, 128), lambda r, p: (p, 0, 0)),
            pl.BlockSpec((None, 8, 512), lambda r, p: (p, 0, 0)), whole(gu), whole(dn), whole(wo)],
        out_specs=[spec, pl.BlockSpec((None, None, L, NT * 256), lambda r, p: (r, p, 0, 0)), spec, hbm, hbm, hbm],
        out_shape=[sds(q.shape, bf), sds((rows, 8, L, NT * 256), bf), sds(q.shape, f32),
                   sds((2, 8) + gu.shape[1:], bf), sds((8,) + dn.shape, bf), sds((8,) + wo.shape, bf)],
        scratch_shapes=[pltpu.VMEM((256, NT * 256), bf), pltpu.VMEM((L, 256), bf), pltpu.VMEM((L, 256), bf), pltpu.VMEM((384, 256), f32), pltpu.VMEM((2, L, 256), f32),
                        pltpu.SemaphoreType.DMA((53,)), pltpu.SemaphoreType.DMA((53,)), pltpu.SemaphoreType.DMA((4,))],
        compiler_params=pltpu.CompilerParams(collective_id=2, has_side_effects=True, vmem_limit_bytes=56 * 2**20),
        name="attn_fwd_gather")(q, k, v, mask, far, w, gu, dn, wo)

DRAIN = 6

def rs_scratch(n, rows, cols):
    h = rows // 2
    pair = pltpu.VMEM((2, 2, h, cols), bf)
    single = pltpu.VMEM((2, h, cols), bf)
    ring = lambda k: pltpu.VMEM((k, rows, cols), bf)
    dma = pltpu.SemaphoreType.DMA
    return [pltpu.VMEM((2, 4, 2, rows, cols), bf), pltpu.VMEM((2, 4, rows, cols), bf)] + [pair] * 6 + [single] * 2 + [ring(4), ring(4), ring(2), ring(n)] + [dma((5, 2)), dma((5, 2)), dma((3, n)), dma((3, n))]

def plus(a, b):
    return a + b

def rs_greet():
    b, m, c, mx, my, md = places()
    greet([(b, mx, c), (b, my, c), (b, m, 1 - c), (b + 1 - 2 * lax.rem(b, 2), m, c), (3 - b, m, c)])

def rs_step(s, n, bufs):
    src, cbuf, sx, sy, kt, kb, xt, yb, t2, b2, part, inward, across, done, send, recv, zsend, zrecv = bufs
    b, m, c, mx, my, md = places()
    o = 1 - c
    nx, ny, nc = (b, mx, c), (b, my, c), (b, m, o)
    nz, na = (b + 1 - 2 * lax.rem(b, 2), m, c), (3 - b, m, c)
    outer = (b == 0) | (b == 3)
    inner = (b == 1) | (b == 2)
    h = kt.shape[2]
    def copy(kind, k, a, z, to):
        return pltpu.make_async_remote_copy(src_ref=a, dst_ref=z, send_sem=send.at[kind, k], recv_sem=recv.at[kind, k], device_id=to, device_id_type=MESH)
    def zcopy(kind, t, a, z, to):
        return pltpu.make_async_remote_copy(src_ref=a, dst_ref=z, send_sem=zsend.at[kind, t], recv_sem=zrecv.at[kind, t], device_id=to, device_id_type=MESH)
    core = lambda k: copy(0, k, src.at[k, :, o], cbuf.at[k], nc)
    x1 = lambda k: copy(1, k, sx.at[k], xt.at[k], nx)
    y1 = lambda k: copy(2, k, sy.at[k], yb.at[k], ny)
    y2 = lambda k: copy(3, k, kt.at[k, 1], t2.at[k], ny)
    x2 = lambda k: copy(4, k, kb.at[k, 1], b2.at[k], nx)
    up = lambda t: zcopy(0, t, part.at[lax.rem(t, 4)], inward.at[lax.rem(t, 4)], nz)
    over = lambda t: zcopy(1, t, part.at[lax.rem(t, 4)], across.at[lax.rem(t, 2)], na)
    down = lambda t: zcopy(2, t, done.at[t], done.at[t], nz)
    def stage(t, act, also=None):
        live = (t >= 0) & (t < n)
        pl.when(live if also is None else live & also)(lambda: act(t))
    def outer_done(t):
        up(t).wait_send()
        down(t).wait_recv()
    def inner_done(t):
        down(t).wait_send()
    def inner_sum(t):
        over(t).wait()
        done[t] = plus(part[lax.rem(t, 4)], across[lax.rem(t, 2)])
        down(t).start()
    def inner_part(t):
        up(t).wait_recv()
        part[lax.rem(t, 4)] = plus(part[lax.rem(t, 4)], inward[lax.rem(t, 4)])
        over(t).start()
    def finish_plane(t):
        k = lax.rem(t, 2)
        y2(k).wait()
        x2(k).wait()
        part[lax.rem(t, 4), 0:h] = plus(kt[k, 0], t2[k])
        part[lax.rem(t, 4), h:2 * h] = plus(kb[k, 0], b2[k])
    def second(t):
        k = lax.rem(t, 2)
        x1(k).wait()
        y1(k).wait()
        kt[k] = plus(kt[k], xt[k])
        kb[k] = plus(kb[k], yb[k])
        y2(k).start()
        x2(k).start()
    def first(t):
        k = lax.rem(t, 2)
        core(k).wait()
        top = lambda i: plus(src[k, i, c, 0:h], cbuf[k, i, 0:h])
        low = lambda i: plus(src[k, i, c, h:2 * h], cbuf[k, i, h:2 * h])
        sx[k, 0], sx[k, 1] = top(mx), top(md)
        sy[k, 0], sy[k, 1] = low(my), low(md)
        x1(k).start()
        y1(k).start()
        kt[k, 0], kt[k, 1] = top(m), top(my)
        kb[k, 0], kb[k, 1] = low(m), low(mx)
    stage(s - 6, outer_done, outer)
    stage(s - 6, inner_done, inner)
    stage(s - 5, inner_sum, inner)
    stage(s - 4, inner_part, inner)
    stage(s - 3, finish_plane)
    stage(s - 3, lambda t: up(t).start(), outer)
    stage(s - 2, second)
    stage(s - 1, first)
    stage(s, lambda t: core(lax.rem(t, 2)).start())

GELU_C = float(np.sqrt(2.0 / np.pi))
def dot_nt(a, b):
    return lax.dot_general(a, b, (((1,), (1,)), ((), ())), preferred_element_type=f32)

def ffn_open(x_ref, ctx_ref, gain_ref, wo_ref, gres_ref, res, n, acc):
    for t in range(0, x_ref.shape[0], 384):
        s = slice(t, t + 384)
        y = x_ref[s, :].astype(f32) + dot(ctx_ref[s, :], wo_ref[...])
        res[s, :] = y
        acc[s, :] = y
        n[s, :] = (y * lax.rsqrt(jnp.mean(y * y, axis=-1, keepdims=True) + EPS) * gain_ref[0:1, :]).astype(bf)
    gres_ref[...] = jnp.zeros_like(gres_ref)

def ffn_block(g_ref, gu_ref, dn_ref, gres_ref, ddn_ref, n, acc):
    d = n.shape[1]
    wg = gu_ref[0].reshape(d, gu_ref.shape[-1])
    wu = gu_ref[1].reshape(d, gu_ref.shape[-1])
    wd = dn_ref[...]
    nn = n[...]
    g = g_ref[...]
    v = dot(nn, wg)
    u = dot(nn, wu)
    gh = dot_nt(g, wd)
    v2 = v * v
    th = jnp.tanh(GELU_C * v * (1.0 + 0.044715 * v2))
    half = 0.5 * (1.0 + th)
    gel = v * half
    h = (gel * u).astype(bf)
    dgel = half + 0.5 * v * (1.0 - th * th) * (GELU_C * (1.0 + 3 * 0.044715 * v2))
    gg = (gh * u * dgel).astype(bf)
    gu = (gh * gel).astype(bf)
    acc[...] = acc[...] + dot(h, wd)
    gres_ref[...] = gres_ref[...] + dot_nt(jnp.concatenate([gg, gu], 1), jnp.concatenate([wg, wu], 1))
    ddn_ref[...] = dot_tl(h, g).astype(bf)
    return dot_tl(nn, gg).astype(bf), dot_tl(nn, gu).astype(bf)

def ffn_close(s, g_ref, gain_ref, wo_ref, out_ref, gres_ref, gctx_ref, res, n, acc):
    out_ref[s, :] = acc[s, :].astype(bf)
    y = res[s, :]
    r = lax.rsqrt(jnp.mean(y * y, axis=-1, keepdims=True) + EPS)
    m = y * r
    gn = gres_ref[s, :]
    w = gn * gain_ref[0:1, :]
    gr = g_ref[s, :].astype(f32) + r * (w - m * jnp.mean(w * m, axis=-1, keepdims=True))
    gres_ref[s, :] = gr
    low = gr.astype(bf)
    n[s, :] = low
    gctx_ref[s, :] = dot_nt(low, wo_ref[...]).astype(bf)
    return jnp.sum(gn * m, axis=0, keepdims=True)

def ffn_kernel(x_ref, ctx_ref, g_ref, gain_ref, wo_ref, gu_ref, dn_ref,
               out_ref, gres_ref, gctx_ref, dwo_ref, ggain_ref, ddn_ref, dgu_ref, res, n, acc):
    j = pl.program_id(0)
    @pl.when(j == 0)
    def _():
        ffn_open(x_ref, ctx_ref, gain_ref, wo_ref, gres_ref, res, n, acc)
    a, b = ffn_block(g_ref, gu_ref, dn_ref, gres_ref, ddn_ref, n, acc)
    dgu_ref[0] = a.reshape(dgu_ref.shape[1:])
    dgu_ref[1] = b.reshape(dgu_ref.shape[1:])
    @pl.when(j == pl.num_programs(0) - 1)
    def _():
        R = x_ref.shape[0]
        total = sum(ffn_close(slice(t, t + 384), g_ref, gain_ref, wo_ref, out_ref, gres_ref, gctx_ref, res, n, acc) for t in range(0, R, 384))
        ggain_ref[...] = jnp.broadcast_to(total, ggain_ref.shape)
        dwo_ref[...] = dot_tl(ctx_ref[...], n[...]).astype(bf)

def ffn_sum_kernel(x_ref, ctx_ref, g_ref, gain_ref, wo_ref, gu_ref, dn_ref,
                   out_ref, gres_ref, gctx_ref, dwo_ref, ggain_ref, ddn_ref, dgu_ref, res, n, acc, *bufs):
    j = pl.program_id(0)
    N = pl.num_programs(0) - DRAIN
    src, done = bufs[0], bufs[13]
    @pl.when(j == 0)
    def _():
        rs_greet()
        ffn_open(x_ref, ctx_ref, gain_ref, wo_ref, gres_ref, res, n, acc)
        ggain_ref[...] = jnp.zeros_like(ggain_ref)
    @pl.when(j < N)
    def _():
        a, b = ffn_block(g_ref, gu_ref, dn_ref, gres_ref, ddn_ref, n, acc)
        k = lax.rem(j, 2)
        rows = a.shape[0] // 8
        src[k, :, :, 0:rows] = a.reshape(4, 2, rows, a.shape[1])
        src[k, :, :, rows:2 * rows] = b.reshape(4, 2, rows, a.shape[1])
    @pl.when(j >= N)
    def _():
        part = x_ref.shape[0] // DRAIN
        s = pl.ds(pl.multiple_of((j - N) * part, part), part)
        total = ffn_close(s, g_ref, gain_ref, wo_ref, out_ref, gres_ref, gctx_ref, res, n, acc)
        ggain_ref[...] = ggain_ref[...] + jnp.broadcast_to(total, ggain_ref.shape)
    rs_step(j, N, bufs)
    @pl.when(j == N + DRAIN - 1)
    def _():
        dwo_ref[...] = dot_tl(ctx_ref[...], n[...]).astype(bf)
        dgu_ref[...] = done[...]

def ffn(x, ctx, g, gain, wo, gu, dn, near, block=256):
    R, d = x.shape
    F = dn.shape[0]
    k = gu.shape[1]
    N = F // block
    sds = jax.ShapeDtypeStruct
    one = lambda *s: pl.BlockSpec(s, lambda j: (0,) * len(s), pipeline_mode=pl.Buffered(1))
    at = lambda j: jnp.minimum(j, N - 1)
    gub = pl.BlockSpec((2, k, d // k, block), lambda j: (0, 0, 0, at(j)))
    dnb = pl.BlockSpec((block, d), lambda j: (at(j), 0))
    rows = 2 * (d // k)
    if near:
        body, extra, steps, last = ffn_sum_kernel, rs_scratch(N, rows, block), N + DRAIN, (one(N, rows, block), sds((N, rows, block), bf))
        params = pltpu.CompilerParams(vmem_limit_bytes=61 * 2**20, collective_id=3, has_side_effects=True)
    else:
        body, extra, steps, last = ffn_kernel, [], N, (gub, sds(gu.shape, bf))
        params = pltpu.CompilerParams(vmem_limit_bytes=61 * 2**20)
    return pl.pallas_call(body, grid=(steps,),
        in_specs=[one(R, d), one(R, d), one(R, d), one(1, d), one(d, d), gub, dnb],
        out_specs=[one(R, d), one(R, d), one(R, d), one(d, d), one(8, d), dnb, last[0]],
        out_shape=[sds((R, d), bf), sds((R, d), f32), sds((R, d), bf), sds((d, d), bf), sds((8, d), f32), sds(dn.shape, bf), last[1]],
        scratch_shapes=[pltpu.VMEM((R, d), f32), pltpu.VMEM((R, d), bf), pltpu.VMEM((R, d), f32)] + extra,
        compiler_params=params, name="ffn")(x, ctx, g, gain, wo, gu, dn)

def sum_rounds(s, box, inbox, send, recv):
    b, m, c, mx, my, md = places()
    peers = [(b, m, 1 - c), (b, mx, c), (b, my, c), (b + 1 - 2 * lax.rem(b, 2), m, c), (3 - b, m, c)]
    def copy(r):
        return pltpu.make_async_remote_copy(src_ref=box.at[r], dst_ref=inbox.at[r], send_sem=send.at[r], recv_sem=recv.at[r], device_id=peers[r], device_id_type=MESH)
    for r in range(5):
        @pl.when(s == r)
        def _():
            copy(r).start()
        @pl.when(s == r + 1)
        def _():
            copy(r).wait()
            box[r + 1] = box[r] + inbox[r]

def bwd_sum_kernel(q_ref, k_ref, v_ref, do_ref, o_ref, r_ref, e_ref, n_ref, x_ref, gres_ref, gain_ref, wq_ref, wk_ref, wv_ref, dn_ref, wo_ref, gain2_ref,
                   gtok_ref, small_ref, out_a, out_b, rhs, vaug, dobd, qaug, ds_ref, nacc, near_ref, far_ref, ggain, box, inbox, ssend, srecv, *bufs):
    p = pl.program_id(0)
    N = pl.num_programs(0) - DRAIN
    half = len(bufs) // 2
    bufs_a, bufs_b = bufs[:half], bufs[half:]
    src_a, done_a = bufs_a[0], bufs_a[13]
    src_b, done_b = bufs_b[0], bufs_b[13]
    NA = done_a.shape[0]
    d = gtok_ref.shape[1]
    k = lax.rem(p, 2)
    def put(src, arrays):
        h = src.shape[3] // 2
        at = 0
        for a in arrays:
            r = a.shape[1] // 2
            a = a.reshape((4, 2) + a.shape[1:])
            src[k, :, :, at:at + r] = a[:, :, 0:r]
            src[k, :, :, h + at:h + at + r] = a[:, :, r:2 * r]
            at += r
    @pl.when(p == 0)
    def _():
        rs_greet()
        bwd_open(rhs, vaug, qaug)
        gtok_ref[...] = jnp.zeros_like(gtok_ref)
        ggain[...] = jnp.zeros_like(ggain)
        box[0] = jnp.zeros(box.shape[1:], f32)
    @pl.when(p < NA)
    def _():
        put(src_a, (dn_ref[...], wo_ref[...]))
    @pl.when(p < N)
    def _():
        g = jnp.concatenate(bwd_pair(q_ref, k_ref, v_ref, do_ref, o_ref, r_ref, e_ref, near_ref, far_ref, rhs, vaug, dobd, qaug, ds_ref, nacc), 1)
        for a in range(2):
            for t in range(4):
                box[0, p, 4 * a + t:4 * a + t + 1] = near_ref[a:a + 1, 128 * t:128 * t + 128]
        box[0, N + p] = far_ref[...]
        gw = dot_tl(n_ref[...], g).astype(bf)
        put(src_b, [gw[:, 128 * t:128 * t + 128].reshape(8, d // 8, 128) for t in range(3)])
        w = jnp.concatenate([w_ref[...].reshape(d, 128) for w_ref in (wq_ref, wk_ref, wv_ref)], 1)
        gtok_ref[...] = gtok_ref[...] + dot_nt(g, w)
    @pl.when((p >= N) & (p < N + 2))
    def _():
        rows = x_ref.shape[0]
        step = rows // 3
        total = jnp.zeros((1, d), f32)
        for t in range(3):
            s = pl.ds(pl.multiple_of((p - N) * rows + t * step, step), step)
            x = x_ref[t * step:t * step + step, :].astype(f32)
            r = lax.rsqrt(jnp.mean(x * x, axis=-1, keepdims=True) + EPS)
            m = x * r
            gn = gtok_ref[s, :]
            w = gn * gain_ref[0:1, :]
            gtok_ref[s, :] = gres_ref[t * step:t * step + step, :] + r * (w - m * jnp.mean(w * m, axis=-1, keepdims=True))
            total = total + jnp.sum(gn * m, axis=0, keepdims=True)
        ggain[...] = ggain[...] + jnp.broadcast_to(total, ggain.shape)
    @pl.when(p == N + 1)
    def _():
        for t in range(8):
            w = d // 8
            box[0, 2 * N, t:t + 1] = ggain[0:1, w * t:w * t + w]
            box[0, 2 * N + 1, t:t + 1] = gain2_ref[0:1, w * t:w * t + w]
    sum_rounds(p - N - 1, box, inbox, ssend, srecv)
    rs_step(p, NA, bufs_a)
    rs_step(p, N, bufs_b)
    @pl.when(p == N + DRAIN - 1)
    def _():
        sum_rounds(5, box, inbox, ssend, srecv)
        small_ref[...] = box[5]
        out_a[...] = done_a[...]
        out_b[...] = done_b[...]

def attn_bwd_sum(q, k, v, do, o, r, e, n, x, gres, gain, qkv_w, dn, wo, gain2):
    R, d = q.shape
    N = d // 128
    NA, wide = 4, d // 4
    rows_a, rows_b = dn.shape[1] + wo.shape[1], 3 * (d // 8)
    sds = jax.ShapeDtypeStruct
    at = lambda p: jnp.minimum(p, N - 1)
    after = lambda p: jnp.clip(p - N, 0, 1)
    spec = pl.BlockSpec((R, 128), lambda p: (0, at(p)))
    one = lambda *s: pl.BlockSpec(s, lambda p: (0,) * len(s), pipeline_mode=pl.Buffered(1))
    part = pl.BlockSpec((R // 2, d), lambda p: (after(p), 0), pipeline_mode=pl.Buffered(1))
    cols = lambda a, t: pl.BlockSpec((8, a.shape[1], 128), lambda p: (0, 0, t * N + at(p)))
    early = lambda a: pl.BlockSpec((8, a.shape[1], wide), lambda p: (0, 0, jnp.minimum(p, NA - 1)), pipeline_mode=pl.Buffered(1))
    dma = pltpu.SemaphoreType.DMA
    small = (2 * N + 2, 8, d // 8)
    return pl.pallas_call(bwd_sum_kernel, grid=(N + DRAIN,),
        in_specs=[spec] * 6 + [pl.BlockSpec((None, None, R, NT * 256), lambda p: (0, at(p), 0, 0)), one(R, d), part, part, one(1, d),
                  cols(qkv_w, 0), cols(qkv_w, 1), cols(qkv_w, 2), early(dn), early(wo), one(8, d)],
        out_specs=[one(R, d), one(*small), one(NA, rows_a, wide), one(N, rows_b, 128)],
        out_shape=[sds((R, d), f32), sds(small, f32), sds((NA, rows_a, wide), bf), sds((N, rows_b, 128), bf)],
        scratch_shapes=[pltpu.VMEM((256, NT * 256), bf), pltpu.VMEM((R, 256), bf), pltpu.VMEM((NT * 256, 128), bf), pltpu.VMEM((NT * 256, 256), bf), pltpu.VMEM((R, NT * 256), bf), pltpu.VMEM((384, 256), f32),
                        pltpu.VMEM((8, 512), f32), pltpu.VMEM((8, 128), f32), pltpu.VMEM((8, d), f32), pltpu.VMEM((6,) + small, f32), pltpu.VMEM((5,) + small, f32), dma((5,)), dma((5,))]
                       + rs_scratch(NA, rows_a, wide) + rs_scratch(N, rows_b, 128),
        compiler_params=pltpu.CompilerParams(vmem_limit_bytes=63 * 2**20, collective_id=4, has_side_effects=True), name="attn_bwd_sum")(
            q, k, v, do, o, r, e, n, x, gres, gain, qkv_w, qkv_w, qkv_w, dn, wo, gain2)

def split_sums(out, sizes):
    h = out.shape[1] // 2
    parts, at = [], 0
    for r in sizes:
        r = r // 2
        a = jnp.concatenate([out[:, at:at + r], out[:, h + at:h + at + r]], 1)
        parts.append(jnp.moveaxis(a, 0, 1).reshape(2 * r, -1).astype(f32))
        at += r
    return parts

def contract_rows(left, right):
    return lax.dot_general(left, right, (((0,), (0,)), ((), ())), preferred_element_type=f32)

def contract_cols(left, right):
    return lax.dot_general(left, right, (((1,), (1,)), ((), ())), preferred_element_type=f32)

def rms_norm(inputs, gain):
    return inputs * lax.rsqrt(jnp.mean(inputs * inputs, axis=-1, keepdims=True) + EPS) * gain

def gather(x):
    return lax.all_gather(x, SHARD, axis=0, tiled=False)

def scatter(x):
    return lax.psum_scatter(x, SHARD, scatter_dimension=0, tiled=True)

def per_device(near, tokens, row_kind, text_length, gain_attn, position_bias_table, weight_query, weight_key, weight_value, weight_out, gain_ffn, weight_gate, weight_up, weight_down, cotangent):
    n1, d = weight_query.shape
    n2 = position_bias_table.shape[0]
    gu_shard = jnp.stack([weight_gate, weight_up])
    mask = mask_cols(row_kind, text_length)
    inputs = tokens.astype(f32)
    if near:
        small = jnp.pad(jnp.stack([gain_attn, gain_ffn, jnp.pad(position_bias_table, (0, n1 - n2))]), ((0, n1 - 3), (0, 0)))
        q, k, v, normed, qkv_w = gather_qkv(tokens, small, weight_query, weight_key, weight_value)
        small = qkv_w[:, 0:3, 3 * d:]
        gain_one = small[:, 0].reshape(d).astype(f32)
    else:
        small = gather(jnp.stack([gain_attn, gain_ffn, jnp.pad(position_bias_table, (0, n1 - n2))]))
        qkv_w = gather(jnp.concatenate([weight_query, weight_key, weight_value], 1))
        gain_one = small[:, 0].reshape(d).astype(f32)
        normed = rms_norm(inputs, gain_one).astype(bf)
        q, k, v = (dot(normed, qkv_w[:, :, t * d:t * d + d].reshape(d, d)).astype(bf) for t in range(3))
    gain_two = small[:, 1].reshape(d).astype(f32)
    far, w = tables(small[:, 2, :n2].reshape(-1))
    if near:
        context, e, r, gu_w, down_w, out_w = attn_fwd_gather(q, k, v, mask, far, w, gu_shard, weight_down, weight_out)
    else:
        context, e, r = attn_fwd(q, k, v, mask, far, w)
        gu_w, down_w, out_w = jnp.moveaxis(gather(gu_shard), 0, 1), gather(weight_down), gather(weight_out)
    ff = gu_w.shape[-1]
    output, grad_residual, grad_context, grad_out_w, g_gain_two, ddn, dgu = ffn(
        tokens, context, cotangent, gain_two.reshape(1, d), out_w.reshape(d, d), gu_w, down_w.reshape(ff, d), near)
    if near:
        shards = gu_w.shape[1]
        grad_tokens, small_g, sums_a, sums_b = attn_bwd_sum(
            q, k, v, grad_context, context, r, e, normed, tokens, grad_residual, gain_one.reshape(1, d), qkv_w,
            ddn.reshape(shards, ff // shards, d), grad_out_w.reshape(shards, n1, d), g_gain_two)
        pairs = (small_g.shape[0] - 2) // 2
        near_sums = small_g[:pairs].reshape(1, pairs, 2, -1)
        far_sums = small_g[None, pairs:2 * pairs]
        g_gain_one, g_gain_two = small_g[2 * pairs].reshape(d), small_g[2 * pairs + 1].reshape(d)
        s_down, s_out = split_sums(sums_a, (ff // shards, n1))
        s_q, s_k, s_v = split_sums(sums_b, (n1, n1, n1))
        dgu = dgu.reshape(dgu.shape[0], 2, n1, -1).transpose(1, 2, 0, 3).reshape(2, n1, ff).astype(f32)
        s_gate, s_up = dgu[0], dgu[1]
    else:
        total = lambda x: lax.psum(scatter(x), "batch").astype(f32)
        gq, gk, gv, near_sums, far_sums = attn_bwd(q, k, v, grad_context, context, r, e)
        grads = (gq, gk, gv)
        s_gate, s_up, s_down, s_out = (total(x) for x in (dgu[0].reshape(d, ff), dgu[1].reshape(d, ff), ddn, grad_out_w))
        s_q, s_k, s_v = (total(contract_rows(normed, x).astype(bf)) for x in grads)
        grad_normed = sum(contract_cols(x, qkv_w[:, :, t * d:t * d + d].reshape(d, d)) for t, x in enumerate(grads))
        _, first_pull = jax.vjp(rms_norm, inputs, gain_one)
        share, g_gain_one = first_pull(grad_normed)
        grad_tokens = grad_residual + share
    g_table = table_grad(near_sums, far_sums)
    if not near:
        small_g = lax.psum(jnp.concatenate([g_gain_one, g_gain_two[0], g_table]), ("batch", "dp", "narrow"))
        g_gain_one, g_gain_two, g_table = small_g[:d], small_g[d:2 * d], small_g[2 * d:]
    at = lax.axis_index("dp") * lax.axis_size("narrow") + lax.axis_index("narrow")
    r_gain_one = lax.dynamic_slice_in_dim(g_gain_one, at * n1, n1)
    r_gain_two = lax.dynamic_slice_in_dim(g_gain_two, at * n1, n1)
    r_table = lax.dynamic_slice_in_dim(g_table, at * n2, n2)
    return (output, grad_tokens, r_gain_one, r_table, s_q, s_k, s_v, s_out, r_gain_two, s_gate, s_up, s_down)

def solution(mesh):
    near = (mesh.shape["batch"], mesh.shape["dp"], mesh.shape["narrow"]) == (4, 4, 2)
    placed = (
        P(("batch", "dp", "narrow"), None),
        P(("batch", "dp", "narrow")),
        P(("batch", "dp", "narrow"), None),
        P(("dp", "narrow")),
        P(("dp", "narrow")),
        P(("dp", "narrow"), None),
        P(("dp", "narrow"), None),
        P(("dp", "narrow"), None),
        P(("dp", "narrow"), None),
        P(("dp", "narrow")),
        P(("dp", "narrow"), None),
        P(("dp", "narrow"), None),
        P(("dp", "narrow"), None),
        P(("batch", "dp", "narrow"), None),
    )
    return jax.shard_map(
        functools.partial(per_device, near),
        mesh=mesh,
        in_specs=placed,
        out_specs=(
            P(("batch", "dp", "narrow"), None),
            P(("batch", "dp", "narrow"), None),
            P(("dp", "narrow")),
            P(("dp", "narrow")),
            P(("dp", "narrow"), None),
            P(("dp", "narrow"), None),
            P(("dp", "narrow"), None),
            P(("dp", "narrow"), None),
            P(("dp", "narrow")),
            P(("dp", "narrow"), None),
            P(("dp", "narrow"), None),
            P(("dp", "narrow"), None),
        ),
        check_vma=False,
    )
```

```python
import functools

import jax
import jax.numpy as jnp
import numpy as np
from jax import lax
from jax.experimental import pallas as pl
from jax.experimental.pallas import tpu as pltpu
from jax.sharding import PartitionSpec as P

EPS = 1e-06
SHARD = ("dp", "narrow")
bf=jnp.bfloat16; f32=jnp.float32
T=128; L=1152; NT=L//T
NEG=-1e30
def dot(a,b): return jnp.dot(a,b,preferred_element_type=f32)
def dot_tl(a,b): return lax.dot_general(a,b,(((0,),(0,)),((),())),preferred_element_type=f32)

def fwd_open(rhs,vaug):
    rhs[...]=jnp.zeros_like(rhs)
    row=lax.broadcasted_iota(jnp.int32,(128,NT*256),0)
    col=lax.broadcasted_iota(jnp.int32,(128,NT*256),1)
    rhs[128:256,:]=(row==col//128).astype(f32).astype(bf)
    vaug[:,128:256]=jnp.ones((L,128),bf)

def fwd_pair(q,k,v,mask,lo,hi,bias,o_ref,e_ref,r_ref,rhs,kaug,vaug,bn,s_ref):
    qT=q.T
    for i in range(NT):
        rhs[0:64,256*i:256*i+128]=qT[0:64,128*i:128*i+128]
        rhs[64:128,256*i+128:256*i+256]=qT[64:128,128*i:128*i+128]
    kaug[:,0:128]=k
    row=lax.broadcasted_iota(jnp.int32,(L,128),0)//128
    col=lax.broadcasted_iota(jnp.int32,(L,128),1)//2
    far=jnp.where(row<col-1,lo,jnp.where(row>col+1,hi,0.0))
    kaug[:,128:256]=(mask+far).astype(bf)
    vaug[:,0:128]=v
    for a in range(2):
        wb=jnp.broadcast_to(bias[a:a+1,:],(384,512))
        bn[:,128*a:128*a+128]=pltpu.roll(wb,0,1,stride=1,stride_axis=0)[:,0:128]
    def scores(i,slot):
        ri=rhs[:,256*i:256*i+256]
        first,last=max(0,i-1)*128,min(NT,i+2)*128
        off=(first//128-(i-1))*128
        x=dot(kaug[...],ri)
        xn=x[first:last]+bn[off:off+last-first,:]
        ms=[jnp.max(xn,axis=0,keepdims=True)]
        s_ref[slot,first:last,:]=xn
        if first>0:
            s_ref[slot,0:first,:]=x[0:first]; ms.append(jnp.max(x[0:first],axis=0,keepdims=True))
        if last<L:
            s_ref[slot,last:L,:]=x[last:L]; ms.append(jnp.max(x[last:L],axis=0,keepdims=True))
        m=ms[0]
        for y in ms[1:]: m=jnp.maximum(m,y)
        return m
    lane=lax.broadcasted_iota(jnp.int32,(128,128),1)<64
    def finish(i,slot,m):
        e=jnp.exp(s_ref[slot]-m).astype(bf)
        e_ref[:,pl.ds(i*256,256)]=e
        o=dot_tl(e,vaug[...])
        num=jnp.where(lane,o[0:128,0:128],o[128:256,0:128])
        den=jnp.where(lane,o[0:128,128:256],o[128:256,128:256])
        r=1.0/den
        rows=pl.ds(i*128,128)
        o_ref[rows,:]=(num*r).astype(bf)
        r_ref[rows,:]=r
    m=scores(0,0)
    for i in range(NT):
        mn=scores(i+1,(i+1)%2) if i+1<NT else None
        finish(i,i%2,m)
        m=mn

def fwd_kernel(q_ref,k_ref,v_ref,mask_ref,far_ref,w_ref,o_ref,e_ref,r_ref,rhs,kaug,vaug,bn,s_ref):
    @pl.when((pl.program_id(0)==0)&(pl.program_id(1)==0))
    def _():
        fwd_open(rhs,vaug)
    fwd_pair(q_ref[...],k_ref[...],v_ref[...],mask_ref[...],far_ref[0:1,:],far_ref[1:2,:],w_ref[...],o_ref,e_ref,r_ref,rhs,kaug,vaug,bn,s_ref)

def attn_fwd(q,k,v,mask,far,w):
    rows=q.shape[0]//L
    spec=pl.BlockSpec((L,128),lambda r,p:(r,p))
    return pl.pallas_call(fwd_kernel,
        grid=(rows,8),
        in_specs=[spec,spec,spec,
            pl.BlockSpec((None,L,128),lambda r,p:(r,0,0)),
            pl.BlockSpec((None,8,128),lambda r,p:(p,0,0)),
            pl.BlockSpec((None,8,512),lambda r,p:(p,0,0))],
        out_specs=[spec,pl.BlockSpec((None,None,L,NT*256),lambda r,p:(r,p,0,0)),spec],
        out_shape=[jax.ShapeDtypeStruct(q.shape,bf),jax.ShapeDtypeStruct((rows,8,L,NT*256),bf),jax.ShapeDtypeStruct(q.shape,f32)],
        scratch_shapes=[pltpu.VMEM((256,NT*256),bf),pltpu.VMEM((L,256),bf),pltpu.VMEM((L,256),bf),pltpu.VMEM((384,256),f32),pltpu.VMEM((2,L,256),f32)],
        compiler_params=pltpu.CompilerParams(vmem_limit_bytes=56*2**20),
        name="attn_fwd",
    )(q,k,v,mask,far,w)

THR=(12,16,23,32,46,64,91)
def bucket_np(d):
    n=np.abs(d); c=np.full_like(n,8)
    for t in THR: c=c+(n>=t)
    return np.where(n<8,n,c)+16*(d>0)
def tables(table):
    t=table.reshape(16,32).astype(f32)
    y=np.arange(512); y=np.where(y>=128,y-512,y)
    d=-128-y
    oh=(np.arange(32)[:,None]==bucket_np(d)[None,:]).astype(np.float32)
    w=jnp.dot(t,jnp.asarray(oh),precision=lax.Precision.HIGHEST)
    w=jnp.pad(w.reshape(8,2,512),((0,0),(0,6),(0,0)))
    lo=jnp.tile(t[:,15].reshape(8,1,2),(1,1,64)); hi=jnp.tile(t[:,31].reshape(8,1,2),(1,1,64))
    far=jnp.pad(jnp.concatenate([lo,hi],1),((0,0),(0,6),(0,0)))
    return far,w
def mask_cols(row_kind,text_length):
    pos=np.arange(L)
    kind=row_kind[:,None]
    seg=kind*(pos//384)[None]
    off=pos[None]-seg*384
    img=jnp.where(kind==1,256,1024)
    tl=jnp.where(seg==0,text_length[:,0:1],jnp.where(seg==1,text_length[:,1:2],text_length[:,2:3]))
    live=off<img+tl
    qseg=kind*np.minimum(np.arange(128)//2//3,2)[None]
    ok=live[:,:,None]&(seg[:,:,None]==qseg[:,None,:])
    return jnp.where(ok,0.0,NEG).astype(f32)

def bwd_open(rhs,vaug,qaug):
    rhs[...]=jnp.zeros_like(rhs)
    c=lax.broadcasted_iota(jnp.int32,(L,128),1)
    vaug[:,128:256]=(c<3).astype(f32).astype(bf)
    row=lax.broadcasted_iota(jnp.int32,(NT*256,128),0)
    col=lax.broadcasted_iota(jnp.int32,(NT*256,128),1)
    qaug[:,128:256]=(row//128==col).astype(f32).astype(bf)

def bwd_pair(q_ref,k_ref,v_ref,do_ref,o_ref,r_ref,e_ref,near_ref,far_ref,rhs,vaug,dobd,qaug,ds_ref,nacc):
    q=q_ref[...]; k=k_ref[...]
    vaug[:,0:128]=v_ref[...]
    dof=do_ref[...].astype(f32)*r_ref[...]
    dos=dof.astype(bf)
    dT=dos.T
    pT=(dos.astype(f32)*o_ref[...].astype(f32)).T
    D=jnp.concatenate([jnp.sum(pT[0:64],axis=0,keepdims=True),jnp.sum(pT[64:128],axis=0,keepdims=True)],0)
    D=-D
    D1=D.astype(bf); D2=(D-D1.astype(f32)); D3=(D2-D2.astype(bf).astype(f32)).astype(bf); D2=D2.astype(bf)
    lane=lax.broadcasted_iota(jnp.int32,(128,128),1)<64
    zero=jnp.zeros((128,128),bf)
    z13=jnp.zeros((13,128),bf)
    for i in range(NT):
        t=slice(128*i,128*i+128)
        for a in range(2):
            h=slice(64*a,64*a+64)
            c=slice(256*i+128*a,256*i+128*a+128)
            rhs[h,c]=dT[h,t]
            rhs[128:144,c]=jnp.concatenate([D1[a:a+1,t],D2[a:a+1,t],D3[a:a+1,t],z13],0)
            dobd[c,:]=jnp.where(lane==(a==0),dos[t],zero)
            qaug[c,0:128]=jnp.where(lane==(a==0),q[t],zero)
    nacc[...]=jnp.zeros_like(nacc)
    dqs=[]
    for i in range(NT):
        c=slice(256*i,256*i+256)
        lo,hi=max(0,i-1)*128,min(NT,i+2)*128
        off=(lo//128-(i-1))*128
        dp=dot(vaug[...],rhs[:,c])
        ds=e_ref[:,c].astype(f32)*dp
        nacc[off:off+hi-lo,:]+=ds[lo:hi]
        dsb=ds.astype(bf)
        ds_ref[:,c]=dsb
        g=dot_tl(dsb,k)
        dqs.append(jnp.where(lane,g[0:128],g[128:256]).astype(bf))
    dv=dot(e_ref[...],dobd[...]).astype(bf)
    g=dot(ds_ref[...],qaug[...])
    dk=g[:,0:128].astype(bf)
    G=g[:,128:256]
    row=lax.broadcasted_iota(jnp.int32,(L,128),0)//128
    col=lax.broadcasted_iota(jnp.int32,(L,128),1)//2
    far_ref[0:1,:]=jnp.sum(jnp.where(row<col-1,G,0.0),axis=0,keepdims=True)
    far_ref[1:2,:]=jnp.sum(jnp.where(row>col+1,G,0.0),axis=0,keepdims=True)
    far_ref[2:8,:]=jnp.zeros((6,128),f32)
    near_ref[2:8,:]=jnp.zeros((6,512),f32)
    rev=(lax.broadcasted_iota(jnp.int32,(128,128),0)+lax.broadcasted_iota(jnp.int32,(128,128),1)==127).astype(f32)
    for a in range(2):
        x=jnp.dot(nacc[:,128*a:128*a+128],rev,precision=lax.Precision.HIGHEST,preferred_element_type=f32)
        x=jnp.concatenate([x,jnp.zeros((384,384),f32)],1)
        x=pltpu.roll(x,0,1,stride=1,stride_axis=0)
        near_ref[a:a+1,:]=jnp.sum(x,axis=0,keepdims=True)
    return jnp.concatenate(dqs,0),dk,dv

def bwd_kernel(q_ref,k_ref,v_ref,do_ref,o_ref,r_ref,e_ref,dq_ref,dk_ref,dv_ref,near_ref,far_ref,rhs,vaug,dobd,qaug,ds_ref,nacc):
    @pl.when((pl.program_id(0)==0)&(pl.program_id(1)==0))
    def _():
        bwd_open(rhs,vaug,qaug)
    dq_ref[...],dk_ref[...],dv_ref[...]=bwd_pair(q_ref,k_ref,v_ref,do_ref,o_ref,r_ref,e_ref,near_ref,far_ref,rhs,vaug,dobd,qaug,ds_ref,nacc)

def attn_bwd(q,k,v,do,o,r,e):
    rows=q.shape[0]//L
    spec=pl.BlockSpec((L,128),lambda r,p:(r,p))
    sds=jax.ShapeDtypeStruct
    return pl.pallas_call(bwd_kernel,
        grid=(rows,8),
        in_specs=[spec]*6+[pl.BlockSpec((None,None,L,NT*256),lambda r,p:(r,p,0,0))],
        out_specs=[spec]*3+[pl.BlockSpec((None,None,8,512),lambda r,p:(r,p,0,0)),pl.BlockSpec((None,None,8,128),lambda r,p:(r,p,0,0))],
        out_shape=[sds(q.shape,bf)]*3+[sds((rows,8,8,512),f32),sds((rows,8,8,128),f32)],
        scratch_shapes=[pltpu.VMEM((256,NT*256),bf),pltpu.VMEM((L,256),bf),pltpu.VMEM((NT*256,128),bf),pltpu.VMEM((NT*256,256),bf),pltpu.VMEM((L,NT*256),bf),pltpu.VMEM((384,256),f32)],
        compiler_params=pltpu.CompilerParams(vmem_limit_bytes=58*2**20),
        name="attn_bwd",
    )(q,k,v,do,o,r,e)
def table_grad(near,far):
    y=np.arange(512)
    oh=(bucket_np(y-255)[:,None]==np.arange(32)[None,:]).astype(np.float32)
    n=jnp.sum(near[:,:,0:2],0).reshape(16,512)
    g=jnp.dot(n,jnp.asarray(oh),precision=lax.Precision.HIGHEST)
    f=jnp.sum(far[:,:,0:2],0).reshape(8,2,64,2).sum(2)
    lo=f[:,0].reshape(16,1); hi=f[:,1].reshape(16,1)
    g=g+lo*np.eye(32,dtype=np.float32)[15][None]+hi*np.eye(32,dtype=np.float32)[31][None]
    return g.reshape(512)

MESH = pl.DeviceIdType.MESH

def places():
    b, m, c = lax.axis_index("batch"), lax.axis_index("dp"), lax.axis_index("narrow")
    x, y = lax.rem(m, 2), m // 2
    mx = y * 2 + (1 - x)
    my = (1 - y) * 2 + x
    md = (1 - y) * 2 + (1 - x)
    return b, m, c, mx, my, md

def greet(devices):
    barrier = pltpu.get_barrier_semaphore()
    for d in devices:
        pl.semaphore_signal(barrier, inc=1, device_id=d, device_id_type=MESH)
    pl.semaphore_wait(barrier, len(devices))

def gather_steps(gu_in, dn_in, wo_in, gu, dn, wo, send, recv, local):
    b, m, c, mx, my, md = places()
    o = 1 - c
    z = lax.rem(b, 2)
    oz = 1 - z
    nx, ny, nc, nz = (b, mx, c), (b, my, c), (b, m, o), (b + 1 - 2 * z, m, c)
    me, it = m * 2 + c, m * 2 + o
    ix, iy, idg = mx * 2 + c, my * 2 + c, md * 2 + c
    jx, jy, jdg = mx * 2 + o, my * 2 + o, md * 2 + o
    def copy(src, dst, n, to):
        return pltpu.make_async_remote_copy(src_ref=src, dst_ref=dst, send_sem=send.at[n], recv_sem=recv.at[n], device_id=to, device_id_type=MESH)
    def push(ref, n, to):
        return copy(ref, ref, n, to)
    def got(ref, n):
        copy(ref, ref, n, nc).wait_recv()
    def first(src, dst, n):
        for t, to in enumerate((nx, ny, nc)):
            copy(src, dst, n + t, to).start()
    def halves(ref, i):
        h = ref.shape[1] // 2
        return ref.at[i, pl.ds(0, h)], ref.at[i, pl.ds(h, h)]
    def second(ref, n, onward=None):
        got(ref.at[ix], n)
        push(halves(ref, ix)[0], n + 3, ny).start()
        push(ref.at[ix], n + 5, nc).start()
        if onward is not None:
            push(ref.at[ix], onward, nz).start()
        got(ref.at[iy], n + 1)
        push(halves(ref, iy)[1], n + 4, nx).start()
        push(ref.at[iy], n + 6, nc).start()
        if onward is not None:
            push(ref.at[iy], onward + 1, nz).start()
    def third(ref, n, onward=None):
        got(halves(ref, idg)[0], n + 3)
        got(halves(ref, idg)[1], n + 4)
        push(ref.at[idg], n + 7, nc).start()
        if onward is not None:
            push(ref.at[idg], onward + 2, nz).start()
    def last(src, ref, n, onward=None):
        for t, i in ((2, it), (5, jx), (6, jy), (7, jdg)):
            got(ref.at[i], n + t)
        for t in (0, 1, 2):
            copy(src, ref.at[me], n + t, nc).wait_send()
        push(halves(ref, ix)[0], n + 3, ny).wait_send()
        push(halves(ref, iy)[1], n + 4, nx).wait_send()
        for t, i in ((5, ix), (6, iy), (7, idg)):
            push(ref.at[i], n + t, nc).wait_send()
        if onward is not None:
            for t, i in enumerate((ix, iy, idg)):
                push(ref.at[i], onward + t, nz).wait_send()
    def part(ref, i):
        cut = ref.shape[-1] // 384 * 128
        return ref.at[..., pl.ds(0, cut)] if i == 0 else ref.at[..., pl.ds(cut, ref.shape[-1] - cut)]
    mine, other = gu.at[z], gu.at[oz]
    m0, m1, o0, o1 = part(mine, 0), part(mine, 1), part(other, 0), part(other, 1)
    in0, in1 = part(gu_in.at[z], 0), part(gu_in.at[z], 1)
    d0, d1, dn0, dn1 = part(dn, 0), part(dn, 1), part(dn_in, 0), part(dn_in, 1)
    keeps = [pltpu.make_async_copy(gu_in.at[0], gu.at[0, me], local.at[0]), pltpu.make_async_copy(gu_in.at[1], gu.at[1, me], local.at[1]),
             pltpu.make_async_copy(dn_in, dn.at[me], local.at[2]), pltpu.make_async_copy(wo_in, wo.at[me], local.at[3])]
    W, D0, D1, G0, G1, Z0, Z1, OWN = 0, 8, 16, 24, 32, 40, 46, 52
    def z_second(ref, n, ts):
        for t in ts:
            i = (ix, iy, idg)[t]
            got(ref.at[i], n + t)
            push(ref.at[i], n + 3 + t, nc).start()
    def begin():
        first(in0, m0.at[me], G0)
        first(in1, m1.at[me], G1)
        copy(gu_in.at[oz], other.at[me], OWN, nc).start()
        for k in keeps:
            k.start()
    def at0():
        second(m0, G0, Z0)
        first(wo_in, wo.at[me], W)
    def at2():
        second(m1, G1, Z1)
        third(m0, G0, Z0)
        first(dn0, d0.at[me], D0)
    def at3():
        second(wo, W)
        first(dn1, d1.at[me], D1)
    def at4():
        third(m1, G1, Z1)
        z_second(o0, Z0, (0, 1))
    def at6():
        second(d0, D0)
        third(wo, W)
    def end():
        z_second(o1, Z1, (0, 1))
        z_second(o0, Z0, (2,))
        third(d0, D0)
        second(d1, D1)
        third(d1, D1)
        z_second(o1, Z1, (2,))
        last(wo_in, wo, W)
        last(in0, m0, G0, Z0)
        last(in1, m1, G1, Z1)
        got(other.at[it], OWN)
        copy(gu_in.at[oz], other.at[me], OWN, nc).wait_send()
        for ref, n in ((o0, Z0), (o1, Z1)):
            for t, i, j in ((0, ix, jx), (1, iy, jy), (2, idg, jdg)):
                got(ref.at[j], n + 3 + t)
                push(ref.at[i], n + 3 + t, nc).wait_send()
        last(dn0, d0, D0)
        last(dn1, d1, D1)
        for k in keeps:
            k.wait()
    return begin, {1: at0, 3: at2, 4: at3, 5: at4, 7: at6}, end


def bias_consts():
    y = np.arange(512)
    y = np.where(y >= 128, y - 512, y)
    ids = bucket_np(-128 - y)
    out = np.zeros((128, 1280), np.float32)
    for a in range(2):
        out[32 * a + ids, 512 * a + np.arange(512)] = 1
        out[32 * a + 15, 1024 + a:1152:2] = 1
        out[32 * a + 31, 1152 + a:1280:2] = 1
    return jnp.asarray(out, bf)

def mask_block(kind, text):
    pos = lax.broadcasted_iota(jnp.int32, (L, 128), 0)
    tile = lax.broadcasted_iota(jnp.int32, (L, 128), 1) // 2
    seg = jnp.where(kind == 1, pos // 384, 0)
    mine = jnp.where(kind == 1, tile // 3, 0)
    length = jnp.where(seg == 0, text[0], jnp.where(seg == 1, text[1], text[2]))
    live = pos - seg * 384 < jnp.where(kind == 1, 256, 1024) + length
    return jnp.where(live & (seg == mine), 0.0, NEG)

def front_kernel(kind_ref, text_ref, x_ref, gain1_ref, gain2_ref, table_ref, wq_ref, wk_ref, wv_ref, gate_ref, up_ref, dn_in, wo_in, const_ref,
                 o_ref, e_ref, r_ref, n_ref, qkv_out, w_out, gu, dn, wo,
                 W, acc, rstd, qkv, gu_in, mask, rhs, kaug, vaug, bn, s_ref, wsend, wrecv, wlocal, send, recv, local):
    b, m, c, mx, my, md = places()
    o = 1 - c
    nx, ny, nc, nz = (b, mx, c), (b, my, c), (b, m, o), (b + 1 - 2 * lax.rem(b, 2), m, c)
    d = wq_ref.shape[1]
    rows = wq_ref.shape[0]
    half = rows // 2
    me = m * 2 + c
    p = pl.program_id(0)
    begin, during, end = gather_steps(gu_in, dn_in, wo_in, gu, dn, wo, send, recv, local)
    keeps = (pltpu.make_async_copy(W, w_out, wlocal.at[0]), pltpu.make_async_copy(qkv, qkv_out, wlocal.at[1]))
    def push(src, n, to):
        return pltpu.make_async_remote_copy(src_ref=src, dst_ref=src, send_sem=wsend.at[n], recv_sem=wrecv.at[n], device_id=to, device_id_type=MESH)
    def got(ref, n):
        push(ref, n, nc).wait_recv()
    def chunk(j, first):
        cols = pl.ds(pl.multiple_of(j * 2 * rows, 2 * rows), 2 * rows)
        gain = jnp.concatenate([W[2 * j, 0:1, 3 * d:3 * d + rows], W[2 * j + 1, 0:1, 3 * d:3 * d + rows]], 1).astype(f32)
        n = (x_ref[:, cols].astype(f32) * rstd[...] * gain).astype(bf)
        n_ref[:, cols] = n
        for t in range(3):
            y = dot(n, W[pl.ds(2 * j, 2), :, t * d:t * d + d].reshape(2 * rows, d))
            if first:
                acc[:, t * d:t * d + d] = y
            else:
                acc[:, t * d:t * d + d] = acc[:, t * d:t * d + d] + y
    @pl.when(p == 0)
    def _():
        W[me, :, 0:d] = wq_ref[...]
        W[me, :, d:2 * d] = wk_ref[...]
        W[me, :, 2 * d:3 * d] = wv_ref[...]
        W[me, :, 3 * d:3 * d + 128] = jnp.zeros((rows, 128), bf)
        W[me, 0:1, 3 * d:3 * d + rows] = gain1_ref[...]
        W[me, 1:2, 3 * d:3 * d + rows] = gain2_ref[...]
        W[me, 2:3, 3 * d:3 * d + table_ref.shape[1]] = table_ref[...]
        greet([nx, ny, nc, nz])
        top, low = pl.ds(0, half), pl.ds(half, half)
        sends = [push(W.at[me], 0, nx), push(W.at[me], 1, ny), push(W.at[me], 2, nc)]
        for s in sends:
            s.start()
        gu_in[0] = gate_ref[...]
        gu_in[1] = up_ref[...]
        for t in range(0, L, 384):
            x = x_ref[t:t + 384, :].astype(f32)
            rstd[t:t + 384, :] = lax.rsqrt(jnp.mean(x * x, axis=-1, keepdims=True) + EPS)
        mask[...] = mask_block(kind_ref[0], (text_ref[0, 0], text_ref[0, 1], text_ref[0, 2]))
        fwd_open(rhs, vaug)
        ix, iy, idg = mx * 2 + c, my * 2 + c, md * 2 + c
        jx, jy, jdg = mx * 2 + o, my * 2 + o, md * 2 + o
        got(W.at[m * 2 + o], 2)
        chunk(m, True)
        got(W.at[ix], 0)
        more = [push(W.at[ix, top], 3, ny), push(W.at[ix], 5, nc)]
        got(W.at[iy], 1)
        more += [push(W.at[iy, low], 4, nx), push(W.at[iy], 6, nc)]
        for s in more:
            s.start()
        begin()
        got(W.at[jx], 5)
        chunk(mx, False)
        got(W.at[jy], 6)
        chunk(my, False)
        got(W.at[idg, top], 3)
        got(W.at[idg, low], 4)
        more.append(push(W.at[idg], 7, nc))
        more[-1].start()
        got(W.at[jdg], 7)
        keeps[0].start()
        chunk(md, False)
        for t in range(3 * d // 128):
            qkv[t] = acc[:, 128 * t:128 * t + 128].astype(bf)
        keeps[1].start()
        for s in sends + more:
            s.wait_send()
    for at, act in during.items():
        pl.when(p == at)(act)
    @pl.when(p > 0)
    def _():
        h = p - 1
        N = d // 128
        values = jnp.broadcast_to(W[h, 2:3, 3 * d:3 * d + 128], (16, 128))
        bias = dot(values, const_ref[...])
        fwd_pair(qkv[h], qkv[N + h], qkv[2 * N + h], mask[...], bias[0:1, 1024:1152], bias[0:1, 1152:1280],
                 jnp.concatenate([bias[0:1, 0:512], bias[0:1, 512:1024]], 0), o_ref, e_ref, r_ref, rhs, kaug, vaug, bn, s_ref)
    @pl.when(p == pl.num_programs(0) - 1)
    def _():
        end()
        for k in keeps:
            k.wait()

def front(kind, text, x, gain1, gain2, table, wq, wk, wv, gate, up, dn, wo):
    R, d = x.shape
    rows = wq.shape[0]
    N = d // 128
    at = lambda p: jnp.maximum(p - 1, 0)
    spec = pl.BlockSpec((R, 128), lambda p: (0, at(p)))
    hbm = pl.BlockSpec(memory_space=pl.ANY)
    whole = lambda a: pl.BlockSpec(a.shape, lambda p: (0,) * a.ndim, pipeline_mode=pl.Buffered(1))
    smem = pl.BlockSpec(memory_space=pltpu.SMEM)
    sds = jax.ShapeDtypeStruct
    dma = pltpu.SemaphoreType.DMA
    row = lambda a: a.reshape(1, -1)
    vectors = (x, row(gain1), row(gain2), row(table), wq, wk, wv, gate, up, dn, wo, bias_consts())
    wide = 3 * d + 128
    return pl.pallas_call(front_kernel, grid=(1 + N,),
        in_specs=[smem, smem] + [whole(a) for a in vectors],
        out_specs=[spec, pl.BlockSpec((None, None, R, NT * 256), lambda p: (0, at(p), 0, 0)), spec,
                   pl.BlockSpec((R, d), lambda p: (0, 0), pipeline_mode=pl.Buffered(1))] + [hbm] * 5,
        out_shape=[sds((R, d), bf), sds((1, N, R, NT * 256), bf), sds((R, d), f32), sds((R, d), bf), sds((3 * N, R, 128), bf),
                   sds((8, rows, wide), bf), sds((2, 8) + gate.shape, bf), sds((8,) + dn.shape, bf), sds((8,) + wo.shape, bf)],
        scratch_shapes=[pltpu.VMEM((8, rows, wide), bf), pltpu.VMEM((R, 3 * d), f32), pltpu.VMEM((R, 1), f32), pltpu.VMEM((3 * N, R, 128), bf),
                        pltpu.VMEM((2,) + gate.shape, bf), pltpu.VMEM((R, 128), f32),
                        pltpu.VMEM((256, NT * 256), bf), pltpu.VMEM((R, 256), bf), pltpu.VMEM((R, 256), bf), pltpu.VMEM((384, 256), f32), pltpu.VMEM((2, R, 256), f32),
                        dma((8,)), dma((8,)), dma((2,)), dma((53,)), dma((53,)), dma((4,))],
        compiler_params=pltpu.CompilerParams(collective_id=1, has_side_effects=True, vmem_limit_bytes=63 * 2**20),
        name="front")(kind, text, *vectors)

DRAIN = 6

def rs_scratch(n, rows, cols):
    h = rows // 2
    pair = pltpu.VMEM((2, 2, h, cols), bf)
    single = pltpu.VMEM((2, h, cols), bf)
    ring = lambda k: pltpu.VMEM((k, rows, cols), bf)
    dma = pltpu.SemaphoreType.DMA
    return [pltpu.VMEM((2, 4, 2, rows, cols), bf), pltpu.VMEM((2, 4, rows, cols), bf)] + [pair] * 6 + [single] * 2 + [ring(4), ring(4), ring(2), ring(n)] + [dma((5, 2)), dma((5, 2)), dma((3, n)), dma((3, n))]

def plus(a, b):
    return a + b

def rs_greet():
    b, m, c, mx, my, md = places()
    greet([(b, mx, c), (b, my, c), (b, m, 1 - c), (b + 1 - 2 * lax.rem(b, 2), m, c), (3 - b, m, c)])

def rs_step(s, n, bufs):
    src, cbuf, sx, sy, kt, kb, xt, yb, t2, b2, part, inward, across, done, send, recv, zsend, zrecv = bufs
    b, m, c, mx, my, md = places()
    o = 1 - c
    nx, ny, nc = (b, mx, c), (b, my, c), (b, m, o)
    nz, na = (b + 1 - 2 * lax.rem(b, 2), m, c), (3 - b, m, c)
    outer = (b == 0) | (b == 3)
    inner = (b == 1) | (b == 2)
    h = kt.shape[2]
    def copy(kind, k, a, z, to):
        return pltpu.make_async_remote_copy(src_ref=a, dst_ref=z, send_sem=send.at[kind, k], recv_sem=recv.at[kind, k], device_id=to, device_id_type=MESH)
    def zcopy(kind, t, a, z, to):
        return pltpu.make_async_remote_copy(src_ref=a, dst_ref=z, send_sem=zsend.at[kind, t], recv_sem=zrecv.at[kind, t], device_id=to, device_id_type=MESH)
    core = lambda k: copy(0, k, src.at[k, :, o], cbuf.at[k], nc)
    x1 = lambda k: copy(1, k, sx.at[k], xt.at[k], nx)
    y1 = lambda k: copy(2, k, sy.at[k], yb.at[k], ny)
    y2 = lambda k: copy(3, k, kt.at[k, 1], t2.at[k], ny)
    x2 = lambda k: copy(4, k, kb.at[k, 1], b2.at[k], nx)
    up = lambda t: zcopy(0, t, part.at[lax.rem(t, 4)], inward.at[lax.rem(t, 4)], nz)
    over = lambda t: zcopy(1, t, part.at[lax.rem(t, 4)], across.at[lax.rem(t, 2)], na)
    down = lambda t: zcopy(2, t, done.at[t], done.at[t], nz)
    def stage(t, act, also=None):
        live = (t >= 0) & (t < n)
        pl.when(live if also is None else live & also)(lambda: act(t))
    def outer_done(t):
        up(t).wait_send()
        down(t).wait_recv()
    def inner_done(t):
        down(t).wait_send()
    def inner_sum(t):
        over(t).wait()
        done[t] = plus(part[lax.rem(t, 4)], across[lax.rem(t, 2)])
        down(t).start()
    def inner_part(t):
        up(t).wait_recv()
        part[lax.rem(t, 4)] = plus(part[lax.rem(t, 4)], inward[lax.rem(t, 4)])
        over(t).start()
    def finish_plane(t):
        k = lax.rem(t, 2)
        y2(k).wait()
        x2(k).wait()
        part[lax.rem(t, 4), 0:h] = plus(kt[k, 0], t2[k])
        part[lax.rem(t, 4), h:2 * h] = plus(kb[k, 0], b2[k])
    def second(t):
        k = lax.rem(t, 2)
        x1(k).wait()
        y1(k).wait()
        kt[k] = plus(kt[k], xt[k])
        kb[k] = plus(kb[k], yb[k])
        y2(k).start()
        x2(k).start()
    def first(t):
        k = lax.rem(t, 2)
        core(k).wait()
        top = lambda i: plus(src[k, i, c, 0:h], cbuf[k, i, 0:h])
        low = lambda i: plus(src[k, i, c, h:2 * h], cbuf[k, i, h:2 * h])
        sx[k, 0], sx[k, 1] = top(mx), top(md)
        sy[k, 0], sy[k, 1] = low(my), low(md)
        x1(k).start()
        y1(k).start()
        kt[k, 0], kt[k, 1] = top(m), top(my)
        kb[k, 0], kb[k, 1] = low(m), low(mx)
    stage(s - 6, outer_done, outer)
    stage(s - 6, inner_done, inner)
    stage(s - 5, inner_sum, inner)
    stage(s - 4, inner_part, inner)
    stage(s - 3, finish_plane)
    stage(s - 3, lambda t: up(t).start(), outer)
    stage(s - 2, second)
    stage(s - 1, first)
    stage(s, lambda t: core(lax.rem(t, 2)).start())

GELU_C = float(np.sqrt(2.0 / np.pi))
def dot_nt(a, b):
    return lax.dot_general(a, b, (((1,), (1,)), ((), ())), preferred_element_type=f32)

def ffn_open(x_ref, ctx_ref, gain_ref, wo_ref, gres_ref, res, n, acc):
    for t in range(0, x_ref.shape[0], 384):
        s = slice(t, t + 384)
        y = x_ref[s, :].astype(f32) + dot(ctx_ref[s, :], wo_ref[...])
        res[s, :] = y
        acc[s, :] = y
        n[s, :] = (y * lax.rsqrt(jnp.mean(y * y, axis=-1, keepdims=True) + EPS) * gain_ref[0:1, :]).astype(bf)
    gres_ref[...] = jnp.zeros_like(gres_ref)

def ffn_block(g_ref, gu_ref, dn_ref, gres_ref, ddn_ref, n, acc):
    d = n.shape[1]
    wg = gu_ref[0].reshape(d, gu_ref.shape[-1])
    wu = gu_ref[1].reshape(d, gu_ref.shape[-1])
    wd = dn_ref[...]
    nn = n[...]
    g = g_ref[...]
    v = dot(nn, wg)
    u = dot(nn, wu)
    gh = dot_nt(g, wd)
    v2 = v * v
    th = jnp.tanh(GELU_C * v * (1.0 + 0.044715 * v2))
    half = 0.5 * (1.0 + th)
    gel = v * half
    h = (gel * u).astype(bf)
    dgel = half + 0.5 * v * (1.0 - th * th) * (GELU_C * (1.0 + 3 * 0.044715 * v2))
    gg = (gh * u * dgel).astype(bf)
    gu = (gh * gel).astype(bf)
    acc[...] = acc[...] + dot(h, wd)
    gres_ref[...] = gres_ref[...] + dot_nt(jnp.concatenate([gg, gu], 1), jnp.concatenate([wg, wu], 1))
    ddn_ref[...] = dot_tl(h, g).astype(bf)
    return dot_tl(nn, gg).astype(bf), dot_tl(nn, gu).astype(bf)

def ffn_close(s, g_ref, gain_ref, wo_ref, out_ref, gres_ref, gctx_ref, res, n, acc):
    out_ref[s, :] = acc[s, :].astype(bf)
    y = res[s, :]
    r = lax.rsqrt(jnp.mean(y * y, axis=-1, keepdims=True) + EPS)
    m = y * r
    gn = gres_ref[s, :]
    w = gn * gain_ref[0:1, :]
    gr = g_ref[s, :].astype(f32) + r * (w - m * jnp.mean(w * m, axis=-1, keepdims=True))
    gres_ref[s, :] = gr
    low = gr.astype(bf)
    n[s, :] = low
    gctx_ref[s, :] = dot_nt(low, wo_ref[...]).astype(bf)
    return jnp.sum(gn * m, axis=0, keepdims=True)

def ffn_kernel(x_ref, ctx_ref, g_ref, gain_ref, wo_ref, gu_ref, dn_ref,
               out_ref, gres_ref, gctx_ref, dwo_ref, ggain_ref, ddn_ref, dgu_ref, res, n, acc):
    j = pl.program_id(0)
    @pl.when(j == 0)
    def _():
        ffn_open(x_ref, ctx_ref, gain_ref, wo_ref, gres_ref, res, n, acc)
    a, b = ffn_block(g_ref, gu_ref, dn_ref, gres_ref, ddn_ref, n, acc)
    dgu_ref[0] = a.reshape(dgu_ref.shape[1:])
    dgu_ref[1] = b.reshape(dgu_ref.shape[1:])
    @pl.when(j == pl.num_programs(0) - 1)
    def _():
        R = x_ref.shape[0]
        total = sum(ffn_close(slice(t, t + 384), g_ref, gain_ref, wo_ref, out_ref, gres_ref, gctx_ref, res, n, acc) for t in range(0, R, 384))
        ggain_ref[...] = jnp.broadcast_to(total, ggain_ref.shape)
        dwo_ref[...] = dot_tl(ctx_ref[...], n[...]).astype(bf)

def ffn_sum_kernel(x_ref, ctx_ref, g_ref, gain_ref, wo_ref, gu_ref, dn_ref,
                   out_ref, gres_ref, gctx_ref, dwo_ref, ggain_ref, ddn_ref, dgu_ref, res, n, acc, *bufs):
    j = pl.program_id(0)
    N = pl.num_programs(0) - DRAIN
    src, done = bufs[0], bufs[13]
    @pl.when(j == 0)
    def _():
        rs_greet()
        ffn_open(x_ref, ctx_ref, gain_ref, wo_ref, gres_ref, res, n, acc)
        ggain_ref[...] = jnp.zeros_like(ggain_ref)
    @pl.when(j < N)
    def _():
        a, b = ffn_block(g_ref, gu_ref, dn_ref, gres_ref, ddn_ref, n, acc)
        k = lax.rem(j, 2)
        rows = a.shape[0] // 8
        src[k, :, :, 0:rows] = a.reshape(4, 2, rows, a.shape[1])
        src[k, :, :, rows:2 * rows] = b.reshape(4, 2, rows, a.shape[1])
    @pl.when(j >= N)
    def _():
        part = x_ref.shape[0] // DRAIN
        s = pl.ds(pl.multiple_of((j - N) * part, part), part)
        total = ffn_close(s, g_ref, gain_ref, wo_ref, out_ref, gres_ref, gctx_ref, res, n, acc)
        ggain_ref[...] = ggain_ref[...] + jnp.broadcast_to(total, ggain_ref.shape)
    rs_step(j, N, bufs)
    @pl.when(j == N + DRAIN - 1)
    def _():
        dwo_ref[...] = dot_tl(ctx_ref[...], n[...]).astype(bf)
        dgu_ref[...] = done[...]

def ffn(x, ctx, g, gain, wo, gu, dn, near, block=256):
    R, d = x.shape
    F = dn.shape[0]
    k = gu.shape[1]
    N = F // block
    sds = jax.ShapeDtypeStruct
    one = lambda *s: pl.BlockSpec(s, lambda j: (0,) * len(s), pipeline_mode=pl.Buffered(1))
    at = lambda j: jnp.minimum(j, N - 1)
    gub = pl.BlockSpec((2, k, d // k, block), lambda j: (0, 0, 0, at(j)))
    dnb = pl.BlockSpec((block, d), lambda j: (at(j), 0))
    rows = 2 * (d // k)
    if near:
        body, extra, steps, last = ffn_sum_kernel, rs_scratch(N, rows, block), N + DRAIN, (one(N, rows, block), sds((N, rows, block), bf))
        params = pltpu.CompilerParams(vmem_limit_bytes=61 * 2**20, collective_id=3, has_side_effects=True)
    else:
        body, extra, steps, last = ffn_kernel, [], N, (gub, sds(gu.shape, bf))
        params = pltpu.CompilerParams(vmem_limit_bytes=61 * 2**20)
    return pl.pallas_call(body, grid=(steps,),
        in_specs=[one(R, d), one(R, d), one(R, d), one(1, d), one(d, d), gub, dnb],
        out_specs=[one(R, d), one(R, d), one(R, d), one(d, d), one(8, d), dnb, last[0]],
        out_shape=[sds((R, d), bf), sds((R, d), f32), sds((R, d), bf), sds((d, d), bf), sds((8, d), f32), sds(dn.shape, bf), last[1]],
        scratch_shapes=[pltpu.VMEM((R, d), f32), pltpu.VMEM((R, d), bf), pltpu.VMEM((R, d), f32)] + extra,
        compiler_params=params, name="ffn")(x, ctx, g, gain, wo, gu, dn)

def sum_rounds(s, box, inbox, send, recv):
    b, m, c, mx, my, md = places()
    peers = [(b, m, 1 - c), (b, mx, c), (b, my, c), (b + 1 - 2 * lax.rem(b, 2), m, c), (3 - b, m, c)]
    def copy(r):
        return pltpu.make_async_remote_copy(src_ref=box.at[r], dst_ref=inbox.at[r], send_sem=send.at[r], recv_sem=recv.at[r], device_id=peers[r], device_id_type=MESH)
    for r in range(5):
        @pl.when(s == r)
        def _():
            copy(r).start()
        @pl.when(s == r + 1)
        def _():
            copy(r).wait()
            box[r + 1] = box[r] + inbox[r]

def bwd_sum_kernel(q_ref, k_ref, v_ref, do_ref, o_ref, r_ref, e_ref, n_ref, x_ref, gres_ref, gain_ref, wq_ref, wk_ref, wv_ref, dn_ref, wo_ref, gain2_ref,
                   gtok_ref, small_ref, out_a, out_b, rhs, vaug, dobd, qaug, ds_ref, nacc, near_ref, far_ref, ggain, box, inbox, ssend, srecv, *bufs):
    p = pl.program_id(0)
    N = pl.num_programs(0) - DRAIN
    half = len(bufs) // 2
    bufs_a, bufs_b = bufs[:half], bufs[half:]
    src_a, done_a = bufs_a[0], bufs_a[13]
    src_b, done_b = bufs_b[0], bufs_b[13]
    NA = done_a.shape[0]
    d = gtok_ref.shape[1]
    k = lax.rem(p, 2)
    def put(src, arrays):
        h = src.shape[3] // 2
        at = 0
        for a in arrays:
            r = a.shape[1] // 2
            a = a.reshape((4, 2) + a.shape[1:])
            src[k, :, :, at:at + r] = a[:, :, 0:r]
            src[k, :, :, h + at:h + at + r] = a[:, :, r:2 * r]
            at += r
    @pl.when(p == 0)
    def _():
        rs_greet()
        bwd_open(rhs, vaug, qaug)
        gtok_ref[...] = jnp.zeros_like(gtok_ref)
        ggain[...] = jnp.zeros_like(ggain)
        box[0] = jnp.zeros(box.shape[1:], f32)
    @pl.when(p < NA)
    def _():
        put(src_a, (dn_ref[...], wo_ref[...]))
    @pl.when(p < N)
    def _():
        g = jnp.concatenate(bwd_pair(q_ref, k_ref, v_ref, do_ref, o_ref, r_ref, e_ref, near_ref, far_ref, rhs, vaug, dobd, qaug, ds_ref, nacc), 1)
        for a in range(2):
            for t in range(4):
                box[0, p, 4 * a + t:4 * a + t + 1] = near_ref[a:a + 1, 128 * t:128 * t + 128]
        box[0, N + p] = far_ref[...]
        gw = dot_tl(n_ref[...], g).astype(bf)
        put(src_b, [gw[:, 128 * t:128 * t + 128].reshape(8, d // 8, 128) for t in range(3)])
        w = jnp.concatenate([w_ref[...].reshape(d, 128) for w_ref in (wq_ref, wk_ref, wv_ref)], 1)
        gtok_ref[...] = gtok_ref[...] + dot_nt(g, w)
    @pl.when((p >= N) & (p < N + 2))
    def _():
        rows = x_ref.shape[0]
        step = rows // 3
        total = jnp.zeros((1, d), f32)
        for t in range(3):
            s = pl.ds(pl.multiple_of((p - N) * rows + t * step, step), step)
            x = x_ref[t * step:t * step + step, :].astype(f32)
            r = lax.rsqrt(jnp.mean(x * x, axis=-1, keepdims=True) + EPS)
            m = x * r
            gn = gtok_ref[s, :]
            w = gn * gain_ref[0:1, :]
            gtok_ref[s, :] = gres_ref[t * step:t * step + step, :] + r * (w - m * jnp.mean(w * m, axis=-1, keepdims=True))
            total = total + jnp.sum(gn * m, axis=0, keepdims=True)
        ggain[...] = ggain[...] + jnp.broadcast_to(total, ggain.shape)
    @pl.when(p == N + 1)
    def _():
        for t in range(8):
            w = d // 8
            box[0, 2 * N, t:t + 1] = ggain[0:1, w * t:w * t + w]
            box[0, 2 * N + 1, t:t + 1] = gain2_ref[0:1, w * t:w * t + w]
    sum_rounds(p - N - 1, box, inbox, ssend, srecv)
    rs_step(p, NA, bufs_a)
    rs_step(p, N, bufs_b)
    @pl.when(p == N + DRAIN - 1)
    def _():
        sum_rounds(5, box, inbox, ssend, srecv)
        small_ref[...] = box[5]
        out_a[...] = done_a[...]
        out_b[...] = done_b[...]

def attn_bwd_sum(qkv, do, o, r, e, n, x, gres, gain, qkv_w, dn, wo, gain2):
    R, d = x.shape
    N = d // 128
    NA, wide = 4, d // 4
    rows_a, rows_b = dn.shape[1] + wo.shape[1], 3 * (d // 8)
    sds = jax.ShapeDtypeStruct
    at = lambda p: jnp.minimum(p, N - 1)
    after = lambda p: jnp.clip(p - N, 0, 1)
    spec = pl.BlockSpec((R, 128), lambda p: (0, at(p)))
    head = lambda t: pl.BlockSpec((None, R, 128), lambda p: (t * N + at(p), 0, 0))
    one = lambda *s: pl.BlockSpec(s, lambda p: (0,) * len(s), pipeline_mode=pl.Buffered(1))
    part = pl.BlockSpec((R // 2, d), lambda p: (after(p), 0), pipeline_mode=pl.Buffered(1))
    cols = lambda a, t: pl.BlockSpec((8, a.shape[1], 128), lambda p: (0, 0, t * N + at(p)))
    early = lambda a: pl.BlockSpec((8, a.shape[1], wide), lambda p: (0, 0, jnp.minimum(p, NA - 1)), pipeline_mode=pl.Buffered(1))
    dma = pltpu.SemaphoreType.DMA
    small = (2 * N + 2, 8, d // 8)
    return pl.pallas_call(bwd_sum_kernel, grid=(N + DRAIN,),
        in_specs=[head(0), head(1), head(2)] + [spec] * 3 + [pl.BlockSpec((None, None, R, NT * 256), lambda p: (0, at(p), 0, 0)), one(R, d), part, part, one(1, d),
                  cols(qkv_w, 0), cols(qkv_w, 1), cols(qkv_w, 2), early(dn), early(wo), one(8, d)],
        out_specs=[one(R, d), one(*small), one(NA, rows_a, wide), one(N, rows_b, 128)],
        out_shape=[sds((R, d), f32), sds(small, f32), sds((NA, rows_a, wide), bf), sds((N, rows_b, 128), bf)],
        scratch_shapes=[pltpu.VMEM((256, NT * 256), bf), pltpu.VMEM((R, 256), bf), pltpu.VMEM((NT * 256, 128), bf), pltpu.VMEM((NT * 256, 256), bf), pltpu.VMEM((R, NT * 256), bf), pltpu.VMEM((384, 256), f32),
                        pltpu.VMEM((8, 512), f32), pltpu.VMEM((8, 128), f32), pltpu.VMEM((8, d), f32), pltpu.VMEM((6,) + small, f32), pltpu.VMEM((5,) + small, f32), dma((5,)), dma((5,))]
                       + rs_scratch(NA, rows_a, wide) + rs_scratch(N, rows_b, 128),
        compiler_params=pltpu.CompilerParams(vmem_limit_bytes=63 * 2**20, collective_id=4, has_side_effects=True), name="attn_bwd_sum")(
            qkv, qkv, qkv, do, o, r, e, n, x, gres, gain, qkv_w, qkv_w, qkv_w, dn, wo, gain2)

def split_sums(out, sizes):
    h = out.shape[1] // 2
    parts, at = [], 0
    for r in sizes:
        r = r // 2
        a = jnp.concatenate([out[:, at:at + r], out[:, h + at:h + at + r]], 1)
        parts.append(jnp.moveaxis(a, 0, 1).reshape(2 * r, -1).astype(f32))
        at += r
    return parts

def contract_rows(left, right):
    return lax.dot_general(left, right, (((0,), (0,)), ((), ())), preferred_element_type=f32)

def contract_cols(left, right):
    return lax.dot_general(left, right, (((1,), (1,)), ((), ())), preferred_element_type=f32)

def rms_norm(inputs, gain):
    return inputs * lax.rsqrt(jnp.mean(inputs * inputs, axis=-1, keepdims=True) + EPS) * gain

def gather(x):
    return lax.all_gather(x, SHARD, axis=0, tiled=False)

def scatter(x):
    return lax.psum_scatter(x, SHARD, scatter_dimension=0, tiled=True)

def per_device(near, tokens, row_kind, text_length, gain_attn, position_bias_table, weight_query, weight_key, weight_value, weight_out, gain_ffn, weight_gate, weight_up, weight_down, cotangent):
    n1, d = weight_query.shape
    n2 = position_bias_table.shape[0]
    inputs = tokens.astype(f32)
    if near:
        context, e, r, normed, qkv, qkv_w, gu_w, down_w, out_w = front(
            row_kind, text_length, tokens, gain_attn, gain_ffn, position_bias_table, weight_query, weight_key, weight_value, weight_gate, weight_up, weight_down, weight_out)
        small = qkv_w[:, 0:2, 3 * d:3 * d + n1]
        gain_one, gain_two = small[:, 0].reshape(d).astype(f32), small[:, 1].reshape(d).astype(f32)
    else:
        small = gather(jnp.stack([gain_attn, gain_ffn, jnp.pad(position_bias_table, (0, n1 - n2))]))
        qkv_w = gather(jnp.concatenate([weight_query, weight_key, weight_value], 1))
        gain_one, gain_two = small[:, 0].reshape(d).astype(f32), small[:, 1].reshape(d).astype(f32)
        normed = rms_norm(inputs, gain_one).astype(bf)
        q, k, v = (dot(normed, qkv_w[:, :, t * d:t * d + d].reshape(d, d)).astype(bf) for t in range(3))
        far, w = tables(small[:, 2, :n2].reshape(-1))
        context, e, r = attn_fwd(q, k, v, mask_cols(row_kind, text_length), far, w)
        gu_w, down_w, out_w = jnp.moveaxis(gather(jnp.stack([weight_gate, weight_up])), 0, 1), gather(weight_down), gather(weight_out)
    ff = gu_w.shape[-1]
    output, grad_residual, grad_context, grad_out_w, g_gain_two, ddn, dgu = ffn(
        tokens, context, cotangent, gain_two.reshape(1, d), out_w.reshape(d, d), gu_w, down_w.reshape(ff, d), near)
    if near:
        shards = gu_w.shape[1]
        grad_tokens, small_g, sums_a, sums_b = attn_bwd_sum(
            qkv, grad_context, context, r, e, normed, tokens, grad_residual, gain_one.reshape(1, d), qkv_w,
            ddn.reshape(shards, ff // shards, d), grad_out_w.reshape(shards, n1, d), g_gain_two)
        pairs = (small_g.shape[0] - 2) // 2
        near_sums = small_g[:pairs].reshape(1, pairs, 2, -1)
        far_sums = small_g[None, pairs:2 * pairs]
        g_gain_one, g_gain_two = small_g[2 * pairs].reshape(d), small_g[2 * pairs + 1].reshape(d)
        s_down, s_out = split_sums(sums_a, (ff // shards, n1))
        s_q, s_k, s_v = split_sums(sums_b, (n1, n1, n1))
        dgu = dgu.reshape(dgu.shape[0], 2, n1, -1).transpose(1, 2, 0, 3).reshape(2, n1, ff).astype(f32)
        s_gate, s_up = dgu[0], dgu[1]
    else:
        total = lambda x: lax.psum(scatter(x), "batch").astype(f32)
        gq, gk, gv, near_sums, far_sums = attn_bwd(q, k, v, grad_context, context, r, e)
        grads = (gq, gk, gv)
        s_gate, s_up, s_down, s_out = (total(x) for x in (dgu[0].reshape(d, ff), dgu[1].reshape(d, ff), ddn, grad_out_w))
        s_q, s_k, s_v = (total(contract_rows(normed, x).astype(bf)) for x in grads)
        grad_normed = sum(contract_cols(x, qkv_w[:, :, t * d:t * d + d].reshape(d, d)) for t, x in enumerate(grads))
        _, first_pull = jax.vjp(rms_norm, inputs, gain_one)
        share, g_gain_one = first_pull(grad_normed)
        grad_tokens = grad_residual + share
    g_table = table_grad(near_sums, far_sums)
    if not near:
        small_g = lax.psum(jnp.concatenate([g_gain_one, g_gain_two[0], g_table]), ("batch", "dp", "narrow"))
        g_gain_one, g_gain_two, g_table = small_g[:d], small_g[d:2 * d], small_g[2 * d:]
    at = lax.axis_index("dp") * lax.axis_size("narrow") + lax.axis_index("narrow")
    r_gain_one = lax.dynamic_slice_in_dim(g_gain_one, at * n1, n1)
    r_gain_two = lax.dynamic_slice_in_dim(g_gain_two, at * n1, n1)
    r_table = lax.dynamic_slice_in_dim(g_table, at * n2, n2)
    return (output, grad_tokens, r_gain_one, r_table, s_q, s_k, s_v, s_out, r_gain_two, s_gate, s_up, s_down)

def solution(mesh):
    near = (mesh.shape["batch"], mesh.shape["dp"], mesh.shape["narrow"]) == (4, 4, 2)
    placed = (
        P(("batch", "dp", "narrow"), None),
        P(("batch", "dp", "narrow")),
        P(("batch", "dp", "narrow"), None),
        P(("dp", "narrow")),
        P(("dp", "narrow")),
        P(("dp", "narrow"), None),
        P(("dp", "narrow"), None),
        P(("dp", "narrow"), None),
        P(("dp", "narrow"), None),
        P(("dp", "narrow")),
        P(("dp", "narrow"), None),
        P(("dp", "narrow"), None),
        P(("dp", "narrow"), None),
        P(("batch", "dp", "narrow"), None),
    )
    return jax.shard_map(
        functools.partial(per_device, near),
        mesh=mesh,
        in_specs=placed,
        out_specs=(
            P(("batch", "dp", "narrow"), None),
            P(("batch", "dp", "narrow"), None),
            P(("dp", "narrow")),
            P(("dp", "narrow")),
            P(("dp", "narrow"), None),
            P(("dp", "narrow"), None),
            P(("dp", "narrow"), None),
            P(("dp", "narrow"), None),
            P(("dp", "narrow")),
            P(("dp", "narrow"), None),
            P(("dp", "narrow"), None),
            P(("dp", "narrow"), None),
        ),
        check_vma=False,
    )
```

```python
import functools

import jax
import jax.numpy as jnp
import numpy as np
from jax import lax
from jax.experimental import pallas as pl
from jax.experimental.pallas import tpu as pltpu
from jax.sharding import PartitionSpec as P

EPS = 1e-06
SHARD = ("dp", "narrow")
BUCKETS = 32
bf=jnp.bfloat16; f32=jnp.float32
T=128; L=1152; NT=L//T
NEG=-1e30
def dot(a,b): return jnp.dot(a,b,preferred_element_type=f32)
def dot_tl(a,b): return lax.dot_general(a,b,(((0,),(0,)),((),())),preferred_element_type=f32)

def fwd_open(rhs,vaug):
    rhs[...]=jnp.zeros_like(rhs)
    row=lax.broadcasted_iota(jnp.int32,(128,NT*256),0)
    col=lax.broadcasted_iota(jnp.int32,(128,NT*256),1)
    rhs[128:256,:]=(row==col//128).astype(f32).astype(bf)
    vaug[:,128:256]=jnp.ones((L,128),bf)

def fwd_pair(q,k,v,mask,lo,hi,bias,o_ref,e_ref,r_ref,rhs,kaug,vaug,bn,s_ref):
    qT=q.T
    for i in range(NT):
        rhs[0:64,256*i:256*i+128]=qT[0:64,128*i:128*i+128]
        rhs[64:128,256*i+128:256*i+256]=qT[64:128,128*i:128*i+128]
    kaug[:,0:128]=k
    row=lax.broadcasted_iota(jnp.int32,(L,128),0)//128
    col=lax.broadcasted_iota(jnp.int32,(L,128),1)//2
    far=jnp.where(row<col-1,lo,jnp.where(row>col+1,hi,0.0))
    kaug[:,128:256]=(mask+far).astype(bf)
    vaug[:,0:128]=v
    for a in range(2):
        wb=jnp.broadcast_to(bias[a:a+1,:],(384,512))
        bn[:,128*a:128*a+128]=pltpu.roll(wb,0,1,stride=1,stride_axis=0)[:,0:128]
    def scores(i,slot):
        ri=rhs[:,256*i:256*i+256]
        first,last=max(0,i-1)*128,min(NT,i+2)*128
        off=(first//128-(i-1))*128
        x=dot(kaug[...],ri)
        xn=x[first:last]+bn[off:off+last-first,:]
        ms=[jnp.max(xn,axis=0,keepdims=True)]
        s_ref[slot,first:last,:]=xn
        if first>0:
            s_ref[slot,0:first,:]=x[0:first]; ms.append(jnp.max(x[0:first],axis=0,keepdims=True))
        if last<L:
            s_ref[slot,last:L,:]=x[last:L]; ms.append(jnp.max(x[last:L],axis=0,keepdims=True))
        m=ms[0]
        for y in ms[1:]: m=jnp.maximum(m,y)
        return m
    lane=lax.broadcasted_iota(jnp.int32,(128,128),1)<64
    def finish(i,slot,m):
        e=jnp.exp(s_ref[slot]-m).astype(bf)
        e_ref[:,pl.ds(i*256,256)]=e
        o=dot_tl(e,vaug[...])
        num=jnp.where(lane,o[0:128,0:128],o[128:256,0:128])
        den=jnp.where(lane,o[0:128,128:256],o[128:256,128:256])
        r=1.0/den
        rows=pl.ds(i*128,128)
        o_ref[rows,:]=(num*r).astype(bf)
        r_ref[rows,:]=r
    m=scores(0,0)
    for i in range(NT):
        mn=scores(i+1,(i+1)%2) if i+1<NT else None
        finish(i,i%2,m)
        m=mn

def fwd_kernel(q_ref,k_ref,v_ref,mask_ref,far_ref,w_ref,o_ref,e_ref,r_ref,rhs,kaug,vaug,bn,s_ref):
    @pl.when((pl.program_id(0)==0)&(pl.program_id(1)==0))
    def _():
        fwd_open(rhs,vaug)
    fwd_pair(q_ref[...],k_ref[...],v_ref[...],mask_ref[...],far_ref[0:1,:],far_ref[1:2,:],w_ref[...],o_ref,e_ref,r_ref,rhs,kaug,vaug,bn,s_ref)

def attn_fwd(q,k,v,mask,far,w):
    rows=q.shape[0]//L
    spec=pl.BlockSpec((L,128),lambda r,p:(r,p))
    return pl.pallas_call(fwd_kernel,
        grid=(rows,8),
        in_specs=[spec,spec,spec,
            pl.BlockSpec((None,L,128),lambda r,p:(r,0,0)),
            pl.BlockSpec((None,8,128),lambda r,p:(p,0,0)),
            pl.BlockSpec((None,8,512),lambda r,p:(p,0,0))],
        out_specs=[spec,pl.BlockSpec((None,None,L,NT*256),lambda r,p:(r,p,0,0)),spec],
        out_shape=[jax.ShapeDtypeStruct(q.shape,bf),jax.ShapeDtypeStruct((rows,8,L,NT*256),bf),jax.ShapeDtypeStruct(q.shape,f32)],
        scratch_shapes=[pltpu.VMEM((256,NT*256),bf),pltpu.VMEM((L,256),bf),pltpu.VMEM((L,256),bf),pltpu.VMEM((384,256),f32),pltpu.VMEM((2,L,256),f32)],
        compiler_params=pltpu.CompilerParams(vmem_limit_bytes=56*2**20),
        name="attn_fwd",
    )(q,k,v,mask,far,w)

THR=(12,16,23,32,46,64,91)
def bucket_np(d):
    n=np.abs(d); c=np.full_like(n,8)
    for t in THR: c=c+(n>=t)
    return np.where(n<8,n,c)+16*(d>0)
def tables(table):
    t=table.reshape(16,32).astype(f32)
    y=np.arange(512); y=np.where(y>=128,y-512,y)
    d=-128-y
    oh=(np.arange(32)[:,None]==bucket_np(d)[None,:]).astype(np.float32)
    w=jnp.dot(t,jnp.asarray(oh),precision=lax.Precision.HIGHEST)
    w=jnp.pad(w.reshape(8,2,512),((0,0),(0,6),(0,0)))
    lo=jnp.tile(t[:,15].reshape(8,1,2),(1,1,64)); hi=jnp.tile(t[:,31].reshape(8,1,2),(1,1,64))
    far=jnp.pad(jnp.concatenate([lo,hi],1),((0,0),(0,6),(0,0)))
    return far,w
def mask_cols(row_kind,text_length):
    pos=np.arange(L)
    kind=row_kind[:,None]
    seg=kind*(pos//384)[None]
    off=pos[None]-seg*384
    img=jnp.where(kind==1,256,1024)
    tl=jnp.where(seg==0,text_length[:,0:1],jnp.where(seg==1,text_length[:,1:2],text_length[:,2:3]))
    live=off<img+tl
    qseg=kind*np.minimum(np.arange(128)//2//3,2)[None]
    ok=live[:,:,None]&(seg[:,:,None]==qseg[:,None,:])
    return jnp.where(ok,0.0,NEG).astype(f32)

def bwd_open(rhs,vaug,qaug):
    rhs[...]=jnp.zeros_like(rhs)
    c=lax.broadcasted_iota(jnp.int32,(L,128),1)
    vaug[:,128:256]=(c<3).astype(f32).astype(bf)
    row=lax.broadcasted_iota(jnp.int32,(NT*256,128),0)
    col=lax.broadcasted_iota(jnp.int32,(NT*256,128),1)
    qaug[:,128:256]=(row//128==col).astype(f32).astype(bf)

def bwd_pair(q_ref,k_ref,v_ref,do_ref,o_ref,r_ref,e_ref,near_ref,far_ref,rhs,vaug,dobd,qaug,ds_ref,nacc):
    q=q_ref[...]; k=k_ref[...]
    vaug[:,0:128]=v_ref[...]
    dof=do_ref[...].astype(f32)*r_ref[...]
    dos=dof.astype(bf)
    dT=dos.T
    pT=(dos.astype(f32)*o_ref[...].astype(f32)).T
    D=jnp.concatenate([jnp.sum(pT[0:64],axis=0,keepdims=True),jnp.sum(pT[64:128],axis=0,keepdims=True)],0)
    D=-D
    D1=D.astype(bf); D2=(D-D1.astype(f32)); D3=(D2-D2.astype(bf).astype(f32)).astype(bf); D2=D2.astype(bf)
    lane=lax.broadcasted_iota(jnp.int32,(128,128),1)<64
    zero=jnp.zeros((128,128),bf)
    z13=jnp.zeros((13,128),bf)
    for i in range(NT):
        t=slice(128*i,128*i+128)
        for a in range(2):
            h=slice(64*a,64*a+64)
            c=slice(256*i+128*a,256*i+128*a+128)
            rhs[h,c]=dT[h,t]
            rhs[128:144,c]=jnp.concatenate([D1[a:a+1,t],D2[a:a+1,t],D3[a:a+1,t],z13],0)
            dobd[c,:]=jnp.where(lane==(a==0),dos[t],zero)
            qaug[c,0:128]=jnp.where(lane==(a==0),q[t],zero)
    nacc[...]=jnp.zeros_like(nacc)
    dqs=[]
    for i in range(NT):
        c=slice(256*i,256*i+256)
        lo,hi=max(0,i-1)*128,min(NT,i+2)*128
        off=(lo//128-(i-1))*128
        dp=dot(vaug[...],rhs[:,c])
        ds=e_ref[:,c].astype(f32)*dp
        nacc[off:off+hi-lo,:]+=ds[lo:hi]
        dsb=ds.astype(bf)
        ds_ref[:,c]=dsb
        g=dot_tl(dsb,k)
        dqs.append(jnp.where(lane,g[0:128],g[128:256]).astype(bf))
    dv=dot(e_ref[...],dobd[...]).astype(bf)
    g=dot(ds_ref[...],qaug[...])
    dk=g[:,0:128].astype(bf)
    G=g[:,128:256]
    row=lax.broadcasted_iota(jnp.int32,(L,128),0)//128
    col=lax.broadcasted_iota(jnp.int32,(L,128),1)//2
    far_ref[0:1,:]=jnp.sum(jnp.where(row<col-1,G,0.0),axis=0,keepdims=True)
    far_ref[1:2,:]=jnp.sum(jnp.where(row>col+1,G,0.0),axis=0,keepdims=True)
    far_ref[2:8,:]=jnp.zeros((6,128),f32)
    near_ref[2:8,:]=jnp.zeros((6,512),f32)
    rev=(lax.broadcasted_iota(jnp.int32,(128,128),0)+lax.broadcasted_iota(jnp.int32,(128,128),1)==127).astype(f32)
    for a in range(2):
        x=jnp.dot(nacc[:,128*a:128*a+128],rev,precision=lax.Precision.HIGHEST,preferred_element_type=f32)
        x=jnp.concatenate([x,jnp.zeros((384,384),f32)],1)
        x=pltpu.roll(x,0,1,stride=1,stride_axis=0)
        near_ref[a:a+1,:]=jnp.sum(x,axis=0,keepdims=True)
    return jnp.concatenate(dqs,0),dk,dv

def bwd_kernel(q_ref,k_ref,v_ref,do_ref,o_ref,r_ref,e_ref,dq_ref,dk_ref,dv_ref,near_ref,far_ref,rhs,vaug,dobd,qaug,ds_ref,nacc):
    @pl.when((pl.program_id(0)==0)&(pl.program_id(1)==0))
    def _():
        bwd_open(rhs,vaug,qaug)
    dq_ref[...],dk_ref[...],dv_ref[...]=bwd_pair(q_ref,k_ref,v_ref,do_ref,o_ref,r_ref,e_ref,near_ref,far_ref,rhs,vaug,dobd,qaug,ds_ref,nacc)

def attn_bwd(q,k,v,do,o,r,e):
    rows=q.shape[0]//L
    spec=pl.BlockSpec((L,128),lambda r,p:(r,p))
    sds=jax.ShapeDtypeStruct
    return pl.pallas_call(bwd_kernel,
        grid=(rows,8),
        in_specs=[spec]*6+[pl.BlockSpec((None,None,L,NT*256),lambda r,p:(r,p,0,0))],
        out_specs=[spec]*3+[pl.BlockSpec((None,None,8,512),lambda r,p:(r,p,0,0)),pl.BlockSpec((None,None,8,128),lambda r,p:(r,p,0,0))],
        out_shape=[sds(q.shape,bf)]*3+[sds((rows,8,8,512),f32),sds((rows,8,8,128),f32)],
        scratch_shapes=[pltpu.VMEM((256,NT*256),bf),pltpu.VMEM((L,256),bf),pltpu.VMEM((NT*256,128),bf),pltpu.VMEM((NT*256,256),bf),pltpu.VMEM((L,NT*256),bf),pltpu.VMEM((384,256),f32)],
        compiler_params=pltpu.CompilerParams(vmem_limit_bytes=58*2**20),
        name="attn_bwd",
    )(q,k,v,do,o,r,e)
def table_grad(near,far):
    y=np.arange(512)
    oh=(bucket_np(y-255)[:,None]==np.arange(32)[None,:]).astype(np.float32)
    n=jnp.sum(near[:,:,0:2],0).reshape(16,512)
    g=jnp.dot(n,jnp.asarray(oh),precision=lax.Precision.HIGHEST)
    f=jnp.sum(far[:,:,0:2],0).reshape(8,2,64,2).sum(2)
    lo=f[:,0].reshape(16,1); hi=f[:,1].reshape(16,1)
    g=g+lo*np.eye(32,dtype=np.float32)[15][None]+hi*np.eye(32,dtype=np.float32)[31][None]
    return g.reshape(512)

MESH = pl.DeviceIdType.MESH

def places():
    b, m, c = lax.axis_index("batch"), lax.axis_index("dp"), lax.axis_index("narrow")
    x, y = lax.rem(m, 2), m // 2
    mx = y * 2 + (1 - x)
    my = (1 - y) * 2 + x
    md = (1 - y) * 2 + (1 - x)
    return b, m, c, mx, my, md

def greet(devices):
    barrier = pltpu.get_barrier_semaphore()
    for d in devices:
        pl.semaphore_signal(barrier, inc=1, device_id=d, device_id_type=MESH)
    pl.semaphore_wait(barrier, len(devices))

def gather_steps(gu_in, dn_in, wo_in, gu, dn, wo, send, recv, local):
    b, m, c, mx, my, md = places()
    o = 1 - c
    z = lax.rem(b, 2)
    oz = 1 - z
    nx, ny, nc, nz = (b, mx, c), (b, my, c), (b, m, o), (b + 1 - 2 * z, m, c)
    me, it = m * 2 + c, m * 2 + o
    ix, iy, idg = mx * 2 + c, my * 2 + c, md * 2 + c
    jx, jy, jdg = mx * 2 + o, my * 2 + o, md * 2 + o
    def copy(src, dst, n, to):
        return pltpu.make_async_remote_copy(src_ref=src, dst_ref=dst, send_sem=send.at[n], recv_sem=recv.at[n], device_id=to, device_id_type=MESH)
    def push(ref, n, to):
        return copy(ref, ref, n, to)
    def got(ref, n):
        copy(ref, ref, n, nc).wait_recv()
    def first(src, dst, n):
        for t, to in enumerate((nx, ny, nc)):
            copy(src, dst, n + t, to).start()
    def halves(ref, i):
        h = ref.shape[1] // 2
        return ref.at[i, pl.ds(0, h)], ref.at[i, pl.ds(h, h)]
    def second(ref, n, onward=None):
        got(ref.at[ix], n)
        push(halves(ref, ix)[0], n + 3, ny).start()
        push(ref.at[ix], n + 5, nc).start()
        if onward is not None:
            push(ref.at[ix], onward, nz).start()
        got(ref.at[iy], n + 1)
        push(halves(ref, iy)[1], n + 4, nx).start()
        push(ref.at[iy], n + 6, nc).start()
        if onward is not None:
            push(ref.at[iy], onward + 1, nz).start()
    def third(ref, n, onward=None):
        got(halves(ref, idg)[0], n + 3)
        got(halves(ref, idg)[1], n + 4)
        push(ref.at[idg], n + 7, nc).start()
        if onward is not None:
            push(ref.at[idg], onward + 2, nz).start()
    def last(src, ref, n, onward=None):
        for t, i in ((2, it), (5, jx), (6, jy), (7, jdg)):
            got(ref.at[i], n + t)
        for t in (0, 1, 2):
            copy(src, ref.at[me], n + t, nc).wait_send()
        push(halves(ref, ix)[0], n + 3, ny).wait_send()
        push(halves(ref, iy)[1], n + 4, nx).wait_send()
        for t, i in ((5, ix), (6, iy), (7, idg)):
            push(ref.at[i], n + t, nc).wait_send()
        if onward is not None:
            for t, i in enumerate((ix, iy, idg)):
                push(ref.at[i], onward + t, nz).wait_send()
    def part(ref, i):
        cut = ref.shape[-1] // 384 * 128
        return ref.at[..., pl.ds(0, cut)] if i == 0 else ref.at[..., pl.ds(cut, ref.shape[-1] - cut)]
    mine, other = gu.at[z], gu.at[oz]
    m0, m1, o0, o1 = part(mine, 0), part(mine, 1), part(other, 0), part(other, 1)
    in0, in1 = part(gu_in.at[z], 0), part(gu_in.at[z], 1)
    d0, d1, dn0, dn1 = part(dn, 0), part(dn, 1), part(dn_in, 0), part(dn_in, 1)
    keeps = [pltpu.make_async_copy(gu_in.at[0], gu.at[0, me], local.at[0]), pltpu.make_async_copy(gu_in.at[1], gu.at[1, me], local.at[1]),
             pltpu.make_async_copy(dn_in, dn.at[me], local.at[2]), pltpu.make_async_copy(wo_in, wo.at[me], local.at[3])]
    W, D0, D1, G0, G1, Z0, Z1, OWN = 0, 8, 16, 24, 32, 40, 46, 52
    def z_second(ref, n, ts):
        for t in ts:
            i = (ix, iy, idg)[t]
            got(ref.at[i], n + t)
            push(ref.at[i], n + 3 + t, nc).start()
    def begin():
        first(in0, m0.at[me], G0)
        first(in1, m1.at[me], G1)
        copy(gu_in.at[oz], other.at[me], OWN, nc).start()
        for k in keeps:
            k.start()
    def at0():
        second(m0, G0, Z0)
        first(wo_in, wo.at[me], W)
    def at2():
        second(m1, G1, Z1)
        third(m0, G0, Z0)
        first(dn0, d0.at[me], D0)
    def at3():
        second(wo, W)
        first(dn1, d1.at[me], D1)
    def at4():
        third(m1, G1, Z1)
        z_second(o0, Z0, (0, 1))
    def at6():
        second(d0, D0)
        third(wo, W)
    def end():
        z_second(o1, Z1, (0, 1))
        z_second(o0, Z0, (2,))
        third(d0, D0)
        second(d1, D1)
        third(d1, D1)
        z_second(o1, Z1, (2,))
        last(wo_in, wo, W)
        last(in0, m0, G0, Z0)
        last(in1, m1, G1, Z1)
        got(other.at[it], OWN)
        copy(gu_in.at[oz], other.at[me], OWN, nc).wait_send()
        for ref, n in ((o0, Z0), (o1, Z1)):
            for t, i, j in ((0, ix, jx), (1, iy, jy), (2, idg, jdg)):
                got(ref.at[j], n + 3 + t)
                push(ref.at[i], n + 3 + t, nc).wait_send()
        last(dn0, d0, D0)
        last(dn1, d1, D1)
        for k in keeps:
            k.wait()
    return begin, {1: at0, 3: at2, 4: at3, 5: at4, 7: at6}, end


def bias_consts():
    y = np.arange(512)
    y = np.where(y >= 128, y - 512, y)
    ids = bucket_np(-128 - y)
    out = np.zeros((128, 1280), np.float32)
    for a in range(2):
        out[32 * a + ids, 512 * a + np.arange(512)] = 1
        out[32 * a + 15, 1024 + a:1152:2] = 1
        out[32 * a + 31, 1152 + a:1280:2] = 1
    return jnp.asarray(out, bf)

def mask_block(kind, text):
    pos = lax.broadcasted_iota(jnp.int32, (L, 128), 0)
    tile = lax.broadcasted_iota(jnp.int32, (L, 128), 1) // 2
    seg = jnp.where(kind == 1, pos // 384, 0)
    mine = jnp.where(kind == 1, tile // 3, 0)
    length = jnp.where(seg == 0, text[0], jnp.where(seg == 1, text[1], text[2]))
    live = pos - seg * 384 < jnp.where(kind == 1, 256, 1024) + length
    return jnp.where(live & (seg == mine), 0.0, NEG)

def front_kernel(kind_ref, text_ref, x_ref, gain1_ref, gain2_ref, table_ref, wq_ref, wk_ref, wv_ref, gate_ref, up_ref, dn_in, wo_in, const_ref,
                 o_ref, e_ref, r_ref, n_ref, qkv_out, w_out, gu, dn, wo,
                 W, acc, rstd, qkv, gu_in, mask, rhs, kaug, vaug, bn, s_ref, wsend, wrecv, wlocal, send, recv, local):
    b, m, c, mx, my, md = places()
    o = 1 - c
    nx, ny, nc, nz = (b, mx, c), (b, my, c), (b, m, o), (b + 1 - 2 * lax.rem(b, 2), m, c)
    d = wq_ref.shape[1]
    rows = wq_ref.shape[0]
    half = rows // 2
    me = m * 2 + c
    p = pl.program_id(0)
    begin, during, end = gather_steps(gu_in, dn_in, wo_in, gu, dn, wo, send, recv, local)
    keeps = (pltpu.make_async_copy(W, w_out, wlocal.at[0]), pltpu.make_async_copy(qkv, qkv_out, wlocal.at[1]))
    def push(src, n, to):
        return pltpu.make_async_remote_copy(src_ref=src, dst_ref=src, send_sem=wsend.at[n], recv_sem=wrecv.at[n], device_id=to, device_id_type=MESH)
    def got(ref, n):
        push(ref, n, nc).wait_recv()
    def chunk(j, first):
        cols = pl.ds(pl.multiple_of(j * 2 * rows, 2 * rows), 2 * rows)
        gain = jnp.concatenate([W[2 * j, 0:1, 3 * d:3 * d + rows], W[2 * j + 1, 0:1, 3 * d:3 * d + rows]], 1).astype(f32)
        n = (x_ref[:, cols].astype(f32) * rstd[...] * gain).astype(bf)
        n_ref[:, cols] = n
        for t in range(3):
            y = dot(n, W[pl.ds(2 * j, 2), :, t * d:t * d + d].reshape(2 * rows, d))
            if first:
                acc[:, t * d:t * d + d] = y
            else:
                acc[:, t * d:t * d + d] = acc[:, t * d:t * d + d] + y
    @pl.when(p == 0)
    def _():
        W[me, :, 0:d] = wq_ref[...]
        W[me, :, d:2 * d] = wk_ref[...]
        W[me, :, 2 * d:3 * d] = wv_ref[...]
        W[me, :, 3 * d:3 * d + 128] = jnp.zeros((rows, 128), bf)
        W[me, 0:1, 3 * d:3 * d + rows] = gain1_ref[...]
        W[me, 1:2, 3 * d:3 * d + rows] = gain2_ref[...]
        W[me, 2:3, 3 * d:3 * d + table_ref.shape[1]] = table_ref[...]
        greet([nx, ny, nc, nz])
        top, low = pl.ds(0, half), pl.ds(half, half)
        sends = [push(W.at[me], 0, nx), push(W.at[me], 1, ny), push(W.at[me], 2, nc)]
        for s in sends:
            s.start()
        gu_in[0] = gate_ref[...]
        gu_in[1] = up_ref[...]
        for t in range(0, L, 384):
            x = x_ref[t:t + 384, :].astype(f32)
            rstd[t:t + 384, :] = lax.rsqrt(jnp.mean(x * x, axis=-1, keepdims=True) + EPS)
        mask[...] = mask_block(kind_ref[0], (text_ref[0, 0], text_ref[0, 1], text_ref[0, 2]))
        fwd_open(rhs, vaug)
        ix, iy, idg = mx * 2 + c, my * 2 + c, md * 2 + c
        jx, jy, jdg = mx * 2 + o, my * 2 + o, md * 2 + o
        got(W.at[m * 2 + o], 2)
        chunk(m, True)
        got(W.at[ix], 0)
        more = [push(W.at[ix, top], 3, ny), push(W.at[ix], 5, nc)]
        got(W.at[iy], 1)
        more += [push(W.at[iy, low], 4, nx), push(W.at[iy], 6, nc)]
        for s in more:
            s.start()
        begin()
        got(W.at[jx], 5)
        chunk(mx, False)
        got(W.at[jy], 6)
        chunk(my, False)
        got(W.at[idg, top], 3)
        got(W.at[idg, low], 4)
        more.append(push(W.at[idg], 7, nc))
        more[-1].start()
        got(W.at[jdg], 7)
        keeps[0].start()
        chunk(md, False)
        for t in range(3 * d // 128):
            qkv[t] = acc[:, 128 * t:128 * t + 128].astype(bf)
        keeps[1].start()
        for s in sends + more:
            s.wait_send()
    for at, act in during.items():
        pl.when(p == at)(act)
    @pl.when(p > 0)
    def _():
        h = p - 1
        N = d // 128
        values = jnp.broadcast_to(W[h, 2:3, 3 * d:3 * d + 128], (16, 128))
        bias = dot(values, const_ref[...])
        fwd_pair(qkv[h], qkv[N + h], qkv[2 * N + h], mask[...], bias[0:1, 1024:1152], bias[0:1, 1152:1280],
                 jnp.concatenate([bias[0:1, 0:512], bias[0:1, 512:1024]], 0), o_ref, e_ref, r_ref, rhs, kaug, vaug, bn, s_ref)
    @pl.when(p == pl.num_programs(0) - 1)
    def _():
        end()
        for k in keeps:
            k.wait()

def front(kind, text, x, gain1, gain2, table, wq, wk, wv, gate, up, dn, wo):
    R, d = x.shape
    rows = wq.shape[0]
    N = d // 128
    at = lambda p: jnp.maximum(p - 1, 0)
    spec = pl.BlockSpec((R, 128), lambda p: (0, at(p)))
    hbm = pl.BlockSpec(memory_space=pl.ANY)
    whole = lambda a: pl.BlockSpec(a.shape, lambda p: (0,) * a.ndim, pipeline_mode=pl.Buffered(1))
    smem = pl.BlockSpec(memory_space=pltpu.SMEM)
    sds = jax.ShapeDtypeStruct
    dma = pltpu.SemaphoreType.DMA
    row = lambda a: a.reshape(1, -1)
    vectors = (x, row(gain1), row(gain2), row(table), wq, wk, wv, gate, up, dn, wo, bias_consts())
    wide = 3 * d + 128
    return pl.pallas_call(front_kernel, grid=(1 + N,),
        in_specs=[smem, smem] + [whole(a) for a in vectors],
        out_specs=[spec, pl.BlockSpec((None, None, R, NT * 256), lambda p: (0, at(p), 0, 0)), spec,
                   pl.BlockSpec((R, d), lambda p: (0, 0), pipeline_mode=pl.Buffered(1))] + [hbm] * 5,
        out_shape=[sds((R, d), bf), sds((1, N, R, NT * 256), bf), sds((R, d), f32), sds((R, d), bf), sds((3 * N, R, 128), bf),
                   sds((8, rows, wide), bf), sds((2, 8) + gate.shape, bf), sds((8,) + dn.shape, bf), sds((8,) + wo.shape, bf)],
        scratch_shapes=[pltpu.VMEM((8, rows, wide), bf), pltpu.VMEM((R, 3 * d), f32), pltpu.VMEM((R, 1), f32), pltpu.VMEM((3 * N, R, 128), bf),
                        pltpu.VMEM((2,) + gate.shape, bf), pltpu.VMEM((R, 128), f32),
                        pltpu.VMEM((256, NT * 256), bf), pltpu.VMEM((R, 256), bf), pltpu.VMEM((R, 256), bf), pltpu.VMEM((384, 256), f32), pltpu.VMEM((2, R, 256), f32),
                        dma((8,)), dma((8,)), dma((2,)), dma((53,)), dma((53,)), dma((4,))],
        compiler_params=pltpu.CompilerParams(collective_id=1, has_side_effects=True, vmem_limit_bytes=63 * 2**20),
        name="front")(kind, text, *vectors)

DRAIN = 6

def plane_scratch(rows, cols):
    h = rows // 2
    pair = pltpu.VMEM((2, 2, h, cols), bf)
    single = pltpu.VMEM((2, h, cols), bf)
    dma = pltpu.SemaphoreType.DMA
    return [pltpu.VMEM((2, 4, 2, rows, cols), bf), pltpu.VMEM((2, 4, rows, cols), bf)] + [pair] * 6 + [single] * 2 + [dma((5, 2)), dma((5, 2))]

def z_scratch(n, rows, cols):
    ring = lambda k: pltpu.VMEM((k, rows, cols), bf)
    dma = pltpu.SemaphoreType.DMA
    return [ring(4), ring(4), ring(2), ring(n), dma((3, n)), dma((3, n))]

def plus(a, b):
    return a + b

def rs_greet():
    b, m, c, mx, my, md = places()
    greet([(b, mx, c), (b, my, c), (b, m, 1 - c), (b + 1 - 2 * lax.rem(b, 2), m, c), (3 - b, m, c)])

def stage(t, n, act, also=None):
    live = (t >= 0) & (t < n)
    pl.when(live if also is None else live & also)(lambda: act(t))

def plane_step(s, n, bufs, put):
    src, cbuf, sx, sy, kt, kb, xt, yb, t2, b2, send, recv = bufs
    b, m, c, mx, my, md = places()
    o = 1 - c
    nx, ny, nc = (b, mx, c), (b, my, c), (b, m, o)
    h = kt.shape[2]
    def copy(kind, k, a, z, to):
        return pltpu.make_async_remote_copy(src_ref=a, dst_ref=z, send_sem=send.at[kind, k], recv_sem=recv.at[kind, k], device_id=to, device_id_type=MESH)
    core = lambda k: copy(0, k, src.at[k, :, o], cbuf.at[k], nc)
    x1 = lambda k: copy(1, k, sx.at[k], xt.at[k], nx)
    y1 = lambda k: copy(2, k, sy.at[k], yb.at[k], ny)
    y2 = lambda k: copy(3, k, kt.at[k, 1], t2.at[k], ny)
    x2 = lambda k: copy(4, k, kb.at[k, 1], b2.at[k], nx)
    def third(t):
        k = lax.rem(t, 2)
        y2(k).wait()
        x2(k).wait()
        put(t, plus(kt[k, 0], t2[k]), plus(kb[k, 0], b2[k]))
    def second(t):
        k = lax.rem(t, 2)
        x1(k).wait()
        y1(k).wait()
        kt[k] = plus(kt[k], xt[k])
        kb[k] = plus(kb[k], yb[k])
        y2(k).start()
        x2(k).start()
    def first(t):
        k = lax.rem(t, 2)
        core(k).wait()
        top = lambda i: plus(src[k, i, c, 0:h], cbuf[k, i, 0:h])
        low = lambda i: plus(src[k, i, c, h:2 * h], cbuf[k, i, h:2 * h])
        sx[k, 0], sx[k, 1] = top(mx), top(md)
        sy[k, 0], sy[k, 1] = low(my), low(md)
        x1(k).start()
        y1(k).start()
        kt[k, 0], kt[k, 1] = top(m), top(my)
        kb[k, 0], kb[k, 1] = low(m), low(mx)
    stage(s - 3, n, third)
    stage(s - 2, n, second)
    stage(s - 1, n, first)
    stage(s, n, lambda t: core(lax.rem(t, 2)).start())

def z_step(s, n, bufs, before):
    part, inward, across, done, send, recv = bufs
    b, m, c, mx, my, md = places()
    nz, na = (b + 1 - 2 * lax.rem(b, 2), m, c), (3 - b, m, c)
    outer = (b == 0) | (b == 3)
    inner = (b == 1) | (b == 2)
    def copy(kind, t, a, z, to):
        return pltpu.make_async_remote_copy(src_ref=a, dst_ref=z, send_sem=send.at[kind, t], recv_sem=recv.at[kind, t], device_id=to, device_id_type=MESH)
    up = lambda t: copy(0, t, part.at[lax.rem(t, 4)], inward.at[lax.rem(t, 4)], nz)
    over = lambda t: copy(1, t, part.at[lax.rem(t, 4)], across.at[lax.rem(t, 2)], na)
    down = lambda t: copy(2, t, done.at[t], done.at[t], nz)
    def outer_done(t):
        up(t).wait_send()
        down(t).wait_recv()
    def inner_done(t):
        down(t).wait_send()
    def inner_sum(t):
        over(t).wait()
        done[t] = plus(part[lax.rem(t, 4)], across[lax.rem(t, 2)])
        down(t).start()
    def inner_part(t):
        up(t).wait_recv()
        part[lax.rem(t, 4)] = plus(part[lax.rem(t, 4)], inward[lax.rem(t, 4)])
        over(t).start()
    stage(s - 3, n, outer_done, outer)
    stage(s - 3, n, inner_done, inner)
    stage(s - 2, n, inner_sum, inner)
    stage(s - 1, n, inner_part, inner)
    before()
    stage(s, n, lambda t: up(t).start(), outer)

def sum_step(s, n, plane, z):
    h = plane[4].shape[2]
    part = z[0]
    def put(t, top, low):
        part[lax.rem(t, 4), 0:h] = top
        part[lax.rem(t, 4), h:2 * h] = low
    z_step(s - 3, n, z, lambda: plane_step(s, n, plane, put))

GELU_C = float(np.sqrt(2.0 / np.pi))
def dot_nt(a, b):
    return lax.dot_general(a, b, (((1,), (1,)), ((), ())), preferred_element_type=f32)

def ffn_open(x_ref, ctx_ref, gain_ref, wo_ref, gres_ref, res, n, acc):
    for t in range(0, x_ref.shape[0], 384):
        s = slice(t, t + 384)
        y = x_ref[s, :].astype(f32) + dot(ctx_ref[s, :], wo_ref[...])
        res[s, :] = y
        acc[s, :] = y
        n[s, :] = (y * lax.rsqrt(jnp.mean(y * y, axis=-1, keepdims=True) + EPS) * gain_ref[0:1, :]).astype(bf)
    gres_ref[...] = jnp.zeros_like(gres_ref)

def ffn_block(g_ref, gu_ref, dn_ref, gres_ref, ddn_ref, n, acc):
    d = n.shape[1]
    wg = gu_ref[0].reshape(d, gu_ref.shape[-1])
    wu = gu_ref[1].reshape(d, gu_ref.shape[-1])
    wd = dn_ref[...]
    nn = n[...]
    g = g_ref[...]
    v = dot(nn, wg)
    u = dot(nn, wu)
    gh = dot_nt(g, wd)
    v2 = v * v
    th = jnp.tanh(GELU_C * v * (1.0 + 0.044715 * v2))
    half = 0.5 * (1.0 + th)
    gel = v * half
    h = (gel * u).astype(bf)
    dgel = half + 0.5 * v * (1.0 - th * th) * (GELU_C * (1.0 + 3 * 0.044715 * v2))
    gg = (gh * u * dgel).astype(bf)
    gu = (gh * gel).astype(bf)
    acc[...] = acc[...] + dot(h, wd)
    gres_ref[...] = gres_ref[...] + dot_nt(jnp.concatenate([gg, gu], 1), jnp.concatenate([wg, wu], 1))
    ddn_ref[...] = dot_tl(h, g).astype(bf)
    return dot_tl(nn, gg).astype(bf), dot_tl(nn, gu).astype(bf)

def ffn_close(s, g_ref, gain_ref, wo_ref, out_ref, gres_ref, gctx_ref, res, n, acc):
    out_ref[s, :] = acc[s, :].astype(bf)
    y = res[s, :]
    r = lax.rsqrt(jnp.mean(y * y, axis=-1, keepdims=True) + EPS)
    m = y * r
    gn = gres_ref[s, :]
    w = gn * gain_ref[0:1, :]
    gr = g_ref[s, :].astype(f32) + r * (w - m * jnp.mean(w * m, axis=-1, keepdims=True))
    gres_ref[s, :] = gr
    low = gr.astype(bf)
    n[s, :] = low
    gctx_ref[s, :] = dot_nt(low, wo_ref[...]).astype(bf)
    return jnp.sum(gn * m, axis=0, keepdims=True)

def ffn_kernel(x_ref, ctx_ref, g_ref, gain_ref, wo_ref, gu_ref, dn_ref,
               out_ref, gres_ref, gctx_ref, dwo_ref, ggain_ref, ddn_ref, dgu_ref, res, n, acc):
    j = pl.program_id(0)
    @pl.when(j == 0)
    def _():
        ffn_open(x_ref, ctx_ref, gain_ref, wo_ref, gres_ref, res, n, acc)
    a, b = ffn_block(g_ref, gu_ref, dn_ref, gres_ref, ddn_ref, n, acc)
    dgu_ref[0] = a.reshape(dgu_ref.shape[1:])
    dgu_ref[1] = b.reshape(dgu_ref.shape[1:])
    @pl.when(j == pl.num_programs(0) - 1)
    def _():
        R = x_ref.shape[0]
        total = sum(ffn_close(slice(t, t + 384), g_ref, gain_ref, wo_ref, out_ref, gres_ref, gctx_ref, res, n, acc) for t in range(0, R, 384))
        ggain_ref[...] = jnp.broadcast_to(total, ggain_ref.shape)
        dwo_ref[...] = dot_tl(ctx_ref[...], n[...]).astype(bf)

def ffn_sum_kernel(x_ref, ctx_ref, g_ref, gain_ref, wo_ref, gu_ref, dn_ref,
                   out_ref, gres_ref, gctx_ref, dwo_ref, ggain_ref, ddn_ref, dgu_ref, res, n, acc, *bufs):
    j = pl.program_id(0)
    N = pl.num_programs(0) - 3
    src = bufs[0]
    @pl.when(j == 0)
    def _():
        b, m, c, mx, my, md = places()
        greet([(b, mx, c), (b, my, c), (b, m, 1 - c)])
        ffn_open(x_ref, ctx_ref, gain_ref, wo_ref, gres_ref, res, n, acc)
        ggain_ref[...] = jnp.zeros_like(ggain_ref)
    @pl.when(j < N)
    def _():
        a, b = ffn_block(g_ref, gu_ref, dn_ref, gres_ref, ddn_ref, n, acc)
        k = lax.rem(j, 2)
        rows = a.shape[0] // 8
        src[k, :, :, 0:rows] = a.reshape(4, 2, rows, a.shape[1])
        src[k, :, :, rows:2 * rows] = b.reshape(4, 2, rows, a.shape[1])
    @pl.when(j >= N)
    def _():
        part = x_ref.shape[0] // 3
        s = pl.ds(pl.multiple_of((j - N) * part, part), part)
        total = ffn_close(s, g_ref, gain_ref, wo_ref, out_ref, gres_ref, gctx_ref, res, n, acc)
        ggain_ref[...] = ggain_ref[...] + jnp.broadcast_to(total, ggain_ref.shape)
    h = dgu_ref.shape[1] // 2
    def put(t, top, low):
        dgu_ref[t, 0:h] = top
        dgu_ref[t, h:2 * h] = low
    plane_step(j, N, bufs, put)
    @pl.when(j == N + 2)
    def _():
        dwo_ref[...] = dot_tl(ctx_ref[...], n[...]).astype(bf)

def ffn(x, ctx, g, gain, wo, gu, dn, near, block=256):
    R, d = x.shape
    F = dn.shape[0]
    k = gu.shape[1]
    N = F // block
    sds = jax.ShapeDtypeStruct
    one = lambda *s: pl.BlockSpec(s, lambda j: (0,) * len(s), pipeline_mode=pl.Buffered(1))
    at = lambda j: jnp.minimum(j, N - 1)
    gub = pl.BlockSpec((2, k, d // k, block), lambda j: (0, 0, 0, at(j)))
    dnb = pl.BlockSpec((block, d), lambda j: (at(j), 0))
    rows = 2 * (d // k)
    if near:
        body, extra, steps, last = ffn_sum_kernel, plane_scratch(rows, block), N + 3, (one(N, rows, block), sds((N, rows, block), bf))
        params = pltpu.CompilerParams(vmem_limit_bytes=61 * 2**20, collective_id=3, has_side_effects=True)
    else:
        body, extra, steps, last = ffn_kernel, [], N, (gub, sds(gu.shape, bf))
        params = pltpu.CompilerParams(vmem_limit_bytes=61 * 2**20)
    return pl.pallas_call(body, grid=(steps,),
        in_specs=[one(R, d), one(R, d), one(R, d), one(1, d), one(d, d), gub, dnb],
        out_specs=[one(R, d), one(R, d), one(R, d), one(d, d), one(8, d), dnb, last[0]],
        out_shape=[sds((R, d), bf), sds((R, d), f32), sds((R, d), bf), sds((d, d), bf), sds((8, d), f32), sds(dn.shape, bf), last[1]],
        scratch_shapes=[pltpu.VMEM((R, d), f32), pltpu.VMEM((R, d), bf), pltpu.VMEM((R, d), f32)] + extra,
        compiler_params=params, name="ffn")(x, ctx, g, gain, wo, gu, dn)

def sum_rounds(s, box, inbox, send, recv):
    b, m, c, mx, my, md = places()
    peers = [(b, m, 1 - c), (b, mx, c), (b, my, c), (b + 1 - 2 * lax.rem(b, 2), m, c), (3 - b, m, c)]
    def copy(r):
        return pltpu.make_async_remote_copy(src_ref=box.at[r], dst_ref=inbox.at[r], send_sem=send.at[r], recv_sem=recv.at[r], device_id=peers[r], device_id_type=MESH)
    for r in range(5):
        @pl.when(s == r)
        def _():
            copy(r).start()
        @pl.when(s == r + 1)
        def _():
            copy(r).wait()
            box[r + 1] = box[r] + inbox[r]

def bwd_sum_kernel(q_ref, k_ref, v_ref, do_ref, o_ref, r_ref, e_ref, n_ref, x_ref, gres_ref, gain_ref, wq_ref, wk_ref, wv_ref, dn_ref, wo_ref, gain2_ref, gu_ref, const_ref,
                   gtok_ref, small_ref, out_a, out_b, out_c, rhs, vaug, dobd, qaug, ds_ref, nacc, near_ref, far_ref, ggain, tab, g_all, box, inbox, ssend, srecv, osem, *bufs):
    p = pl.program_id(0)
    N = pl.num_programs(0) - DRAIN
    plane_a, z_a, plane_b, z_b, z_c = bufs[0:12], bufs[12:18], bufs[18:30], bufs[30:36], bufs[36:42]
    src_a, src_b = plane_a[0], plane_b[0]
    done_a, done_b, done_c = z_a[3], z_b[3], z_c[3]
    NA = done_a.shape[0]
    d = gtok_ref.shape[1]
    k = lax.rem(p, 2)
    def put(src, arrays):
        h = src.shape[3] // 2
        at = 0
        for a in arrays:
            r = a.shape[1] // 2
            a = a.reshape((4, 2) + a.shape[1:])
            src[k, :, :, at:at + r] = a[:, :, 0:r]
            src[k, :, :, h + at:h + at + r] = a[:, :, r:2 * r]
            at += r
    @pl.when(p == 0)
    def _():
        rs_greet()
        bwd_open(rhs, vaug, qaug)
        gtok_ref[...] = jnp.zeros_like(gtok_ref)
        ggain[...] = jnp.zeros_like(ggain)
    @pl.when(p < NA)
    def _():
        put(src_a, (dn_ref[...], wo_ref[...]))
    @pl.when(p < N)
    def _():
        g = jnp.concatenate(bwd_pair(q_ref, k_ref, v_ref, do_ref, o_ref, r_ref, e_ref, near_ref, far_ref, rhs, vaug, dobd, qaug, ds_ref, nacc), 1)
        lane = lax.broadcasted_iota(jnp.int32, (1, 128), 1)
        sums = jnp.dot(near_ref[...], const_ref[...], precision=lax.Precision.HIGHEST, preferred_element_type=f32)
        for a in range(2):
            lo, hi = (jnp.sum(jnp.where(lax.rem(lane, 2) == a, far_ref[i:i + 1, :], 0.0), axis=1, keepdims=True) for i in range(2))
            tab[p, a:a + 1, :] = sums[a:a + 1, :] + jnp.where(lane == 15, lo, 0.0) + jnp.where(lane == 31, hi, 0.0)
        g_all[p] = g
        gw = dot_tl(n_ref[...], g)
        half = pl.ds(pl.multiple_of(lax.rem(p, 2) * 128, 128), 128)
        w = jnp.concatenate([w_ref[:, :, half].reshape(d, 128) for w_ref in (wq_ref, wk_ref, wv_ref)], 1)
        ggain[...] = ggain[...] + sum((gw * w.astype(f32))[:, 128 * t:128 * t + 128] for t in range(3))
        gw = gw.astype(bf)
        put(src_b, [gw[:, 128 * t:128 * t + 128].reshape(8, d // 8, 128) for t in range(3)])
    @pl.when((p >= N) & (p < N + N // 2))
    def _():
        i = 2 * (p - N)
        g = jnp.concatenate([g_all[i], g_all[i + 1]], 1)
        w = jnp.concatenate([w_ref[:, :, 128 * t:128 * t + 128].reshape(d, 128) for t in range(2) for w_ref in (wq_ref, wk_ref, wv_ref)], 1)
        gtok_ref[...] = gtok_ref[...] + dot_nt(g, w)
    @pl.when(p >= N + N // 2)
    def _():
        rows = x_ref.shape[0]
        step = rows // 3
        for t in range(3):
            s = pl.ds(pl.multiple_of((p - N - N // 2) * rows + t * step, step), step)
            x = x_ref[t * step:t * step + step, :].astype(f32)
            r = lax.rsqrt(jnp.mean(x * x, axis=-1, keepdims=True) + EPS)
            m = x * r
            w = gtok_ref[s, :] * gain_ref[0:1, :]
            gtok_ref[s, :] = gres_ref[t * step:t * step + step, :] + r * (w - m * jnp.mean(w * m, axis=-1, keepdims=True))
    @pl.when(p == N - 1)
    def _():
        for t in range(N):
            box[0, 2 * t:2 * t + 2] = tab[t, 0:2]
        w = d // 8
        one = jnp.sum(ggain[...].T, axis=0, keepdims=True) / gain_ref[0:1, :]
        for t in range(8):
            box[0, 2 * N + t:2 * N + t + 1] = one[:, w * t:w * t + w]
            box[0, 2 * N + 8 + t:2 * N + 9 + t] = gain2_ref[0:1, w * t:w * t + w]
    sum_rounds(p - N + 1, box, inbox, ssend, srecv)
    sum_step(p, NA, plane_a, z_a)
    sum_step(p, N, plane_b, z_b)
    def take():
        @pl.when(p < N)
        def _():
            z_c[0][lax.rem(p, 4)] = gu_ref[...]
    z_step(p, N, z_c, take)
    @pl.when(p == N + DRAIN - 1)
    def _():
        small_ref[...] = box[5]
        keeps = [pltpu.make_async_copy(a, o, osem.at[i]) for i, (a, o) in enumerate(((done_a, out_a), (done_b, out_b), (done_c, out_c)))]
        for copy in keeps:
            copy.start()
        for copy in keeps:
            copy.wait()

def attn_bwd_sum(qkv, do, o, r, e, n, x, gres, gain, qkv_w, dn, wo, gain2, gu):
    R, d = x.shape
    N = d // 128
    NA, wide = N, 128
    rows_a, rows_b = dn.shape[1] + wo.shape[1], 3 * (d // 8)
    sds = jax.ShapeDtypeStruct
    at = lambda p: jnp.minimum(p, N - 1)
    after = lambda p: jnp.clip(p - N - N // 2, 0, 1)
    spec = pl.BlockSpec((R, 128), lambda p: (0, at(p)))
    head = lambda t: pl.BlockSpec((None, R, 128), lambda p: (t * N + at(p), 0, 0))
    one = lambda *s: pl.BlockSpec(s, lambda p: (0,) * len(s), pipeline_mode=pl.Buffered(1))
    part = pl.BlockSpec((R // 2, d), lambda p: (after(p), 0), pipeline_mode=pl.Buffered(1))
    cols = lambda a, t: pl.BlockSpec((8, a.shape[1], 256), lambda p: (0, 0, t * (N // 2) + jnp.where(p < N, p // 2, jnp.minimum(p - N, N // 2 - 1))))
    early = lambda a: pl.BlockSpec((8, a.shape[1], wide), lambda p: (0, 0, jnp.minimum(p, NA - 1)), pipeline_mode=pl.Buffered(1))
    hbm = pl.BlockSpec(memory_space=pl.ANY)
    dma = pltpu.SemaphoreType.DMA
    small = (2 * N + 16, d // 8)
    gu = gu.reshape(N, -1, gu.shape[2])
    to_bucket = jnp.asarray((bucket_np(np.arange(512) - 255)[:, None] == np.arange(128)[None, :]).astype(np.float32))
    return pl.pallas_call(bwd_sum_kernel, grid=(N + DRAIN,),
        in_specs=[head(0), head(1), head(2)] + [spec] * 3 + [pl.BlockSpec((None, None, R, NT * 256), lambda p: (0, at(p), 0, 0)), one(R, d), part, part, one(1, d),
                  cols(qkv_w, 0), cols(qkv_w, 1), cols(qkv_w, 2), early(dn), early(wo), one(8, d),
                  pl.BlockSpec((None,) + gu.shape[1:], lambda p: (at(p), 0, 0)), one(512, 128)],
        out_specs=[one(R, d), one(*small), hbm, hbm, hbm],
        out_shape=[sds((R, d), f32), sds(small, f32), sds((NA, rows_a, wide), bf), sds((N, rows_b, 128), bf), sds(gu.shape, bf)],
        scratch_shapes=[pltpu.VMEM((256, NT * 256), bf), pltpu.VMEM((R, 256), bf), pltpu.VMEM((NT * 256, 128), bf), pltpu.VMEM((NT * 256, 256), bf), pltpu.VMEM((R, NT * 256), bf), pltpu.VMEM((384, 256), f32),
                        pltpu.VMEM((8, 512), f32), pltpu.VMEM((8, 128), f32), pltpu.VMEM((d, 128), f32), pltpu.VMEM((N, 8, 128), f32), pltpu.VMEM((N, R, 384), bf), pltpu.VMEM((6,) + small, f32), pltpu.VMEM((5,) + small, f32), dma((5,)), dma((5,)), dma((3,))]
                       + plane_scratch(rows_a, wide) + z_scratch(NA, rows_a, wide) + plane_scratch(rows_b, 128) + z_scratch(N, rows_b, 128) + z_scratch(*gu.shape),
        compiler_params=pltpu.CompilerParams(vmem_limit_bytes=63 * 2**20, collective_id=4, has_side_effects=True), name="attn_bwd_sum")(
            qkv, qkv, qkv, do, o, r, e, n, x, gres, gain, qkv_w, qkv_w, qkv_w, dn, wo, gain2, gu, to_bucket)

def finish_kernel(gtok_in, out_in, a_in, b_in, c_in, small_in, at_ref, gtok, out, q, k, v, wo, gate, up, dn, gain1, gain2, table):
    gtok[...] = gtok_in[...]
    out[...] = out_in[...]
    @pl.when(pl.program_id(0) == 0)
    def _():
        def spread(src, targets):
            n, h, w = src.shape[0], src.shape[1] // 2, src.shape[2]
            for t in range(n):
                at = 0
                for ref in targets:
                    r = ref.shape[0] // 2
                    ref[0:r, w * t:w * t + w] = src[t, at:at + r].astype(f32)
                    ref[r:2 * r, w * t:w * t + w] = src[t, h + at:h + at + r].astype(f32)
                    at += r
        spread(a_in, (dn, wo))
        spread(b_in, (q, k, v))
        r = gate.shape[0]
        w = c_in.shape[1]
        for t in range(c_in.shape[0] // (2 * r)):
            gate[:, w * t:w * t + w] = c_in[2 * r * t:2 * r * t + r].astype(f32)
            up[:, w * t:w * t + w] = c_in[2 * r * t + r:2 * r * t + 2 * r].astype(f32)
        me = at_ref[0]
        heads = small_in.shape[0] - 16
        per = heads // 8
        gain1[...] = small_in[pl.ds(heads + me, 1), :]
        gain2[...] = small_in[pl.ds(heads + 8 + me, 1), :]
        table[...] = small_in[pl.ds(per * me, per), :]

def finish(gtok, out, a, b, c, small, at, rows, ff):
    R, d = gtok.shape
    steps = 8
    sds = jax.ShapeDtypeStruct
    block = pl.BlockSpec((R // steps, d), lambda i: (i, 0))
    one = lambda *s: pl.BlockSpec(s, lambda i: (0,) * len(s), pipeline_mode=pl.Buffered(1))
    whole = lambda x: one(*x.shape)
    shapes = [(rows, d)] * 4 + [(rows, ff)] * 2 + [(ff // 8, d), (1, d // 8), (1, d // 8), ((small.shape[0] - 16) // 8, d // 8)]
    c = c.reshape(-1, c.shape[2])
    return pl.pallas_call(finish_kernel, grid=(steps,),
        in_specs=[block, block, whole(a), whole(b), whole(c), whole(small), pl.BlockSpec(memory_space=pltpu.SMEM)],
        out_specs=[block, block] + [one(*s) for s in shapes],
        out_shape=[sds((R, d), f32), sds((R, d), bf)] + [sds(s, f32) for s in shapes],
        compiler_params=pltpu.CompilerParams(vmem_limit_bytes=62 * 2**20), name="finish")(gtok, out, a, b, c, small, at)

def contract_rows(left, right):
    return lax.dot_general(left, right, (((0,), (0,)), ((), ())), preferred_element_type=f32)

def contract_cols(left, right):
    return lax.dot_general(left, right, (((1,), (1,)), ((), ())), preferred_element_type=f32)

def rms_norm(inputs, gain):
    return inputs * lax.rsqrt(jnp.mean(inputs * inputs, axis=-1, keepdims=True) + EPS) * gain

def gather(x):
    return lax.all_gather(x, SHARD, axis=0, tiled=False)

def scatter(x):
    return lax.psum_scatter(x, SHARD, scatter_dimension=0, tiled=True)

def per_device(near, tokens, row_kind, text_length, gain_attn, position_bias_table, weight_query, weight_key, weight_value, weight_out, gain_ffn, weight_gate, weight_up, weight_down, cotangent):
    n1, d = weight_query.shape
    n2 = position_bias_table.shape[0]
    inputs = tokens.astype(f32)
    at = lax.axis_index("dp") * lax.axis_size("narrow") + lax.axis_index("narrow")
    if near:
        context, e, r, normed, qkv, qkv_w, gu_w, down_w, out_w = front(
            row_kind, text_length, tokens, gain_attn, gain_ffn, position_bias_table, weight_query, weight_key, weight_value, weight_gate, weight_up, weight_down, weight_out)
        small = qkv_w[:, 0:2, 3 * d:3 * d + n1]
        gain_one, gain_two = small[:, 0].reshape(d).astype(f32), small[:, 1].reshape(d).astype(f32)
    else:
        small = gather(jnp.stack([gain_attn, gain_ffn, jnp.pad(position_bias_table, (0, n1 - n2))]))
        qkv_w = gather(jnp.concatenate([weight_query, weight_key, weight_value], 1))
        gain_one, gain_two = small[:, 0].reshape(d).astype(f32), small[:, 1].reshape(d).astype(f32)
        normed = rms_norm(inputs, gain_one).astype(bf)
        q, k, v = (dot(normed, qkv_w[:, :, t * d:t * d + d].reshape(d, d)).astype(bf) for t in range(3))
        far, w = tables(small[:, 2, :n2].reshape(-1))
        context, e, r = attn_fwd(q, k, v, mask_cols(row_kind, text_length), far, w)
        gu_w, down_w, out_w = jnp.moveaxis(gather(jnp.stack([weight_gate, weight_up])), 0, 1), gather(weight_down), gather(weight_out)
    ff = gu_w.shape[-1]
    output, grad_residual, grad_context, grad_out_w, g_gain_two, ddn, dgu = ffn(
        tokens, context, cotangent, gain_two.reshape(1, d), out_w.reshape(d, d), gu_w, down_w.reshape(ff, d), near)
    if near:
        shards = gu_w.shape[1]
        grad_tokens, small_g, sums_a, sums_b, sums_c = attn_bwd_sum(
            qkv, grad_context, context, r, e, normed, tokens, grad_residual, gain_one.reshape(1, d), qkv_w,
            ddn.reshape(shards, ff // shards, d), grad_out_w.reshape(shards, n1, d), g_gain_two, dgu)
        grad_tokens, output, s_q, s_k, s_v, s_out, s_gate, s_up, s_down, r_gain_one, r_gain_two, r_table = finish(
            grad_tokens, output, sums_a, sums_b, sums_c, small_g, at.reshape(1), n1, ff)
        r_gain_one, r_gain_two, r_table = r_gain_one.reshape(n1), r_gain_two.reshape(n1), r_table[:, :BUCKETS].reshape(n2)
    else:
        total = lambda x: lax.psum(scatter(x), "batch").astype(f32)
        gq, gk, gv, near_sums, far_sums = attn_bwd(q, k, v, grad_context, context, r, e)
        grads = (gq, gk, gv)
        s_gate, s_up, s_down, s_out = (total(x) for x in (dgu[0].reshape(d, ff), dgu[1].reshape(d, ff), ddn, grad_out_w))
        s_q, s_k, s_v = (total(contract_rows(normed, x).astype(bf)) for x in grads)
        grad_normed = sum(contract_cols(x, qkv_w[:, :, t * d:t * d + d].reshape(d, d)) for t, x in enumerate(grads))
        _, first_pull = jax.vjp(rms_norm, inputs, gain_one)
        share, g_gain_one = first_pull(grad_normed)
        grad_tokens = grad_residual + share
        g_table = table_grad(near_sums, far_sums)
        small_g = lax.psum(jnp.concatenate([g_gain_one, g_gain_two[0], g_table]), ("batch", "dp", "narrow"))
        r_gain_one = lax.dynamic_slice_in_dim(small_g, at * n1, n1)
        r_gain_two = lax.dynamic_slice_in_dim(small_g, d + at * n1, n1)
        r_table = lax.dynamic_slice_in_dim(small_g, 2 * d + at * n2, n2)
    return (output, grad_tokens, r_gain_one, r_table, s_q, s_k, s_v, s_out, r_gain_two, s_gate, s_up, s_down)

def solution(mesh):
    near = (mesh.shape["batch"], mesh.shape["dp"], mesh.shape["narrow"]) == (4, 4, 2)
    placed = (
        P(("batch", "dp", "narrow"), None),
        P(("batch", "dp", "narrow")),
        P(("batch", "dp", "narrow"), None),
        P(("dp", "narrow")),
        P(("dp", "narrow")),
        P(("dp", "narrow"), None),
        P(("dp", "narrow"), None),
        P(("dp", "narrow"), None),
        P(("dp", "narrow"), None),
        P(("dp", "narrow")),
        P(("dp", "narrow"), None),
        P(("dp", "narrow"), None),
        P(("dp", "narrow"), None),
        P(("batch", "dp", "narrow"), None),
    )
    return jax.shard_map(
        functools.partial(per_device, near),
        mesh=mesh,
        in_specs=placed,
        out_specs=(
            P(("batch", "dp", "narrow"), None),
            P(("batch", "dp", "narrow"), None),
            P(("dp", "narrow")),
            P(("dp", "narrow")),
            P(("dp", "narrow"), None),
            P(("dp", "narrow"), None),
            P(("dp", "narrow"), None),
            P(("dp", "narrow"), None),
            P(("dp", "narrow")),
            P(("dp", "narrow"), None),
            P(("dp", "narrow"), None),
            P(("dp", "narrow"), None),
        ),
        check_vma=False,
    )
```

```python
import functools

import jax
import jax.numpy as jnp
import numpy as np
from jax import lax
from jax.experimental import pallas as pl
from jax.experimental.pallas import tpu as pltpu
from jax.sharding import PartitionSpec as P

EPS = 1e-06
SHARD = ("dp", "narrow")
BUCKETS = 32
bf=jnp.bfloat16; f32=jnp.float32
T=128; L=1152; NT=L//T
NEG=-1e30
def dot(a,b): return jnp.dot(a,b,preferred_element_type=f32)
def dot_tl(a,b): return lax.dot_general(a,b,(((0,),(0,)),((),())),preferred_element_type=f32)

def fwd_open(rhs,vaug):
    rhs[...]=jnp.zeros_like(rhs)
    row=lax.broadcasted_iota(jnp.int32,(128,NT*256),0)
    col=lax.broadcasted_iota(jnp.int32,(128,NT*256),1)
    rhs[128:256,:]=(row==col//128).astype(f32).astype(bf)
    vaug[:,128:256]=jnp.ones((L,128),bf)

def fwd_pair(q,k,v,mask,lo,hi,bias,o_ref,e_ref,r_ref,rhs,kaug,vaug,bn,s_ref):
    qT=q.T
    for i in range(NT):
        rhs[0:64,256*i:256*i+128]=qT[0:64,128*i:128*i+128]
        rhs[64:128,256*i+128:256*i+256]=qT[64:128,128*i:128*i+128]
    kaug[:,0:128]=k
    row=lax.broadcasted_iota(jnp.int32,(L,128),0)//128
    col=lax.broadcasted_iota(jnp.int32,(L,128),1)//2
    far=jnp.where(row<col-1,lo,jnp.where(row>col+1,hi,0.0))
    kaug[:,128:256]=(mask+far).astype(bf)
    vaug[:,0:128]=v
    for a in range(2):
        wb=jnp.broadcast_to(bias[a:a+1,:],(384,512))
        bn[:,128*a:128*a+128]=pltpu.roll(wb,0,1,stride=1,stride_axis=0)[:,0:128]
    def scores(i,slot):
        ri=rhs[:,256*i:256*i+256]
        first,last=max(0,i-1)*128,min(NT,i+2)*128
        off=(first//128-(i-1))*128
        x=dot(kaug[...],ri)
        xn=x[first:last]+bn[off:off+last-first,:]
        ms=[jnp.max(xn,axis=0,keepdims=True)]
        s_ref[slot,first:last,:]=xn
        if first>0:
            s_ref[slot,0:first,:]=x[0:first]; ms.append(jnp.max(x[0:first],axis=0,keepdims=True))
        if last<L:
            s_ref[slot,last:L,:]=x[last:L]; ms.append(jnp.max(x[last:L],axis=0,keepdims=True))
        m=ms[0]
        for y in ms[1:]: m=jnp.maximum(m,y)
        return m
    lane=lax.broadcasted_iota(jnp.int32,(128,128),1)<64
    def finish(i,slot,m):
        e=jnp.exp(s_ref[slot]-m).astype(bf)
        e_ref[:,pl.ds(i*256,256)]=e
        o=dot_tl(e,vaug[...])
        num=jnp.where(lane,o[0:128,0:128],o[128:256,0:128])
        den=jnp.where(lane,o[0:128,128:256],o[128:256,128:256])
        r=1.0/den
        rows=pl.ds(i*128,128)
        o_ref[rows,:]=(num*r).astype(bf)
        r_ref[rows,:]=r
    m=scores(0,0)
    for i in range(NT):
        mn=scores(i+1,(i+1)%2) if i+1<NT else None
        finish(i,i%2,m)
        m=mn

def fwd_kernel(q_ref,k_ref,v_ref,mask_ref,far_ref,w_ref,o_ref,e_ref,r_ref,rhs,kaug,vaug,bn,s_ref):
    @pl.when((pl.program_id(0)==0)&(pl.program_id(1)==0))
    def _():
        fwd_open(rhs,vaug)
    fwd_pair(q_ref[...],k_ref[...],v_ref[...],mask_ref[...],far_ref[0:1,:],far_ref[1:2,:],w_ref[...],o_ref,e_ref,r_ref,rhs,kaug,vaug,bn,s_ref)

def attn_fwd(q,k,v,mask,far,w):
    rows=q.shape[0]//L
    spec=pl.BlockSpec((L,128),lambda r,p:(r,p))
    return pl.pallas_call(fwd_kernel,
        grid=(rows,8),
        in_specs=[spec,spec,spec,
            pl.BlockSpec((None,L,128),lambda r,p:(r,0,0)),
            pl.BlockSpec((None,8,128),lambda r,p:(p,0,0)),
            pl.BlockSpec((None,8,512),lambda r,p:(p,0,0))],
        out_specs=[spec,pl.BlockSpec((None,None,L,NT*256),lambda r,p:(r,p,0,0)),spec],
        out_shape=[jax.ShapeDtypeStruct(q.shape,bf),jax.ShapeDtypeStruct((rows,8,L,NT*256),bf),jax.ShapeDtypeStruct(q.shape,f32)],
        scratch_shapes=[pltpu.VMEM((256,NT*256),bf),pltpu.VMEM((L,256),bf),pltpu.VMEM((L,256),bf),pltpu.VMEM((384,256),f32),pltpu.VMEM((2,L,256),f32)],
        compiler_params=pltpu.CompilerParams(vmem_limit_bytes=56*2**20),
        name="attn_fwd",
    )(q,k,v,mask,far,w)

THR=(12,16,23,32,46,64,91)
def bucket_np(d):
    n=np.abs(d); c=np.full_like(n,8)
    for t in THR: c=c+(n>=t)
    return np.where(n<8,n,c)+16*(d>0)
def tables(table):
    t=table.reshape(16,32).astype(f32)
    y=np.arange(512); y=np.where(y>=128,y-512,y)
    d=-128-y
    oh=(np.arange(32)[:,None]==bucket_np(d)[None,:]).astype(np.float32)
    w=jnp.dot(t,jnp.asarray(oh),precision=lax.Precision.HIGHEST)
    w=jnp.pad(w.reshape(8,2,512),((0,0),(0,6),(0,0)))
    lo=jnp.tile(t[:,15].reshape(8,1,2),(1,1,64)); hi=jnp.tile(t[:,31].reshape(8,1,2),(1,1,64))
    far=jnp.pad(jnp.concatenate([lo,hi],1),((0,0),(0,6),(0,0)))
    return far,w
def mask_cols(row_kind,text_length):
    pos=np.arange(L)
    kind=row_kind[:,None]
    seg=kind*(pos//384)[None]
    off=pos[None]-seg*384
    img=jnp.where(kind==1,256,1024)
    tl=jnp.where(seg==0,text_length[:,0:1],jnp.where(seg==1,text_length[:,1:2],text_length[:,2:3]))
    live=off<img+tl
    qseg=kind*np.minimum(np.arange(128)//2//3,2)[None]
    ok=live[:,:,None]&(seg[:,:,None]==qseg[:,None,:])
    return jnp.where(ok,0.0,NEG).astype(f32)

def bwd_open(rhs,vaug,qaug):
    rhs[...]=jnp.zeros_like(rhs)
    c=lax.broadcasted_iota(jnp.int32,(L,128),1)
    vaug[:,128:256]=(c<3).astype(f32).astype(bf)
    row=lax.broadcasted_iota(jnp.int32,(NT*256,128),0)
    col=lax.broadcasted_iota(jnp.int32,(NT*256,128),1)
    qaug[:,128:256]=(row//128==col).astype(f32).astype(bf)

def bwd_pair(q_ref,k_ref,v_ref,do_ref,o_ref,r_ref,e_ref,near_ref,far_ref,rhs,vaug,dobd,qaug,ds_ref,nacc):
    q=q_ref[...]; k=k_ref[...]
    vaug[:,0:128]=v_ref[...]
    dof=do_ref[...].astype(f32)*r_ref[...]
    dos=dof.astype(bf)
    dT=dos.T
    pT=(dos.astype(f32)*o_ref[...].astype(f32)).T
    D=jnp.concatenate([jnp.sum(pT[0:64],axis=0,keepdims=True),jnp.sum(pT[64:128],axis=0,keepdims=True)],0)
    D=-D
    D1=D.astype(bf); D2=(D-D1.astype(f32)); D3=(D2-D2.astype(bf).astype(f32)).astype(bf); D2=D2.astype(bf)
    lane=lax.broadcasted_iota(jnp.int32,(128,128),1)<64
    zero=jnp.zeros((128,128),bf)
    z13=jnp.zeros((13,128),bf)
    for i in range(NT):
        t=slice(128*i,128*i+128)
        for a in range(2):
            h=slice(64*a,64*a+64)
            c=slice(256*i+128*a,256*i+128*a+128)
            rhs[h,c]=dT[h,t]
            rhs[128:144,c]=jnp.concatenate([D1[a:a+1,t],D2[a:a+1,t],D3[a:a+1,t],z13],0)
            dobd[c,:]=jnp.where(lane==(a==0),dos[t],zero)
            qaug[c,0:128]=jnp.where(lane==(a==0),q[t],zero)
    nacc[...]=jnp.zeros_like(nacc)
    dqs=[]
    for i in range(NT):
        c=slice(256*i,256*i+256)
        lo,hi=max(0,i-1)*128,min(NT,i+2)*128
        off=(lo//128-(i-1))*128
        dp=dot(vaug[...],rhs[:,c])
        ds=e_ref[:,c].astype(f32)*dp
        nacc[off:off+hi-lo,:]+=ds[lo:hi]
        dsb=ds.astype(bf)
        ds_ref[:,c]=dsb
        g=dot_tl(dsb,k)
        dqs.append(jnp.where(lane,g[0:128],g[128:256]).astype(bf))
    dv=dot(e_ref[...],dobd[...]).astype(bf)
    g=dot(ds_ref[...],qaug[...])
    dk=g[:,0:128].astype(bf)
    G=g[:,128:256]
    row=lax.broadcasted_iota(jnp.int32,(L,128),0)//128
    col=lax.broadcasted_iota(jnp.int32,(L,128),1)//2
    far_ref[0:1,:]=jnp.sum(jnp.where(row<col-1,G,0.0),axis=0,keepdims=True)
    far_ref[1:2,:]=jnp.sum(jnp.where(row>col+1,G,0.0),axis=0,keepdims=True)
    far_ref[2:8,:]=jnp.zeros((6,128),f32)
    near_ref[2:8,:]=jnp.zeros((6,512),f32)
    rev=(lax.broadcasted_iota(jnp.int32,(128,128),0)+lax.broadcasted_iota(jnp.int32,(128,128),1)==127).astype(f32)
    for a in range(2):
        x=jnp.dot(nacc[:,128*a:128*a+128],rev,precision=lax.Precision.HIGHEST,preferred_element_type=f32)
        x=jnp.concatenate([x,jnp.zeros((384,384),f32)],1)
        x=pltpu.roll(x,0,1,stride=1,stride_axis=0)
        near_ref[a:a+1,:]=jnp.sum(x,axis=0,keepdims=True)
    return jnp.concatenate(dqs,0),dk,dv

def bwd_kernel(q_ref,k_ref,v_ref,do_ref,o_ref,r_ref,e_ref,dq_ref,dk_ref,dv_ref,near_ref,far_ref,rhs,vaug,dobd,qaug,ds_ref,nacc):
    @pl.when((pl.program_id(0)==0)&(pl.program_id(1)==0))
    def _():
        bwd_open(rhs,vaug,qaug)
    dq_ref[...],dk_ref[...],dv_ref[...]=bwd_pair(q_ref,k_ref,v_ref,do_ref,o_ref,r_ref,e_ref,near_ref,far_ref,rhs,vaug,dobd,qaug,ds_ref,nacc)

def attn_bwd(q,k,v,do,o,r,e):
    rows=q.shape[0]//L
    spec=pl.BlockSpec((L,128),lambda r,p:(r,p))
    sds=jax.ShapeDtypeStruct
    return pl.pallas_call(bwd_kernel,
        grid=(rows,8),
        in_specs=[spec]*6+[pl.BlockSpec((None,None,L,NT*256),lambda r,p:(r,p,0,0))],
        out_specs=[spec]*3+[pl.BlockSpec((None,None,8,512),lambda r,p:(r,p,0,0)),pl.BlockSpec((None,None,8,128),lambda r,p:(r,p,0,0))],
        out_shape=[sds(q.shape,bf)]*3+[sds((rows,8,8,512),f32),sds((rows,8,8,128),f32)],
        scratch_shapes=[pltpu.VMEM((256,NT*256),bf),pltpu.VMEM((L,256),bf),pltpu.VMEM((NT*256,128),bf),pltpu.VMEM((NT*256,256),bf),pltpu.VMEM((L,NT*256),bf),pltpu.VMEM((384,256),f32)],
        compiler_params=pltpu.CompilerParams(vmem_limit_bytes=58*2**20),
        name="attn_bwd",
    )(q,k,v,do,o,r,e)
def table_grad(near,far):
    y=np.arange(512)
    oh=(bucket_np(y-255)[:,None]==np.arange(32)[None,:]).astype(np.float32)
    n=jnp.sum(near[:,:,0:2],0).reshape(16,512)
    g=jnp.dot(n,jnp.asarray(oh),precision=lax.Precision.HIGHEST)
    f=jnp.sum(far[:,:,0:2],0).reshape(8,2,64,2).sum(2)
    lo=f[:,0].reshape(16,1); hi=f[:,1].reshape(16,1)
    g=g+lo*np.eye(32,dtype=np.float32)[15][None]+hi*np.eye(32,dtype=np.float32)[31][None]
    return g.reshape(512)

MESH = pl.DeviceIdType.MESH

def places():
    b, m, c = lax.axis_index("batch"), lax.axis_index("dp"), lax.axis_index("narrow")
    x, y = lax.rem(m, 2), m // 2
    mx = y * 2 + (1 - x)
    my = (1 - y) * 2 + x
    md = (1 - y) * 2 + (1 - x)
    return b, m, c, mx, my, md

def greet(devices):
    barrier = pltpu.get_barrier_semaphore()
    for d in devices:
        pl.semaphore_signal(barrier, inc=1, device_id=d, device_id_type=MESH)
    pl.semaphore_wait(barrier, len(devices))

def gather_steps(gu_in, dn_in, wo_in, gu, dn, wo, send, recv, local):
    b, m, c, mx, my, md = places()
    o = 1 - c
    z = lax.rem(b, 2)
    oz = 1 - z
    nx, ny, nc, nz = (b, mx, c), (b, my, c), (b, m, o), (b + 1 - 2 * z, m, c)
    me, it = m * 2 + c, m * 2 + o
    ix, iy, idg = mx * 2 + c, my * 2 + c, md * 2 + c
    jx, jy, jdg = mx * 2 + o, my * 2 + o, md * 2 + o
    def copy(src, dst, n, to):
        return pltpu.make_async_remote_copy(src_ref=src, dst_ref=dst, send_sem=send.at[n], recv_sem=recv.at[n], device_id=to, device_id_type=MESH)
    def push(ref, n, to):
        return copy(ref, ref, n, to)
    def got(ref, n):
        copy(ref, ref, n, nc).wait_recv()
    def first(src, dst, n):
        for t, to in enumerate((nx, ny, nc)):
            copy(src, dst, n + t, to).start()
    def halves(ref, i):
        h = ref.shape[1] // 2
        return ref.at[i, pl.ds(0, h)], ref.at[i, pl.ds(h, h)]
    def second(ref, n, onward=None):
        got(ref.at[ix], n)
        push(halves(ref, ix)[0], n + 3, ny).start()
        push(ref.at[ix], n + 5, nc).start()
        if onward is not None:
            push(ref.at[ix], onward, nz).start()
        got(ref.at[iy], n + 1)
        push(halves(ref, iy)[1], n + 4, nx).start()
        push(ref.at[iy], n + 6, nc).start()
        if onward is not None:
            push(ref.at[iy], onward + 1, nz).start()
    def third(ref, n, onward=None):
        got(halves(ref, idg)[0], n + 3)
        got(halves(ref, idg)[1], n + 4)
        push(ref.at[idg], n + 7, nc).start()
        if onward is not None:
            push(ref.at[idg], onward + 2, nz).start()
    def last(src, ref, n, onward=None):
        for t, i in ((2, it), (5, jx), (6, jy), (7, jdg)):
            got(ref.at[i], n + t)
        for t in (0, 1, 2):
            copy(src, ref.at[me], n + t, nc).wait_send()
        push(halves(ref, ix)[0], n + 3, ny).wait_send()
        push(halves(ref, iy)[1], n + 4, nx).wait_send()
        for t, i in ((5, ix), (6, iy), (7, idg)):
            push(ref.at[i], n + t, nc).wait_send()
        if onward is not None:
            for t, i in enumerate((ix, iy, idg)):
                push(ref.at[i], onward + t, nz).wait_send()
    def part(ref, i):
        cut = ref.shape[-1] // 384 * 128
        return ref.at[..., pl.ds(0, cut)] if i == 0 else ref.at[..., pl.ds(cut, ref.shape[-1] - cut)]
    mine, other = gu.at[z], gu.at[oz]
    m0, m1, o0, o1 = part(mine, 0), part(mine, 1), part(other, 0), part(other, 1)
    in0, in1 = part(gu_in.at[z], 0), part(gu_in.at[z], 1)
    d0, d1, dn0, dn1 = part(dn, 0), part(dn, 1), part(dn_in, 0), part(dn_in, 1)
    keeps = [pltpu.make_async_copy(gu_in.at[0], gu.at[0, me], local.at[0]), pltpu.make_async_copy(gu_in.at[1], gu.at[1, me], local.at[1]),
             pltpu.make_async_copy(dn_in, dn.at[me], local.at[2]), pltpu.make_async_copy(wo_in, wo.at[me], local.at[3])]
    W, D0, D1, G0, G1, Z0, Z1, OWN = 0, 8, 16, 24, 32, 40, 46, 52
    def z_second(ref, n, ts):
        for t in ts:
            i = (ix, iy, idg)[t]
            got(ref.at[i], n + t)
            push(ref.at[i], n + 3 + t, nc).start()
    def begin():
        first(in0, m0.at[me], G0)
        first(in1, m1.at[me], G1)
        copy(gu_in.at[oz], other.at[me], OWN, nc).start()
        for k in keeps:
            k.start()
    def at0():
        second(m0, G0, Z0)
        first(wo_in, wo.at[me], W)
    def at2():
        second(m1, G1, Z1)
        third(m0, G0, Z0)
        first(dn0, d0.at[me], D0)
    def at3():
        second(wo, W)
        first(dn1, d1.at[me], D1)
    def at4():
        third(m1, G1, Z1)
        z_second(o0, Z0, (0, 1))
    def at6():
        second(d0, D0)
        third(wo, W)
    def end():
        z_second(o1, Z1, (0, 1))
        z_second(o0, Z0, (2,))
        third(d0, D0)
        second(d1, D1)
        third(d1, D1)
        z_second(o1, Z1, (2,))
        last(wo_in, wo, W)
        last(in0, m0, G0, Z0)
        last(in1, m1, G1, Z1)
        got(other.at[it], OWN)
        copy(gu_in.at[oz], other.at[me], OWN, nc).wait_send()
        for ref, n in ((o0, Z0), (o1, Z1)):
            for t, i, j in ((0, ix, jx), (1, iy, jy), (2, idg, jdg)):
                got(ref.at[j], n + 3 + t)
                push(ref.at[i], n + 3 + t, nc).wait_send()
        last(dn0, d0, D0)
        last(dn1, d1, D1)
        for k in keeps:
            k.wait()
    return begin, {1: at0, 3: at2, 4: at3, 5: at4, 7: at6}, end


def bias_consts():
    y = np.arange(512)
    y = np.where(y >= 128, y - 512, y)
    ids = bucket_np(-128 - y)
    out = np.zeros((128, 1280), np.float32)
    for a in range(2):
        out[32 * a + ids, 512 * a + np.arange(512)] = 1
        out[32 * a + 15, 1024 + a:1152:2] = 1
        out[32 * a + 31, 1152 + a:1280:2] = 1
    return jnp.asarray(out, bf)

def mask_block(kind, text):
    pos = lax.broadcasted_iota(jnp.int32, (L, 128), 0)
    tile = lax.broadcasted_iota(jnp.int32, (L, 128), 1) // 2
    seg = jnp.where(kind == 1, pos // 384, 0)
    mine = jnp.where(kind == 1, tile // 3, 0)
    length = jnp.where(seg == 0, text[0], jnp.where(seg == 1, text[1], text[2]))
    live = pos - seg * 384 < jnp.where(kind == 1, 256, 1024) + length
    return jnp.where(live & (seg == mine), 0.0, NEG)

def front_kernel(kind_ref, text_ref, x_ref, gain1_ref, gain2_ref, table_ref, wq_ref, wk_ref, wv_ref, gate_ref, up_ref, dn_in, wo_in, const_ref,
                 o_ref, e_ref, r_ref, n_ref, qkv_out, w_out, gu, dn, wo,
                 W, acc, rstd, qkv, gu_in, mask, rhs, kaug, vaug, bn, s_ref, wsend, wrecv, wlocal, send, recv, local):
    b, m, c, mx, my, md = places()
    o = 1 - c
    nx, ny, nc, nz = (b, mx, c), (b, my, c), (b, m, o), (b + 1 - 2 * lax.rem(b, 2), m, c)
    d = wq_ref.shape[1]
    rows = wq_ref.shape[0]
    half = rows // 2
    me = m * 2 + c
    p = pl.program_id(0)
    begin, during, end = gather_steps(gu_in, dn_in, wo_in, gu, dn, wo, send, recv, local)
    keeps = (pltpu.make_async_copy(W, w_out, wlocal.at[0]), pltpu.make_async_copy(qkv, qkv_out, wlocal.at[1]))
    def push(src, n, to):
        return pltpu.make_async_remote_copy(src_ref=src, dst_ref=src, send_sem=wsend.at[n], recv_sem=wrecv.at[n], device_id=to, device_id_type=MESH)
    def got(ref, n):
        push(ref, n, nc).wait_recv()
    def chunk(j, first):
        cols = pl.ds(pl.multiple_of(j * 2 * rows, 2 * rows), 2 * rows)
        gain = jnp.concatenate([W[2 * j, 0:1, 3 * d:3 * d + rows], W[2 * j + 1, 0:1, 3 * d:3 * d + rows]], 1).astype(f32)
        n = (x_ref[:, cols].astype(f32) * rstd[...] * gain).astype(bf)
        n_ref[:, cols] = n
        for t in range(3):
            y = dot(n, W[pl.ds(2 * j, 2), :, t * d:t * d + d].reshape(2 * rows, d))
            if first:
                acc[:, t * d:t * d + d] = y
            else:
                acc[:, t * d:t * d + d] = acc[:, t * d:t * d + d] + y
    @pl.when(p == 0)
    def _():
        W[me, :, 0:d] = wq_ref[...]
        W[me, :, d:2 * d] = wk_ref[...]
        W[me, :, 2 * d:3 * d] = wv_ref[...]
        W[me, :, 3 * d:3 * d + 128] = jnp.zeros((rows, 128), bf)
        W[me, 0:1, 3 * d:3 * d + rows] = gain1_ref[...]
        W[me, 1:2, 3 * d:3 * d + rows] = gain2_ref[...]
        W[me, 2:3, 3 * d:3 * d + table_ref.shape[1]] = table_ref[...]
        greet([nx, ny, nc, nz])
        top, low = pl.ds(0, half), pl.ds(half, half)
        sends = [push(W.at[me], 0, nx), push(W.at[me], 1, ny), push(W.at[me], 2, nc)]
        for s in sends:
            s.start()
        gu_in[0] = gate_ref[...]
        gu_in[1] = up_ref[...]
        for t in range(0, L, 384):
            x = x_ref[t:t + 384, :].astype(f32)
            rstd[t:t + 384, :] = lax.rsqrt(jnp.mean(x * x, axis=-1, keepdims=True) + EPS)
        mask[...] = mask_block(kind_ref[0], (text_ref[0, 0], text_ref[0, 1], text_ref[0, 2]))
        fwd_open(rhs, vaug)
        ix, iy, idg = mx * 2 + c, my * 2 + c, md * 2 + c
        jx, jy, jdg = mx * 2 + o, my * 2 + o, md * 2 + o
        got(W.at[m * 2 + o], 2)
        chunk(m, True)
        got(W.at[ix], 0)
        more = [push(W.at[ix, top], 3, ny), push(W.at[ix], 5, nc)]
        got(W.at[iy], 1)
        more += [push(W.at[iy, low], 4, nx), push(W.at[iy], 6, nc)]
        for s in more:
            s.start()
        begin()
        got(W.at[jx], 5)
        chunk(mx, False)
        got(W.at[jy], 6)
        chunk(my, False)
        got(W.at[idg, top], 3)
        got(W.at[idg, low], 4)
        more.append(push(W.at[idg], 7, nc))
        more[-1].start()
        got(W.at[jdg], 7)
        keeps[0].start()
        chunk(md, False)
        for t in range(3 * d // 128):
            qkv[t] = acc[:, 128 * t:128 * t + 128].astype(bf)
        keeps[1].start()
        for s in sends + more:
            s.wait_send()
    for at, act in during.items():
        pl.when(p == at)(act)
    @pl.when(p > 0)
    def _():
        h = p - 1
        N = d // 128
        values = jnp.broadcast_to(W[h, 2:3, 3 * d:3 * d + 128], (16, 128))
        bias = dot(values, const_ref[...])
        fwd_pair(qkv[h], qkv[N + h], qkv[2 * N + h], mask[...], bias[0:1, 1024:1152], bias[0:1, 1152:1280],
                 jnp.concatenate([bias[0:1, 0:512], bias[0:1, 512:1024]], 0), o_ref, e_ref, r_ref, rhs, kaug, vaug, bn, s_ref)
    @pl.when(p == pl.num_programs(0) - 1)
    def _():
        end()
        for k in keeps:
            k.wait()

def front(kind, text, x, gain1, gain2, table, wq, wk, wv, gate, up, dn, wo):
    R, d = x.shape
    rows = wq.shape[0]
    N = d // 128
    at = lambda p: jnp.maximum(p - 1, 0)
    spec = pl.BlockSpec((R, 128), lambda p: (0, at(p)))
    hbm = pl.BlockSpec(memory_space=pl.ANY)
    whole = lambda a: pl.BlockSpec(a.shape, lambda p: (0,) * a.ndim, pipeline_mode=pl.Buffered(1))
    smem = pl.BlockSpec(memory_space=pltpu.SMEM)
    sds = jax.ShapeDtypeStruct
    dma = pltpu.SemaphoreType.DMA
    row = lambda a: a.reshape(1, -1)
    vectors = (x, row(gain1), row(gain2), row(table), wq, wk, wv, gate, up, dn, wo, bias_consts())
    wide = 3 * d + 128
    return pl.pallas_call(front_kernel, grid=(1 + N,),
        in_specs=[smem, smem] + [whole(a) for a in vectors],
        out_specs=[spec, pl.BlockSpec((None, None, R, NT * 256), lambda p: (0, at(p), 0, 0)), spec,
                   pl.BlockSpec((R, d), lambda p: (0, 0), pipeline_mode=pl.Buffered(1))] + [hbm] * 5,
        out_shape=[sds((R, d), bf), sds((1, N, R, NT * 256), bf), sds((R, d), f32), sds((R, d), bf), sds((3 * N, R, 128), bf),
                   sds((8, rows, wide), bf), sds((2, 8) + gate.shape, bf), sds((8,) + dn.shape, bf), sds((8,) + wo.shape, bf)],
        scratch_shapes=[pltpu.VMEM((8, rows, wide), bf), pltpu.VMEM((R, 3 * d), f32), pltpu.VMEM((R, 1), f32), pltpu.VMEM((3 * N, R, 128), bf),
                        pltpu.VMEM((2,) + gate.shape, bf), pltpu.VMEM((R, 128), f32),
                        pltpu.VMEM((256, NT * 256), bf), pltpu.VMEM((R, 256), bf), pltpu.VMEM((R, 256), bf), pltpu.VMEM((384, 256), f32), pltpu.VMEM((2, R, 256), f32),
                        dma((8,)), dma((8,)), dma((2,)), dma((53,)), dma((53,)), dma((4,))],
        compiler_params=pltpu.CompilerParams(collective_id=1, has_side_effects=True, vmem_limit_bytes=63 * 2**20),
        name="front")(kind, text, *vectors)

DRAIN = 6

def plane_scratch(rows, cols):
    h = rows // 2
    pair = pltpu.VMEM((2, 2, h, cols), bf)
    single = pltpu.VMEM((2, h, cols), bf)
    dma = pltpu.SemaphoreType.DMA
    return [pltpu.VMEM((2, 4, 2, rows, cols), bf), pltpu.VMEM((2, 4, rows, cols), bf)] + [pair] * 6 + [single] * 2 + [dma((5, 2)), dma((5, 2))]

def z_scratch(n, rows, cols):
    ring = lambda k: pltpu.VMEM((k, rows, cols), bf)
    dma = pltpu.SemaphoreType.DMA
    return [ring(4), ring(4), ring(2), ring(n), dma((3, n)), dma((3, n))]

def plus(a, b):
    return a + b

def rs_greet():
    b, m, c, mx, my, md = places()
    greet([(b, mx, c), (b, my, c), (b, m, 1 - c), (b + 1 - 2 * lax.rem(b, 2), m, c), (3 - b, m, c)])

def stage(t, n, act, also=None):
    live = (t >= 0) & (t < n)
    pl.when(live if also is None else live & also)(lambda: act(t))

def plane_step(s, n, bufs, put):
    src, cbuf, sx, sy, kt, kb, xt, yb, t2, b2, send, recv = bufs
    b, m, c, mx, my, md = places()
    o = 1 - c
    nx, ny, nc = (b, mx, c), (b, my, c), (b, m, o)
    h = kt.shape[2]
    def copy(kind, k, a, z, to):
        return pltpu.make_async_remote_copy(src_ref=a, dst_ref=z, send_sem=send.at[kind, k], recv_sem=recv.at[kind, k], device_id=to, device_id_type=MESH)
    core = lambda k: copy(0, k, src.at[k, :, o], cbuf.at[k], nc)
    x1 = lambda k: copy(1, k, sx.at[k], xt.at[k], nx)
    y1 = lambda k: copy(2, k, sy.at[k], yb.at[k], ny)
    y2 = lambda k: copy(3, k, kt.at[k, 1], t2.at[k], ny)
    x2 = lambda k: copy(4, k, kb.at[k, 1], b2.at[k], nx)
    def third(t):
        k = lax.rem(t, 2)
        y2(k).wait()
        x2(k).wait()
        put(t, plus(kt[k, 0], t2[k]), plus(kb[k, 0], b2[k]))
    def second(t):
        k = lax.rem(t, 2)
        x1(k).wait()
        y1(k).wait()
        kt[k] = plus(kt[k], xt[k])
        kb[k] = plus(kb[k], yb[k])
        y2(k).start()
        x2(k).start()
    def first(t):
        k = lax.rem(t, 2)
        core(k).wait()
        top = lambda i: plus(src[k, i, c, 0:h], cbuf[k, i, 0:h])
        low = lambda i: plus(src[k, i, c, h:2 * h], cbuf[k, i, h:2 * h])
        sx[k, 0], sx[k, 1] = top(mx), top(md)
        sy[k, 0], sy[k, 1] = low(my), low(md)
        x1(k).start()
        y1(k).start()
        kt[k, 0], kt[k, 1] = top(m), top(my)
        kb[k, 0], kb[k, 1] = low(m), low(mx)
    stage(s - 3, n, third)
    stage(s - 2, n, second)
    stage(s - 1, n, first)
    stage(s, n, lambda t: core(lax.rem(t, 2)).start())

def z_step(s, n, bufs, before):
    part, inward, across, done, send, recv = bufs
    b, m, c, mx, my, md = places()
    nz, na = (b + 1 - 2 * lax.rem(b, 2), m, c), (3 - b, m, c)
    outer = (b == 0) | (b == 3)
    inner = (b == 1) | (b == 2)
    def copy(kind, t, a, z, to):
        return pltpu.make_async_remote_copy(src_ref=a, dst_ref=z, send_sem=send.at[kind, t], recv_sem=recv.at[kind, t], device_id=to, device_id_type=MESH)
    up = lambda t: copy(0, t, part.at[lax.rem(t, 4)], inward.at[lax.rem(t, 4)], nz)
    over = lambda t: copy(1, t, part.at[lax.rem(t, 4)], across.at[lax.rem(t, 2)], na)
    down = lambda t: copy(2, t, done.at[t], done.at[t], nz)
    def outer_done(t):
        up(t).wait_send()
        down(t).wait_recv()
    def inner_done(t):
        down(t).wait_send()
    def inner_sum(t):
        over(t).wait()
        done[t] = plus(part[lax.rem(t, 4)], across[lax.rem(t, 2)])
        down(t).start()
    def inner_part(t):
        up(t).wait_recv()
        part[lax.rem(t, 4)] = plus(part[lax.rem(t, 4)], inward[lax.rem(t, 4)])
        over(t).start()
    stage(s - 3, n, outer_done, outer)
    stage(s - 3, n, inner_done, inner)
    stage(s - 2, n, inner_sum, inner)
    stage(s - 1, n, inner_part, inner)
    before()
    stage(s, n, lambda t: up(t).start(), outer)

def sum_step(s, n, plane, z):
    h = plane[4].shape[2]
    part = z[0]
    def put(t, top, low):
        part[lax.rem(t, 4), 0:h] = top
        part[lax.rem(t, 4), h:2 * h] = low
    z_step(s - 3, n, z, lambda: plane_step(s, n, plane, put))

GELU_C = float(np.sqrt(2.0 / np.pi))
def dot_nt(a, b):
    return lax.dot_general(a, b, (((1,), (1,)), ((), ())), preferred_element_type=f32)

def ffn_open(x_ref, ctx_ref, gain_ref, wo_ref, gres_ref, res, n, acc):
    for t in range(0, x_ref.shape[0], 384):
        s = slice(t, t + 384)
        y = x_ref[s, :].astype(f32) + dot(ctx_ref[s, :], wo_ref[...])
        res[s, :] = y
        acc[s, :] = y
        n[s, :] = (y * lax.rsqrt(jnp.mean(y * y, axis=-1, keepdims=True) + EPS) * gain_ref[0:1, :]).astype(bf)
    gres_ref[...] = jnp.zeros_like(gres_ref)

def ffn_block(g_ref, gu_ref, dn_ref, gres_ref, ddn_ref, n, acc):
    d = n.shape[1]
    wg = gu_ref[0].reshape(d, gu_ref.shape[-1])
    wu = gu_ref[1].reshape(d, gu_ref.shape[-1])
    wd = dn_ref[...]
    nn = n[...]
    g = g_ref[...]
    v = dot(nn, wg)
    u = dot(nn, wu)
    gh = dot_nt(g, wd)
    v2 = v * v
    th = jnp.tanh(GELU_C * v * (1.0 + 0.044715 * v2))
    half = 0.5 * (1.0 + th)
    gel = v * half
    h = (gel * u).astype(bf)
    dgel = half + 0.5 * v * (1.0 - th * th) * (GELU_C * (1.0 + 3 * 0.044715 * v2))
    gg = (gh * u * dgel).astype(bf)
    gu = (gh * gel).astype(bf)
    acc[...] = acc[...] + dot(h, wd)
    gres_ref[...] = gres_ref[...] + dot_nt(jnp.concatenate([gg, gu], 1), jnp.concatenate([wg, wu], 1))
    ddn_ref[...] = dot_tl(h, g).astype(bf)
    return dot_tl(nn, gg).astype(bf), dot_tl(nn, gu).astype(bf)

def ffn_close(s, g_ref, gain_ref, wo_ref, out_ref, gres_ref, gctx_ref, res, n, acc):
    out_ref[s, :] = acc[s, :].astype(bf)
    y = res[s, :]
    r = lax.rsqrt(jnp.mean(y * y, axis=-1, keepdims=True) + EPS)
    m = y * r
    gn = gres_ref[s, :]
    w = gn * gain_ref[0:1, :]
    gr = g_ref[s, :].astype(f32) + r * (w - m * jnp.mean(w * m, axis=-1, keepdims=True))
    gres_ref[s, :] = gr
    low = gr.astype(bf)
    n[s, :] = low
    gctx_ref[s, :] = dot_nt(low, wo_ref[...]).astype(bf)
    return jnp.sum(gn * m, axis=0, keepdims=True)

def ffn_kernel(x_ref, ctx_ref, g_ref, gain_ref, wo_ref, gu_ref, dn_ref,
               out_ref, gres_ref, gctx_ref, dwo_ref, ggain_ref, ddn_ref, dgu_ref, res, n, acc):
    j = pl.program_id(0)
    @pl.when(j == 0)
    def _():
        ffn_open(x_ref, ctx_ref, gain_ref, wo_ref, gres_ref, res, n, acc)
    a, b = ffn_block(g_ref, gu_ref, dn_ref, gres_ref, ddn_ref, n, acc)
    dgu_ref[0] = a.reshape(dgu_ref.shape[1:])
    dgu_ref[1] = b.reshape(dgu_ref.shape[1:])
    @pl.when(j == pl.num_programs(0) - 1)
    def _():
        R = x_ref.shape[0]
        total = sum(ffn_close(slice(t, t + 384), g_ref, gain_ref, wo_ref, out_ref, gres_ref, gctx_ref, res, n, acc) for t in range(0, R, 384))
        ggain_ref[...] = jnp.broadcast_to(total, ggain_ref.shape)
        dwo_ref[...] = dot_tl(ctx_ref[...], n[...]).astype(bf)

def ffn_sum_kernel(x_ref, ctx_ref, g_ref, gain_ref, wo_ref, gu_ref, dn_ref,
                   out_ref, gres_ref, gctx_ref, dwo_ref, ggain_ref, ddn_ref, dgu_ref, res, n, acc, *bufs):
    j = pl.program_id(0)
    N = pl.num_programs(0) - 3
    src = bufs[0]
    @pl.when(j == 0)
    def _():
        rs_greet()
        ffn_open(x_ref, ctx_ref, gain_ref, wo_ref, gres_ref, res, n, acc)
        ggain_ref[...] = jnp.zeros_like(ggain_ref)
    @pl.when(j < N)
    def _():
        a, b = ffn_block(g_ref, gu_ref, dn_ref, gres_ref, ddn_ref, n, acc)
        k = lax.rem(j, 2)
        rows = a.shape[0] // 8
        src[k, :, :, 0:rows] = a.reshape(4, 2, rows, a.shape[1])
        src[k, :, :, rows:2 * rows] = b.reshape(4, 2, rows, a.shape[1])
    @pl.when(j >= N)
    def _():
        part = x_ref.shape[0] // 3
        s = pl.ds(pl.multiple_of((j - N) * part, part), part)
        total = ffn_close(s, g_ref, gain_ref, wo_ref, out_ref, gres_ref, gctx_ref, res, n, acc)
        ggain_ref[...] = ggain_ref[...] + jnp.broadcast_to(total, ggain_ref.shape)
    h = dgu_ref.shape[1] // 2
    plane, z = bufs[:12], bufs[12:]
    ahead = z[3].shape[0]
    def put(t, top, low):
        @pl.when(t < ahead)
        def _():
            z[0][lax.rem(t, 4), 0:h] = top
            z[0][lax.rem(t, 4), h:2 * h] = low
        @pl.when(t >= ahead)
        def _():
            dgu_ref[t, 0:h] = top
            dgu_ref[t, h:2 * h] = low
    z_step(j - 3, ahead, z, lambda: plane_step(j, N, plane, put))
    @pl.when(j == N + 2)
    def _():
        dwo_ref[...] = dot_tl(ctx_ref[...], n[...]).astype(bf)
        dgu_ref[0:ahead] = z[3][...]

def ffn(x, ctx, g, gain, wo, gu, dn, near, block=256):
    R, d = x.shape
    F = dn.shape[0]
    k = gu.shape[1]
    N = F // block
    sds = jax.ShapeDtypeStruct
    one = lambda *s: pl.BlockSpec(s, lambda j: (0,) * len(s), pipeline_mode=pl.Buffered(1))
    at = lambda j: jnp.minimum(j, N - 1)
    gub = pl.BlockSpec((2, k, d // k, block), lambda j: (0, 0, 0, at(j)))
    dnb = pl.BlockSpec((block, d), lambda j: (at(j), 0))
    rows = 2 * (d // k)
    if near:
        body, extra, steps, last = ffn_sum_kernel, plane_scratch(rows, block) + z_scratch(N - 3, rows, block), N + 3, (one(N, rows, block), sds((N, rows, block), bf))
        params = pltpu.CompilerParams(vmem_limit_bytes=61 * 2**20, collective_id=3, has_side_effects=True)
    else:
        body, extra, steps, last = ffn_kernel, [], N, (gub, sds(gu.shape, bf))
        params = pltpu.CompilerParams(vmem_limit_bytes=61 * 2**20)
    return pl.pallas_call(body, grid=(steps,),
        in_specs=[one(R, d), one(R, d), one(R, d), one(1, d), one(d, d), gub, dnb],
        out_specs=[one(R, d), one(R, d), one(R, d), one(d, d), one(8, d), dnb, last[0]],
        out_shape=[sds((R, d), bf), sds((R, d), f32), sds((R, d), bf), sds((d, d), bf), sds((8, d), f32), sds(dn.shape, bf), last[1]],
        scratch_shapes=[pltpu.VMEM((R, d), f32), pltpu.VMEM((R, d), bf), pltpu.VMEM((R, d), f32)] + extra,
        compiler_params=params, name="ffn")(x, ctx, g, gain, wo, gu, dn)

def sum_rounds(s, box, inbox, send, recv):
    b, m, c, mx, my, md = places()
    peers = [(b, m, 1 - c), (b, mx, c), (b, my, c), (b + 1 - 2 * lax.rem(b, 2), m, c), (3 - b, m, c)]
    def copy(r):
        return pltpu.make_async_remote_copy(src_ref=box.at[r], dst_ref=inbox.at[r], send_sem=send.at[r], recv_sem=recv.at[r], device_id=peers[r], device_id_type=MESH)
    for r in range(5):
        @pl.when(s == r)
        def _():
            copy(r).start()
        @pl.when(s == r + 1)
        def _():
            copy(r).wait()
            box[r + 1] = box[r] + inbox[r]

def bwd_sum_kernel(q_ref, k_ref, v_ref, do_ref, o_ref, r_ref, e_ref, n_ref, x_ref, gres_ref, gain_ref, wq_ref, wk_ref, wv_ref, dn_ref, wo_ref, gain2_ref, gu_ref, const_ref,
                   gtok_ref, small_ref, out_a, out_b, out_c, rhs, vaug, dobd, qaug, ds_ref, nacc, near_ref, far_ref, ggain, tab, g_all, box, inbox, ssend, srecv, osem, *bufs):
    p = pl.program_id(0)
    N = pl.num_programs(0) - DRAIN
    plane_a, z_a, plane_b, z_b, z_c = bufs[0:12], bufs[12:18], bufs[18:30], bufs[30:36], bufs[36:42]
    src_a, src_b = plane_a[0], plane_b[0]
    done_a, done_b, done_c = z_a[3], z_b[3], z_c[3]
    NA, NC = done_a.shape[0], done_c.shape[0]
    d = gtok_ref.shape[1]
    k = lax.rem(p, 2)
    def put(src, arrays):
        h = src.shape[3] // 2
        at = 0
        for a in arrays:
            r = a.shape[1] // 2
            a = a.reshape((4, 2) + a.shape[1:])
            src[k, :, :, at:at + r] = a[:, :, 0:r]
            src[k, :, :, h + at:h + at + r] = a[:, :, r:2 * r]
            at += r
    @pl.when(p == 0)
    def _():
        rs_greet()
        bwd_open(rhs, vaug, qaug)
        gtok_ref[...] = jnp.zeros_like(gtok_ref)
        ggain[...] = jnp.zeros_like(ggain)
    @pl.when(p < NA)
    def _():
        put(src_a, (dn_ref[...], wo_ref[...]))
    sum_step(p, NA, plane_a, z_a)
    @pl.when(p < N)
    def _():
        g = jnp.concatenate(bwd_pair(q_ref, k_ref, v_ref, do_ref, o_ref, r_ref, e_ref, near_ref, far_ref, rhs, vaug, dobd, qaug, ds_ref, nacc), 1)
        lane = lax.broadcasted_iota(jnp.int32, (1, 128), 1)
        sums = jnp.dot(near_ref[...], const_ref[...], precision=lax.Precision.HIGHEST, preferred_element_type=f32)
        for a in range(2):
            lo, hi = (jnp.sum(jnp.where(lax.rem(lane, 2) == a, far_ref[i:i + 1, :], 0.0), axis=1, keepdims=True) for i in range(2))
            tab[p, a:a + 1, :] = sums[a:a + 1, :] + jnp.where(lane == 15, lo, 0.0) + jnp.where(lane == 31, hi, 0.0)
        g_all[p] = g
        gw = dot_tl(n_ref[...], g)
        half = pl.ds(pl.multiple_of(lax.rem(p, 2) * 128, 128), 128)
        w = jnp.concatenate([w_ref[:, :, half].reshape(d, 128) for w_ref in (wq_ref, wk_ref, wv_ref)], 1)
        ggain[...] = ggain[...] + sum((gw * w.astype(f32))[:, 128 * t:128 * t + 128] for t in range(3))
        gw = gw.astype(bf)
        put(src_b, [gw[:, 128 * t:128 * t + 128].reshape(8, d // 8, 128) for t in range(3)])
    @pl.when((p >= N) & (p < N + N // 2))
    def _():
        i = 2 * (p - N)
        g = jnp.concatenate([g_all[i], g_all[i + 1]], 1)
        w = jnp.concatenate([w_ref[:, :, 128 * t:128 * t + 128].reshape(d, 128) for t in range(2) for w_ref in (wq_ref, wk_ref, wv_ref)], 1)
        gtok_ref[...] = gtok_ref[...] + dot_nt(g, w)
    @pl.when(p >= N + N // 2)
    def _():
        rows = x_ref.shape[0]
        step = rows // 3
        for t in range(3):
            s = pl.ds(pl.multiple_of((p - N - N // 2) * rows + t * step, step), step)
            x = x_ref[t * step:t * step + step, :].astype(f32)
            r = lax.rsqrt(jnp.mean(x * x, axis=-1, keepdims=True) + EPS)
            m = x * r
            w = gtok_ref[s, :] * gain_ref[0:1, :]
            gtok_ref[s, :] = gres_ref[t * step:t * step + step, :] + r * (w - m * jnp.mean(w * m, axis=-1, keepdims=True))
    @pl.when(p == N - 1)
    def _():
        for t in range(N):
            box[0, 2 * t:2 * t + 2] = tab[t, 0:2]
        w = d // 8
        one = jnp.sum(ggain[...].T, axis=0, keepdims=True) / gain_ref[0:1, :]
        for t in range(8):
            box[0, 2 * N + t:2 * N + t + 1] = one[:, w * t:w * t + w]
            box[0, 2 * N + 8 + t:2 * N + 9 + t] = gain2_ref[0:1, w * t:w * t + w]
    sum_rounds(p - N + 1, box, inbox, ssend, srecv)
    sum_step(p, N, plane_b, z_b)
    def take():
        @pl.when(p < NC)
        def _():
            z_c[0][lax.rem(p, 4)] = gu_ref[...]
    z_step(p, NC, z_c, take)
    @pl.when(p == N + DRAIN - 1)
    def _():
        small_ref[...] = box[5]
        keeps = [pltpu.make_async_copy(a, o, osem.at[i]) for i, (a, o) in enumerate(((done_a, out_a), (done_b, out_b), (done_c, out_c)))]
        for copy in keeps:
            copy.start()
        for copy in keeps:
            copy.wait()

def attn_bwd_sum(qkv, do, o, r, e, n, x, gres, gain, qkv_w, dn, wo, gain2, gu):
    R, d = x.shape
    N = d // 128
    NA, wide = N, 128
    rows_a, rows_b = dn.shape[1] + wo.shape[1], 3 * (d // 8)
    sds = jax.ShapeDtypeStruct
    at = lambda p: jnp.minimum(p, N - 1)
    after = lambda p: jnp.clip(p - N - N // 2, 0, 1)
    spec = pl.BlockSpec((R, 128), lambda p: (0, at(p)))
    head = lambda t: pl.BlockSpec((None, R, 128), lambda p: (t * N + at(p), 0, 0))
    one = lambda *s: pl.BlockSpec(s, lambda p: (0,) * len(s), pipeline_mode=pl.Buffered(1))
    part = pl.BlockSpec((R // 2, d), lambda p: (after(p), 0), pipeline_mode=pl.Buffered(1))
    cols = lambda a, t: pl.BlockSpec((8, a.shape[1], 256), lambda p: (0, 0, t * (N // 2) + jnp.where(p < N, p // 2, jnp.minimum(p - N, N // 2 - 1))))
    early = lambda a: pl.BlockSpec((8, a.shape[1], wide), lambda p: (0, 0, jnp.minimum(p, NA - 1)), pipeline_mode=pl.Buffered(1))
    hbm = pl.BlockSpec(memory_space=pl.ANY)
    dma = pltpu.SemaphoreType.DMA
    small = (2 * N + 16, d // 8)
    NC = 3
    left = gu.shape[0] - NC
    rest = (NC,) + gu.shape[1:]
    to_bucket = jnp.asarray((bucket_np(np.arange(512) - 255)[:, None] == np.arange(128)[None, :]).astype(np.float32))
    return pl.pallas_call(bwd_sum_kernel, grid=(N + DRAIN,),
        in_specs=[head(0), head(1), head(2)] + [spec] * 3 + [pl.BlockSpec((None, None, R, NT * 256), lambda p: (0, at(p), 0, 0)), one(R, d), part, part, one(1, d),
                  cols(qkv_w, 0), cols(qkv_w, 1), cols(qkv_w, 2), early(dn), early(wo), one(8, d),
                  pl.BlockSpec((None,) + gu.shape[1:], lambda p: (left + jnp.minimum(p, NC - 1), 0, 0)), one(512, 128)],
        out_specs=[one(R, d), one(*small), hbm, hbm, hbm],
        out_shape=[sds((R, d), f32), sds(small, f32), sds((NA, rows_a, wide), bf), sds((N, rows_b, 128), bf), sds(rest, bf)],
        scratch_shapes=[pltpu.VMEM((256, NT * 256), bf), pltpu.VMEM((R, 256), bf), pltpu.VMEM((NT * 256, 128), bf), pltpu.VMEM((NT * 256, 256), bf), pltpu.VMEM((R, NT * 256), bf), pltpu.VMEM((384, 256), f32),
                        pltpu.VMEM((8, 512), f32), pltpu.VMEM((8, 128), f32), pltpu.VMEM((d, 128), f32), pltpu.VMEM((N, 8, 128), f32), pltpu.VMEM((N, R, 384), bf), pltpu.VMEM((6,) + small, f32), pltpu.VMEM((5,) + small, f32), dma((5,)), dma((5,)), dma((3,))]
                       + plane_scratch(rows_a, wide) + z_scratch(NA, rows_a, wide) + plane_scratch(rows_b, 128) + z_scratch(N, rows_b, 128) + z_scratch(*rest),
        compiler_params=pltpu.CompilerParams(vmem_limit_bytes=63 * 2**20, collective_id=4, has_side_effects=True), name="attn_bwd_sum")(
            qkv, qkv, qkv, do, o, r, e, n, x, gres, gain, qkv_w, qkv_w, qkv_w, dn, wo, gain2, gu, to_bucket)

def finish_kernel(gtok_in, out_in, a_in, b_in, c_in, d_in, small_in, at_ref, gtok, out, q, k, v, wo, gate, up, dn, gain1, gain2, table):
    gtok[...] = gtok_in[...]
    out[...] = out_in[...]
    @pl.when(pl.program_id(0) == 0)
    def _():
        def spread(src, targets):
            n, h, w = src.shape[0], src.shape[1] // 2, src.shape[2]
            for t in range(n):
                at = 0
                for ref in targets:
                    r = ref.shape[0] // 2
                    ref[0:r, w * t:w * t + w] = src[t, at:at + r].astype(f32)
                    ref[r:2 * r, w * t:w * t + w] = src[t, h + at:h + at + r].astype(f32)
                    at += r
        spread(a_in, (dn, wo))
        spread(b_in, (q, k, v))
        r = gate.shape[0]
        w = c_in.shape[2]
        left = c_in.shape[0] - d_in.shape[0]
        for t in range(c_in.shape[0]):
            both = c_in[t] if t < left else d_in[t - left]
            gate[:, w * t:w * t + w] = both[0:r].astype(f32)
            up[:, w * t:w * t + w] = both[r:2 * r].astype(f32)
        me = at_ref[0]
        heads = small_in.shape[0] - 16
        per = heads // 8
        gain1[...] = small_in[pl.ds(heads + me, 1), :]
        gain2[...] = small_in[pl.ds(heads + 8 + me, 1), :]
        table[...] = small_in[pl.ds(per * me, per), :]

def finish(gtok, out, a, b, c, last, small, at, rows, ff):
    R, d = gtok.shape
    steps = 8
    sds = jax.ShapeDtypeStruct
    block = pl.BlockSpec((R // steps, d), lambda i: (i, 0))
    one = lambda *s: pl.BlockSpec(s, lambda i: (0,) * len(s), pipeline_mode=pl.Buffered(1))
    whole = lambda x: one(*x.shape)
    shapes = [(rows, d)] * 4 + [(rows, ff)] * 2 + [(ff // 8, d), (1, d // 8), (1, d // 8), ((small.shape[0] - 16) // 8, d // 8)]
    return pl.pallas_call(finish_kernel, grid=(steps,),
        in_specs=[block, block, whole(a), whole(b), whole(c), whole(last), whole(small), pl.BlockSpec(memory_space=pltpu.SMEM)],
        out_specs=[block, block] + [one(*s) for s in shapes],
        out_shape=[sds((R, d), f32), sds((R, d), bf)] + [sds(s, f32) for s in shapes],
        compiler_params=pltpu.CompilerParams(vmem_limit_bytes=62 * 2**20), name="finish")(gtok, out, a, b, c, last, small, at)

def contract_rows(left, right):
    return lax.dot_general(left, right, (((0,), (0,)), ((), ())), preferred_element_type=f32)

def contract_cols(left, right):
    return lax.dot_general(left, right, (((1,), (1,)), ((), ())), preferred_element_type=f32)

def rms_norm(inputs, gain):
    return inputs * lax.rsqrt(jnp.mean(inputs * inputs, axis=-1, keepdims=True) + EPS) * gain

def gather(x):
    return lax.all_gather(x, SHARD, axis=0, tiled=False)

def scatter(x):
    return lax.psum_scatter(x, SHARD, scatter_dimension=0, tiled=True)

def per_device(near, tokens, row_kind, text_length, gain_attn, position_bias_table, weight_query, weight_key, weight_value, weight_out, gain_ffn, weight_gate, weight_up, weight_down, cotangent):
    n1, d = weight_query.shape
    n2 = position_bias_table.shape[0]
    inputs = tokens.astype(f32)
    at = lax.axis_index("dp") * lax.axis_size("narrow") + lax.axis_index("narrow")
    if near:
        context, e, r, normed, qkv, qkv_w, gu_w, down_w, out_w = front(
            row_kind, text_length, tokens, gain_attn, gain_ffn, position_bias_table, weight_query, weight_key, weight_value, weight_gate, weight_up, weight_down, weight_out)
        small = qkv_w[:, 0:2, 3 * d:3 * d + n1]
        gain_one, gain_two = small[:, 0].reshape(d).astype(f32), small[:, 1].reshape(d).astype(f32)
    else:
        small = gather(jnp.stack([gain_attn, gain_ffn, jnp.pad(position_bias_table, (0, n1 - n2))]))
        qkv_w = gather(jnp.concatenate([weight_query, weight_key, weight_value], 1))
        gain_one, gain_two = small[:, 0].reshape(d).astype(f32), small[:, 1].reshape(d).astype(f32)
        normed = rms_norm(inputs, gain_one).astype(bf)
        q, k, v = (dot(normed, qkv_w[:, :, t * d:t * d + d].reshape(d, d)).astype(bf) for t in range(3))
        far, w = tables(small[:, 2, :n2].reshape(-1))
        context, e, r = attn_fwd(q, k, v, mask_cols(row_kind, text_length), far, w)
        gu_w, down_w, out_w = jnp.moveaxis(gather(jnp.stack([weight_gate, weight_up])), 0, 1), gather(weight_down), gather(weight_out)
    ff = gu_w.shape[-1]
    output, grad_residual, grad_context, grad_out_w, g_gain_two, ddn, dgu = ffn(
        tokens, context, cotangent, gain_two.reshape(1, d), out_w.reshape(d, d), gu_w, down_w.reshape(ff, d), near)
    if near:
        shards = gu_w.shape[1]
        grad_tokens, small_g, sums_a, sums_b, sums_c = attn_bwd_sum(
            qkv, grad_context, context, r, e, normed, tokens, grad_residual, gain_one.reshape(1, d), qkv_w,
            ddn.reshape(shards, ff // shards, d), grad_out_w.reshape(shards, n1, d), g_gain_two, dgu)
        grad_tokens, output, s_q, s_k, s_v, s_out, s_gate, s_up, s_down, r_gain_one, r_gain_two, r_table = finish(
            grad_tokens, output, sums_a, sums_b, dgu, sums_c, small_g, at.reshape(1), n1, ff)
        r_gain_one, r_gain_two, r_table = r_gain_one.reshape(n1), r_gain_two.reshape(n1), r_table[:, :BUCKETS].reshape(n2)
    else:
        total = lambda x: lax.psum(scatter(x), "batch").astype(f32)
        gq, gk, gv, near_sums, far_sums = attn_bwd(q, k, v, grad_context, context, r, e)
        grads = (gq, gk, gv)
        s_gate, s_up, s_down, s_out = (total(x) for x in (dgu[0].reshape(d, ff), dgu[1].reshape(d, ff), ddn, grad_out_w))
        s_q, s_k, s_v = (total(contract_rows(normed, x).astype(bf)) for x in grads)
        grad_normed = sum(contract_cols(x, qkv_w[:, :, t * d:t * d + d].reshape(d, d)) for t, x in enumerate(grads))
        _, first_pull = jax.vjp(rms_norm, inputs, gain_one)
        share, g_gain_one = first_pull(grad_normed)
        grad_tokens = grad_residual + share
        g_table = table_grad(near_sums, far_sums)
        small_g = lax.psum(jnp.concatenate([g_gain_one, g_gain_two[0], g_table]), ("batch", "dp", "narrow"))
        r_gain_one = lax.dynamic_slice_in_dim(small_g, at * n1, n1)
        r_gain_two = lax.dynamic_slice_in_dim(small_g, d + at * n1, n1)
        r_table = lax.dynamic_slice_in_dim(small_g, 2 * d + at * n2, n2)
    return (output, grad_tokens, r_gain_one, r_table, s_q, s_k, s_v, s_out, r_gain_two, s_gate, s_up, s_down)

def solution(mesh):
    near = (mesh.shape["batch"], mesh.shape["dp"], mesh.shape["narrow"]) == (4, 4, 2)
    placed = (
        P(("batch", "dp", "narrow"), None),
        P(("batch", "dp", "narrow")),
        P(("batch", "dp", "narrow"), None),
        P(("dp", "narrow")),
        P(("dp", "narrow")),
        P(("dp", "narrow"), None),
        P(("dp", "narrow"), None),
        P(("dp", "narrow"), None),
        P(("dp", "narrow"), None),
        P(("dp", "narrow")),
        P(("dp", "narrow"), None),
        P(("dp", "narrow"), None),
        P(("dp", "narrow"), None),
        P(("batch", "dp", "narrow"), None),
    )
    return jax.shard_map(
        functools.partial(per_device, near),
        mesh=mesh,
        in_specs=placed,
        out_specs=(
            P(("batch", "dp", "narrow"), None),
            P(("batch", "dp", "narrow"), None),
            P(("dp", "narrow")),
            P(("dp", "narrow")),
            P(("dp", "narrow"), None),
            P(("dp", "narrow"), None),
            P(("dp", "narrow"), None),
            P(("dp", "narrow"), None),
            P(("dp", "narrow")),
            P(("dp", "narrow"), None),
            P(("dp", "narrow"), None),
            P(("dp", "narrow"), None),
        ),
        check_vma=False,
    )
```

```python
import functools

import jax
import jax.numpy as jnp
import numpy as np
from jax import lax
from jax.experimental import pallas as pl
from jax.experimental.pallas import tpu as pltpu
from jax.sharding import PartitionSpec as P

EPS = 1e-06
SHARD = ("dp", "narrow")
BUCKETS = 32
bf=jnp.bfloat16; f32=jnp.float32
T=128; L=1152; NT=L//T
NEG=-1e30
def dot(a,b): return jnp.dot(a,b,preferred_element_type=f32)
def dot_tl(a,b): return lax.dot_general(a,b,(((0,),(0,)),((),())),preferred_element_type=f32)

def fwd_open(rhs,vaug):
    rhs[...]=jnp.zeros_like(rhs)
    row=lax.broadcasted_iota(jnp.int32,(128,NT*256),0)
    col=lax.broadcasted_iota(jnp.int32,(128,NT*256),1)
    rhs[128:256,:]=(row==col//128).astype(f32).astype(bf)
    vaug[:,128:256]=jnp.ones((L,128),bf)

def fwd_pair(q,k,v,mask,lo,hi,bias,o_ref,e_ref,r_ref,rhs,kaug,vaug,bn,s_ref):
    qT=q.T
    for i in range(NT):
        rhs[0:64,256*i:256*i+128]=qT[0:64,128*i:128*i+128]
        rhs[64:128,256*i+128:256*i+256]=qT[64:128,128*i:128*i+128]
    kaug[:,0:128]=k
    row=lax.broadcasted_iota(jnp.int32,(L,128),0)//128
    col=lax.broadcasted_iota(jnp.int32,(L,128),1)//2
    far=jnp.where(row<col-1,lo,jnp.where(row>col+1,hi,0.0))
    kaug[:,128:256]=(mask+far).astype(bf)
    vaug[:,0:128]=v
    for a in range(2):
        wb=jnp.broadcast_to(bias[a:a+1,:],(384,512))
        bn[:,128*a:128*a+128]=pltpu.roll(wb,0,1,stride=1,stride_axis=0)[:,0:128]
    def scores(i,slot):
        ri=rhs[:,256*i:256*i+256]
        first,last=max(0,i-1)*128,min(NT,i+2)*128
        off=(first//128-(i-1))*128
        x=dot(kaug[...],ri)
        xn=x[first:last]+bn[off:off+last-first,:]
        ms=[jnp.max(xn,axis=0,keepdims=True)]
        s_ref[slot,first:last,:]=xn
        if first>0:
            s_ref[slot,0:first,:]=x[0:first]; ms.append(jnp.max(x[0:first],axis=0,keepdims=True))
        if last<L:
            s_ref[slot,last:L,:]=x[last:L]; ms.append(jnp.max(x[last:L],axis=0,keepdims=True))
        m=ms[0]
        for y in ms[1:]: m=jnp.maximum(m,y)
        return m
    lane=lax.broadcasted_iota(jnp.int32,(128,128),1)<64
    def finish(i,slot,m):
        e=jnp.exp(s_ref[slot]-m).astype(bf)
        e_ref[:,pl.ds(i*256,256)]=e
        o=dot_tl(e,vaug[...])
        num=jnp.where(lane,o[0:128,0:128],o[128:256,0:128])
        den=jnp.where(lane,o[0:128,128:256],o[128:256,128:256])
        r=1.0/den
        rows=pl.ds(i*128,128)
        o_ref[rows,:]=(num*r).astype(bf)
        r_ref[rows,:]=r
    m=scores(0,0)
    for i in range(NT):
        mn=scores(i+1,(i+1)%2) if i+1<NT else None
        finish(i,i%2,m)
        m=mn

def fwd_kernel(q_ref,k_ref,v_ref,mask_ref,far_ref,w_ref,o_ref,e_ref,r_ref,rhs,kaug,vaug,bn,s_ref):
    @pl.when((pl.program_id(0)==0)&(pl.program_id(1)==0))
    def _():
        fwd_open(rhs,vaug)
    fwd_pair(q_ref[...],k_ref[...],v_ref[...],mask_ref[...],far_ref[0:1,:],far_ref[1:2,:],w_ref[...],o_ref,e_ref,r_ref,rhs,kaug,vaug,bn,s_ref)

def attn_fwd(q,k,v,mask,far,w):
    rows=q.shape[0]//L
    spec=pl.BlockSpec((L,128),lambda r,p:(r,p))
    return pl.pallas_call(fwd_kernel,
        grid=(rows,8),
        in_specs=[spec,spec,spec,
            pl.BlockSpec((None,L,128),lambda r,p:(r,0,0)),
            pl.BlockSpec((None,8,128),lambda r,p:(p,0,0)),
            pl.BlockSpec((None,8,512),lambda r,p:(p,0,0))],
        out_specs=[spec,pl.BlockSpec((None,None,L,NT*256),lambda r,p:(r,p,0,0)),spec],
        out_shape=[jax.ShapeDtypeStruct(q.shape,bf),jax.ShapeDtypeStruct((rows,8,L,NT*256),bf),jax.ShapeDtypeStruct(q.shape,f32)],
        scratch_shapes=[pltpu.VMEM((256,NT*256),bf),pltpu.VMEM((L,256),bf),pltpu.VMEM((L,256),bf),pltpu.VMEM((384,256),f32),pltpu.VMEM((2,L,256),f32)],
        compiler_params=pltpu.CompilerParams(vmem_limit_bytes=56*2**20),
        name="attn_fwd",
    )(q,k,v,mask,far,w)

THR=(12,16,23,32,46,64,91)
def bucket_np(d):
    n=np.abs(d); c=np.full_like(n,8)
    for t in THR: c=c+(n>=t)
    return np.where(n<8,n,c)+16*(d>0)
def tables(table):
    t=table.reshape(16,32).astype(f32)
    y=np.arange(512); y=np.where(y>=128,y-512,y)
    d=-128-y
    oh=(np.arange(32)[:,None]==bucket_np(d)[None,:]).astype(np.float32)
    w=jnp.dot(t,jnp.asarray(oh),precision=lax.Precision.HIGHEST)
    w=jnp.pad(w.reshape(8,2,512),((0,0),(0,6),(0,0)))
    lo=jnp.tile(t[:,15].reshape(8,1,2),(1,1,64)); hi=jnp.tile(t[:,31].reshape(8,1,2),(1,1,64))
    far=jnp.pad(jnp.concatenate([lo,hi],1),((0,0),(0,6),(0,0)))
    return far,w
def mask_cols(row_kind,text_length):
    pos=np.arange(L)
    kind=row_kind[:,None]
    seg=kind*(pos//384)[None]
    off=pos[None]-seg*384
    img=jnp.where(kind==1,256,1024)
    tl=jnp.where(seg==0,text_length[:,0:1],jnp.where(seg==1,text_length[:,1:2],text_length[:,2:3]))
    live=off<img+tl
    qseg=kind*np.minimum(np.arange(128)//2//3,2)[None]
    ok=live[:,:,None]&(seg[:,:,None]==qseg[:,None,:])
    return jnp.where(ok,0.0,NEG).astype(f32)

def bwd_open(rhs,vaug,qaug):
    rhs[...]=jnp.zeros_like(rhs)
    c=lax.broadcasted_iota(jnp.int32,(L,128),1)
    vaug[:,128:256]=(c<3).astype(f32).astype(bf)
    row=lax.broadcasted_iota(jnp.int32,(NT*256,128),0)
    col=lax.broadcasted_iota(jnp.int32,(NT*256,128),1)
    qaug[:,128:256]=(row//128==col).astype(f32).astype(bf)

def bwd_pair(q_ref,k_ref,v_ref,do_ref,o_ref,r_ref,e_ref,near_ref,far_ref,rhs,vaug,dobd,qaug,ds_ref,nacc):
    q=q_ref[...]; k=k_ref[...]
    vaug[:,0:128]=v_ref[...]
    dof=do_ref[...].astype(f32)*r_ref[...]
    dos=dof.astype(bf)
    dT=dos.T
    pT=(dos.astype(f32)*o_ref[...].astype(f32)).T
    D=jnp.concatenate([jnp.sum(pT[0:64],axis=0,keepdims=True),jnp.sum(pT[64:128],axis=0,keepdims=True)],0)
    D=-D
    D1=D.astype(bf); D2=(D-D1.astype(f32)); D3=(D2-D2.astype(bf).astype(f32)).astype(bf); D2=D2.astype(bf)
    lane=lax.broadcasted_iota(jnp.int32,(128,128),1)<64
    zero=jnp.zeros((128,128),bf)
    z13=jnp.zeros((13,128),bf)
    for i in range(NT):
        t=slice(128*i,128*i+128)
        for a in range(2):
            h=slice(64*a,64*a+64)
            c=slice(256*i+128*a,256*i+128*a+128)
            rhs[h,c]=dT[h,t]
            rhs[128:144,c]=jnp.concatenate([D1[a:a+1,t],D2[a:a+1,t],D3[a:a+1,t],z13],0)
            dobd[c,:]=jnp.where(lane==(a==0),dos[t],zero)
            qaug[c,0:128]=jnp.where(lane==(a==0),q[t],zero)
    nacc[...]=jnp.zeros_like(nacc)
    dqs=[]
    for i in range(NT):
        c=slice(256*i,256*i+256)
        lo,hi=max(0,i-1)*128,min(NT,i+2)*128
        off=(lo//128-(i-1))*128
        dp=dot(vaug[...],rhs[:,c])
        ds=e_ref[:,c].astype(f32)*dp
        nacc[off:off+hi-lo,:]+=ds[lo:hi]
        dsb=ds.astype(bf)
        ds_ref[:,c]=dsb
        g=dot_tl(dsb,k)
        dqs.append(jnp.where(lane,g[0:128],g[128:256]).astype(bf))
    dv=dot(e_ref[...],dobd[...]).astype(bf)
    g=dot(ds_ref[...],qaug[...])
    dk=g[:,0:128].astype(bf)
    G=g[:,128:256]
    row=lax.broadcasted_iota(jnp.int32,(L,128),0)//128
    col=lax.broadcasted_iota(jnp.int32,(L,128),1)//2
    far_ref[0:1,:]=jnp.sum(jnp.where(row<col-1,G,0.0),axis=0,keepdims=True)
    far_ref[1:2,:]=jnp.sum(jnp.where(row>col+1,G,0.0),axis=0,keepdims=True)
    far_ref[2:8,:]=jnp.zeros((6,128),f32)
    near_ref[2:8,:]=jnp.zeros((6,512),f32)
    rev=(lax.broadcasted_iota(jnp.int32,(128,128),0)+lax.broadcasted_iota(jnp.int32,(128,128),1)==127).astype(f32)
    for a in range(2):
        x=jnp.dot(nacc[:,128*a:128*a+128],rev,precision=lax.Precision.HIGHEST,preferred_element_type=f32)
        x=jnp.concatenate([x,jnp.zeros((384,384),f32)],1)
        x=pltpu.roll(x,0,1,stride=1,stride_axis=0)
        near_ref[a:a+1,:]=jnp.sum(x,axis=0,keepdims=True)
    return jnp.concatenate(dqs,0),dk,dv

def bwd_kernel(q_ref,k_ref,v_ref,do_ref,o_ref,r_ref,e_ref,dq_ref,dk_ref,dv_ref,near_ref,far_ref,rhs,vaug,dobd,qaug,ds_ref,nacc):
    @pl.when((pl.program_id(0)==0)&(pl.program_id(1)==0))
    def _():
        bwd_open(rhs,vaug,qaug)
    dq_ref[...],dk_ref[...],dv_ref[...]=bwd_pair(q_ref,k_ref,v_ref,do_ref,o_ref,r_ref,e_ref,near_ref,far_ref,rhs,vaug,dobd,qaug,ds_ref,nacc)

def attn_bwd(q,k,v,do,o,r,e):
    rows=q.shape[0]//L
    spec=pl.BlockSpec((L,128),lambda r,p:(r,p))
    sds=jax.ShapeDtypeStruct
    return pl.pallas_call(bwd_kernel,
        grid=(rows,8),
        in_specs=[spec]*6+[pl.BlockSpec((None,None,L,NT*256),lambda r,p:(r,p,0,0))],
        out_specs=[spec]*3+[pl.BlockSpec((None,None,8,512),lambda r,p:(r,p,0,0)),pl.BlockSpec((None,None,8,128),lambda r,p:(r,p,0,0))],
        out_shape=[sds(q.shape,bf)]*3+[sds((rows,8,8,512),f32),sds((rows,8,8,128),f32)],
        scratch_shapes=[pltpu.VMEM((256,NT*256),bf),pltpu.VMEM((L,256),bf),pltpu.VMEM((NT*256,128),bf),pltpu.VMEM((NT*256,256),bf),pltpu.VMEM((L,NT*256),bf),pltpu.VMEM((384,256),f32)],
        compiler_params=pltpu.CompilerParams(vmem_limit_bytes=58*2**20),
        name="attn_bwd",
    )(q,k,v,do,o,r,e)
def table_grad(near,far):
    y=np.arange(512)
    oh=(bucket_np(y-255)[:,None]==np.arange(32)[None,:]).astype(np.float32)
    n=jnp.sum(near[:,:,0:2],0).reshape(16,512)
    g=jnp.dot(n,jnp.asarray(oh),precision=lax.Precision.HIGHEST)
    f=jnp.sum(far[:,:,0:2],0).reshape(8,2,64,2).sum(2)
    lo=f[:,0].reshape(16,1); hi=f[:,1].reshape(16,1)
    g=g+lo*np.eye(32,dtype=np.float32)[15][None]+hi*np.eye(32,dtype=np.float32)[31][None]
    return g.reshape(512)

MESH = pl.DeviceIdType.MESH

def places():
    b, m, c = lax.axis_index("batch"), lax.axis_index("dp"), lax.axis_index("narrow")
    x, y = lax.rem(m, 2), m // 2
    mx = y * 2 + (1 - x)
    my = (1 - y) * 2 + x
    md = (1 - y) * 2 + (1 - x)
    return b, m, c, mx, my, md

def greet(devices):
    barrier = pltpu.get_barrier_semaphore()
    for d in devices:
        pl.semaphore_signal(barrier, inc=1, device_id=d, device_id_type=MESH)
    pl.semaphore_wait(barrier, len(devices))

def gather_steps(gu_in, dn_in, wo_in, gu, dn, wo, send, recv, local):
    b, m, c, mx, my, md = places()
    o = 1 - c
    z = lax.rem(b, 2)
    oz = 1 - z
    nx, ny, nc, nz = (b, mx, c), (b, my, c), (b, m, o), (b + 1 - 2 * z, m, c)
    me, it = m * 2 + c, m * 2 + o
    ix, iy, idg = mx * 2 + c, my * 2 + c, md * 2 + c
    jx, jy, jdg = mx * 2 + o, my * 2 + o, md * 2 + o
    def copy(src, dst, n, to):
        return pltpu.make_async_remote_copy(src_ref=src, dst_ref=dst, send_sem=send.at[n], recv_sem=recv.at[n], device_id=to, device_id_type=MESH)
    def push(ref, n, to):
        return copy(ref, ref, n, to)
    def got(ref, n):
        copy(ref, ref, n, nc).wait_recv()
    def first(src, dst, n):
        for t, to in enumerate((nx, ny, nc)):
            copy(src, dst, n + t, to).start()
    def halves(ref, i):
        h = ref.shape[1] // 2
        return ref.at[i, pl.ds(0, h)], ref.at[i, pl.ds(h, h)]
    def second(ref, n, onward=None):
        got(ref.at[ix], n)
        push(halves(ref, ix)[0], n + 3, ny).start()
        push(ref.at[ix], n + 5, nc).start()
        if onward is not None:
            push(ref.at[ix], onward, nz).start()
        got(ref.at[iy], n + 1)
        push(halves(ref, iy)[1], n + 4, nx).start()
        push(ref.at[iy], n + 6, nc).start()
        if onward is not None:
            push(ref.at[iy], onward + 1, nz).start()
    def third(ref, n, onward=None):
        got(halves(ref, idg)[0], n + 3)
        got(halves(ref, idg)[1], n + 4)
        push(ref.at[idg], n + 7, nc).start()
        if onward is not None:
            push(ref.at[idg], onward + 2, nz).start()
    def last(src, ref, n, onward=None):
        for t, i in ((2, it), (5, jx), (6, jy), (7, jdg)):
            got(ref.at[i], n + t)
        for t in (0, 1, 2):
            copy(src, ref.at[me], n + t, nc).wait_send()
        push(halves(ref, ix)[0], n + 3, ny).wait_send()
        push(halves(ref, iy)[1], n + 4, nx).wait_send()
        for t, i in ((5, ix), (6, iy), (7, idg)):
            push(ref.at[i], n + t, nc).wait_send()
        if onward is not None:
            for t, i in enumerate((ix, iy, idg)):
                push(ref.at[i], onward + t, nz).wait_send()
    def part(ref, i):
        cut = ref.shape[-1] // 384 * 128
        return ref.at[..., pl.ds(0, cut)] if i == 0 else ref.at[..., pl.ds(cut, ref.shape[-1] - cut)]
    mine, other = gu.at[z], gu.at[oz]
    m0, m1, o0, o1 = part(mine, 0), part(mine, 1), part(other, 0), part(other, 1)
    in0, in1 = part(gu_in.at[z], 0), part(gu_in.at[z], 1)
    d0, d1, dn0, dn1 = part(dn, 0), part(dn, 1), part(dn_in, 0), part(dn_in, 1)
    keeps = [pltpu.make_async_copy(gu_in.at[0], gu.at[0, me], local.at[0]), pltpu.make_async_copy(gu_in.at[1], gu.at[1, me], local.at[1]),
             pltpu.make_async_copy(dn_in, dn.at[me], local.at[2]), pltpu.make_async_copy(wo_in, wo.at[me], local.at[3])]
    W, D0, D1, G0, G1, Z0, Z1, OWN = 0, 8, 16, 24, 32, 40, 46, 52
    def z_second(ref, n, ts):
        for t in ts:
            i = (ix, iy, idg)[t]
            got(ref.at[i], n + t)
            push(ref.at[i], n + 3 + t, nc).start()
    def begin():
        first(in0, m0.at[me], G0)
        first(in1, m1.at[me], G1)
        copy(gu_in.at[oz], other.at[me], OWN, nc).start()
        for k in keeps:
            k.start()
    def at0():
        second(m0, G0, Z0)
        first(dn0, d0.at[me], D0)
    def at2():
        second(m1, G1, Z1)
        third(m0, G0, Z0)
        first(dn1, d1.at[me], D1)
    def at3():
        second(d0, D0)
        first(wo_in, wo.at[me], W)
    def at4():
        third(m1, G1, Z1)
        z_second(o0, Z0, (0, 1))
    def at6():
        second(d1, D1)
        third(d0, D0)
    def end():
        z_second(o1, Z1, (0, 1))
        z_second(o0, Z0, (2,))
        second(wo, W)
        third(d1, D1)
        third(wo, W)
        z_second(o1, Z1, (2,))
        last(wo_in, wo, W)
        last(in0, m0, G0, Z0)
        last(in1, m1, G1, Z1)
        got(other.at[it], OWN)
        copy(gu_in.at[oz], other.at[me], OWN, nc).wait_send()
        for ref, n in ((o0, Z0), (o1, Z1)):
            for t, i, j in ((0, ix, jx), (1, iy, jy), (2, idg, jdg)):
                got(ref.at[j], n + 3 + t)
                push(ref.at[i], n + 3 + t, nc).wait_send()
        last(dn0, d0, D0)
        last(dn1, d1, D1)
        for k in keeps:
            k.wait()
    return begin, {1: at0, 3: at2, 4: at3, 5: at4, 7: at6}, end


def bias_consts():
    y = np.arange(512)
    y = np.where(y >= 128, y - 512, y)
    ids = bucket_np(-128 - y)
    out = np.zeros((128, 1280), np.float32)
    for a in range(2):
        out[32 * a + ids, 512 * a + np.arange(512)] = 1
        out[32 * a + 15, 1024 + a:1152:2] = 1
        out[32 * a + 31, 1152 + a:1280:2] = 1
    return jnp.asarray(out, bf)

def mask_block(kind, text):
    pos = lax.broadcasted_iota(jnp.int32, (L, 128), 0)
    tile = lax.broadcasted_iota(jnp.int32, (L, 128), 1) // 2
    seg = jnp.where(kind == 1, pos // 384, 0)
    mine = jnp.where(kind == 1, tile // 3, 0)
    length = jnp.where(seg == 0, text[0], jnp.where(seg == 1, text[1], text[2]))
    live = pos - seg * 384 < jnp.where(kind == 1, 256, 1024) + length
    return jnp.where(live & (seg == mine), 0.0, NEG)

def front_kernel(kind_ref, text_ref, x_ref, gain1_ref, gain2_ref, table_ref, wq_ref, wk_ref, wv_ref, gate_ref, up_ref, dn_in, wo_in, const_ref,
                 o_ref, e_ref, r_ref, n_ref, qkv_out, w_out, gu, dn, wo,
                 W, acc, rstd, qkv, gu_in, mask, rhs, kaug, vaug, bn, s_ref, wsend, wrecv, wlocal, send, recv, local):
    b, m, c, mx, my, md = places()
    o = 1 - c
    nx, ny, nc, nz = (b, mx, c), (b, my, c), (b, m, o), (b + 1 - 2 * lax.rem(b, 2), m, c)
    d = wq_ref.shape[1]
    rows = wq_ref.shape[0]
    half = rows // 2
    me = m * 2 + c
    p = pl.program_id(0)
    begin, during, end = gather_steps(gu_in, dn_in, wo_in, gu, dn, wo, send, recv, local)
    keeps = (pltpu.make_async_copy(W, w_out, wlocal.at[0]), pltpu.make_async_copy(qkv, qkv_out, wlocal.at[1]))
    def push(src, n, to):
        return pltpu.make_async_remote_copy(src_ref=src, dst_ref=src, send_sem=wsend.at[n], recv_sem=wrecv.at[n], device_id=to, device_id_type=MESH)
    def got(ref, n):
        push(ref, n, nc).wait_recv()
    def chunk(j, first):
        cols = pl.ds(pl.multiple_of(j * 2 * rows, 2 * rows), 2 * rows)
        gain = jnp.concatenate([W[2 * j, 0:1, 3 * d:3 * d + rows], W[2 * j + 1, 0:1, 3 * d:3 * d + rows]], 1).astype(f32)
        n = (x_ref[:, cols].astype(f32) * rstd[...] * gain).astype(bf)
        n_ref[:, cols] = n
        for t in range(3):
            y = dot(n, W[pl.ds(2 * j, 2), :, t * d:t * d + d].reshape(2 * rows, d))
            if first:
                acc[:, t * d:t * d + d] = y
            else:
                acc[:, t * d:t * d + d] = acc[:, t * d:t * d + d] + y
    @pl.when(p == 0)
    def _():
        W[me, :, 0:d] = wq_ref[...]
        W[me, :, d:2 * d] = wk_ref[...]
        W[me, :, 2 * d:3 * d] = wv_ref[...]
        W[me, :, 3 * d:3 * d + 128] = jnp.zeros((rows, 128), bf)
        W[me, 0:1, 3 * d:3 * d + rows] = gain1_ref[...]
        W[me, 1:2, 3 * d:3 * d + rows] = gain2_ref[...]
        W[me, 2:3, 3 * d:3 * d + table_ref.shape[1]] = table_ref[...]
        greet([nx, ny, nc, nz])
        top, low = pl.ds(0, half), pl.ds(half, half)
        sends = [push(W.at[me], 0, nx), push(W.at[me], 1, ny), push(W.at[me], 2, nc)]
        for s in sends:
            s.start()
        gu_in[0] = gate_ref[...]
        gu_in[1] = up_ref[...]
        for t in range(0, L, 384):
            x = x_ref[t:t + 384, :].astype(f32)
            rstd[t:t + 384, :] = lax.rsqrt(jnp.mean(x * x, axis=-1, keepdims=True) + EPS)
        mask[...] = mask_block(kind_ref[0], (text_ref[0, 0], text_ref[0, 1], text_ref[0, 2]))
        fwd_open(rhs, vaug)
        ix, iy, idg = mx * 2 + c, my * 2 + c, md * 2 + c
        jx, jy, jdg = mx * 2 + o, my * 2 + o, md * 2 + o
        got(W.at[m * 2 + o], 2)
        chunk(m, True)
        got(W.at[ix], 0)
        more = [push(W.at[ix, top], 3, ny), push(W.at[ix], 5, nc)]
        got(W.at[iy], 1)
        more += [push(W.at[iy, low], 4, nx), push(W.at[iy], 6, nc)]
        for s in more:
            s.start()
        begin()
        got(W.at[jx], 5)
        chunk(mx, False)
        got(W.at[jy], 6)
        chunk(my, False)
        got(W.at[idg, top], 3)
        got(W.at[idg, low], 4)
        more.append(push(W.at[idg], 7, nc))
        more[-1].start()
        got(W.at[jdg], 7)
        keeps[0].start()
        chunk(md, False)
        for t in range(3 * d // 128):
            qkv[t] = acc[:, 128 * t:128 * t + 128].astype(bf)
        keeps[1].start()
        for s in sends + more:
            s.wait_send()
    for at, act in during.items():
        pl.when(p == at)(act)
    @pl.when(p > 0)
    def _():
        h = p - 1
        N = d // 128
        values = jnp.broadcast_to(W[h, 2:3, 3 * d:3 * d + 128], (16, 128))
        bias = dot(values, const_ref[...])
        fwd_pair(qkv[h], qkv[N + h], qkv[2 * N + h], mask[...], bias[0:1, 1024:1152], bias[0:1, 1152:1280],
                 jnp.concatenate([bias[0:1, 0:512], bias[0:1, 512:1024]], 0), o_ref, e_ref, r_ref, rhs, kaug, vaug, bn, s_ref)
    @pl.when(p == pl.num_programs(0) - 1)
    def _():
        end()
        for k in keeps:
            k.wait()

def front(kind, text, x, gain1, gain2, table, wq, wk, wv, gate, up, dn, wo):
    R, d = x.shape
    rows = wq.shape[0]
    N = d // 128
    at = lambda p: jnp.maximum(p - 1, 0)
    spec = pl.BlockSpec((R, 128), lambda p: (0, at(p)))
    hbm = pl.BlockSpec(memory_space=pl.ANY)
    whole = lambda a: pl.BlockSpec(a.shape, lambda p: (0,) * a.ndim, pipeline_mode=pl.Buffered(1))
    smem = pl.BlockSpec(memory_space=pltpu.SMEM)
    sds = jax.ShapeDtypeStruct
    dma = pltpu.SemaphoreType.DMA
    row = lambda a: a.reshape(1, -1)
    vectors = (x, row(gain1), row(gain2), row(table), wq, wk, wv, gate, up, dn, wo, bias_consts())
    wide = 3 * d + 128
    return pl.pallas_call(front_kernel, grid=(1 + N,),
        in_specs=[smem, smem] + [whole(a) for a in vectors],
        out_specs=[spec, pl.BlockSpec((None, None, R, NT * 256), lambda p: (0, at(p), 0, 0)), spec,
                   pl.BlockSpec((R, d), lambda p: (0, 0), pipeline_mode=pl.Buffered(1))] + [hbm] * 5,
        out_shape=[sds((R, d), bf), sds((1, N, R, NT * 256), bf), sds((R, d), f32), sds((R, d), bf), sds((3 * N, R, 128), bf),
                   sds((8, rows, wide), bf), sds((2, 8) + gate.shape, bf), sds((8,) + dn.shape, bf), sds((8,) + wo.shape, bf)],
        scratch_shapes=[pltpu.VMEM((8, rows, wide), bf), pltpu.VMEM((R, 3 * d), f32), pltpu.VMEM((R, 1), f32), pltpu.VMEM((3 * N, R, 128), bf),
                        pltpu.VMEM((2,) + gate.shape, bf), pltpu.VMEM((R, 128), f32),
                        pltpu.VMEM((256, NT * 256), bf), pltpu.VMEM((R, 256), bf), pltpu.VMEM((R, 256), bf), pltpu.VMEM((384, 256), f32), pltpu.VMEM((2, R, 256), f32),
                        dma((8,)), dma((8,)), dma((2,)), dma((53,)), dma((53,)), dma((4,))],
        compiler_params=pltpu.CompilerParams(collective_id=1, has_side_effects=True, vmem_limit_bytes=63 * 2**20),
        name="front")(kind, text, *vectors)

DRAIN = 6

def plane_scratch(rows, cols):
    h = rows // 2
    pair = pltpu.VMEM((2, 2, h, cols), bf)
    single = pltpu.VMEM((2, h, cols), bf)
    dma = pltpu.SemaphoreType.DMA
    return [pltpu.VMEM((2, 4, 2, rows, cols), bf), pltpu.VMEM((2, 4, rows, cols), bf)] + [pair] * 6 + [single] * 2 + [dma((5, 2)), dma((5, 2))]

def z_scratch(n, rows, cols):
    ring = lambda k: pltpu.VMEM((k, rows, cols), bf)
    dma = pltpu.SemaphoreType.DMA
    return [ring(4), ring(4), ring(2), ring(n), dma((3, n)), dma((3, n))]

def plus(a, b):
    return a + b

def rs_greet():
    b, m, c, mx, my, md = places()
    greet([(b, mx, c), (b, my, c), (b, m, 1 - c), (b + 1 - 2 * lax.rem(b, 2), m, c), (3 - b, m, c)])

def stage(t, n, act, also=None):
    live = (t >= 0) & (t < n)
    pl.when(live if also is None else live & also)(lambda: act(t))

def plane_step(s, n, bufs, put):
    src, cbuf, sx, sy, kt, kb, xt, yb, t2, b2, send, recv = bufs
    b, m, c, mx, my, md = places()
    o = 1 - c
    nx, ny, nc = (b, mx, c), (b, my, c), (b, m, o)
    h = kt.shape[2]
    def copy(kind, k, a, z, to):
        return pltpu.make_async_remote_copy(src_ref=a, dst_ref=z, send_sem=send.at[kind, k], recv_sem=recv.at[kind, k], device_id=to, device_id_type=MESH)
    core = lambda k: copy(0, k, src.at[k, :, o], cbuf.at[k], nc)
    x1 = lambda k: copy(1, k, sx.at[k], xt.at[k], nx)
    y1 = lambda k: copy(2, k, sy.at[k], yb.at[k], ny)
    y2 = lambda k: copy(3, k, kt.at[k, 1], t2.at[k], ny)
    x2 = lambda k: copy(4, k, kb.at[k, 1], b2.at[k], nx)
    def third(t):
        k = lax.rem(t, 2)
        y2(k).wait()
        x2(k).wait()
        put(t, plus(kt[k, 0], t2[k]), plus(kb[k, 0], b2[k]))
    def second(t):
        k = lax.rem(t, 2)
        x1(k).wait()
        y1(k).wait()
        kt[k] = plus(kt[k], xt[k])
        kb[k] = plus(kb[k], yb[k])
        y2(k).start()
        x2(k).start()
    def first(t):
        k = lax.rem(t, 2)
        core(k).wait()
        top = lambda i: plus(src[k, i, c, 0:h], cbuf[k, i, 0:h])
        low = lambda i: plus(src[k, i, c, h:2 * h], cbuf[k, i, h:2 * h])
        sx[k, 0], sx[k, 1] = top(mx), top(md)
        sy[k, 0], sy[k, 1] = low(my), low(md)
        x1(k).start()
        y1(k).start()
        kt[k, 0], kt[k, 1] = top(m), top(my)
        kb[k, 0], kb[k, 1] = low(m), low(mx)
    stage(s - 3, n, third)
    stage(s - 2, n, second)
    stage(s - 1, n, first)
    stage(s, n, lambda t: core(lax.rem(t, 2)).start())

def z_step(s, n, bufs, before):
    part, inward, across, done, send, recv = bufs
    b, m, c, mx, my, md = places()
    nz, na = (b + 1 - 2 * lax.rem(b, 2), m, c), (3 - b, m, c)
    outer = (b == 0) | (b == 3)
    inner = (b == 1) | (b == 2)
    def copy(kind, t, a, z, to):
        return pltpu.make_async_remote_copy(src_ref=a, dst_ref=z, send_sem=send.at[kind, t], recv_sem=recv.at[kind, t], device_id=to, device_id_type=MESH)
    up = lambda t: copy(0, t, part.at[lax.rem(t, 4)], inward.at[lax.rem(t, 4)], nz)
    over = lambda t: copy(1, t, part.at[lax.rem(t, 4)], across.at[lax.rem(t, 2)], na)
    down = lambda t: copy(2, t, done.at[t], done.at[t], nz)
    def outer_done(t):
        up(t).wait_send()
        down(t).wait_recv()
    def inner_done(t):
        down(t).wait_send()
    def inner_sum(t):
        over(t).wait()
        done[t] = plus(part[lax.rem(t, 4)], across[lax.rem(t, 2)])
        down(t).start()
    def inner_part(t):
        up(t).wait_recv()
        part[lax.rem(t, 4)] = plus(part[lax.rem(t, 4)], inward[lax.rem(t, 4)])
        over(t).start()
    stage(s - 3, n, outer_done, outer)
    stage(s - 3, n, inner_done, inner)
    stage(s - 2, n, inner_sum, inner)
    stage(s - 1, n, inner_part, inner)
    before()
    stage(s, n, lambda t: up(t).start(), outer)

def sum_step(s, n, plane, z):
    h = plane[4].shape[2]
    part = z[0]
    def put(t, top, low):
        part[lax.rem(t, 4), 0:h] = top
        part[lax.rem(t, 4), h:2 * h] = low
    z_step(s - 3, n, z, lambda: plane_step(s, n, plane, put))

GELU_C = float(np.sqrt(2.0 / np.pi))
def dot_nt(a, b):
    return lax.dot_general(a, b, (((1,), (1,)), ((), ())), preferred_element_type=f32)

def ffn_open(x_ref, ctx_ref, gain_ref, wo_ref, gres_ref, res, n, acc):
    for t in range(0, x_ref.shape[0], 384):
        s = slice(t, t + 384)
        y = x_ref[s, :].astype(f32) + dot(ctx_ref[s, :], wo_ref[...])
        res[s, :] = y
        acc[s, :] = y
        n[s, :] = (y * lax.rsqrt(jnp.mean(y * y, axis=-1, keepdims=True) + EPS) * gain_ref[0:1, :]).astype(bf)
    gres_ref[...] = jnp.zeros_like(gres_ref)

def ffn_block(g_ref, gu_ref, dn_ref, gres_ref, ddn_ref, n, acc):
    d = n.shape[1]
    wg = gu_ref[0].reshape(d, gu_ref.shape[-1])
    wu = gu_ref[1].reshape(d, gu_ref.shape[-1])
    wd = dn_ref[...]
    nn = n[...]
    g = g_ref[...]
    v = dot(nn, wg)
    u = dot(nn, wu)
    gh = dot_nt(g, wd)
    v2 = v * v
    th = jnp.tanh(GELU_C * v * (1.0 + 0.044715 * v2))
    half = 0.5 * (1.0 + th)
    gel = v * half
    h = (gel * u).astype(bf)
    dgel = half + 0.5 * v * (1.0 - th * th) * (GELU_C * (1.0 + 3 * 0.044715 * v2))
    gg = (gh * u * dgel).astype(bf)
    gu = (gh * gel).astype(bf)
    acc[...] = acc[...] + dot(h, wd)
    gres_ref[...] = gres_ref[...] + dot_nt(jnp.concatenate([gg, gu], 1), jnp.concatenate([wg, wu], 1))
    ddn_ref[...] = dot_tl(h, g).astype(bf)
    return dot_tl(nn, gg).astype(bf), dot_tl(nn, gu).astype(bf)

def ffn_close(s, g_ref, gain_ref, wo_ref, out_ref, gres_ref, gctx_ref, res, n, acc):
    out_ref[s, :] = acc[s, :].astype(bf)
    y = res[s, :]
    r = lax.rsqrt(jnp.mean(y * y, axis=-1, keepdims=True) + EPS)
    m = y * r
    gn = gres_ref[s, :]
    w = gn * gain_ref[0:1, :]
    gr = g_ref[s, :].astype(f32) + r * (w - m * jnp.mean(w * m, axis=-1, keepdims=True))
    gres_ref[s, :] = gr
    low = gr.astype(bf)
    n[s, :] = low
    gctx_ref[s, :] = dot_nt(low, wo_ref[...]).astype(bf)
    return jnp.sum(gn * m, axis=0, keepdims=True)

def ffn_kernel(x_ref, ctx_ref, g_ref, gain_ref, wo_ref, gu_ref, dn_ref,
               out_ref, gres_ref, gctx_ref, dwo_ref, ggain_ref, ddn_ref, dgu_ref, res, n, acc):
    j = pl.program_id(0)
    @pl.when(j == 0)
    def _():
        ffn_open(x_ref, ctx_ref, gain_ref, wo_ref, gres_ref, res, n, acc)
    a, b = ffn_block(g_ref, gu_ref, dn_ref, gres_ref, ddn_ref, n, acc)
    dgu_ref[0] = a.reshape(dgu_ref.shape[1:])
    dgu_ref[1] = b.reshape(dgu_ref.shape[1:])
    @pl.when(j == pl.num_programs(0) - 1)
    def _():
        R = x_ref.shape[0]
        total = sum(ffn_close(slice(t, t + 384), g_ref, gain_ref, wo_ref, out_ref, gres_ref, gctx_ref, res, n, acc) for t in range(0, R, 384))
        ggain_ref[...] = jnp.broadcast_to(total, ggain_ref.shape)
        dwo_ref[...] = dot_tl(ctx_ref[...], n[...]).astype(bf)

def ffn_sum_kernel(x_ref, ctx_ref, g_ref, small_ref, wo_ref, gu_ref, dn_ref,
                   out_ref, gres_ref, gctx_ref, dwo_ref, ggain_ref, ddn_ref, dgu_ref, res, n, acc, gain_ref, *bufs):
    j = pl.program_id(0)
    N = pl.num_programs(0) - 3
    src = bufs[0]
    @pl.when(j == 0)
    def _():
        rs_greet()
        for t in range(8):
            gain_ref[:, 128 * t:128 * t + 128] = small_ref[t, 1:2, :].astype(f32)
        ffn_open(x_ref, ctx_ref, gain_ref, wo_ref, gres_ref, res, n, acc)
        ggain_ref[...] = jnp.zeros_like(ggain_ref)
    @pl.when(j < N)
    def _():
        a, b = ffn_block(g_ref, gu_ref, dn_ref, gres_ref, ddn_ref, n, acc)
        k = lax.rem(j, 2)
        rows = a.shape[0] // 8
        src[k, :, :, 0:rows] = a.reshape(4, 2, rows, a.shape[1])
        src[k, :, :, rows:2 * rows] = b.reshape(4, 2, rows, a.shape[1])
    @pl.when(j >= N)
    def _():
        part = x_ref.shape[0] // 3
        s = pl.ds(pl.multiple_of((j - N) * part, part), part)
        total = ffn_close(s, g_ref, gain_ref, wo_ref, out_ref, gres_ref, gctx_ref, res, n, acc)
        ggain_ref[...] = ggain_ref[...] + jnp.broadcast_to(total, ggain_ref.shape)
    h = dgu_ref.shape[1] // 2
    plane, z = bufs[:12], bufs[12:]
    ahead = z[3].shape[0]
    def put(t, top, low):
        @pl.when(t < ahead)
        def _():
            z[0][lax.rem(t, 4), 0:h] = top
            z[0][lax.rem(t, 4), h:2 * h] = low
        @pl.when(t >= ahead)
        def _():
            dgu_ref[t, 0:h] = top
            dgu_ref[t, h:2 * h] = low
    z_step(j - 3, ahead, z, lambda: plane_step(j, N, plane, put))
    @pl.when(j == N + 2)
    def _():
        dwo_ref[...] = dot_tl(ctx_ref[...], n[...]).astype(bf)
        dgu_ref[0:ahead] = z[3][...]

def ffn(x, ctx, g, gain, wo, gu, dn, near, block=256):
    R, d = x.shape
    F = dn.shape[0]
    k = gu.shape[1]
    N = F // block
    sds = jax.ShapeDtypeStruct
    one = lambda *s: pl.BlockSpec(s, lambda j: (0,) * len(s), pipeline_mode=pl.Buffered(1))
    at = lambda j: jnp.minimum(j, N - 1)
    gub = pl.BlockSpec((2, k, d // k, block), lambda j: (0, 0, 0, at(j)))
    dnb = pl.BlockSpec((block, d), lambda j: (at(j), 0))
    rows = 2 * (d // k)
    gain_spec = pl.BlockSpec((8, 16, 128), lambda j: (0, 0, 3 * d // 128), pipeline_mode=pl.Buffered(1)) if near else one(1, d)
    if near:
        body, extra, steps, last = ffn_sum_kernel, [pltpu.VMEM((1, d), f32)] + plane_scratch(rows, block) + z_scratch(N - 3, rows, block), N + 3, (one(N, rows, block), sds((N, rows, block), bf))
        params = pltpu.CompilerParams(vmem_limit_bytes=61 * 2**20, collective_id=3, has_side_effects=True)
    else:
        body, extra, steps, last = ffn_kernel, [], N, (gub, sds(gu.shape, bf))
        params = pltpu.CompilerParams(vmem_limit_bytes=61 * 2**20)
    return pl.pallas_call(body, grid=(steps,),
        in_specs=[one(R, d), one(R, d), one(R, d), gain_spec, one(d, d), gub, dnb],
        out_specs=[one(R, d), one(R, d), one(R, d), one(d, d), one(8, d), dnb, last[0]],
        out_shape=[sds((R, d), bf), sds((R, d), f32), sds((R, d), bf), sds((d, d), bf), sds((8, d), f32), sds(dn.shape, bf), last[1]],
        scratch_shapes=[pltpu.VMEM((R, d), f32), pltpu.VMEM((R, d), bf), pltpu.VMEM((R, d), f32)] + extra,
        compiler_params=params, name="ffn")(x, ctx, g, gain, wo, gu, dn)

def sum_rounds(s, box, inbox, send, recv):
    b, m, c, mx, my, md = places()
    peers = [(b, m, 1 - c), (b, mx, c), (b, my, c), (b + 1 - 2 * lax.rem(b, 2), m, c), (3 - b, m, c)]
    def copy(r):
        return pltpu.make_async_remote_copy(src_ref=box.at[r], dst_ref=inbox.at[r], send_sem=send.at[r], recv_sem=recv.at[r], device_id=peers[r], device_id_type=MESH)
    for r in range(5):
        @pl.when(s == r)
        def _():
            copy(r).start()
        @pl.when(s == r + 1)
        def _():
            copy(r).wait()
            box[r + 1] = box[r] + inbox[r]

def bwd_sum_kernel(q_ref, k_ref, v_ref, do_ref, o_ref, r_ref, e_ref, n_ref, x_ref, gres_ref, gains_ref, wq_ref, wk_ref, wv_ref, dn_ref, wo_ref, gain2_ref, gu_ref, const_ref,
                   gtok_ref, small_ref, out_a, out_b, out_c, rhs, vaug, dobd, qaug, ds_ref, nacc, near_ref, far_ref, ggain, tab, g_all, gain_ref, box, inbox, ssend, srecv, osem, *bufs):
    p = pl.program_id(0)
    N = pl.num_programs(0) - DRAIN
    plane_a, z_a, plane_b, z_b, z_c = bufs[0:12], bufs[12:18], bufs[18:30], bufs[30:36], bufs[36:42]
    src_a, src_b = plane_a[0], plane_b[0]
    done_a, done_b, done_c = z_a[3], z_b[3], z_c[3]
    NA, NC = done_a.shape[0], done_c.shape[0]
    d = gtok_ref.shape[1]
    k = lax.rem(p, 2)
    def put(src, arrays):
        h = src.shape[3] // 2
        at = 0
        for a in arrays:
            r = a.shape[1] // 2
            a = a.reshape((4, 2) + a.shape[1:])
            src[k, :, :, at:at + r] = a[:, :, 0:r]
            src[k, :, :, h + at:h + at + r] = a[:, :, r:2 * r]
            at += r
    @pl.when(p == 0)
    def _():
        rs_greet()
        for t in range(8):
            gain_ref[:, 128 * t:128 * t + 128] = gains_ref[t, 0:1, :].astype(f32)
        bwd_open(rhs, vaug, qaug)
        gtok_ref[...] = jnp.zeros_like(gtok_ref)
        ggain[...] = jnp.zeros_like(ggain)
    @pl.when(p < NA)
    def _():
        put(src_a, (dn_ref[...], wo_ref[...]))
    sum_step(p, NA, plane_a, z_a)
    @pl.when(p < N)
    def _():
        g = jnp.concatenate(bwd_pair(q_ref, k_ref, v_ref, do_ref, o_ref, r_ref, e_ref, near_ref, far_ref, rhs, vaug, dobd, qaug, ds_ref, nacc), 1)
        lane = lax.broadcasted_iota(jnp.int32, (1, 128), 1)
        sums = jnp.dot(near_ref[...], const_ref[...], precision=lax.Precision.HIGHEST, preferred_element_type=f32)
        for a in range(2):
            lo, hi = (jnp.sum(jnp.where(lax.rem(lane, 2) == a, far_ref[i:i + 1, :], 0.0), axis=1, keepdims=True) for i in range(2))
            tab[p, a:a + 1, :] = sums[a:a + 1, :] + jnp.where(lane == 15, lo, 0.0) + jnp.where(lane == 31, hi, 0.0)
        g_all[p] = g
        gw = dot_tl(n_ref[...], g)
        half = pl.ds(pl.multiple_of(lax.rem(p, 2) * 128, 128), 128)
        w = jnp.concatenate([w_ref[:, :, half].reshape(d, 128) for w_ref in (wq_ref, wk_ref, wv_ref)], 1)
        ggain[...] = ggain[...] + sum((gw * w.astype(f32))[:, 128 * t:128 * t + 128] for t in range(3))
        gw = gw.astype(bf)
        put(src_b, [gw[:, 128 * t:128 * t + 128].reshape(8, d // 8, 128) for t in range(3)])
    @pl.when((p >= N) & (p < N + N // 2))
    def _():
        i = 2 * (p - N)
        g = jnp.concatenate([g_all[i], g_all[i + 1]], 1)
        w = jnp.concatenate([w_ref[:, :, 128 * t:128 * t + 128].reshape(d, 128) for t in range(2) for w_ref in (wq_ref, wk_ref, wv_ref)], 1)
        gtok_ref[...] = gtok_ref[...] + dot_nt(g, w)
    @pl.when(p >= N + N // 2)
    def _():
        rows = x_ref.shape[0]
        step = rows // 3
        for t in range(3):
            s = pl.ds(pl.multiple_of((p - N - N // 2) * rows + t * step, step), step)
            x = x_ref[t * step:t * step + step, :].astype(f32)
            r = lax.rsqrt(jnp.mean(x * x, axis=-1, keepdims=True) + EPS)
            m = x * r
            w = gtok_ref[s, :] * gain_ref[0:1, :]
            gtok_ref[s, :] = gres_ref[t * step:t * step + step, :] + r * (w - m * jnp.mean(w * m, axis=-1, keepdims=True))
    @pl.when(p == N - 1)
    def _():
        for t in range(N):
            box[0, 2 * t:2 * t + 2] = tab[t, 0:2]
        w = d // 8
        one = jnp.sum(ggain[...].T, axis=0, keepdims=True) / gain_ref[0:1, :]
        for t in range(8):
            box[0, 2 * N + t:2 * N + t + 1] = one[:, w * t:w * t + w]
            box[0, 2 * N + 8 + t:2 * N + 9 + t] = gain2_ref[0:1, w * t:w * t + w]
    sum_rounds(p - N + 1, box, inbox, ssend, srecv)
    sum_step(p, N, plane_b, z_b)
    def take():
        @pl.when(p < NC)
        def _():
            z_c[0][lax.rem(p, 4)] = gu_ref[...]
    z_step(p, NC, z_c, take)
    @pl.when(p == N + DRAIN - 1)
    def _():
        small_ref[...] = box[5]
        keeps = [pltpu.make_async_copy(a, o, osem.at[i]) for i, (a, o) in enumerate(((done_a, out_a), (done_b, out_b), (done_c, out_c)))]
        for copy in keeps:
            copy.start()
        for copy in keeps:
            copy.wait()

def attn_bwd_sum(qkv, do, o, r, e, n, x, gres, qkv_w, dn, wo, gain2, gu):
    R, d = x.shape
    N = d // 128
    NA, wide = N, 128
    rows_a, rows_b = dn.shape[1] + wo.shape[1], 3 * (d // 8)
    sds = jax.ShapeDtypeStruct
    at = lambda p: jnp.minimum(p, N - 1)
    after = lambda p: jnp.clip(p - N - N // 2, 0, 1)
    spec = pl.BlockSpec((R, 128), lambda p: (0, at(p)))
    head = lambda t: pl.BlockSpec((None, R, 128), lambda p: (t * N + at(p), 0, 0))
    one = lambda *s: pl.BlockSpec(s, lambda p: (0,) * len(s), pipeline_mode=pl.Buffered(1))
    part = pl.BlockSpec((R // 2, d), lambda p: (after(p), 0), pipeline_mode=pl.Buffered(1))
    cols = lambda a, t: pl.BlockSpec((8, a.shape[1], 256), lambda p: (0, 0, t * (N // 2) + jnp.where(p < N, p // 2, jnp.minimum(p - N, N // 2 - 1))))
    early = lambda a: pl.BlockSpec((8, a.shape[1], wide), lambda p: (0, 0, jnp.minimum(p, NA - 1)), pipeline_mode=pl.Buffered(1))
    hbm = pl.BlockSpec(memory_space=pl.ANY)
    dma = pltpu.SemaphoreType.DMA
    small = (2 * N + 16, d // 8)
    NC = 3
    left = gu.shape[0] - NC
    rest = (NC,) + gu.shape[1:]
    to_bucket = jnp.asarray((bucket_np(np.arange(512) - 255)[:, None] == np.arange(128)[None, :]).astype(np.float32))
    return pl.pallas_call(bwd_sum_kernel, grid=(N + DRAIN,),
        in_specs=[head(0), head(1), head(2)] + [spec] * 3 + [pl.BlockSpec((None, None, R, NT * 256), lambda p: (0, at(p), 0, 0)), one(R, d), part, part, pl.BlockSpec((8, 16, 128), lambda p: (0, 0, 3 * d // 128), pipeline_mode=pl.Buffered(1)),
                  cols(qkv_w, 0), cols(qkv_w, 1), cols(qkv_w, 2), early(dn), early(wo), one(8, d),
                  pl.BlockSpec((None,) + gu.shape[1:], lambda p: (left + jnp.minimum(p, NC - 1), 0, 0)), one(512, 128)],
        out_specs=[one(R, d), one(*small), hbm, hbm, hbm],
        out_shape=[sds((R, d), f32), sds(small, f32), sds((NA, rows_a, wide), bf), sds((N, rows_b, 128), bf), sds(rest, bf)],
        scratch_shapes=[pltpu.VMEM((256, NT * 256), bf), pltpu.VMEM((R, 256), bf), pltpu.VMEM((NT * 256, 128), bf), pltpu.VMEM((NT * 256, 256), bf), pltpu.VMEM((R, NT * 256), bf), pltpu.VMEM((384, 256), f32),
                        pltpu.VMEM((8, 512), f32), pltpu.VMEM((8, 128), f32), pltpu.VMEM((d, 128), f32), pltpu.VMEM((N, 8, 128), f32), pltpu.VMEM((N, R, 384), bf), pltpu.VMEM((1, d), f32), pltpu.VMEM((6,) + small, f32), pltpu.VMEM((5,) + small, f32), dma((5,)), dma((5,)), dma((3,))]
                       + plane_scratch(rows_a, wide) + z_scratch(NA, rows_a, wide) + plane_scratch(rows_b, 128) + z_scratch(N, rows_b, 128) + z_scratch(*rest),
        compiler_params=pltpu.CompilerParams(vmem_limit_bytes=63 * 2**20, collective_id=4, has_side_effects=True), name="attn_bwd_sum")(
            qkv, qkv, qkv, do, o, r, e, n, x, gres, qkv_w, qkv_w, qkv_w, qkv_w, dn, wo, gain2, gu, to_bucket)

def finish_kernel(gtok_in, out_in, a_in, b_in, c_in, d_in, small_in, at_ref, gtok, out, *rest):
    outs, (gain1, gain2, table), big, sem = rest[:7], rest[7:10], rest[10:17], rest[17]
    q, k, v, wo, gate, up, dn = big
    keeps = [pltpu.make_async_copy(a, b, sem.at[i]) for i, (a, b) in enumerate(zip(big, outs))]
    gtok[...] = gtok_in[...]
    out[...] = out_in[...]
    @pl.when(pl.program_id(0) == 0)
    def _():
        def spread(src, targets):
            n, h, w = src.shape[0], src.shape[1] // 2, src.shape[2]
            for t in range(n):
                at = 0
                for ref in targets:
                    r = ref.shape[0] // 2
                    ref[0:r, w * t:w * t + w] = src[t, at:at + r].astype(f32)
                    ref[r:2 * r, w * t:w * t + w] = src[t, h + at:h + at + r].astype(f32)
                    at += r
        spread(a_in, (dn, wo))
        spread(b_in, (q, k, v))
        r = gate.shape[0]
        w = c_in.shape[2]
        left = c_in.shape[0] - d_in.shape[0]
        for t in range(c_in.shape[0]):
            both = c_in[t] if t < left else d_in[t - left]
            gate[:, w * t:w * t + w] = both[0:r].astype(f32)
            up[:, w * t:w * t + w] = both[r:2 * r].astype(f32)
        me = at_ref[0]
        heads = small_in.shape[0] - 16
        per = heads // 8
        gain1[...] = small_in[pl.ds(heads + me, 1), :]
        gain2[...] = small_in[pl.ds(heads + 8 + me, 1), :]
        rows = small_in[pl.ds(per * me, per), :]
        for t in range(per):
            table[:, BUCKETS * t:BUCKETS * t + BUCKETS] = rows[t:t + 1, 0:BUCKETS]
        for copy in keeps:
            copy.start()
    @pl.when(pl.program_id(0) == pl.num_programs(0) - 1)
    def _():
        for copy in keeps:
            copy.wait()

def finish(gtok, out, a, b, c, last, small, at, rows, ff):
    R, d = gtok.shape
    steps = 4
    sds = jax.ShapeDtypeStruct
    block = pl.BlockSpec((R // steps, d), lambda i: (i, 0))
    one = lambda *s: pl.BlockSpec(s, lambda i: (0,) * len(s), pipeline_mode=pl.Buffered(1))
    whole = lambda x: one(*x.shape)
    shapes = [(rows, d)] * 4 + [(rows, ff)] * 2 + [(ff // 8, d), (1, d // 8), (1, d // 8), (1, (small.shape[0] - 16) // 8 * BUCKETS)]
    return pl.pallas_call(finish_kernel, grid=(steps,),
        in_specs=[block, block, whole(a), whole(b), whole(c), whole(last), whole(small), pl.BlockSpec(memory_space=pltpu.SMEM)],
        out_specs=[block, block] + [pl.BlockSpec(memory_space=pl.ANY)] * 7 + [one(*s) for s in shapes[7:]],
        out_shape=[sds((R, d), f32), sds((R, d), bf)] + [sds(s, f32) for s in shapes],
        scratch_shapes=[pltpu.VMEM(s, f32) for s in shapes[:7]] + [pltpu.SemaphoreType.DMA((7,))],
        compiler_params=pltpu.CompilerParams(vmem_limit_bytes=62 * 2**20), name="finish")(gtok, out, a, b, c, last, small, at)

def contract_rows(left, right):
    return lax.dot_general(left, right, (((0,), (0,)), ((), ())), preferred_element_type=f32)

def contract_cols(left, right):
    return lax.dot_general(left, right, (((1,), (1,)), ((), ())), preferred_element_type=f32)

def rms_norm(inputs, gain):
    return inputs * lax.rsqrt(jnp.mean(inputs * inputs, axis=-1, keepdims=True) + EPS) * gain

def gather(x):
    return lax.all_gather(x, SHARD, axis=0, tiled=False)

def scatter(x):
    return lax.psum_scatter(x, SHARD, scatter_dimension=0, tiled=True)

def per_device(near, tokens, row_kind, text_length, gain_attn, position_bias_table, weight_query, weight_key, weight_value, weight_out, gain_ffn, weight_gate, weight_up, weight_down, cotangent):
    n1, d = weight_query.shape
    n2 = position_bias_table.shape[0]
    inputs = tokens.astype(f32)
    at = lax.axis_index("dp") * lax.axis_size("narrow") + lax.axis_index("narrow")
    if near:
        context, e, r, normed, qkv, qkv_w, gu_w, down_w, out_w = front(
            row_kind, text_length, tokens, gain_attn, gain_ffn, position_bias_table, weight_query, weight_key, weight_value, weight_gate, weight_up, weight_down, weight_out)
    else:
        small = gather(jnp.stack([gain_attn, gain_ffn, jnp.pad(position_bias_table, (0, n1 - n2))]))
        qkv_w = gather(jnp.concatenate([weight_query, weight_key, weight_value], 1))
        gain_one, gain_two = small[:, 0].reshape(d).astype(f32), small[:, 1].reshape(d).astype(f32)
        normed = rms_norm(inputs, gain_one).astype(bf)
        q, k, v = (dot(normed, qkv_w[:, :, t * d:t * d + d].reshape(d, d)).astype(bf) for t in range(3))
        far, w = tables(small[:, 2, :n2].reshape(-1))
        context, e, r = attn_fwd(q, k, v, mask_cols(row_kind, text_length), far, w)
        gu_w, down_w, out_w = jnp.moveaxis(gather(jnp.stack([weight_gate, weight_up])), 0, 1), gather(weight_down), gather(weight_out)
    ff = gu_w.shape[-1]
    output, grad_residual, grad_context, grad_out_w, g_gain_two, ddn, dgu = ffn(
        tokens, context, cotangent, qkv_w if near else gain_two.reshape(1, d), out_w.reshape(d, d), gu_w, down_w.reshape(ff, d), near)
    if near:
        shards = gu_w.shape[1]
        grad_tokens, small_g, sums_a, sums_b, sums_c = attn_bwd_sum(
            qkv, grad_context, context, r, e, normed, tokens, grad_residual, qkv_w,
            ddn.reshape(shards, ff // shards, d), grad_out_w.reshape(shards, n1, d), g_gain_two, dgu)
        grad_tokens, output, s_q, s_k, s_v, s_out, s_gate, s_up, s_down, r_gain_one, r_gain_two, r_table = finish(
            grad_tokens, output, sums_a, sums_b, dgu, sums_c, small_g, at.reshape(1), n1, ff)
        r_gain_one, r_gain_two, r_table = r_gain_one.reshape(n1), r_gain_two.reshape(n1), r_table.reshape(n2)
    else:
        total = lambda x: lax.psum(scatter(x), "batch").astype(f32)
        gq, gk, gv, near_sums, far_sums = attn_bwd(q, k, v, grad_context, context, r, e)
        grads = (gq, gk, gv)
        s_gate, s_up, s_down, s_out = (total(x) for x in (dgu[0].reshape(d, ff), dgu[1].reshape(d, ff), ddn, grad_out_w))
        s_q, s_k, s_v = (total(contract_rows(normed, x).astype(bf)) for x in grads)
        grad_normed = sum(contract_cols(x, qkv_w[:, :, t * d:t * d + d].reshape(d, d)) for t, x in enumerate(grads))
        _, first_pull = jax.vjp(rms_norm, inputs, gain_one)
        share, g_gain_one = first_pull(grad_normed)
        grad_tokens = grad_residual + share
        g_table = table_grad(near_sums, far_sums)
        small_g = lax.psum(jnp.concatenate([g_gain_one, g_gain_two[0], g_table]), ("batch", "dp", "narrow"))
        r_gain_one = lax.dynamic_slice_in_dim(small_g, at * n1, n1)
        r_gain_two = lax.dynamic_slice_in_dim(small_g, d + at * n1, n1)
        r_table = lax.dynamic_slice_in_dim(small_g, 2 * d + at * n2, n2)
    return (output, grad_tokens, r_gain_one, r_table, s_q, s_k, s_v, s_out, r_gain_two, s_gate, s_up, s_down)

def solution(mesh):
    near = (mesh.shape["batch"], mesh.shape["dp"], mesh.shape["narrow"]) == (4, 4, 2)
    placed = (
        P(("batch", "dp", "narrow"), None),
        P(("batch", "dp", "narrow")),
        P(("batch", "dp", "narrow"), None),
        P(("dp", "narrow")),
        P(("dp", "narrow")),
        P(("dp", "narrow"), None),
        P(("dp", "narrow"), None),
        P(("dp", "narrow"), None),
        P(("dp", "narrow"), None),
        P(("dp", "narrow")),
        P(("dp", "narrow"), None),
        P(("dp", "narrow"), None),
        P(("dp", "narrow"), None),
        P(("batch", "dp", "narrow"), None),
    )
    return jax.shard_map(
        functools.partial(per_device, near),
        mesh=mesh,
        in_specs=placed,
        out_specs=(
            P(("batch", "dp", "narrow"), None),
            P(("batch", "dp", "narrow"), None),
            P(("dp", "narrow")),
            P(("dp", "narrow")),
            P(("dp", "narrow"), None),
            P(("dp", "narrow"), None),
            P(("dp", "narrow"), None),
            P(("dp", "narrow"), None),
            P(("dp", "narrow")),
            P(("dp", "narrow"), None),
            P(("dp", "narrow"), None),
            P(("dp", "narrow"), None),
        ),
        check_vma=False,
    )
```

```python
import functools

import jax
import jax.numpy as jnp
import numpy as np
from jax import lax
from jax.experimental import pallas as pl
from jax.experimental.pallas import tpu as pltpu
from jax.sharding import PartitionSpec as P

EPS = 1e-06
SHARD = ("dp", "narrow")
BUCKETS = 32
bf=jnp.bfloat16; f32=jnp.float32
T=128; L=1152; NT=L//T
NEG=-1e30
def dot(a,b): return jnp.dot(a,b,preferred_element_type=f32)
def dot_tl(a,b): return lax.dot_general(a,b,(((0,),(0,)),((),())),preferred_element_type=f32)

def fwd_open(rhs,vaug):
    rhs[...]=jnp.zeros_like(rhs)
    row=lax.broadcasted_iota(jnp.int32,(128,NT*256),0)
    col=lax.broadcasted_iota(jnp.int32,(128,NT*256),1)
    rhs[128:256,:]=(row==col//128).astype(f32).astype(bf)
    vaug[:,128:256]=jnp.ones((L,128),bf)

def fwd_pair(q,k,v,mask,lo,hi,bias,o_ref,e_ref,r_ref,rhs,kaug,vaug,bn,s_ref):
    qT=q.T
    for i in range(NT):
        rhs[0:64,256*i:256*i+128]=qT[0:64,128*i:128*i+128]
        rhs[64:128,256*i+128:256*i+256]=qT[64:128,128*i:128*i+128]
    kaug[:,0:128]=k
    row=lax.broadcasted_iota(jnp.int32,(L,128),0)//128
    col=lax.broadcasted_iota(jnp.int32,(L,128),1)//2
    far=jnp.where(row<col-1,lo,jnp.where(row>col+1,hi,0.0))
    kaug[:,128:256]=(mask+far).astype(bf)
    vaug[:,0:128]=v
    for a in range(2):
        wb=jnp.broadcast_to(bias[a:a+1,:],(384,512))
        bn[:,128*a:128*a+128]=pltpu.roll(wb,0,1,stride=1,stride_axis=0)[:,0:128]
    def scores(i,slot):
        ri=rhs[:,256*i:256*i+256]
        first,last=max(0,i-1)*128,min(NT,i+2)*128
        off=(first//128-(i-1))*128
        x=dot(kaug[...],ri)
        xn=x[first:last]+bn[off:off+last-first,:]
        ms=[jnp.max(xn,axis=0,keepdims=True)]
        s_ref[slot,first:last,:]=xn
        if first>0:
            s_ref[slot,0:first,:]=x[0:first]; ms.append(jnp.max(x[0:first],axis=0,keepdims=True))
        if last<L:
            s_ref[slot,last:L,:]=x[last:L]; ms.append(jnp.max(x[last:L],axis=0,keepdims=True))
        m=ms[0]
        for y in ms[1:]: m=jnp.maximum(m,y)
        return m
    lane=lax.broadcasted_iota(jnp.int32,(128,128),1)<64
    def finish(i,slot,m):
        e=jnp.exp(s_ref[slot]-m).astype(bf)
        e_ref[:,pl.ds(i*256,256)]=e
        o=dot_tl(e,vaug[...])
        num=jnp.where(lane,o[0:128,0:128],o[128:256,0:128])
        den=jnp.where(lane,o[0:128,128:256],o[128:256,128:256])
        r=1.0/den
        rows=pl.ds(i*128,128)
        o_ref[rows,:]=(num*r).astype(bf)
        r_ref[rows,:]=r
    m=scores(0,0)
    for i in range(NT):
        mn=scores(i+1,(i+1)%2) if i+1<NT else None
        finish(i,i%2,m)
        m=mn

def fwd_kernel(q_ref,k_ref,v_ref,mask_ref,far_ref,w_ref,o_ref,e_ref,r_ref,rhs,kaug,vaug,bn,s_ref):
    @pl.when((pl.program_id(0)==0)&(pl.program_id(1)==0))
    def _():
        fwd_open(rhs,vaug)
    fwd_pair(q_ref[...],k_ref[...],v_ref[...],mask_ref[...],far_ref[0:1,:],far_ref[1:2,:],w_ref[...],o_ref,e_ref,r_ref,rhs,kaug,vaug,bn,s_ref)

def attn_fwd(q,k,v,mask,far,w):
    rows=q.shape[0]//L
    spec=pl.BlockSpec((L,128),lambda r,p:(r,p))
    return pl.pallas_call(fwd_kernel,
        grid=(rows,8),
        in_specs=[spec,spec,spec,
            pl.BlockSpec((None,L,128),lambda r,p:(r,0,0)),
            pl.BlockSpec((None,8,128),lambda r,p:(p,0,0)),
            pl.BlockSpec((None,8,512),lambda r,p:(p,0,0))],
        out_specs=[spec,pl.BlockSpec((None,None,L,NT*256),lambda r,p:(r,p,0,0)),spec],
        out_shape=[jax.ShapeDtypeStruct(q.shape,bf),jax.ShapeDtypeStruct((rows,8,L,NT*256),bf),jax.ShapeDtypeStruct(q.shape,f32)],
        scratch_shapes=[pltpu.VMEM((256,NT*256),bf),pltpu.VMEM((L,256),bf),pltpu.VMEM((L,256),bf),pltpu.VMEM((384,256),f32),pltpu.VMEM((2,L,256),f32)],
        compiler_params=pltpu.CompilerParams(vmem_limit_bytes=56*2**20),
        name="attn_fwd",
    )(q,k,v,mask,far,w)

THR=(12,16,23,32,46,64,91)
def bucket_np(d):
    n=np.abs(d); c=np.full_like(n,8)
    for t in THR: c=c+(n>=t)
    return np.where(n<8,n,c)+16*(d>0)
def tables(table):
    t=table.reshape(16,32).astype(f32)
    y=np.arange(512); y=np.where(y>=128,y-512,y)
    d=-128-y
    oh=(np.arange(32)[:,None]==bucket_np(d)[None,:]).astype(np.float32)
    w=jnp.dot(t,jnp.asarray(oh),precision=lax.Precision.HIGHEST)
    w=jnp.pad(w.reshape(8,2,512),((0,0),(0,6),(0,0)))
    lo=jnp.tile(t[:,15].reshape(8,1,2),(1,1,64)); hi=jnp.tile(t[:,31].reshape(8,1,2),(1,1,64))
    far=jnp.pad(jnp.concatenate([lo,hi],1),((0,0),(0,6),(0,0)))
    return far,w
def mask_cols(row_kind,text_length):
    pos=np.arange(L)
    kind=row_kind[:,None]
    seg=kind*(pos//384)[None]
    off=pos[None]-seg*384
    img=jnp.where(kind==1,256,1024)
    tl=jnp.where(seg==0,text_length[:,0:1],jnp.where(seg==1,text_length[:,1:2],text_length[:,2:3]))
    live=off<img+tl
    qseg=kind*np.minimum(np.arange(128)//2//3,2)[None]
    ok=live[:,:,None]&(seg[:,:,None]==qseg[:,None,:])
    return jnp.where(ok,0.0,NEG).astype(f32)

def bwd_open(rhs,vaug,qaug):
    rhs[...]=jnp.zeros_like(rhs)
    c=lax.broadcasted_iota(jnp.int32,(L,128),1)
    vaug[:,128:256]=(c<3).astype(f32).astype(bf)
    row=lax.broadcasted_iota(jnp.int32,(NT*256,128),0)
    col=lax.broadcasted_iota(jnp.int32,(NT*256,128),1)
    qaug[:,128:256]=(row//128==col).astype(f32).astype(bf)

def bwd_pair(q_ref,k_ref,v_ref,do_ref,o_ref,r_ref,e_ref,near_ref,far_ref,rhs,vaug,dobd,qaug,ds_ref,nacc):
    q=q_ref[...]; k=k_ref[...]
    vaug[:,0:128]=v_ref[...]
    dof=do_ref[...].astype(f32)*r_ref[...]
    dos=dof.astype(bf)
    dT=dos.T
    pT=(dos.astype(f32)*o_ref[...].astype(f32)).T
    D=jnp.concatenate([jnp.sum(pT[0:64],axis=0,keepdims=True),jnp.sum(pT[64:128],axis=0,keepdims=True)],0)
    D=-D
    D1=D.astype(bf); D2=(D-D1.astype(f32)); D3=(D2-D2.astype(bf).astype(f32)).astype(bf); D2=D2.astype(bf)
    lane=lax.broadcasted_iota(jnp.int32,(128,128),1)<64
    zero=jnp.zeros((128,128),bf)
    z13=jnp.zeros((13,128),bf)
    for i in range(NT):
        t=slice(128*i,128*i+128)
        for a in range(2):
            h=slice(64*a,64*a+64)
            c=slice(256*i+128*a,256*i+128*a+128)
            rhs[h,c]=dT[h,t]
            rhs[128:144,c]=jnp.concatenate([D1[a:a+1,t],D2[a:a+1,t],D3[a:a+1,t],z13],0)
            dobd[c,:]=jnp.where(lane==(a==0),dos[t],zero)
            qaug[c,0:128]=jnp.where(lane==(a==0),q[t],zero)
    nacc[...]=jnp.zeros_like(nacc)
    dqs=[]
    for i in range(NT):
        c=slice(256*i,256*i+256)
        lo,hi=max(0,i-1)*128,min(NT,i+2)*128
        off=(lo//128-(i-1))*128
        dp=dot(vaug[...],rhs[:,c])
        ds=e_ref[:,c].astype(f32)*dp
        nacc[off:off+hi-lo,:]+=ds[lo:hi]
        dsb=ds.astype(bf)
        ds_ref[:,c]=dsb
        g=dot_tl(dsb,k)
        dqs.append(jnp.where(lane,g[0:128],g[128:256]).astype(bf))
    dv=dot(e_ref[...],dobd[...]).astype(bf)
    g=dot(ds_ref[...],qaug[...])
    dk=g[:,0:128].astype(bf)
    G=g[:,128:256]
    row=lax.broadcasted_iota(jnp.int32,(L,128),0)//128
    col=lax.broadcasted_iota(jnp.int32,(L,128),1)//2
    far_ref[0:1,:]=jnp.sum(jnp.where(row<col-1,G,0.0),axis=0,keepdims=True)
    far_ref[1:2,:]=jnp.sum(jnp.where(row>col+1,G,0.0),axis=0,keepdims=True)
    far_ref[2:8,:]=jnp.zeros((6,128),f32)
    near_ref[2:8,:]=jnp.zeros((6,512),f32)
    rev=(lax.broadcasted_iota(jnp.int32,(128,128),0)+lax.broadcasted_iota(jnp.int32,(128,128),1)==127).astype(f32)
    for a in range(2):
        x=jnp.dot(nacc[:,128*a:128*a+128],rev,precision=lax.Precision.HIGHEST,preferred_element_type=f32)
        x=jnp.concatenate([x,jnp.zeros((384,384),f32)],1)
        x=pltpu.roll(x,0,1,stride=1,stride_axis=0)
        near_ref[a:a+1,:]=jnp.sum(x,axis=0,keepdims=True)
    return jnp.concatenate(dqs,0),dk,dv

def bwd_kernel(q_ref,k_ref,v_ref,do_ref,o_ref,r_ref,e_ref,dq_ref,dk_ref,dv_ref,near_ref,far_ref,rhs,vaug,dobd,qaug,ds_ref,nacc):
    @pl.when((pl.program_id(0)==0)&(pl.program_id(1)==0))
    def _():
        bwd_open(rhs,vaug,qaug)
    dq_ref[...],dk_ref[...],dv_ref[...]=bwd_pair(q_ref,k_ref,v_ref,do_ref,o_ref,r_ref,e_ref,near_ref,far_ref,rhs,vaug,dobd,qaug,ds_ref,nacc)

def attn_bwd(q,k,v,do,o,r,e):
    rows=q.shape[0]//L
    spec=pl.BlockSpec((L,128),lambda r,p:(r,p))
    sds=jax.ShapeDtypeStruct
    return pl.pallas_call(bwd_kernel,
        grid=(rows,8),
        in_specs=[spec]*6+[pl.BlockSpec((None,None,L,NT*256),lambda r,p:(r,p,0,0))],
        out_specs=[spec]*3+[pl.BlockSpec((None,None,8,512),lambda r,p:(r,p,0,0)),pl.BlockSpec((None,None,8,128),lambda r,p:(r,p,0,0))],
        out_shape=[sds(q.shape,bf)]*3+[sds((rows,8,8,512),f32),sds((rows,8,8,128),f32)],
        scratch_shapes=[pltpu.VMEM((256,NT*256),bf),pltpu.VMEM((L,256),bf),pltpu.VMEM((NT*256,128),bf),pltpu.VMEM((NT*256,256),bf),pltpu.VMEM((L,NT*256),bf),pltpu.VMEM((384,256),f32)],
        compiler_params=pltpu.CompilerParams(vmem_limit_bytes=58*2**20),
        name="attn_bwd",
    )(q,k,v,do,o,r,e)
def table_grad(near,far):
    y=np.arange(512)
    oh=(bucket_np(y-255)[:,None]==np.arange(32)[None,:]).astype(np.float32)
    n=jnp.sum(near[:,:,0:2],0).reshape(16,512)
    g=jnp.dot(n,jnp.asarray(oh),precision=lax.Precision.HIGHEST)
    f=jnp.sum(far[:,:,0:2],0).reshape(8,2,64,2).sum(2)
    lo=f[:,0].reshape(16,1); hi=f[:,1].reshape(16,1)
    g=g+lo*np.eye(32,dtype=np.float32)[15][None]+hi*np.eye(32,dtype=np.float32)[31][None]
    return g.reshape(512)

MESH = pl.DeviceIdType.MESH

def places():
    b, m, c = lax.axis_index("batch"), lax.axis_index("dp"), lax.axis_index("narrow")
    x, y = lax.rem(m, 2), m // 2
    mx = y * 2 + (1 - x)
    my = (1 - y) * 2 + x
    md = (1 - y) * 2 + (1 - x)
    return b, m, c, mx, my, md

def greet(devices):
    barrier = pltpu.get_barrier_semaphore()
    for d in devices:
        pl.semaphore_signal(barrier, inc=1, device_id=d, device_id_type=MESH)
    pl.semaphore_wait(barrier, len(devices))

def gather_steps(gu_in, dn_in, wo_in, gu, dn, wo, send, recv, local):
    b, m, c, mx, my, md = places()
    o = 1 - c
    z = lax.rem(b, 2)
    oz = 1 - z
    nx, ny, nc, nz = (b, mx, c), (b, my, c), (b, m, o), (b + 1 - 2 * z, m, c)
    me, it = m * 2 + c, m * 2 + o
    ix, iy, idg = mx * 2 + c, my * 2 + c, md * 2 + c
    jx, jy, jdg = mx * 2 + o, my * 2 + o, md * 2 + o
    def copy(src, dst, n, to):
        return pltpu.make_async_remote_copy(src_ref=src, dst_ref=dst, send_sem=send.at[n], recv_sem=recv.at[n], device_id=to, device_id_type=MESH)
    def push(ref, n, to):
        return copy(ref, ref, n, to)
    def got(ref, n):
        copy(ref, ref, n, nc).wait_recv()
    def first(src, dst, n):
        for t, to in enumerate((nx, ny, nc)):
            copy(src, dst, n + t, to).start()
    def halves(ref, i):
        h = ref.shape[1] // 2
        return ref.at[i, pl.ds(0, h)], ref.at[i, pl.ds(h, h)]
    def second(ref, n, onward=None):
        got(ref.at[ix], n)
        push(halves(ref, ix)[0], n + 3, ny).start()
        push(ref.at[ix], n + 5, nc).start()
        if onward is not None:
            push(ref.at[ix], onward, nz).start()
        got(ref.at[iy], n + 1)
        push(halves(ref, iy)[1], n + 4, nx).start()
        push(ref.at[iy], n + 6, nc).start()
        if onward is not None:
            push(ref.at[iy], onward + 1, nz).start()
    def third(ref, n, onward=None):
        got(halves(ref, idg)[0], n + 3)
        got(halves(ref, idg)[1], n + 4)
        push(ref.at[idg], n + 7, nc).start()
        if onward is not None:
            push(ref.at[idg], onward + 2, nz).start()
    def last(src, ref, n, onward=None):
        for t, i in ((2, it), (5, jx), (6, jy), (7, jdg)):
            got(ref.at[i], n + t)
        for t in (0, 1, 2):
            copy(src, ref.at[me], n + t, nc).wait_send()
        push(halves(ref, ix)[0], n + 3, ny).wait_send()
        push(halves(ref, iy)[1], n + 4, nx).wait_send()
        for t, i in ((5, ix), (6, iy), (7, idg)):
            push(ref.at[i], n + t, nc).wait_send()
        if onward is not None:
            for t, i in enumerate((ix, iy, idg)):
                push(ref.at[i], onward + t, nz).wait_send()
    def part(ref, i):
        cut = ref.shape[-1] // 384 * 128
        return ref.at[..., pl.ds(0, cut)] if i == 0 else ref.at[..., pl.ds(cut, ref.shape[-1] - cut)]
    mine, other = gu.at[z], gu.at[oz]
    m0, m1, o0, o1 = part(mine, 0), part(mine, 1), part(other, 0), part(other, 1)
    in0, in1 = part(gu_in.at[z], 0), part(gu_in.at[z], 1)
    d0, d1, dn0, dn1 = part(dn, 0), part(dn, 1), part(dn_in, 0), part(dn_in, 1)
    keeps = [pltpu.make_async_copy(gu_in.at[0], gu.at[0, me], local.at[0]), pltpu.make_async_copy(gu_in.at[1], gu.at[1, me], local.at[1]),
             pltpu.make_async_copy(dn_in, dn.at[me], local.at[2]), pltpu.make_async_copy(wo_in, wo.at[me], local.at[3])]
    W, D0, D1, G0, G1, Z0, Z1, OWN = 0, 8, 16, 24, 32, 40, 46, 52
    def z_second(ref, n, ts):
        for t in ts:
            i = (ix, iy, idg)[t]
            got(ref.at[i], n + t)
            push(ref.at[i], n + 3 + t, nc).start()
    def begin():
        first(in0, m0.at[me], G0)
        first(in1, m1.at[me], G1)
        copy(gu_in.at[oz], other.at[me], OWN, nc).start()
        for k in keeps:
            k.start()
    def at0():
        second(m0, G0, Z0)
        first(dn0, d0.at[me], D0)
    def at2():
        second(m1, G1, Z1)
        third(m0, G0, Z0)
        first(dn1, d1.at[me], D1)
    def at3():
        second(d0, D0)
        first(wo_in, wo.at[me], W)
    def at4():
        third(m1, G1, Z1)
        z_second(o0, Z0, (0, 1))
    def at6():
        second(d1, D1)
        third(d0, D0)
    def end():
        z_second(o1, Z1, (0, 1))
        z_second(o0, Z0, (2,))
        second(wo, W)
        third(d1, D1)
        third(wo, W)
        z_second(o1, Z1, (2,))
        last(wo_in, wo, W)
        last(in0, m0, G0, Z0)
        last(in1, m1, G1, Z1)
        got(other.at[it], OWN)
        copy(gu_in.at[oz], other.at[me], OWN, nc).wait_send()
        for ref, n in ((o0, Z0), (o1, Z1)):
            for t, i, j in ((0, ix, jx), (1, iy, jy), (2, idg, jdg)):
                got(ref.at[j], n + 3 + t)
                push(ref.at[i], n + 3 + t, nc).wait_send()
        last(dn0, d0, D0)
        last(dn1, d1, D1)
        for k in keeps:
            k.wait()
    return begin, {1: at0, 3: at2, 4: at3, 5: at4, 7: at6}, end


def bias_consts():
    y = np.arange(512)
    y = np.where(y >= 128, y - 512, y)
    ids = bucket_np(-128 - y)
    out = np.zeros((128, 1280), np.float32)
    for a in range(2):
        out[32 * a + ids, 512 * a + np.arange(512)] = 1
        out[32 * a + 15, 1024 + a:1152:2] = 1
        out[32 * a + 31, 1152 + a:1280:2] = 1
    return jnp.asarray(out, bf)

def mask_block(kind, text):
    pos = lax.broadcasted_iota(jnp.int32, (L, 128), 0)
    tile = lax.broadcasted_iota(jnp.int32, (L, 128), 1) // 2
    seg = jnp.where(kind == 1, pos // 384, 0)
    mine = jnp.where(kind == 1, tile // 3, 0)
    length = jnp.where(seg == 0, text[0], jnp.where(seg == 1, text[1], text[2]))
    live = pos - seg * 384 < jnp.where(kind == 1, 256, 1024) + length
    return jnp.where(live & (seg == mine), 0.0, NEG)

def front_kernel(kind_ref, text_ref, x_hbm, gain1_ref, gain2_ref, table_ref, wq_ref, wk_ref, wv_ref, gate_hbm, up_hbm, dn_hbm, wo_hbm, const_ref,
                 o_ref, e_ref, r_ref, n_ref, qkv_out, w_out, gu, dn, wo,
                 W, acc, rstd, qkv, gu_in, x_ref, dn_in, wo_in, loads, mask, rhs, kaug, vaug, bn, s_ref, wsend, wrecv, wlocal, send, recv, local):
    b, m, c, mx, my, md = places()
    o = 1 - c
    nx, ny, nc, nz = (b, mx, c), (b, my, c), (b, m, o), (b + 1 - 2 * lax.rem(b, 2), m, c)
    d = wq_ref.shape[1]
    rows = wq_ref.shape[0]
    half = rows // 2
    me = m * 2 + c
    p = pl.program_id(0)
    begin, during, end = gather_steps(gu_in, dn_in, wo_in, gu, dn, wo, send, recv, local)
    keeps = (pltpu.make_async_copy(W, w_out, wlocal.at[0]), pltpu.make_async_copy(qkv, qkv_out, wlocal.at[1]))
    fetch = [pltpu.make_async_copy(a, z, loads.at[i]) for i, (a, z) in enumerate(((x_hbm, x_ref), (gate_hbm, gu_in.at[0]), (up_hbm, gu_in.at[1]), (dn_hbm, dn_in), (wo_hbm, wo_in)))]
    def push(src, n, to):
        return pltpu.make_async_remote_copy(src_ref=src, dst_ref=src, send_sem=wsend.at[n], recv_sem=wrecv.at[n], device_id=to, device_id_type=MESH)
    def got(ref, n):
        push(ref, n, nc).wait_recv()
    def chunk(j, first):
        cols = pl.ds(pl.multiple_of(j * 2 * rows, 2 * rows), 2 * rows)
        gain = jnp.concatenate([W[2 * j, 0:1, 3 * d:3 * d + rows], W[2 * j + 1, 0:1, 3 * d:3 * d + rows]], 1).astype(f32)
        n = (x_ref[:, cols].astype(f32) * rstd[...] * gain).astype(bf)
        n_ref[:, cols] = n
        for t in range(3):
            y = dot(n, W[pl.ds(2 * j, 2), :, t * d:t * d + d].reshape(2 * rows, d))
            if first:
                acc[:, t * d:t * d + d] = y
            else:
                acc[:, t * d:t * d + d] = acc[:, t * d:t * d + d] + y
    @pl.when(p == 0)
    def _():
        for f in fetch:
            f.start()
        W[me, :, 0:d] = wq_ref[...]
        W[me, :, d:2 * d] = wk_ref[...]
        W[me, :, 2 * d:3 * d] = wv_ref[...]
        W[me, :, 3 * d:3 * d + 128] = jnp.zeros((rows, 128), bf)
        W[me, 0:1, 3 * d:3 * d + rows] = gain1_ref[...]
        W[me, 1:2, 3 * d:3 * d + rows] = gain2_ref[...]
        W[me, 2:3, 3 * d:3 * d + table_ref.shape[1]] = table_ref[...]
        greet([nx, ny, nc, nz])
        top, low = pl.ds(0, half), pl.ds(half, half)
        sends = [push(W.at[me], 0, nx), push(W.at[me], 1, ny), push(W.at[me], 2, nc)]
        for s in sends:
            s.start()
        for f in fetch:
            f.wait()
        for t in range(0, L, 384):
            x = x_ref[t:t + 384, :].astype(f32)
            rstd[t:t + 384, :] = lax.rsqrt(jnp.mean(x * x, axis=-1, keepdims=True) + EPS)
        mask[...] = mask_block(kind_ref[0], (text_ref[0, 0], text_ref[0, 1], text_ref[0, 2]))
        fwd_open(rhs, vaug)
        ix, iy, idg = mx * 2 + c, my * 2 + c, md * 2 + c
        jx, jy, jdg = mx * 2 + o, my * 2 + o, md * 2 + o
        got(W.at[m * 2 + o], 2)
        chunk(m, True)
        got(W.at[ix], 0)
        more = [push(W.at[ix, top], 3, ny), push(W.at[ix], 5, nc)]
        got(W.at[iy], 1)
        more += [push(W.at[iy, low], 4, nx), push(W.at[iy], 6, nc)]
        for s in more:
            s.start()
        begin()
        got(W.at[jx], 5)
        chunk(mx, False)
        got(W.at[jy], 6)
        chunk(my, False)
        got(W.at[idg, top], 3)
        got(W.at[idg, low], 4)
        more.append(push(W.at[idg], 7, nc))
        more[-1].start()
        got(W.at[jdg], 7)
        keeps[0].start()
        chunk(md, False)
        for t in range(3 * d // 128):
            qkv[t] = acc[:, 128 * t:128 * t + 128].astype(bf)
        keeps[1].start()
        for s in sends + more:
            s.wait_send()
    for at, act in during.items():
        pl.when(p == at)(act)
    @pl.when(p > 0)
    def _():
        h = p - 1
        N = d // 128
        values = jnp.broadcast_to(W[h, 2:3, 3 * d:3 * d + 128], (16, 128))
        bias = dot(values, const_ref[...])
        fwd_pair(qkv[h], qkv[N + h], qkv[2 * N + h], mask[...], bias[0:1, 1024:1152], bias[0:1, 1152:1280],
                 jnp.concatenate([bias[0:1, 0:512], bias[0:1, 512:1024]], 0), o_ref, e_ref, r_ref, rhs, kaug, vaug, bn, s_ref)
    @pl.when(p == pl.num_programs(0) - 1)
    def _():
        end()
        for k in keeps:
            k.wait()

def front(kind, text, x, gain1, gain2, table, wq, wk, wv, gate, up, dn, wo):
    R, d = x.shape
    rows = wq.shape[0]
    N = d // 128
    at = lambda p: jnp.maximum(p - 1, 0)
    spec = pl.BlockSpec((R, 128), lambda p: (0, at(p)))
    hbm = pl.BlockSpec(memory_space=pl.ANY)
    whole = lambda a: pl.BlockSpec(a.shape, lambda p: (0,) * a.ndim, pipeline_mode=pl.Buffered(1))
    smem = pl.BlockSpec(memory_space=pltpu.SMEM)
    sds = jax.ShapeDtypeStruct
    dma = pltpu.SemaphoreType.DMA
    row = lambda a: a.reshape(1, -1)
    vectors = (x, row(gain1), row(gain2), row(table), wq, wk, wv, gate, up, dn, wo, bias_consts())
    wide = 3 * d + 128
    return pl.pallas_call(front_kernel, grid=(1 + N,),
        in_specs=[smem, smem] + [hbm if i in (0, 7, 8, 9, 10) else whole(a) for i, a in enumerate(vectors)],
        out_specs=[spec, pl.BlockSpec((None, None, R, NT * 256), lambda p: (0, at(p), 0, 0)), spec,
                   pl.BlockSpec((R, d), lambda p: (0, 0), pipeline_mode=pl.Buffered(1))] + [hbm] * 5,
        out_shape=[sds((R, d), bf), sds((1, N, R, NT * 256), bf), sds((R, d), f32), sds((R, d), bf), sds((3 * N, R, 128), bf),
                   sds((8, rows, wide), bf), sds((2, 8) + gate.shape, bf), sds((8,) + dn.shape, bf), sds((8,) + wo.shape, bf)],
        scratch_shapes=[pltpu.VMEM((8, rows, wide), bf), pltpu.VMEM((R, 3 * d), f32), pltpu.VMEM((R, 1), f32), pltpu.VMEM((3 * N, R, 128), bf),
                        pltpu.VMEM((2,) + gate.shape, bf), pltpu.VMEM((R, d), bf), pltpu.VMEM(dn.shape, bf), pltpu.VMEM(wo.shape, bf), dma((5,)), pltpu.VMEM((R, 128), f32),
                        pltpu.VMEM((256, NT * 256), bf), pltpu.VMEM((R, 256), bf), pltpu.VMEM((R, 256), bf), pltpu.VMEM((384, 256), f32), pltpu.VMEM((2, R, 256), f32),
                        dma((8,)), dma((8,)), dma((2,)), dma((53,)), dma((53,)), dma((4,))],
        compiler_params=pltpu.CompilerParams(collective_id=1, has_side_effects=True, vmem_limit_bytes=63 * 2**20),
        name="front")(kind, text, *vectors)

DRAIN = 6

def plane_scratch(rows, cols):
    h = rows // 2
    pair = pltpu.VMEM((2, 2, h, cols), bf)
    single = pltpu.VMEM((2, h, cols), bf)
    dma = pltpu.SemaphoreType.DMA
    return [pltpu.VMEM((2, 4, 2, rows, cols), bf), pltpu.VMEM((2, 4, rows, cols), bf)] + [pair] * 6 + [single] * 2 + [dma((5, 2)), dma((5, 2))]

def z_scratch(n, rows, cols):
    ring = lambda k: pltpu.VMEM((k, rows, cols), bf)
    dma = pltpu.SemaphoreType.DMA
    return [ring(4), ring(4), ring(2), ring(n), dma((3, n)), dma((3, n))]

def plus(a, b):
    return a + b

def rs_greet():
    b, m, c, mx, my, md = places()
    greet([(b, mx, c), (b, my, c), (b, m, 1 - c), (b + 1 - 2 * lax.rem(b, 2), m, c), (3 - b, m, c)])

def stage(t, n, act, also=None):
    live = (t >= 0) & (t < n)
    pl.when(live if also is None else live & also)(lambda: act(t))

def plane_step(s, n, bufs, put):
    src, cbuf, sx, sy, kt, kb, xt, yb, t2, b2, send, recv = bufs
    b, m, c, mx, my, md = places()
    o = 1 - c
    nx, ny, nc = (b, mx, c), (b, my, c), (b, m, o)
    h = kt.shape[2]
    def copy(kind, k, a, z, to):
        return pltpu.make_async_remote_copy(src_ref=a, dst_ref=z, send_sem=send.at[kind, k], recv_sem=recv.at[kind, k], device_id=to, device_id_type=MESH)
    core = lambda k: copy(0, k, src.at[k, :, o], cbuf.at[k], nc)
    x1 = lambda k: copy(1, k, sx.at[k], xt.at[k], nx)
    y1 = lambda k: copy(2, k, sy.at[k], yb.at[k], ny)
    y2 = lambda k: copy(3, k, kt.at[k, 1], t2.at[k], ny)
    x2 = lambda k: copy(4, k, kb.at[k, 1], b2.at[k], nx)
    def third(t):
        k = lax.rem(t, 2)
        y2(k).wait()
        x2(k).wait()
        put(t, plus(kt[k, 0], t2[k]), plus(kb[k, 0], b2[k]))
    def second(t):
        k = lax.rem(t, 2)
        x1(k).wait()
        y1(k).wait()
        kt[k] = plus(kt[k], xt[k])
        kb[k] = plus(kb[k], yb[k])
        y2(k).start()
        x2(k).start()
    def first(t):
        k = lax.rem(t, 2)
        core(k).wait()
        top = lambda i: plus(src[k, i, c, 0:h], cbuf[k, i, 0:h])
        low = lambda i: plus(src[k, i, c, h:2 * h], cbuf[k, i, h:2 * h])
        sx[k, 0], sx[k, 1] = top(mx), top(md)
        sy[k, 0], sy[k, 1] = low(my), low(md)
        x1(k).start()
        y1(k).start()
        kt[k, 0], kt[k, 1] = top(m), top(my)
        kb[k, 0], kb[k, 1] = low(m), low(mx)
    stage(s - 3, n, third)
    stage(s - 2, n, second)
    stage(s - 1, n, first)
    stage(s, n, lambda t: core(lax.rem(t, 2)).start())

def z_step(s, n, bufs, before):
    part, inward, across, done, send, recv = bufs
    b, m, c, mx, my, md = places()
    nz, na = (b + 1 - 2 * lax.rem(b, 2), m, c), (3 - b, m, c)
    outer = (b == 0) | (b == 3)
    inner = (b == 1) | (b == 2)
    def copy(kind, t, a, z, to):
        return pltpu.make_async_remote_copy(src_ref=a, dst_ref=z, send_sem=send.at[kind, t], recv_sem=recv.at[kind, t], device_id=to, device_id_type=MESH)
    up = lambda t: copy(0, t, part.at[lax.rem(t, 4)], inward.at[lax.rem(t, 4)], nz)
    over = lambda t: copy(1, t, part.at[lax.rem(t, 4)], across.at[lax.rem(t, 2)], na)
    down = lambda t: copy(2, t, done.at[t], done.at[t], nz)
    def outer_done(t):
        up(t).wait_send()
        down(t).wait_recv()
    def inner_done(t):
        down(t).wait_send()
    def inner_sum(t):
        over(t).wait()
        done[t] = plus(part[lax.rem(t, 4)], across[lax.rem(t, 2)])
        down(t).start()
    def inner_part(t):
        up(t).wait_recv()
        part[lax.rem(t, 4)] = plus(part[lax.rem(t, 4)], inward[lax.rem(t, 4)])
        over(t).start()
    stage(s - 3, n, outer_done, outer)
    stage(s - 3, n, inner_done, inner)
    stage(s - 2, n, inner_sum, inner)
    stage(s - 1, n, inner_part, inner)
    before()
    stage(s, n, lambda t: up(t).start(), outer)

def sum_step(s, n, plane, z):
    h = plane[4].shape[2]
    part = z[0]
    def put(t, top, low):
        part[lax.rem(t, 4), 0:h] = top
        part[lax.rem(t, 4), h:2 * h] = low
    z_step(s - 3, n, z, lambda: plane_step(s, n, plane, put))

GELU_C = float(np.sqrt(2.0 / np.pi))
def dot_nt(a, b):
    return lax.dot_general(a, b, (((1,), (1,)), ((), ())), preferred_element_type=f32)

def ffn_open(x_ref, ctx_ref, gain_ref, wo_ref, gres_ref, res, n, acc):
    for t in range(0, x_ref.shape[0], 384):
        s = slice(t, t + 384)
        y = x_ref[s, :].astype(f32) + dot(ctx_ref[s, :], wo_ref[...])
        res[s, :] = y
        acc[s, :] = y
        n[s, :] = (y * lax.rsqrt(jnp.mean(y * y, axis=-1, keepdims=True) + EPS) * gain_ref[0:1, :]).astype(bf)
    gres_ref[...] = jnp.zeros_like(gres_ref)

def ffn_block(g_ref, gu_ref, dn_ref, gres_ref, ddn_ref, n, acc):
    d = n.shape[1]
    wg = gu_ref[0].reshape(d, gu_ref.shape[-1])
    wu = gu_ref[1].reshape(d, gu_ref.shape[-1])
    wd = dn_ref[...]
    nn = n[...]
    g = g_ref[...]
    v = dot(nn, wg)
    u = dot(nn, wu)
    gh = dot_nt(g, wd)
    v2 = v * v
    th = jnp.tanh(GELU_C * v * (1.0 + 0.044715 * v2))
    half = 0.5 * (1.0 + th)
    gel = v * half
    h = (gel * u).astype(bf)
    dgel = half + 0.5 * v * (1.0 - th * th) * (GELU_C * (1.0 + 3 * 0.044715 * v2))
    gg = (gh * u * dgel).astype(bf)
    gu = (gh * gel).astype(bf)
    acc[...] = acc[...] + dot(h, wd)
    gres_ref[...] = gres_ref[...] + dot_nt(jnp.concatenate([gg, gu], 1), jnp.concatenate([wg, wu], 1))
    ddn_ref[...] = dot_tl(h, g).astype(bf)
    return dot_tl(nn, gg).astype(bf), dot_tl(nn, gu).astype(bf)

def ffn_close(s, g_ref, gain_ref, wo_ref, out_ref, gres_ref, gctx_ref, res, n, acc):
    out_ref[s, :] = acc[s, :].astype(bf)
    y = res[s, :]
    r = lax.rsqrt(jnp.mean(y * y, axis=-1, keepdims=True) + EPS)
    m = y * r
    gn = gres_ref[s, :]
    w = gn * gain_ref[0:1, :]
    gr = g_ref[s, :].astype(f32) + r * (w - m * jnp.mean(w * m, axis=-1, keepdims=True))
    gres_ref[s, :] = gr
    low = gr.astype(bf)
    n[s, :] = low
    gctx_ref[s, :] = dot_nt(low, wo_ref[...]).astype(bf)
    return jnp.sum(gn * m, axis=0, keepdims=True)

def ffn_kernel(x_ref, ctx_ref, g_ref, gain_ref, wo_ref, gu_ref, dn_ref,
               out_ref, gres_ref, gctx_ref, dwo_ref, ggain_ref, ddn_ref, dgu_ref, res, n, acc):
    j = pl.program_id(0)
    @pl.when(j == 0)
    def _():
        ffn_open(x_ref, ctx_ref, gain_ref, wo_ref, gres_ref, res, n, acc)
    a, b = ffn_block(g_ref, gu_ref, dn_ref, gres_ref, ddn_ref, n, acc)
    dgu_ref[0] = a.reshape(dgu_ref.shape[1:])
    dgu_ref[1] = b.reshape(dgu_ref.shape[1:])
    @pl.when(j == pl.num_programs(0) - 1)
    def _():
        R = x_ref.shape[0]
        total = sum(ffn_close(slice(t, t + 384), g_ref, gain_ref, wo_ref, out_ref, gres_ref, gctx_ref, res, n, acc) for t in range(0, R, 384))
        ggain_ref[...] = jnp.broadcast_to(total, ggain_ref.shape)
        dwo_ref[...] = dot_tl(ctx_ref[...], n[...]).astype(bf)

def ffn_sum_kernel(x_ref, ctx_ref, g_ref, small_ref, wo_ref, gu_ref, dn_ref,
                   out_ref, gres_ref, gctx_ref, dwo_ref, ggain_ref, ddn_ref, dgu_ref, res, n, acc, gain_ref, *bufs):
    j = pl.program_id(0)
    N = pl.num_programs(0) - 3
    src = bufs[0]
    @pl.when(j == 0)
    def _():
        rs_greet()
        for t in range(8):
            gain_ref[:, 128 * t:128 * t + 128] = small_ref[t, 1:2, :].astype(f32)
        ffn_open(x_ref, ctx_ref, gain_ref, wo_ref, gres_ref, res, n, acc)
        ggain_ref[...] = jnp.zeros_like(ggain_ref)
    @pl.when(j < N)
    def _():
        a, b = ffn_block(g_ref, gu_ref, dn_ref, gres_ref, ddn_ref, n, acc)
        k = lax.rem(j, 2)
        rows = a.shape[0] // 8
        src[k, :, :, 0:rows] = a.reshape(4, 2, rows, a.shape[1])
        src[k, :, :, rows:2 * rows] = b.reshape(4, 2, rows, a.shape[1])
    @pl.when(j >= N)
    def _():
        part = x_ref.shape[0] // 3
        s = pl.ds(pl.multiple_of((j - N) * part, part), part)
        total = ffn_close(s, g_ref, gain_ref, wo_ref, out_ref, gres_ref, gctx_ref, res, n, acc)
        ggain_ref[...] = ggain_ref[...] + jnp.broadcast_to(total, ggain_ref.shape)
    h = dgu_ref.shape[1] // 2
    plane, z = bufs[:12], bufs[12:]
    ahead = z[3].shape[0]
    def put(t, top, low):
        @pl.when(t < ahead)
        def _():
            z[0][lax.rem(t, 4), 0:h] = top
            z[0][lax.rem(t, 4), h:2 * h] = low
        @pl.when(t >= ahead)
        def _():
            dgu_ref[t, 0:h] = top
            dgu_ref[t, h:2 * h] = low
    z_step(j - 3, ahead, z, lambda: plane_step(j, N, plane, put))
    @pl.when(j == N + 2)
    def _():
        dwo_ref[...] = dot_tl(ctx_ref[...], n[...]).astype(bf)
        dgu_ref[0:ahead] = z[3][...]

def ffn(x, ctx, g, gain, wo, gu, dn, near, block=256):
    R, d = x.shape
    F = dn.shape[0]
    k = gu.shape[1]
    N = F // block
    sds = jax.ShapeDtypeStruct
    one = lambda *s: pl.BlockSpec(s, lambda j: (0,) * len(s), pipeline_mode=pl.Buffered(1))
    at = lambda j: jnp.minimum(j, N - 1)
    gub = pl.BlockSpec((2, k, d // k, block), lambda j: (0, 0, 0, at(j)))
    dnb = pl.BlockSpec((block, d), lambda j: (at(j), 0))
    rows = 2 * (d // k)
    gain_spec = pl.BlockSpec((8, 16, 128), lambda j: (0, 0, 3 * d // 128), pipeline_mode=pl.Buffered(1)) if near else one(1, d)
    if near:
        body, extra, steps, last = ffn_sum_kernel, [pltpu.VMEM((1, d), f32)] + plane_scratch(rows, block) + z_scratch(N - 3, rows, block), N + 3, (one(N, rows, block), sds((N, rows, block), bf))
        params = pltpu.CompilerParams(vmem_limit_bytes=61 * 2**20, collective_id=3, has_side_effects=True)
    else:
        body, extra, steps, last = ffn_kernel, [], N, (gub, sds(gu.shape, bf))
        params = pltpu.CompilerParams(vmem_limit_bytes=61 * 2**20)
    return pl.pallas_call(body, grid=(steps,),
        in_specs=[one(R, d), one(R, d), one(R, d), gain_spec, one(d, d), gub, dnb],
        out_specs=[one(R, d), one(R, d), one(R, d), one(d, d), one(8, d), dnb, last[0]],
        out_shape=[sds((R, d), bf), sds((R, d), f32), sds((R, d), bf), sds((d, d), bf), sds((8, d), f32), sds(dn.shape, bf), last[1]],
        scratch_shapes=[pltpu.VMEM((R, d), f32), pltpu.VMEM((R, d), bf), pltpu.VMEM((R, d), f32)] + extra,
        compiler_params=params, name="ffn")(x, ctx, g, gain, wo, gu, dn)

def sum_rounds(s, box, inbox, send, recv):
    b, m, c, mx, my, md = places()
    peers = [(b, m, 1 - c), (b, mx, c), (b, my, c), (b + 1 - 2 * lax.rem(b, 2), m, c), (3 - b, m, c)]
    def copy(r):
        return pltpu.make_async_remote_copy(src_ref=box.at[r], dst_ref=inbox.at[r], send_sem=send.at[r], recv_sem=recv.at[r], device_id=peers[r], device_id_type=MESH)
    for r in range(5):
        @pl.when(s == r)
        def _():
            copy(r).start()
        @pl.when(s == r + 1)
        def _():
            copy(r).wait()
            box[r + 1] = box[r] + inbox[r]

def bwd_sum_kernel(q_ref, k_ref, v_ref, do_ref, o_ref, r_ref, e_ref, n_ref, x_ref, gres_ref, gains_ref, wq_ref, wk_ref, wv_ref, dn_ref, wo_ref, gain2_ref, gu_ref, const_ref,
                   gtok_ref, small_ref, out_a, out_b, out_c, rhs, vaug, dobd, qaug, ds_ref, nacc, near_ref, far_ref, ggain, tab, g_all, gain_ref, box, inbox, ssend, srecv, osem, *bufs):
    p = pl.program_id(0)
    N = pl.num_programs(0) - DRAIN
    plane_a, z_a, plane_b, z_b, z_c = bufs[0:12], bufs[12:18], bufs[18:30], bufs[30:36], bufs[36:42]
    src_a, src_b = plane_a[0], plane_b[0]
    done_a, done_b, done_c = z_a[3], z_b[3], z_c[3]
    NA, NC = done_a.shape[0], done_c.shape[0]
    d = gtok_ref.shape[1]
    k = lax.rem(p, 2)
    def put(src, arrays):
        h = src.shape[3] // 2
        at = 0
        for a in arrays:
            r = a.shape[1] // 2
            a = a.reshape((4, 2) + a.shape[1:])
            src[k, :, :, at:at + r] = a[:, :, 0:r]
            src[k, :, :, h + at:h + at + r] = a[:, :, r:2 * r]
            at += r
    @pl.when(p == 0)
    def _():
        rs_greet()
        for t in range(8):
            gain_ref[:, 128 * t:128 * t + 128] = gains_ref[t, 0:1, :].astype(f32)
        bwd_open(rhs, vaug, qaug)
        gtok_ref[...] = jnp.zeros_like(gtok_ref)
        ggain[...] = jnp.zeros_like(ggain)
    @pl.when(p < NA)
    def _():
        put(src_a, (dn_ref[...], wo_ref[...]))
    sum_step(p, NA, plane_a, z_a)
    @pl.when(p < N)
    def _():
        g = jnp.concatenate(bwd_pair(q_ref, k_ref, v_ref, do_ref, o_ref, r_ref, e_ref, near_ref, far_ref, rhs, vaug, dobd, qaug, ds_ref, nacc), 1)
        lane = lax.broadcasted_iota(jnp.int32, (1, 128), 1)
        sums = jnp.dot(near_ref[...], const_ref[...], precision=lax.Precision.HIGHEST, preferred_element_type=f32)
        for a in range(2):
            lo, hi = (jnp.sum(jnp.where(lax.rem(lane, 2) == a, far_ref[i:i + 1, :], 0.0), axis=1, keepdims=True) for i in range(2))
            tab[p, a:a + 1, :] = sums[a:a + 1, :] + jnp.where(lane == 15, lo, 0.0) + jnp.where(lane == 31, hi, 0.0)
        g_all[p] = g
        gw = dot_tl(n_ref[...], g)
        half = pl.ds(pl.multiple_of(lax.rem(p, 2) * 128, 128), 128)
        w = jnp.concatenate([w_ref[:, :, half].reshape(d, 128) for w_ref in (wq_ref, wk_ref, wv_ref)], 1)
        ggain[...] = ggain[...] + sum((gw * w.astype(f32))[:, 128 * t:128 * t + 128] for t in range(3))
        gw = gw.astype(bf)
        put(src_b, [gw[:, 128 * t:128 * t + 128].reshape(8, d // 8, 128) for t in range(3)])
    @pl.when((p >= N) & (p < N + N // 2))
    def _():
        i = 2 * (p - N)
        g = jnp.concatenate([g_all[i], g_all[i + 1]], 1)
        w = jnp.concatenate([w_ref[:, :, 128 * t:128 * t + 128].reshape(d, 128) for t in range(2) for w_ref in (wq_ref, wk_ref, wv_ref)], 1)
        gtok_ref[...] = gtok_ref[...] + dot_nt(g, w)
    @pl.when(p >= N + N // 2)
    def _():
        rows = x_ref.shape[0]
        step = rows // 3
        for t in range(3):
            s = pl.ds(pl.multiple_of((p - N - N // 2) * rows + t * step, step), step)
            x = x_ref[t * step:t * step + step, :].astype(f32)
            r = lax.rsqrt(jnp.mean(x * x, axis=-1, keepdims=True) + EPS)
            m = x * r
            w = gtok_ref[s, :] * gain_ref[0:1, :]
            gtok_ref[s, :] = gres_ref[t * step:t * step + step, :] + r * (w - m * jnp.mean(w * m, axis=-1, keepdims=True))
    @pl.when(p == N - 1)
    def _():
        for t in range(N):
            box[0, 2 * t:2 * t + 2] = tab[t, 0:2]
        w = d // 8
        one = jnp.sum(ggain[...].T, axis=0, keepdims=True) / gain_ref[0:1, :]
        for t in range(8):
            box[0, 2 * N + t:2 * N + t + 1] = one[:, w * t:w * t + w]
            box[0, 2 * N + 8 + t:2 * N + 9 + t] = gain2_ref[0:1, w * t:w * t + w]
    sum_rounds(p - N + 1, box, inbox, ssend, srecv)
    sum_step(p, N, plane_b, z_b)
    def take():
        @pl.when(p < NC)
        def _():
            z_c[0][lax.rem(p, 4)] = gu_ref[...]
    z_step(p, NC, z_c, take)
    @pl.when(p == N + DRAIN - 1)
    def _():
        small_ref[...] = box[5]
        keeps = [pltpu.make_async_copy(a, o, osem.at[i]) for i, (a, o) in enumerate(((done_a, out_a), (done_b, out_b), (done_c, out_c)))]
        for copy in keeps:
            copy.start()
        for copy in keeps:
            copy.wait()

def attn_bwd_sum(qkv, do, o, r, e, n, x, gres, qkv_w, dn, wo, gain2, gu):
    R, d = x.shape
    N = d // 128
    NA, wide = N, 128
    rows_a, rows_b = dn.shape[1] + wo.shape[1], 3 * (d // 8)
    sds = jax.ShapeDtypeStruct
    at = lambda p: jnp.minimum(p, N - 1)
    after = lambda p: jnp.clip(p - N - N // 2, 0, 1)
    spec = pl.BlockSpec((R, 128), lambda p: (0, at(p)))
    head = lambda t: pl.BlockSpec((None, R, 128), lambda p: (t * N + at(p), 0, 0))
    one = lambda *s: pl.BlockSpec(s, lambda p: (0,) * len(s), pipeline_mode=pl.Buffered(1))
    part = pl.BlockSpec((R // 2, d), lambda p: (after(p), 0), pipeline_mode=pl.Buffered(1))
    cols = lambda a, t: pl.BlockSpec((8, a.shape[1], 256), lambda p: (0, 0, t * (N // 2) + jnp.where(p < N, p // 2, jnp.minimum(p - N, N // 2 - 1))))
    early = lambda a: pl.BlockSpec((8, a.shape[1], wide), lambda p: (0, 0, jnp.minimum(p, NA - 1)), pipeline_mode=pl.Buffered(1))
    hbm = pl.BlockSpec(memory_space=pl.ANY)
    dma = pltpu.SemaphoreType.DMA
    small = (2 * N + 16, d // 8)
    NC = 3
    left = gu.shape[0] - NC
    rest = (NC,) + gu.shape[1:]
    to_bucket = jnp.asarray((bucket_np(np.arange(512) - 255)[:, None] == np.arange(128)[None, :]).astype(np.float32))
    return pl.pallas_call(bwd_sum_kernel, grid=(N + DRAIN,),
        in_specs=[head(0), head(1), head(2)] + [spec] * 3 + [pl.BlockSpec((None, None, R, NT * 256), lambda p: (0, at(p), 0, 0)), one(R, d), part, part, pl.BlockSpec((8, 16, 128), lambda p: (0, 0, 3 * d // 128), pipeline_mode=pl.Buffered(1)),
                  cols(qkv_w, 0), cols(qkv_w, 1), cols(qkv_w, 2), early(dn), early(wo), one(8, d),
                  pl.BlockSpec((None,) + gu.shape[1:], lambda p: (left + jnp.minimum(p, NC - 1), 0, 0)), one(512, 128)],
        out_specs=[one(R, d), one(*small), hbm, hbm, hbm],
        out_shape=[sds((R, d), f32), sds(small, f32), sds((NA, rows_a, wide), bf), sds((N, rows_b, 128), bf), sds(rest, bf)],
        scratch_shapes=[pltpu.VMEM((256, NT * 256), bf), pltpu.VMEM((R, 256), bf), pltpu.VMEM((NT * 256, 128), bf), pltpu.VMEM((NT * 256, 256), bf), pltpu.VMEM((R, NT * 256), bf), pltpu.VMEM((384, 256), f32),
                        pltpu.VMEM((8, 512), f32), pltpu.VMEM((8, 128), f32), pltpu.VMEM((d, 128), f32), pltpu.VMEM((N, 8, 128), f32), pltpu.VMEM((N, R, 384), bf), pltpu.VMEM((1, d), f32), pltpu.VMEM((6,) + small, f32), pltpu.VMEM((5,) + small, f32), dma((5,)), dma((5,)), dma((3,))]
                       + plane_scratch(rows_a, wide) + z_scratch(NA, rows_a, wide) + plane_scratch(rows_b, 128) + z_scratch(N, rows_b, 128) + z_scratch(*rest),
        compiler_params=pltpu.CompilerParams(vmem_limit_bytes=63 * 2**20, collective_id=4, has_side_effects=True), name="attn_bwd_sum")(
            qkv, qkv, qkv, do, o, r, e, n, x, gres, qkv_w, qkv_w, qkv_w, qkv_w, dn, wo, gain2, gu, to_bucket)

def finish_kernel(gtok_in, out_in, a_in, b_in, c_in, d_in, small_in, at_ref, gtok, out, *rest):
    outs, (gain1, gain2, table), big, sem = rest[:7], rest[7:10], rest[10:17], rest[17]
    q, k, v, wo, gate, up, dn = big
    keeps = [pltpu.make_async_copy(a, b, sem.at[i]) for i, (a, b) in enumerate(zip(big, outs))]
    gtok[...] = gtok_in[...]
    out[...] = out_in[...]
    @pl.when(pl.program_id(0) == 0)
    def _():
        def spread(src, targets):
            n, h, w = src.shape[0], src.shape[1] // 2, src.shape[2]
            for t in range(n):
                at = 0
                for ref in targets:
                    r = ref.shape[0] // 2
                    ref[0:r, w * t:w * t + w] = src[t, at:at + r].astype(f32)
                    ref[r:2 * r, w * t:w * t + w] = src[t, h + at:h + at + r].astype(f32)
                    at += r
        spread(a_in, (dn, wo))
        spread(b_in, (q, k, v))
        r = gate.shape[0]
        w = c_in.shape[2]
        left = c_in.shape[0] - d_in.shape[0]
        for t in range(c_in.shape[0]):
            both = c_in[t] if t < left else d_in[t - left]
            gate[:, w * t:w * t + w] = both[0:r].astype(f32)
            up[:, w * t:w * t + w] = both[r:2 * r].astype(f32)
        me = at_ref[0]
        heads = small_in.shape[0] - 16
        per = heads // 8
        gain1[...] = small_in[pl.ds(heads + me, 1), :]
        gain2[...] = small_in[pl.ds(heads + 8 + me, 1), :]
        rows = small_in[pl.ds(per * me, per), :]
        for t in range(per):
            table[:, BUCKETS * t:BUCKETS * t + BUCKETS] = rows[t:t + 1, 0:BUCKETS]
        for copy in keeps:
            copy.start()
    @pl.when(pl.program_id(0) == pl.num_programs(0) - 1)
    def _():
        for copy in keeps:
            copy.wait()

def finish(gtok, out, a, b, c, last, small, at, rows, ff):
    R, d = gtok.shape
    steps = 4
    sds = jax.ShapeDtypeStruct
    block = pl.BlockSpec((R // steps, d), lambda i: (i, 0))
    one = lambda *s: pl.BlockSpec(s, lambda i: (0,) * len(s), pipeline_mode=pl.Buffered(1))
    whole = lambda x: one(*x.shape)
    shapes = [(rows, d)] * 4 + [(rows, ff)] * 2 + [(ff // 8, d), (1, d // 8), (1, d // 8), (1, (small.shape[0] - 16) // 8 * BUCKETS)]
    return pl.pallas_call(finish_kernel, grid=(steps,),
        in_specs=[block, block, whole(a), whole(b), whole(c), whole(last), whole(small), pl.BlockSpec(memory_space=pltpu.SMEM)],
        out_specs=[block, block] + [pl.BlockSpec(memory_space=pl.ANY)] * 7 + [one(*s) for s in shapes[7:]],
        out_shape=[sds((R, d), f32), sds((R, d), bf)] + [sds(s, f32) for s in shapes],
        scratch_shapes=[pltpu.VMEM(s, f32) for s in shapes[:7]] + [pltpu.SemaphoreType.DMA((7,))],
        compiler_params=pltpu.CompilerParams(vmem_limit_bytes=62 * 2**20), name="finish")(gtok, out, a, b, c, last, small, at)

def contract_rows(left, right):
    return lax.dot_general(left, right, (((0,), (0,)), ((), ())), preferred_element_type=f32)

def contract_cols(left, right):
    return lax.dot_general(left, right, (((1,), (1,)), ((), ())), preferred_element_type=f32)

def rms_norm(inputs, gain):
    return inputs * lax.rsqrt(jnp.mean(inputs * inputs, axis=-1, keepdims=True) + EPS) * gain

def gather(x):
    return lax.all_gather(x, SHARD, axis=0, tiled=False)

def scatter(x):
    return lax.psum_scatter(x, SHARD, scatter_dimension=0, tiled=True)

def per_device(near, tokens, row_kind, text_length, gain_attn, position_bias_table, weight_query, weight_key, weight_value, weight_out, gain_ffn, weight_gate, weight_up, weight_down, cotangent):
    n1, d = weight_query.shape
    n2 = position_bias_table.shape[0]
    inputs = tokens.astype(f32)
    at = lax.axis_index("dp") * lax.axis_size("narrow") + lax.axis_index("narrow")
    if near:
        context, e, r, normed, qkv, qkv_w, gu_w, down_w, out_w = front(
            row_kind, text_length, tokens, gain_attn, gain_ffn, position_bias_table, weight_query, weight_key, weight_value, weight_gate, weight_up, weight_down, weight_out)
    else:
        small = gather(jnp.stack([gain_attn, gain_ffn, jnp.pad(position_bias_table, (0, n1 - n2))]))
        qkv_w = gather(jnp.concatenate([weight_query, weight_key, weight_value], 1))
        gain_one, gain_two = small[:, 0].reshape(d).astype(f32), small[:, 1].reshape(d).astype(f32)
        normed = rms_norm(inputs, gain_one).astype(bf)
        q, k, v = (dot(normed, qkv_w[:, :, t * d:t * d + d].reshape(d, d)).astype(bf) for t in range(3))
        far, w = tables(small[:, 2, :n2].reshape(-1))
        context, e, r = attn_fwd(q, k, v, mask_cols(row_kind, text_length), far, w)
        gu_w, down_w, out_w = jnp.moveaxis(gather(jnp.stack([weight_gate, weight_up])), 0, 1), gather(weight_down), gather(weight_out)
    ff = gu_w.shape[-1]
    output, grad_residual, grad_context, grad_out_w, g_gain_two, ddn, dgu = ffn(
        tokens, context, cotangent, qkv_w if near else gain_two.reshape(1, d), out_w.reshape(d, d), gu_w, down_w.reshape(ff, d), near)
    if near:
        shards = gu_w.shape[1]
        grad_tokens, small_g, sums_a, sums_b, sums_c = attn_bwd_sum(
            qkv, grad_context, context, r, e, normed, tokens, grad_residual, qkv_w,
            ddn.reshape(shards, ff // shards, d), grad_out_w.reshape(shards, n1, d), g_gain_two, dgu)
        grad_tokens, output, s_q, s_k, s_v, s_out, s_gate, s_up, s_down, r_gain_one, r_gain_two, r_table = finish(
            grad_tokens, output, sums_a, sums_b, dgu, sums_c, small_g, at.reshape(1), n1, ff)
        r_gain_one, r_gain_two, r_table = r_gain_one.reshape(n1), r_gain_two.reshape(n1), r_table.reshape(n2)
    else:
        total = lambda x: lax.psum(scatter(x), "batch").astype(f32)
        gq, gk, gv, near_sums, far_sums = attn_bwd(q, k, v, grad_context, context, r, e)
        grads = (gq, gk, gv)
        s_gate, s_up, s_down, s_out = (total(x) for x in (dgu[0].reshape(d, ff), dgu[1].reshape(d, ff), ddn, grad_out_w))
        s_q, s_k, s_v = (total(contract_rows(normed, x).astype(bf)) for x in grads)
        grad_normed = sum(contract_cols(x, qkv_w[:, :, t * d:t * d + d].reshape(d, d)) for t, x in enumerate(grads))
        _, first_pull = jax.vjp(rms_norm, inputs, gain_one)
        share, g_gain_one = first_pull(grad_normed)
        grad_tokens = grad_residual + share
        g_table = table_grad(near_sums, far_sums)
        small_g = lax.psum(jnp.concatenate([g_gain_one, g_gain_two[0], g_table]), ("batch", "dp", "narrow"))
        r_gain_one = lax.dynamic_slice_in_dim(small_g, at * n1, n1)
        r_gain_two = lax.dynamic_slice_in_dim(small_g, d + at * n1, n1)
        r_table = lax.dynamic_slice_in_dim(small_g, 2 * d + at * n2, n2)
    return (output, grad_tokens, r_gain_one, r_table, s_q, s_k, s_v, s_out, r_gain_two, s_gate, s_up, s_down)

def solution(mesh):
    near = (mesh.shape["batch"], mesh.shape["dp"], mesh.shape["narrow"]) == (4, 4, 2)
    placed = (
        P(("batch", "dp", "narrow"), None),
        P(("batch", "dp", "narrow")),
        P(("batch", "dp", "narrow"), None),
        P(("dp", "narrow")),
        P(("dp", "narrow")),
        P(("dp", "narrow"), None),
        P(("dp", "narrow"), None),
        P(("dp", "narrow"), None),
        P(("dp", "narrow"), None),
        P(("dp", "narrow")),
        P(("dp", "narrow"), None),
        P(("dp", "narrow"), None),
        P(("dp", "narrow"), None),
        P(("batch", "dp", "narrow"), None),
    )
    return jax.shard_map(
        functools.partial(per_device, near),
        mesh=mesh,
        in_specs=placed,
        out_specs=(
            P(("batch", "dp", "narrow"), None),
            P(("batch", "dp", "narrow"), None),
            P(("dp", "narrow")),
            P(("dp", "narrow")),
            P(("dp", "narrow"), None),
            P(("dp", "narrow"), None),
            P(("dp", "narrow"), None),
            P(("dp", "narrow"), None),
            P(("dp", "narrow")),
            P(("dp", "narrow"), None),
            P(("dp", "narrow"), None),
            P(("dp", "narrow"), None),
        ),
        check_vma=False,
    )
```
